32 devices in a mesh: rep: 4 (over x, core), ctx: 8 (over z, y).
Axes of the slice: x: 2, y: 2, z: 4, core: 2. Of those that a mesh axis runs over, the one named last changes fastest.
Arguments:
- block_in: bfloat16 [2, 4, 1024, 1024], P(None, 'rep', 'ctx'), may hold values from -6 to 6
- lengths: int32 [2, 4], P(None, 'rep'), may hold values from 1024 to 1024, as said below
- norm_gains: bfloat16 [2, 1024], P(None, 'ctx'), may hold values from 0.5 to 1.5
- w_in: bfloat16 [1024, 6144], P('ctx'), may hold values from -0.1875 to 0.1875
- w_small: bfloat16 [1024, 24], P('ctx'), may hold values from -0.1875 to 0.1875
- conv_weight: bfloat16 [4, 5120], P(None, 'ctx'), may hold values from -3 to 3
- decay_log: float32 [8], replicated, may hold values from 0 to 2.7726
- decay_bias: float32 [8], replicated, may hold values from -6.9073 to -2.2521
- out_norm_gain: float32 [128], replicated, may hold values from 0.5 to 1.5
- w_out: bfloat16 [1024, 1024], P('ctx'), may hold values from -0.375 to 0.375
- gate_up_weight: bfloat16 [1024, 5632], P('ctx'), may hold values from -0.1875 to 0.1875
- w_down: bfloat16 [2816, 1024], P('ctx'), may hold values from -0.21875 to 0.21875
- out_cotangent: bfloat16 [2, 4, 1024, 1024], P(None, 'rep', 'ctx'), may hold values from -6 to 6
Outputs:
- block_out: bfloat16 [2, 4, 1024, 1024], P(None, 'rep', 'ctx')
- in_grad: bfloat16 [2, 4, 1024, 1024], P(None, 'rep', 'ctx')
- grad_norm_gains: float32 [2, 1024], P(None, 'ctx')
- grad_w_in: float32 [1024, 6144], P('ctx')
- grad_w_small: float32 [1024, 24], P('ctx')
- grad_conv_weight: float32 [4, 5120], P(None, 'ctx')
- grad_decay_log: float32 [8], replicated
- grad_decay_bias: float32 [8], replicated
- grad_out_norm_gain: float32 [128], replicated
- grad_w_out: float32 [1024, 1024], P('ctx')
- grad_w_gate_up: float32 [1024, 5632], P('ctx')
- grad_w_down: float32 [2816, 1024], P('ctx')
The draws below stay inside these ranges and needn't reach their ends.
Inputs may be any that keep to these rules, and one draw needn't show every extreme that they name: `lengths`: in each micro-batch, one of its 4 sequences has length 1024 and another has length min(1024, 1024).
All inputs are finite; a program needn't handle non-finite values.
Results may differ from the reference program's by a relative error of at most 0.017.
Values may be sent and summed in bfloat16 or wider, within the bound.
A program may use at most 448 MiB of HBM per device.

```python
import math
import jax
import jax.numpy as jnp
from jax import lax

D = 1024
HEADS = 8
HEAD_DIM = 128
FF = 2816
STEPS = 2
CONV = 4
STRETCH = 64
MB = 2
MIN_LEN = 1024
SEQ_LEN = 1024
SEQS_MB = 4


def draw_lengths(key, part):
    lowest = min(MIN_LEN, SEQ_LEN)
    others = max(SEQS_MB - 1, 1)
    key_draw = jax.random.fold_in(key, 11)
    key_full = jax.random.fold_in(key, 23)
    key_short = jax.random.fold_in(key, 37)
    drawn = jax.random.randint(key_draw, (MB, SEQS_MB), lowest, SEQ_LEN + 1)
    full_slot = jax.random.randint(key_full, (MB, 1), 0, SEQS_MB)
    short_step = jax.random.randint(key_short, (MB, 1), 0, others)
    short_slot = (full_slot + 1 + short_step) % SEQS_MB
    slots = lax.broadcasted_iota(jnp.int32, (MB, SEQS_MB), 1)
    with_short = jnp.where(slots == short_slot, lowest, drawn)
    return jnp.where(slots == full_slot, SEQ_LEN, with_short).astype(jnp.int32)


def draw_decay_log(key, part):
    rates = jax.random.uniform(jax.random.fold_in(key, 41), (HEADS,), jnp.float32, 1.0, 16.0)
    return jnp.log(rates).astype(jnp.float32)


def draw_decay_bias(key, part):
    exponent = jax.random.uniform(jax.random.fold_in(key, 53), (HEADS,), jnp.float32, math.log(0.001), math.log(0.1))
    steps_dt = jnp.exp(exponent)
    return jnp.log(jnp.expm1(steps_dt)).astype(jnp.float32)


def level_of(own_key, shape, split, least, largest):
    def one(position, shards_of):
        steps = jax.random.uniform(jax.random.fold_in(jax.random.fold_in(own_key, 6), position), (shards_of,), jnp.float32, least / len(split), largest / len(split))
        return jnp.repeat(jnp.exp(steps), shape[position] // shards_of).reshape((-1,) + (1,) * (len(shape) - position - 1))

    level = one(*split[0])
    for cut in split[1:]:
        level = level * one(*cut)
    return level


def centred(own_key, dims, scale, limit, split=(), kind=jnp.bfloat16):
    factor_of = level_of(own_key, dims, split, -0.22, 0.18) if split else 1.0
    entries = jax.random.normal(own_key, dims, jnp.float32) * scale * factor_of
    return jnp.minimum(jnp.maximum(entries, -limit), limit).astype(kind)


def setup_inputs(seed: int = 0) -> dict:
    keys = jax.random.split(jax.random.key(seed), 14)
    return {
        "block_in": centred(keys[0], (MB, SEQS_MB, SEQ_LEN, D), 1.0, 6.0, ((1, 4), (2, 8))),
        "lengths": draw_lengths(jax.random.fold_in(keys[13], 71), 0),
        "norm_gains": jnp.clip(1.0 + 0.1 * jax.random.normal(keys[2], (2, D), jnp.float32), 0.5, 1.5).astype(jnp.bfloat16),
        "w_in": centred(keys[3], (D, (2 + 2 * STEPS) * D), D ** -0.5, 0.1875, ((0, 8),)),
        "w_small": centred(keys[4], (D, (STEPS + 1) * HEADS), D ** -0.5, 0.1875, ((0, 8),)),
        "conv_weight": centred(keys[5], (CONV, (1 + 2 * STEPS) * D), CONV ** -0.5, 3.0, ((1, 8),)),
        "decay_log": draw_decay_log(jax.random.fold_in(keys[13], 71), 0),
        "decay_bias": draw_decay_bias(jax.random.fold_in(keys[13], 71), 0),
        "out_norm_gain": jnp.clip(1.0 + 0.1 * jax.random.normal(keys[8], (HEAD_DIM,), jnp.float32), 0.5, 1.5),
        "w_out": centred(keys[9], (D, D), (D // 4) ** -0.5, 0.375, ((0, 8),)),
        "gate_up_weight": centred(keys[10], (D, 2 * FF), D ** -0.5, 0.1875, ((0, 8),)),
        "w_down": centred(keys[11], (FF, D), (FF // 4) ** -0.5, 0.21875, ((0, 8),)),
        "out_cotangent": centred(keys[12], (MB, SEQS_MB, SEQ_LEN, D), 1.0, 6.0, ((1, 4), (2, 8))),
    }


@jax.custom_vjp
def low(v):
    return lax.optimization_barrier(v.astype(jnp.bfloat16)).astype(jnp.float32)

@jax.custom_vjp
def low_back(v):
    return v

def low_keep(v):
    return (low(v), None)

def low_pass(kept, grad):
    return (grad,)

def back_keep(v):
    return (v, None)

def back_low(kept, grad):
    return (low(grad),)
low.defvjp(low_keep, low_pass)
low_back.defvjp(back_keep, back_low)
EPS = 1e-06
HIGH_PRECISION = lax.Precision.HIGHEST

def mat_high(left, right):
    return jnp.dot(left, right, precision=HIGH_PRECISION, preferred_element_type=jnp.float32)

def rms_gain(values, gain):
    return values * lax.rsqrt(lax.optimization_barrier(jnp.mean(values * values, axis=-1, keepdims=True)) + EPS) * gain

def token_step(recurrent_state, inputs):
    single_query_row, key_matrix_rows, value_rows, beta_rows, gamma_row = inputs
    recurrent_state = recurrent_state * jnp.exp(gamma_row)[:, None, None]
    for householder_substep in range(STEPS):
        state_readout = jnp.einsum('xa,xag->xg', key_matrix_rows[householder_substep], recurrent_state, precision=HIGH_PRECISION)
        recurrent_state = recurrent_state + beta_rows[householder_substep][:, None, None] * key_matrix_rows[householder_substep][:, :, None] * (value_rows[householder_substep] - state_readout)[:, None, :]
    return (recurrent_state, jnp.einsum('xa,xag->xg', single_query_row, recurrent_state, precision=HIGH_PRECISION))

def block_step(recurrent_state, inputs):
    return lax.scan(token_step, recurrent_state, inputs)

def recurrence(query, key_all, value_all, beta, gamma):
    length = query.shape[0]
    blocks = length // STRETCH

    def folded(array):
        return array.reshape((blocks, STRETCH) + array.shape[1:])
    start = jnp.zeros((HEADS, HEAD_DIM, HEAD_DIM), query.dtype)
    final_state, outputs = lax.scan(jax.checkpoint(block_step), start, tuple((folded(a) for a in (query, key_all, value_all, beta, gamma))))
    return outputs.reshape((length, HEADS, HEAD_DIM))

def layer(seq_in, weight_set, valid):
    gain_pair, w_in, w_small, conv_weight, decay_log, decay_bias, out_gain, w_out, gate_up_weight, w_down = weight_set
    length = seq_in.shape[0]
    channels = (1 + 2 * STEPS) * D
    h_first = low(rms_gain(seq_in, gain_pair[0]))
    projected = low_back(mat_high(h_first, w_in))
    small_proj = low_back(mat_high(h_first, w_small))
    padded_rows = jnp.concatenate([jnp.zeros((CONV - 1, channels), projected.dtype), projected[:, :channels]], axis=0)
    convolved = conv_weight[0] * padded_rows[0:length]
    for offset in range(1, CONV):
        convolved = convolved + conv_weight[offset] * padded_rows[offset:offset + length]
    activated = jax.nn.silu(convolved)
    query = activated[:, :D].reshape(length, HEADS, HEAD_DIM)
    key_all = activated[:, D:(1 + STEPS) * D].reshape(length, STEPS, HEADS, HEAD_DIM)
    key_all = key_all * lax.rsqrt(lax.optimization_barrier(jnp.sum(key_all * key_all, axis=-1, keepdims=True)) + EPS)
    value_all = activated[:, (1 + STEPS) * D:].reshape(length, STEPS, HEADS, HEAD_DIM)
    beta = jax.nn.sigmoid(small_proj[:, :STEPS * HEADS]).reshape(length, STEPS, HEADS)
    gamma = -jnp.exp(decay_log) * jax.nn.softplus(small_proj[:, STEPS * HEADS:] + decay_bias)
    head_out = recurrence(query, key_all, value_all, beta, gamma)
    gate_z = projected[:, channels:].reshape(length, HEADS, HEAD_DIM)
    normed = head_out * lax.rsqrt(lax.optimization_barrier(jnp.mean(head_out * head_out, axis=-1, keepdims=True)) + EPS) * out_gain * jax.nn.silu(gate_z)
    mixer = low(normed.reshape(length, D))
    resid = seq_in + low_back(mat_high(mixer, w_out))
    h_second = low(rms_gain(resid, gain_pair[1]))
    gate_up = low_back(mat_high(h_second, gate_up_weight))
    hidden = low(jax.nn.silu(gate_up[:, :FF]) * gate_up[:, FF:])
    return valid[:, None] * (resid + low_back(mat_high(hidden, w_down)))

def reference(block_in, lengths, norm_gains, w_in, w_small, conv_weight, decay_log, decay_bias, out_norm_gain, w_out, gate_up_weight, w_down, out_cotangent):
    weight_set = tuple((a.astype(jnp.float32) for a in (norm_gains, w_in, w_small, conv_weight, decay_log, decay_bias, out_norm_gain, w_out, gate_up_weight, w_down)))
    seq_total = MB * SEQS_MB
    inputs = block_in.reshape(seq_total, SEQ_LEN, D).astype(jnp.float32)
    cotangents = out_cotangent.reshape(seq_total, SEQ_LEN, D).astype(jnp.float32)
    seq_lengths = lengths.reshape(seq_total).astype(jnp.int32)
    places = jnp.arange(SEQ_LEN, dtype=jnp.int32)

    def per_sequence(summed, item):
        seq_in, seq_cot, seq_len = item
        valid = (places < seq_len).astype(seq_in.dtype)
        result, pull = jax.vjp(lambda rows, weights: layer(rows, weights, valid), seq_in, weight_set)
        grad_rows, grad_weights = pull(seq_cot)
        summed = jax.tree.map(lambda left, right: left + right, summed, grad_weights)
        return (summed, (result.astype(jnp.bfloat16), grad_rows.astype(jnp.bfloat16)))
    start = jax.tree.map(jnp.zeros_like, weight_set)
    summed, (results, grad_rows) = lax.scan(per_sequence, start, (inputs, cotangents, seq_lengths))
    return (results.reshape(block_in.shape), grad_rows.reshape(block_in.shape), summed[0], summed[1], summed[2], summed[3], summed[4], summed[5], summed[6], summed[7], summed[8], summed[9])
```

```python
import functools
import jax
import jax.numpy as jnp
from jax import lax
from jax.experimental import pallas as pl
from jax.experimental.pallas import tpu as pltpu
from jax.sharding import PartitionSpec as P

STEPS = 2
CONV = 4
STRETCH = 64
HEADS = 8
EPS = 1e-06
WIDE = 2 * STRETCH


def low(a):
    return a.astype(jnp.bfloat16)


def halves(a):
    high = low(a)
    return high, low(a - high.astype(jnp.float32))


def dot(a, b, dims):
    return lax.dot_general(a, b, (dims, ((), ())), preferred_element_type=jnp.float32)


def fold(out):
    half = out.shape[1] // 2
    return out[:, :half] + out[:, half:]


def left_nn(parts):
    return jnp.concatenate(parts, axis=1)


def right_nn(parts):
    row = jnp.concatenate(parts, axis=1)
    return jnp.concatenate([row, row], axis=0)


def right_nt(parts):
    high, rest = parts
    return jnp.concatenate(
        [jnp.concatenate([high, high], axis=1), jnp.concatenate([rest, rest], axis=1)], axis=0
    )


def mul(a, b):
    return fold(dot(left_nn(halves(a)), right_nn(halves(b)), ((1,), (0,))))


def mul_nt(a, b):
    return fold(dot(left_nn(halves(a)), right_nt(halves(b)), ((1,), (1,))))


def mul_tn(a, b):
    left = jnp.concatenate(halves(a), axis=0)
    return fold(dot(left, right_nn(halves(b)), ((0,), (0,))))


def low_nn(a, b):
    return dot(low(a), low(b), ((1,), (0,)))


def low_nt(a, b):
    return dot(low(a), low(b), ((1,), (1,)))


def low_tn(a, b):
    return dot(low(a), low(b), ((0,), (0,)))


def iotas(rows, cols):
    return (
        lax.broadcasted_iota(jnp.int32, (rows, cols), 0),
        lax.broadcasted_iota(jnp.int32, (rows, cols), 1),
    )


def order(index):
    return STEPS * lax.rem(index, STRETCH) + lax.div(index, STRETCH)


def sigmoid(a):
    return 1.0 / (1.0 + jnp.exp(-a))


def softplus(a):
    return jnp.maximum(a, 0.0) + jnp.log1p(jnp.exp(-jnp.abs(a)))


def window(ref, halo, seq, base, columns):
    before = ref[seq, pl.ds(pl.multiple_of(jnp.maximum(base - 8, 0), 8), 8), columns]
    ahead = 0.0 if halo is None else halo[seq, :, columns]
    return jnp.concatenate(
        [jnp.where(base == 0, ahead, before), ref[seq, pl.ds(base, STRETCH), columns]], axis=0
    )


def stack(act, at, dim):
    return jnp.concatenate(
        [act[:, at * dim : (at + 1) * dim], act[:, (at + 1) * dim : (at + 2) * dim]], axis=0
    )


def convolve(rows, conv):
    total = None
    for tap in range(CONV):
        start = 8 - (CONV - 1) + tap
        term = conv[tap : tap + 1] * rows[start : start + STRETCH]
        total = term if total is None else total + term
    return total


def rates(small, decay):
    beta = jnp.concatenate([sigmoid(small[:, 0:1]), sigmoid(small[:, 1:2])], axis=0)
    gamma = -jnp.exp(decay[0:1]) * softplus(small + decay[1:2])
    row, col = iotas(STRETCH, STRETCH)
    tri = low(jnp.where(row >= col, 1.0, 0.0))
    high = low(gamma)
    rest = gamma - high.astype(jnp.float32)
    middle = low(rest)
    last = low(rest - middle.astype(jnp.float32))
    running = (
        dot(tri, high, ((1,), (0,))) + dot(tri, middle, ((1,), (0,))) + dot(tri, last, ((1,), (0,)))
    )
    return beta, running


def decays(running):
    column = running[:, 2:3]
    across = jnp.transpose(running)[2:3, :]
    row, col = iotas(STRETCH, STRETCH)
    gap = jnp.broadcast_to(column, (STRETCH, STRETCH)) - across
    upto = jnp.where(row >= col, jnp.exp(jnp.where(row >= col, gap, 0.0)), 0.0)
    before = jnp.where(row > col, upto, 0.0)
    strict = jnp.concatenate(
        [
            jnp.concatenate([before, before], axis=1),
            jnp.concatenate([upto, before], axis=1),
        ],
        axis=0,
    )
    return strict, jnp.concatenate([upto, upto], axis=1)


def level_masks():
    row, col = iotas(WIDE, WIDE)
    row, col = order(row), order(col)
    masks, size = [], 1
    while size < WIDE:
        inside = (lax.div(row, 2 * size) == lax.div(col, 2 * size)) & (
            lax.div(row, size) != lax.div(col, size)
        )
        masks.append(jnp.where(inside, 1.0, 0.0))
        size *= 2
    return [masks[0]] + [low(mask) for mask in masks[1:]]


def inverses(systems, masks):
    row, col = iotas(WIDE, WIDE)
    eye = jnp.where(row == col, 1.0, 0.0)
    solved = [eye - masks[0] * system for system in systems]
    split = [halves(system) for system in systems]
    for mask in masks[1:]:
        parts = [halves(a) for a in solved]
        steps = [
            fold(
                dot(
                    jnp.concatenate([high * mask, rest * mask], axis=1),
                    right_nn(part),
                    ((1,), (0,)),
                )
            )
            for (high, rest), part in zip(split, parts)
        ]
        solved = [
            a - fold(dot(left_nn(part), right_nn(halves(step)), ((1,), (0,))))
            for a, part, step in zip(solved, parts, steps)
        ]
    return solved


def unit_rows(stacked):
    return lax.rsqrt(jnp.sum(stacked * stacked, axis=1, keepdims=True) + EPS)


def twice(column):
    return jnp.concatenate([column, column], axis=0)


def forward_kernel(linked, *refs):
    if linked:
        proj, conv, decay, gain, halo, start, *refs = refs
        *refs, final, product, local, offset = refs
    else:
        proj, conv, decay, gain, *refs = refs
        halo, (*refs, local, offset) = None, refs
    mixer, out, fresh, inv, weights, trans, states = refs
    seqs, length, _ = proj.shape
    dim = gain.shape[1]
    blocks = length // STRETCH
    together = 2 if blocks % 2 == 0 else 1
    masks = level_masks()
    row, col = iotas(dim, dim)
    diagonal = row == col

    def spots(step):
        return [(seq, step * together + k) for k in range(together) for seq in range(seqs)]

    def first(step, _):
        units = spots(step)
        kept = []
        for seq, block in units:
            base = pl.multiple_of(block * STRETCH, STRETCH)
            rows = window(proj, halo, seq, base, pl.ds(0, 5 * dim))
            pre = convolve(rows, conv)
            act = pre * sigmoid(pre)
            raw = stack(act, 1, dim)
            key = raw * unit_rows(raw)
            beta, running = rates(proj[seq, pl.ds(base, STRETCH), pl.ds(6 * dim, dim)], decay)
            kept.append((act[:, :dim], key, stack(act, 3, dim), beta, running))
        systems = []
        for (seq, block), (query, key, value, beta, running) in zip(units, kept):
            at = seq * blocks + block
            strict, upto = decays(running)
            key_halves = halves(key)
            both = fold(
                dot(
                    jnp.concatenate([left_nn(key_halves), left_nn(halves(query))], axis=0),
                    right_nt(key_halves),
                    ((1,), (1,)),
                )
            )
            systems.append(beta * both[:WIDE] * strict)
            local[at] = both[WIDE:] * upto
            offset[at] = query * jnp.exp(running[:, 2:3])
        for (seq, block), (query, key, value, beta, running), solved in zip(
            units, kept, inverses(systems, masks)
        ):
            at = seq * blocks + block
            inv[at] = solved
            grown = twice(jnp.exp(running[:, 2:3]))
            end = running[STRETCH - 1 :, 2:3]
            solved_left = left_nn(halves(solved))
            weight = fold(dot(solved_left, right_nn(halves(beta * key * grown)), ((1,), (0,))))
            value = fold(dot(solved_left, right_nn(halves(beta * value)), ((1,), (0,))))
            weights[at] = weight
            fresh[at] = value
            to_end = jnp.concatenate(halves(key * twice(jnp.exp(end - running[:, 2:3]))), axis=0)
            trans[at] = jnp.where(diagonal, jnp.exp(end), 0.0) - fold(
                dot(to_end, right_nn(halves(weight)), ((0,), (0,)))
            )
            states[at] = fold(dot(to_end, right_nn(halves(value)), ((0,), (0,))))
        return 0

    lax.fori_loop(0, blocks // together, first, 0)

    def chain(block, carried):
        new = []
        for seq in range(seqs):
            at = seq * blocks + block
            state = carried[seq]
            added = states[at]
            states[at] = state
            new.append(mul(trans[at], state) + added)
            if linked:
                product[seq] = mul(trans[at], product[seq])
        return tuple(new)

    if linked:
        for seq in range(seqs):
            product[seq] = jnp.where(diagonal, 1.0, 0.0)
        begin = tuple(start[seq] for seq in range(seqs))
    else:
        begin = (jnp.zeros((dim, dim), jnp.float32),) * seqs
    ended = lax.fori_loop(0, blocks, chain, begin)
    if linked:
        for seq in range(seqs):
            final[seq] = ended[seq]

    def last(step, _):
        units = spots(step)
        reads = [
            mul(
                jnp.concatenate([weights[seq * blocks + block], offset[seq * blocks + block]], axis=0),
                states[seq * blocks + block],
            )
            for seq, block in units
        ]
        for (seq, block), read in zip(units, reads):
            at = seq * blocks + block
            base = pl.multiple_of(block * STRETCH, STRETCH)
            new = fresh[at] - read[:WIDE]
            fresh[at] = new
            result = read[WIDE:] + mul(local[at], new)
            out[seq, pl.ds(base, STRETCH)] = result
            gate = proj[seq, pl.ds(base, STRETCH), pl.ds(5 * dim, dim)]
            scale = lax.rsqrt(jnp.mean(result * result, axis=1, keepdims=True) + EPS)
            mixer[seq, pl.ds(base, STRETCH)] = low(
                result * scale * gain[...] * (gate * sigmoid(gate))
            )
        return 0

    lax.fori_loop(0, blocks // together, last, 0)


def mixer_forward(proj, conv, decay, gain, link=()):
    seqs, length, _ = proj.shape
    dim = gain.shape[1]
    units = seqs * (length // STRETCH)
    square = jax.ShapeDtypeStruct((units, WIDE, dim), jnp.float32)
    state = jax.ShapeDtypeStruct((seqs, dim, dim), jnp.float32)
    shapes = (
        jax.ShapeDtypeStruct((seqs, length, dim), jnp.bfloat16),
        jax.ShapeDtypeStruct((seqs, length, dim), jnp.float32),
        square,
        square,
        square,
        square,
        square,
    )
    if link:
        shapes += (state, state)
    return pl.pallas_call(
        functools.partial(forward_kernel, bool(link)),
        out_shape=shapes,
        in_specs=[pl.BlockSpec(memory_space=pltpu.VMEM)] * (4 + len(link)),
        out_specs=[pl.BlockSpec(memory_space=pltpu.VMEM)] * len(shapes),
        scratch_shapes=[
            pltpu.VMEM((units, STRETCH, WIDE), jnp.float32),
            pltpu.VMEM((units, STRETCH, dim), jnp.float32),
        ],
        compiler_params=pltpu.CompilerParams(vmem_limit_bytes=56 * 2**20),
        cost_estimate=pl.CostEstimate(
            flops=units * 60 * WIDE * WIDE * WIDE,
            bytes_accessed=units * WIDE * WIDE * 30,
            transcendentals=units * WIDE * WIDE * 8,
        ),
        name="mixer_forward",
    )(proj, conv, decay, gain, *link)


def backward_kernel(linked, *refs):
    proj, conv, decay, gain, out, fresh, inv, weights, trans, states, d_mixer, *refs = refs
    if linked:
        halo, end_state, *refs = refs
        d_proj, d_conv, d_small_sums, d_gain, d_start, d_first, *refs = refs
    else:
        halo = None
        d_proj, d_conv, d_small_sums, d_gain, *refs = refs
    d_out, chained = refs
    seqs, length, _ = proj.shape
    dim = gain.shape[1]
    blocks = length // STRETCH
    together = 2 if blocks % 2 == 0 else 1
    all_conv = pl.ds(0, 5 * dim)

    def spots(step):
        return [(seq, blocks - 1 - step * together - k) for k in range(together) for seq in range(seqs)]

    def first(step, gain_sum):
        units = spots(step)
        kept = []
        for seq, block in units:
            at = seq * blocks + block
            base = pl.multiple_of(block * STRETCH, STRETCH)
            result = out[seq, pl.ds(base, STRETCH)]
            gate = proj[seq, pl.ds(base, STRETCH), pl.ds(5 * dim, dim)]
            given = d_mixer[seq, pl.ds(base, STRETCH)].astype(jnp.float32)
            scale = lax.rsqrt(jnp.mean(result * result, axis=1, keepdims=True) + EPS)
            normal = result * scale
            open_ = sigmoid(gate)
            silu = gate * open_
            gain_sum = gain_sum + jnp.sum(given * normal * silu, axis=0, keepdims=True)
            d_proj[seq, pl.ds(base, STRETCH), pl.ds(5 * dim, dim)] = low(
                given * normal * gain[...] * (open_ * (1.0 + gate * (1.0 - open_)))
            )
            inner = given * gain[...] * silu
            d_result = scale * (inner - normal * jnp.mean(inner * normal, axis=1, keepdims=True))
            d_out[at] = d_result
            pre = convolve(window(proj, halo, seq, base, pl.ds(0, 3 * dim)), conv[:, : 3 * dim])
            act = pre * sigmoid(pre)
            raw = stack(act, 1, dim)
            _, running = rates(proj[seq, pl.ds(base, STRETCH), pl.ds(6 * dim, dim)], decay)
            kept.append((act[:, :dim], raw * unit_rows(raw), running, d_result))
        scores = [
            mul_nt(query, key) * decays(running)[1] for query, key, running, _ in kept
        ]
        d_freshes = [mul_tn(score, unit[3]) for score, unit in zip(scores, kept)]
        for (seq, block), (query, _, running, d_result), d_fresh in zip(units, kept, d_freshes):
            at = seq * blocks + block
            chained[at] = mul_tn(
                jnp.concatenate([query * jnp.exp(running[:, 2:3]), -weights[at]], axis=0),
                jnp.concatenate([d_result, d_fresh], axis=0),
            )
        return gain_sum

    d_gain[...] = lax.fori_loop(0, blocks // together, first, jnp.zeros((1, dim), jnp.float32))

    def chain(step, carried):
        block = blocks - 1 - step
        new = []
        for seq in range(seqs):
            at = seq * blocks + block
            later = carried[seq]
            added = chained[at]
            chained[at] = later
            new.append(mul_tn(trans[at], later) + added)
        return tuple(new)

    if linked:
        begin = tuple(end_state[seq] for seq in range(seqs))
    else:
        begin = (jnp.zeros((dim, dim), jnp.float32),) * seqs
    ended = lax.fori_loop(0, blocks, chain, begin)
    if linked:
        for seq in range(seqs):
            d_start[seq] = ended[seq]

    def last(step, sums):
        conv_sum, small_sum, *rims = sums
        units = spots(step)
        ats = [seq * blocks + block for seq, block in units]
        bases = [pl.multiple_of(block * STRETCH, STRETCH) for _, block in units]
        acts, keys, rate_sets = [], [], []
        for (seq, _), base in zip(units, bases):
            pre = convolve(window(proj, halo, seq, base, all_conv), conv)
            gate = sigmoid(pre)
            act = pre * gate
            raw = stack(act, 1, dim)
            unit = unit_rows(raw)
            acts.append((act, gate * (1.0 + pre * (1.0 - gate)), unit))
            keys.append(raw * unit)
            rate_sets.append(rates(proj[seq, pl.ds(base, STRETCH), pl.ds(6 * dim, dim)], decay))
        nears = [
            mul_nt(jnp.concatenate([key, act[:, :dim]], axis=0), key)
            for (act, _, _), key in zip(acts, keys)
        ]
        masks = [decays(running) for _, running in rate_sets]
        d_freshes = [
            mul_tn(near[WIDE:] * upto, d_out[at])
            + mul(key * twice(jnp.exp(running[STRETCH - 1 :, 2:3] - running[:, 2:3])), chained[at])
            for near, (_, upto), at, key, (_, running) in zip(nears, masks, ats, keys, rate_sets)
        ]
        backs = [mul_tn(inv[at], d_fresh) for at, d_fresh in zip(ats, d_freshes)]
        reads = [
            stack(act, 3, dim) - mul(key * twice(jnp.exp(running[:, 2:3])), states[at])
            for (act, _, _), key, (_, running), at in zip(acts, keys, rate_sets, ats)
        ]
        to_state = [
            mul_nt(jnp.concatenate([beta * back, d_out[at]], axis=0), states[at])
            for (beta, _), back, at in zip(rate_sets, backs, ats)
        ]
        to_new = [
            mul_nt(jnp.concatenate([back, d_out[at]], axis=0), fresh[at])
            for back, at in zip(backs, ats)
        ]
        d_ends = [mul_nt(fresh[at], chained[at]) for at in ats]
        shaped = [-cross[:WIDE] * strict for cross, (strict, _) in zip(to_new, masks)]
        insides = [beta * a for (beta, _), a in zip(rate_sets, shaped)]
        d_nears = [cross[WIDE:] * upto for cross, (_, upto) in zip(to_new, masks)]
        towards = [
            mul(jnp.concatenate([inside, d_near], axis=0), key)
            for inside, d_near, key in zip(insides, d_nears, keys)
        ]
        away = [
            mul_tn(
                jnp.concatenate([inside, d_near], axis=0),
                jnp.concatenate([key, act[:, :dim]], axis=0),
            )
            for inside, d_near, key, (act, _, _) in zip(insides, d_nears, keys, acts)
        ]
        d_heres = []
        for k, ((seq, _), at, base) in enumerate(zip(units, ats, bases)):
            act, slope, unit = acts[k]
            query, key = act[:, :dim], keys[k]
            beta, running = rate_sets[k]
            small = proj[seq, pl.ds(base, STRETCH), pl.ds(6 * dim, dim)]
            g = running[:, 2:3]
            end = g[STRETCH - 1 :]
            grown, to_go = jnp.exp(g), jnp.exp(end - g)
            back = backs[k]
            d_scaled, d_query_scaled = -to_state[k][:WIDE], to_state[k][WIDE:]
            with_inside = shaped[k] * nears[k][:WIDE]
            d_beta = jnp.sum(back * reads[k] + with_inside, axis=1, keepdims=True)
            gaps = beta * with_inside
            score_gaps = d_nears[k] * nears[k][WIDE:]
            d_query = towards[k][WIDE:] + d_query_scaled * grown
            from_start, from_end = d_scaled * twice(grown), d_ends[k] * twice(to_go)
            d_key = towards[k][:WIDE] + away[k] + from_start + from_end
            ended = jnp.sum(from_end * key, axis=1, keepdims=True)
            row_terms = jnp.sum(gaps + from_start * key, axis=1, keepdims=True) - ended
            col_terms = jnp.sum(gaps, axis=0, keepdims=True) + jnp.sum(
                score_gaps, axis=0, keepdims=True
            )
            col_terms = jnp.transpose(jnp.broadcast_to(col_terms, (8, WIDE)))[:, 0:1]
            row_terms = row_terms - col_terms
            d_g = (
                row_terms[:STRETCH]
                + row_terms[STRETCH:]
                + jnp.sum(score_gaps + d_query_scaled * grown * query, axis=1, keepdims=True)
            )
            d_end = jnp.sum(ended, axis=0, keepdims=True) + jnp.exp(end) * jnp.sum(
                jnp.sum(states[at] * chained[at], axis=0, keepdims=True), axis=1, keepdims=True
            )
            row, col = iotas(STRETCH, STRETCH)
            across = jnp.transpose(jnp.broadcast_to(d_g, (STRETCH, WIDE)))[:STRETCH]
            d_gamma = jnp.sum(jnp.where(row <= col, across, 0.0), axis=1, keepdims=True) + d_end
            lane = iotas(STRETCH, dim)[1]
            shifted = small + decay[1:2]
            d_soft = -jnp.exp(decay[0:1]) * d_gamma
            d_logit = d_soft * sigmoid(shifted)
            d_rate = jnp.where(lane == 0, d_beta[:STRETCH], d_beta[STRETCH:])
            open_beta = sigmoid(small)
            d_small = jnp.where(
                lane < 2,
                d_rate * open_beta * (1.0 - open_beta),
                jnp.where(lane == 2, d_logit, 0.0),
            )
            d_proj[seq, pl.ds(base, STRETCH), pl.ds(6 * dim, dim)] = low(d_small)
            small_sum = small_sum + jnp.concatenate(
                [
                    jnp.sum(d_soft * softplus(shifted), axis=0, keepdims=True),
                    jnp.sum(d_logit, axis=0, keepdims=True),
                ],
                axis=0,
            )
            d_raw = unit * (d_key - key * jnp.sum(d_key * key, axis=1, keepdims=True))
            d_value = beta * back
            d_act = jnp.concatenate(
                [d_query, d_raw[:STRETCH], d_raw[STRETCH:], d_value[:STRETCH], d_value[STRETCH:]],
                axis=1,
            )
            d_heres.append(d_act * slope)
        for (seq, _), base, d_here in zip(units, bases, d_heres):
            rows = window(proj, halo, seq, base, all_conv)
            first_row = 8 - (CONV - 1)
            conv_sum = conv_sum + jnp.concatenate(
                [
                    jnp.sum(
                        d_here * rows[first_row + tap : first_row + tap + STRETCH],
                        axis=0,
                        keepdims=True,
                    )
                    for tap in range(CONV)
                ],
                axis=0,
            )
            ahead = jnp.concatenate([d_here, rims[seq]], axis=0)
            rims[seq] = d_here[:8]
            total = None
            for tap in range(CONV):
                start = CONV - 1 - tap
                term = conv[tap : tap + 1] * ahead[start : start + STRETCH]
                total = term if total is None else total + term
            d_proj[seq, pl.ds(base, STRETCH), all_conv] = low(total)
        return conv_sum, small_sum, *rims

    conv_sum, small_sum, *rims = lax.fori_loop(
        0,
        blocks // together,
        last,
        (jnp.zeros((CONV, 5 * dim), jnp.float32), jnp.zeros((2, dim), jnp.float32))
        + (jnp.zeros((8, 5 * dim), jnp.float32),) * seqs,
    )
    if linked:
        for seq in range(seqs):
            d_first[seq] = rims[seq]
    d_conv[...] = conv_sum
    d_small_sums[...] = small_sum


def mixer_backward(proj, conv, decay, gain, kept, d_mixer, link=()):
    seqs, length, width = proj.shape
    dim = gain.shape[1]
    units = seqs * (length // STRETCH)
    shapes = (
        jax.ShapeDtypeStruct((seqs, length, width), jnp.bfloat16),
        jax.ShapeDtypeStruct((CONV, 5 * dim), jnp.float32),
        jax.ShapeDtypeStruct((2, dim), jnp.float32),
        jax.ShapeDtypeStruct((1, dim), jnp.float32),
    )
    if link:
        shapes += (
            jax.ShapeDtypeStruct((seqs, dim, dim), jnp.float32),
            jax.ShapeDtypeStruct((seqs, 8, 5 * dim), jnp.float32),
        )
    return pl.pallas_call(
        functools.partial(backward_kernel, bool(link)),
        out_shape=shapes,
        in_specs=[pl.BlockSpec(memory_space=pltpu.VMEM)] * (11 + len(link)),
        out_specs=[pl.BlockSpec(memory_space=pltpu.VMEM)] * len(shapes),
        scratch_shapes=[
            pltpu.VMEM((units, STRETCH, dim), jnp.float32),
            pltpu.VMEM((units, dim, dim), jnp.float32),
        ],
        compiler_params=pltpu.CompilerParams(vmem_limit_bytes=60 * 2**20),
        cost_estimate=pl.CostEstimate(
            flops=units * 60 * WIDE * WIDE * WIDE,
            bytes_accessed=units * WIDE * WIDE * 30,
            transcendentals=units * WIDE * WIDE * 8,
        ),
        name="mixer_backward",
    )(proj, conv, decay, gain, *kept, d_mixer, *link)


def matmul(left, right):
    return jnp.dot(left, right, preferred_element_type=jnp.float32)


def times_transposed(left, right):
    return lax.dot_general(
        left, right, (((1,), (1,)), ((), ())), preferred_element_type=jnp.float32
    )


def transposed_times(left, right):
    return lax.dot_general(
        left, right, (((0,), (0,)), ((), ())), preferred_element_type=jnp.float32
    )


def batched(left, right):
    return jnp.einsum("sij,sjk->sik", left, right, precision=lax.Precision.HIGHEST)


def norm_scale(values):
    return lax.rsqrt(jnp.mean(values * values, axis=-1, keepdims=True) + EPS)


def norm_back(values, gain, given):
    scale = norm_scale(values)
    normal = values * scale
    inner = given * gain
    return scale * (inner - normal * jnp.mean(inner * normal, axis=-1, keepdims=True)), (
        given * normal
    )


def per_device(
    block_in,
    lengths,
    norm_gains,
    w_in,
    w_small,
    conv_weight,
    decay_log,
    decay_bias,
    out_norm_gain,
    w_out,
    gate_up_weight,
    w_down,
    out_cotangent,
):
    micro, seq_count, tokens, width = block_in.shape
    seqs = micro * seq_count
    count = lax.axis_size("ctx")
    groups = lax.axis_size("rep")
    place = lax.axis_index("ctx")
    group = lax.axis_index("rep")
    teams = count // HEADS
    head = lax.rem(place, HEADS)
    team = lax.div(place, HEADS)
    mates = peers = None
    if teams > 1:
        mates = [[t * HEADS + h for h in range(HEADS)] for t in range(teams)]
        peers = [[t * HEADS + h for t in range(teams)] for h in range(HEADS)]
    dim = width // HEADS
    length = HEADS * tokens
    rows = seqs * tokens
    kinds = 2 + 2 * STEPS
    rates_of = STEPS + 1
    f32, bf16 = jnp.float32, jnp.bfloat16

    own = width // count
    small_block = jnp.concatenate(
        [norm_gains.reshape(-1), w_small.reshape(-1), conv_weight.reshape(-1)]
    )
    small_block = jnp.pad(small_block, (0, -small_block.size % 128)).reshape(-1, 128)
    smalls = lax.all_gather(small_block, "ctx", axis=0).reshape(count, -1)
    gains = smalls[:, : 2 * own].reshape(count, 2, own).transpose(1, 0, 2).reshape(2, width)
    gains = gains.astype(f32)
    small_all = smalls[:, 2 * own : (2 + HEADS * rates_of) * own].reshape(width, rates_of, HEADS)
    small_head = lax.dynamic_index_in_dim(small_all, head, 2, keepdims=False)
    taps_at = (2 + HEADS * rates_of) * own
    conv_all = smalls[:, taps_at : taps_at + conv_weight.size].reshape(count, CONV, -1)
    conv_all = conv_all.transpose(1, 0, 2).reshape(CONV, kinds - 1, HEADS, dim)
    conv_head = lax.dynamic_index_in_dim(conv_all, head, 2, keepdims=False)
    conv_head = conv_head.reshape(CONV, -1).astype(f32)
    sequence = lax.all_gather(
        block_in.reshape(seqs, tokens, width), "ctx", axis=1, tiled=True, axis_index_groups=mates
    )
    w_head = w_in.reshape(own, kinds, HEADS, dim).transpose(2, 0, 1, 3)
    w_head = lax.all_to_all(w_head, "ctx", 0, 0, tiled=True, axis_index_groups=mates)
    w_head = w_head.reshape(HEADS * own, kinds * dim)
    if teams > 1:
        w_head = lax.all_gather(w_head, "ctx", axis=0, tiled=True, axis_index_groups=peers)
    w_head = jnp.concatenate(
        [w_head, small_head, jnp.zeros((width, dim - rates_of), bf16)], axis=1
    )
    w_out_full = lax.all_gather(w_out, "ctx", axis=0, tiled=True)
    hidden_own = w_down.shape[0] // groups
    gate_up_part = lax.dynamic_index_in_dim(
        gate_up_weight.reshape(own, 2, count, groups, hidden_own), group, 3, keepdims=False
    )
    gate_up_part = lax.all_gather(gate_up_part.reshape(own, -1), "ctx", axis=0, tiled=True)
    down_part = lax.dynamic_index_in_dim(
        w_down.reshape(groups, hidden_own, width), group, 0, keepdims=False
    )
    down_part = lax.all_gather(down_part, "ctx", axis=0, tiled=True)
    hidden_units = count * hidden_own

    inputs_all = sequence.astype(f32)
    h_first = (inputs_all * norm_scale(inputs_all) * gains[0]).astype(bf16)
    proj = matmul(h_first.reshape(seqs * length, width), w_head).reshape(seqs, length, -1)
    decay = jnp.stack(
        [
            jnp.broadcast_to(lax.dynamic_index_in_dim(decay_log, head, 0), (dim,)),
            jnp.broadcast_to(lax.dynamic_index_in_dim(decay_bias, head, 0), (dim,)),
        ]
    )
    gain = out_norm_gain.reshape(1, dim)
    halo = None
    if teams > 1:
        onward = [(c, c + HEADS) for c in range(count - HEADS)]
        halo = lax.ppermute(proj[:, length - 8 :], "ctx", onward)
        start = jnp.zeros((seqs, dim, dim), f32)
        *_, offset, transfer = mixer_forward(proj, conv_head, decay, gain, (halo, start))
        spans = lax.all_gather((transfer, offset), "ctx", axis_index_groups=peers)
        for turn in range(teams - 1):
            start = jnp.where(turn < team, batched(spans[0][turn], start) + spans[1][turn], start)
        mixer_head, *kept = mixer_forward(proj, conv_head, decay, gain, (halo, start))[:-2]
    else:
        mixer_head, *kept = mixer_forward(proj, conv_head, decay, gain)

    def to_tokens(array):
        split = array.reshape(seqs, HEADS, tokens, dim).transpose(1, 0, 2, 3)
        moved = lax.all_to_all(
            split.reshape(HEADS, rows, dim), "ctx", 0, 0, tiled=True, axis_index_groups=mates
        )
        return moved.transpose(1, 0, 2).reshape(rows, width)

    def to_heads(array):
        split = array.reshape(rows, HEADS, dim).transpose(1, 0, 2)
        moved = lax.all_to_all(split, "ctx", 0, 0, tiled=True, axis_index_groups=mates)
        return moved.reshape(HEADS, seqs, tokens, dim).transpose(1, 0, 2, 3).reshape(
            seqs, length, dim
        )

    mixer = to_tokens(mixer_head)
    inputs = block_in.reshape(rows, width).astype(f32)
    resid = inputs + matmul(mixer, w_out_full)

    h_second = (resid * norm_scale(resid) * gains[1]).astype(bf16)
    places = place * tokens + lax.broadcasted_iota(jnp.int32, (seqs, tokens), 1)
    valid = (places < lengths.reshape(seqs, 1)).astype(f32).reshape(rows, 1)
    grad_out = (out_cotangent.reshape(rows, width).astype(f32) * valid).astype(bf16)
    grad_all = lax.all_gather(grad_out, "rep", axis=0, tiled=True)
    h_all = lax.all_gather(h_second, "rep", axis=0, tiled=True)
    gate_up = matmul(h_all, gate_up_part)
    gate, up = gate_up[:, :hidden_units], gate_up[:, hidden_units:]
    open_gate = jax.nn.sigmoid(gate)
    silu = gate * open_gate
    hidden = (silu * up).astype(bf16)
    down = lax.psum_scatter(
        matmul(hidden, down_part).astype(bf16), "rep", scatter_dimension=0, tiled=True
    )
    result = (valid * (resid + down.astype(f32))).astype(bf16)

    d_hidden = times_transposed(grad_all, down_part)
    d_gate_up = jnp.concatenate(
        [d_hidden * up * (open_gate * (1.0 + gate * (1.0 - open_gate))), d_hidden * silu], axis=1
    ).astype(bf16)
    d_second = lax.psum_scatter(
        times_transposed(d_gate_up, gate_up_part).astype(bf16),
        "rep",
        scatter_dimension=0,
        tiled=True,
    ).astype(f32)
    grad_down = transposed_times(hidden, grad_all)
    grad_gate_up = transposed_times(h_all, d_gate_up)
    d_norm, gain_terms_second = norm_back(resid, gains[1], d_second)
    d_resid = grad_out.astype(f32) + d_norm
    d_branch = d_resid.astype(bf16)
    grad_out_proj = transposed_times(mixer, d_branch)
    d_mixer = times_transposed(d_branch, w_out_full)

    d_mixer = to_heads(d_mixer.astype(bf16))
    if teams > 1:
        later = jnp.zeros((seqs, dim, dim), f32)
        local = mixer_backward(proj, conv_head, decay, gain, kept, d_mixer, (halo, later))[4]
        locals_ = lax.all_gather(local, "ctx", axis_index_groups=peers)
        for turn in range(teams - 1, 0, -1):
            later = jnp.where(
                turn > team,
                batched(spans[0][turn].transpose(0, 2, 1), later) + locals_[turn],
                later,
            )
        d_proj, grad_conv, small_sums, grad_gain, _, rim = mixer_backward(
            proj, conv_head, decay, gain, kept, d_mixer, (halo, later)
        )
        rim = lax.ppermute(rim, "ctx", [(c, c - HEADS) for c in range(HEADS, count)])
        spill = jnp.zeros((seqs, CONV - 1, kinds * dim - dim), f32)
        for ahead in range(1, CONV):
            spill = spill.at[:, CONV - 1 - ahead :].add(
                conv_head[CONV - 1 - ahead] * rim[:, :ahead]
            )
        last = d_proj[:, length - CONV + 1 :, : (kinds - 1) * dim]
        d_proj = d_proj.at[:, length - CONV + 1 :, : (kinds - 1) * dim].set(
            (last.astype(f32) + spill).astype(bf16)
        )
    else:
        d_proj, grad_conv, small_sums, grad_gain = mixer_backward(
            proj, conv_head, decay, gain, kept, d_mixer
        )
    d_proj = d_proj.reshape(seqs * length, -1)
    grad_head = transposed_times(h_first.reshape(seqs * length, width), d_proj)
    d_first = times_transposed(d_proj, w_head).astype(bf16)
    d_first = d_first.reshape(seqs, HEADS, tokens, width).transpose(1, 0, 2, 3)
    d_first = lax.psum_scatter(
        d_first.reshape(HEADS * rows, width),
        "ctx",
        scatter_dimension=0,
        tiled=True,
        axis_index_groups=mates,
    ).astype(f32)
    d_inputs, gain_terms_first = norm_back(inputs, gains[0], d_first)
    in_grad = (d_resid + d_inputs).astype(bf16)

    grad_gate_up = lax.psum_scatter(
        grad_gate_up.astype(bf16), "ctx", scatter_dimension=0, tiled=True
    )
    grad_gate_up = lax.all_gather(
        grad_gate_up.reshape(own, 2, count, hidden_own), "rep", axis=3
    ).reshape(own, -1)
    grad_down = lax.psum_scatter(grad_down.astype(bf16), "ctx", scatter_dimension=0, tiled=True)
    grad_down = lax.all_gather(grad_down, "rep", axis=0, tiled=True)
    grad_out_proj = lax.psum_scatter(
        grad_out_proj.astype(bf16), "ctx", scatter_dimension=0, tiled=True
    )
    grad_in = grad_head[:, : kinds * dim].astype(bf16)
    if teams > 1:
        grad_in = lax.psum_scatter(
            grad_in, "ctx", scatter_dimension=0, tiled=True, axis_index_groups=peers
        )
    grad_in = lax.all_to_all(
        grad_in.reshape(HEADS, own, kinds * dim), "ctx", 0, 0, tiled=True, axis_index_groups=mates
    )
    grad_in = grad_in.reshape(HEADS, own, kinds, dim).transpose(1, 2, 0, 3).reshape(own, -1)
    grad_in, grad_out_proj = lax.psum((grad_in, grad_out_proj), "rep")

    gain_terms = jnp.stack([gain_terms_first.sum(axis=0), gain_terms_second.sum(axis=0)])
    here = jnp.arange(HEADS, dtype=jnp.int32) == head
    grad_small = grad_head[:, kinds * dim : kinds * dim + rates_of]
    packed = jnp.concatenate(
        [
            gain_terms.reshape(-1),
            jnp.where(here[None, None, :], grad_small[:, :, None], 0.0).reshape(-1),
            jnp.where(
                here[None, None, :, None], grad_conv.reshape(CONV, kinds - 1, 1, dim), 0.0
            ).reshape(-1),
            grad_gain.reshape(-1),
            jnp.pad(
                jnp.where(here[None, :], small_sums[:, STEPS : STEPS + 1], 0.0).reshape(-1),
                (0, dim - 2 * HEADS),
            ),
        ]
    ).reshape(-1, 128)
    packed = lax.psum(packed, ("rep", "ctx")).reshape(-1)

    def take(size):
        nonlocal packed
        part, packed = packed[:size], packed[size:]
        return part

    def mine(array, axis, size):
        return lax.dynamic_slice_in_dim(array, place * size, size, axis)

    grad_gains = mine(take(2 * width).reshape(2, width), 1, own)
    grad_small = mine(take(width * rates_of * HEADS).reshape(width, -1), 0, own)
    taps = (kinds - 1) * width
    grad_conv = mine(take(CONV * taps).reshape(CONV, taps), 1, taps // count)
    grad_gain = take(dim)
    decays_sum = take(2 * HEADS).reshape(2, HEADS)
    return (
        result.reshape(block_in.shape),
        in_grad.reshape(block_in.shape),
        grad_gains,
        grad_in.astype(f32),
        grad_small,
        grad_conv,
        decays_sum[0],
        decays_sum[1],
        grad_gain,
        grad_out_proj.astype(f32),
        grad_gate_up.astype(f32),
        grad_down.astype(f32),
    )


def solution(mesh):
    placed = (
        P(None, "rep", "ctx", None),
        P(None, "rep"),
        P(None, "ctx"),
        P("ctx", None),
        P("ctx", None),
        P(None, "ctx"),
        P(),
        P(),
        P(),
        P("ctx", None),
        P("ctx", None),
        P("ctx", None),
        P(None, "rep", "ctx", None),
    )
    return jax.shard_map(
        per_device,
        mesh=mesh,
        in_specs=placed,
        out_specs=(
            P(None, "rep", "ctx", None),
            P(None, "rep", "ctx", None),
            P(None, "ctx"),
            P("ctx", None),
            P("ctx", None),
            P(None, "ctx"),
            P(),
            P(),
            P(),
            P("ctx", None),
            P("ctx", None),
            P("ctx", None),
        ),
        check_vma=False,
    )
```

```python
import functools
import jax
import jax.numpy as jnp
from jax import lax
from jax.experimental import pallas as pl
from jax.experimental.pallas import tpu as pltpu
from jax.sharding import PartitionSpec as P

STEPS = 2
CONV = 4
STRETCH = 64
HEADS = 8
EPS = 1e-06
WIDE = 2 * STRETCH


MESH = pl.DeviceIdType.MESH
ROWS = 2
COLS = HEADS // ROWS


class Spot:
    def __init__(self, groups):
        place = lax.axis_index("ctx")
        self.mate = lax.rem(place, HEADS)
        self.base = place - self.mate
        self.col = lax.div(self.mate, ROWS)
        self.row = lax.rem(self.mate, ROWS)
        self.groups = groups
        self.group = lax.axis_index("rep")
        self.side = lax.rem(self.group, 2)
        self.pair = lax.div(self.group, 2)
        self.twin = self.group + 1 - 2 * self.side

    def to_mate(self, mate):
        return {"ctx": self.base + mate}

    def to_group(self, group):
        return {"rep": group}

    def mate_off(self, k):
        return lax.rem(self.mate + k, HEADS)

    def group_off(self, k):
        return lax.rem(self.group + 2 * k, self.groups)

    def barrier(self, team=True, copies=True):
        sem = pltpu.get_barrier_semaphore()
        others = []
        if team:
            others += [self.to_mate(self.mate_off(k)) for k in range(1, HEADS)]
        if copies:
            others += [self.to_group(self.twin)]
            others += [self.to_group(self.group_off(k)) for k in range(1, self.groups // 2)]
        for other in others:
            pl.semaphore_signal(sem, inc=1, device_id=other, device_id_type=MESH)
        pl.semaphore_wait(sem, len(others))


def remote(src, dst, send, recv, where):
    return pltpu.make_async_remote_copy(
        src_ref=src,
        dst_ref=dst,
        send_sem=send,
        recv_sem=recv,
        device_id=where,
        device_id_type=MESH,
    )


TEAM_SEMS = 3 * COLS + 1


def team_gather(spot, src, out, send, recv, own):
    mate, col = spot.mate, spot.col
    up, down = spot.to_mate(mate + ROWS), spot.to_mate(mate - ROWS)
    across = spot.to_mate(mate + 1 - 2 * spot.row)
    other = mate + 1 - 2 * spot.row
    local = pltpu.make_async_copy(src, out(mate), own)

    def hop(block, origin, slot, where):
        return remote(block, out(origin), send.at[slot], recv.at[slot], where)

    rise, fall, cross_low, cross_high = 0, COLS - 1, 2 * COLS - 2, 3 * COLS - 3
    last = COLS - 1
    local.start()

    @pl.when(col < last)
    def _():
        hop(src, mate, rise, up).start()

    @pl.when(col > 0)
    def _():
        hop(src, mate, fall, down).start()

    hop(src, mate, cross_low, across).start()
    yield
    for k in range(1, COLS):
        below, above = mate - ROWS * k, mate + ROWS * k

        @pl.when(col >= k)
        def _():
            hop(out(below), below, rise + k - 1, up).wait_recv()
            if k < last:

                @pl.when(col < last)
                def _():
                    hop(out(below), below, rise + k, up).start()

            hop(out(below), below, cross_low + k, across).start()

        @pl.when(col + k <= last)
        def _():
            hop(out(above), above, fall + k - 1, down).wait_recv()
            if k < last:

                @pl.when(col > 0)
                def _():
                    hop(out(above), above, fall + k, down).start()

            hop(out(above), above, cross_high + k, across).start()

        yield
    hop(src, other, cross_low, across).wait_recv()
    for k in range(1, COLS):

        @pl.when(col >= k)
        def _():
            hop(src, other - ROWS * k, cross_low + k, across).wait_recv()

        @pl.when(col + k <= last)
        def _():
            hop(src, other + ROWS * k, cross_high + k, across).wait_recv()

    @pl.when(col < last)
    def _():
        hop(src, mate, rise, up).wait_send()

    @pl.when(col > 0)
    def _():
        hop(src, mate, fall, down).wait_send()

    hop(src, mate, cross_low, across).wait_send()
    for k in range(1, COLS):

        @pl.when(col >= k)
        def _():
            if k < last:

                @pl.when(col < last)
                def _():
                    hop(src, mate, rise + k, up).wait_send()

            hop(src, mate, cross_low + k, across).wait_send()

        @pl.when(col + k <= last)
        def _():
            if k < last:

                @pl.when(col > 0)
                def _():
                    hop(src, mate, fall + k, down).wait_send()

            hop(src, mate, cross_high + k, across).wait_send()

    local.wait()
    yield


def rep_gather(spot, src, out, send, recv, own):
    group, twin, half = spot.group, spot.twin, spot.groups // 2
    local = None
    if own is not None:
        local = pltpu.make_async_copy(src, out(group), own)
        local.start()

    def hop(block, origin, slot, where):
        return remote(block, out(origin), send.at[slot], recv.at[slot], spot.to_group(where))

    hop(src, group, 0, twin).start()
    for k in range(1, half):
        hop(src, group, k, spot.group_off(k)).start()
    yield
    for k in range(1, half):
        origin = spot.group_off(half - k)
        hop(out(origin), origin, k, twin).wait_recv()
        hop(out(origin), origin, half + k, twin).start()
    yield
    hop(src, twin, 0, twin).wait_recv()
    for k in range(1, half):
        origin = lax.rem(twin + 2 * (half - k), spot.groups)
        hop(src, origin, half + k, twin).wait_recv()
    hop(src, group, 0, twin).wait_send()
    for k in range(1, half):
        hop(src, group, k, twin).wait_send()
        hop(src, group, half + k, twin).wait_send()
    if local is not None:
        local.wait()
    yield


def team_exchange(spot, src, dst, send, recv, own):
    local = pltpu.make_async_copy(src(spot.mate), dst(spot.mate), own)
    local.start()

    def hop(k):
        to = spot.mate_off(k)
        return remote(src(to), dst(spot.mate), send.at[k], recv.at[k], spot.to_mate(to))

    for k in range(1, HEADS):
        hop(k).start()
    yield
    for k in range(1, HEADS):
        hop(k).wait_recv()
    for k in range(1, HEADS):
        hop(k).wait_send()
    local.wait()
    yield


def dma(*shape):
    return pltpu.SemaphoreType.DMA(shape)


ANY = pl.BlockSpec(memory_space=pl.ANY)
IN_VMEM = pl.BlockSpec(memory_space=pltpu.VMEM)


def finish(*steps):
    for step in steps:
        for _ in step:
            pass


def prologue_kernel(groups, tokens_in, pieces, smalls, given, sequence, w_head, smalls_all, given_all, *sems):
    (ex_send, ex_recv, sm_send, sm_recv, tok_send, tok_recv, rep_send, rep_recv, w_send, w_recv, own) = sems
    spot = Spot(groups)
    span = tokens_in.shape[1]
    spot.barrier()
    small = team_exchange(
        spot, lambda m: smalls, lambda m: smalls_all.at[m], sm_send, sm_recv, own.at[0]
    )
    exchange = team_exchange(
        spot,
        lambda m: pieces.at[m, spot.group],
        lambda m: w_head.at[m, spot.group],
        ex_send,
        ex_recv,
        own.at[1],
    )
    gathers = [
        team_gather(
            spot,
            tokens_in.at[seq],
            lambda m, seq=seq: sequence.at[seq, pl.ds(pl.multiple_of(m * span, span), span)],
            tok_send.at[seq],
            tok_recv.at[seq],
            own.at[4 + seq],
        )
        for seq in range(tokens_in.shape[0])
    ]
    copies = rep_gather(spot, given, lambda g: given_all.at[g], rep_send, rep_recv, own.at[2])
    next(exchange)
    next(small)
    for gather in gathers:
        next(gather)
    next(copies)
    finish(exchange)
    weights = rep_gather(
        spot, w_head.at[:, spot.group], lambda g: w_head.at[:, g], w_send, w_recv, None
    )
    next(weights)
    for _ in range(1, COLS):
        for gather in gathers:
            next(gather)
    next(weights)
    finish(weights, copies, small, *gathers)


def prologue(tokens_in, pieces, smalls, given, groups):
    seqs, span, width = tokens_in.shape
    return pl.pallas_call(
        functools.partial(prologue_kernel, groups),
        out_shape=(
            jax.ShapeDtypeStruct((seqs, HEADS * span, width), tokens_in.dtype),
            jax.ShapeDtypeStruct(pieces.shape, pieces.dtype),
            jax.ShapeDtypeStruct((HEADS,) + smalls.shape, smalls.dtype),
            jax.ShapeDtypeStruct((groups,) + given.shape, given.dtype),
        ),
        in_specs=[ANY] * 4,
        out_specs=[ANY] * 4,
        scratch_shapes=[
            dma(HEADS), dma(HEADS), dma(HEADS), dma(HEADS),
            dma(seqs, TEAM_SEMS), dma(seqs, TEAM_SEMS),
            dma(groups), dma(groups), dma(groups), dma(groups), dma(4 + seqs),
        ],
        compiler_params=pltpu.CompilerParams(collective_id=1, has_side_effects=True),
        name="prologue",
    )(tokens_in, pieces, smalls, given)


def copies_kernel(groups, block, out, send, recv, own):
    spot = Spot(groups)
    spot.barrier(team=False)
    finish(rep_gather(spot, block, lambda g: out.at[g], send, recv, own.at[0]))


def gather_copies(block, groups, number):
    return pl.pallas_call(
        functools.partial(copies_kernel, groups),
        out_shape=jax.ShapeDtypeStruct((groups,) + block.shape, block.dtype),
        in_specs=[ANY],
        out_specs=ANY,
        scratch_shapes=[dma(groups), dma(groups), dma(1)],
        compiler_params=pltpu.CompilerParams(collective_id=number, has_side_effects=True),
        name="gather_copies",
    )(block)


def rep_reduce(spot, part, pairs, sums, others, send, recv):
    half, side = spot.groups // 2, spot.side

    def to_twin(k):
        return remote(
            part(2 * k + 1 - side), pairs.at[k], send.at[k], recv.at[k], spot.to_group(spot.twin)
        )

    def onward(k):
        slot = half + k
        return remote(
            sums.at[k], others.at[k], send.at[slot], recv.at[slot], spot.to_group(spot.group_off(k))
        )

    for k in range(half):
        to_twin(k).start()
    yield
    for k in range(half):
        to_twin(k).wait_recv()

    def both(pair):
        return part(2 * pair + side)[...].astype(jnp.float32) + pairs[pair].astype(jnp.float32)

    for k in range(1, half):
        sums[k] = both(lax.rem(spot.pair + k, half)).astype(sums.dtype)
        onward(k).start()
    yield
    total = both(spot.pair)
    for k in range(1, half):
        onward(k).wait_recv()
        total = total + others[k].astype(jnp.float32)
    for k in range(half):
        to_twin(k).wait_send()
    for k in range(1, half):
        onward(k).wait_send()
    yield total


def reduce_kernel(groups, parts, out, pairs, sums, others, send, recv):
    spot = Spot(groups)
    spot.barrier(team=False)
    *_, total = rep_reduce(spot, lambda g: parts.at[g], pairs, sums, others, send, recv)
    out[...] = total


def reduce_copies(parts, number):
    groups = parts.shape[0]
    block = (groups // 2,) + parts.shape[1:]
    return pl.pallas_call(
        functools.partial(reduce_kernel, groups),
        out_shape=jax.ShapeDtypeStruct(parts.shape[1:], jnp.float32),
        in_specs=[IN_VMEM],
        out_specs=IN_VMEM,
        scratch_shapes=[pltpu.VMEM(block, parts.dtype)] * 3 + [dma(groups), dma(groups)],
        compiler_params=pltpu.CompilerParams(
            collective_id=number, has_side_effects=True, vmem_limit_bytes=40 * 2**20
        ),
        name="reduce_copies",
    )(parts)


def team_reduce(spot, part, seqs, across_in, sums, rising, falling, total, send, recv):
    mate, col, row = spot.mate, spot.col, spot.row
    up, down = spot.to_mate(mate + ROWS), spot.to_mate(mate - ROWS)
    across = spot.to_mate(mate + 1 - 2 * row)
    last = COLS - 1
    f32 = jnp.float32

    def cross(seq, d):
        return remote(
            part(ROWS * d + 1 - row, seq),
            across_in.at[seq, d],
            send.at[0, seq, d],
            recv.at[0, seq, d],
            across,
        )

    def rise(seq, d):
        return remote(
            sums.at[seq, d], rising.at[seq, d], send.at[1, seq, d], recv.at[1, seq, d], up
        )

    def fall(seq, d):
        return remote(
            sums.at[seq, d], falling.at[seq, d], send.at[2, seq, d], recv.at[2, seq, d], down
        )

    order_out = [d for pair in zip(range(last, -1, -1), range(COLS)) for d in pair][:COLS]
    for d in order_out:
        for seq in range(seqs):
            cross(seq, d).start()
    yield
    for d in order_out:
        for seq in range(seqs):
            cross(seq, d).wait_recv()

            def both(seq=seq, d=d):
                own = part(ROWS * d + row, seq)[...].astype(f32)
                return own + across_in[seq, d].astype(f32)

            @pl.when(col == d)
            def _():
                total[seq] = both()

            if d > 0:

                @pl.when(col == 0)
                def _():
                    sums[seq, d] = both().astype(sums.dtype)

                @pl.when((col < d) & (col > 0))
                def _():
                    rise(seq, d).wait_recv()
                    sums[seq, d] = (both() + rising[seq, d].astype(f32)).astype(sums.dtype)

                @pl.when(col < d)
                def _():
                    rise(seq, d).start()

            if d < last:

                @pl.when(col == last)
                def _():
                    sums[seq, d] = both().astype(sums.dtype)

                @pl.when((col > d) & (col < last))
                def _():
                    fall(seq, d).wait_recv()
                    sums[seq, d] = (both() + falling[seq, d].astype(f32)).astype(sums.dtype)

                @pl.when(col > d)
                def _():
                    fall(seq, d).start()

        yield
    for d in range(COLS):
        for seq in range(seqs):
            if d > 0:

                @pl.when(col == d)
                def _():
                    rise(seq, d).wait_recv()
                    total[seq] += rising[seq, d].astype(f32)

            if d < last:

                @pl.when(col == d)
                def _():
                    fall(seq, d).wait_recv()
                    total[seq] += falling[seq, d].astype(f32)

    for d in range(COLS):
        for seq in range(seqs):
            cross(seq, d).wait_send()

            @pl.when(col < d)
            def _():
                rise(seq, d).wait_send()

            @pl.when(col > d)
            def _():
                fall(seq, d).wait_send()

    yield


def epilogue_kernel(groups, d_first, grads, smalls, *refs):
    (d_own, grads_all, smalls_all, across_in, sums, rising, falling,
     pairs, pair_sums, others, quarter, copies, small_sum,
     t_send, t_recv, r_send, r_recv, e_send, e_recv, g_send, g_recv,
     s_send, s_recv, x_send, x_recv, own) = refs
    spot = Spot(groups)
    seqs, length, _ = d_first.shape
    span = length // HEADS
    spot.barrier()
    tokens = team_reduce(
        spot,
        lambda m, seq: d_first.at[seq, pl.ds(pl.multiple_of(m * span, span), span)],
        seqs, across_in, sums, rising, falling, d_own, t_send, t_recv,
    )
    weights = rep_reduce(
        spot, lambda g: grads.at[:, g], pairs, pair_sums, others, r_send, r_recv
    )
    small = rep_gather(spot, smalls, lambda g: copies.at[g], s_send, s_recv, own.at[0])
    next(weights)
    next(small)
    next(tokens)
    next(weights)
    next(small)
    next(tokens)
    quarter[...] = next(weights).astype(quarter.dtype)
    exchange = team_exchange(
        spot,
        lambda m: quarter.at[m],
        lambda m: grads_all.at[spot.group, m],
        e_send, e_recv, own.at[1],
    )
    next(exchange)
    finish(small)
    small_sum[...] = sum(copies[g] for g in range(groups))
    spread = team_exchange(
        spot, lambda m: small_sum, lambda m: smalls_all.at[m], x_send, x_recv, own.at[2]
    )
    next(spread)
    next(tokens)
    finish(exchange)
    gathered = rep_gather(
        spot, grads_all.at[spot.group], lambda g: grads_all.at[g], g_send, g_recv, None
    )
    next(gathered)
    next(tokens)
    next(gathered)
    finish(tokens, gathered, spread)


def epilogue(d_first, grads, smalls):
    seqs, length, width = d_first.shape
    _, groups, piece, cols = grads.shape
    half = groups // 2
    low_, f32 = d_first.dtype, jnp.float32
    span = length // HEADS
    block = pltpu.VMEM((seqs, COLS, span, width), low_)
    part = pltpu.VMEM((half, HEADS, piece, cols), low_)
    return pl.pallas_call(
        functools.partial(epilogue_kernel, groups),
        out_shape=(
            jax.ShapeDtypeStruct((seqs, span, width), f32),
            jax.ShapeDtypeStruct((groups, HEADS, piece, cols), low_),
            jax.ShapeDtypeStruct((HEADS,) + smalls.shape, f32),
        ),
        in_specs=[IN_VMEM] * 3,
        out_specs=[IN_VMEM] * 3,
        scratch_shapes=[
            block, block, block, block, part, part, part,
            pltpu.VMEM((HEADS, piece, cols), low_),
            pltpu.VMEM((groups,) + smalls.shape, f32),
            pltpu.VMEM(smalls.shape, f32),
            dma(3, seqs, COLS), dma(3, seqs, COLS),
            dma(groups), dma(groups), dma(HEADS), dma(HEADS), dma(groups), dma(groups),
            dma(groups), dma(groups), dma(HEADS), dma(HEADS), dma(3),
        ],
        compiler_params=pltpu.CompilerParams(
            collective_id=6, has_side_effects=True, vmem_limit_bytes=50 * 2**20
        ),
        name="epilogue",
    )(d_first, grads, smalls)


def low(a):
    return a.astype(jnp.bfloat16)


def halves(a):
    high = low(a)
    return high, low(a - high.astype(jnp.float32))


def dot(a, b, dims):
    return lax.dot_general(a, b, (dims, ((), ())), preferred_element_type=jnp.float32)


def fold(out):
    half = out.shape[1] // 2
    return out[:, :half] + out[:, half:]


def left_nn(parts):
    return jnp.concatenate(parts, axis=1)


def right_nn(parts):
    row = jnp.concatenate(parts, axis=1)
    return jnp.concatenate([row, row], axis=0)


def right_nt(parts):
    high, rest = parts
    return jnp.concatenate(
        [jnp.concatenate([high, high], axis=1), jnp.concatenate([rest, rest], axis=1)], axis=0
    )


def mul(a, b):
    return fold(dot(left_nn(halves(a)), right_nn(halves(b)), ((1,), (0,))))


def mul_nt(a, b):
    return fold(dot(left_nn(halves(a)), right_nt(halves(b)), ((1,), (1,))))


def mul_tn(a, b):
    left = jnp.concatenate(halves(a), axis=0)
    return fold(dot(left, right_nn(halves(b)), ((0,), (0,))))


def low_nn(a, b):
    return dot(low(a), low(b), ((1,), (0,)))


def low_nt(a, b):
    return dot(low(a), low(b), ((1,), (1,)))


def low_tn(a, b):
    return dot(low(a), low(b), ((0,), (0,)))


def iotas(rows, cols):
    return (
        lax.broadcasted_iota(jnp.int32, (rows, cols), 0),
        lax.broadcasted_iota(jnp.int32, (rows, cols), 1),
    )


def order(index):
    return STEPS * lax.rem(index, STRETCH) + lax.div(index, STRETCH)


def sigmoid(a):
    return 1.0 / (1.0 + jnp.exp(-a))


def softplus(a):
    return jnp.maximum(a, 0.0) + jnp.log1p(jnp.exp(-jnp.abs(a)))


def window(ref, halo, seq, base, columns):
    before = ref[seq, pl.ds(pl.multiple_of(jnp.maximum(base - 8, 0), 8), 8), columns]
    ahead = 0.0 if halo is None else halo[seq, :, columns]
    return jnp.concatenate(
        [jnp.where(base == 0, ahead, before), ref[seq, pl.ds(base, STRETCH), columns]], axis=0
    )


def stack(act, at, dim):
    return jnp.concatenate(
        [act[:, at * dim : (at + 1) * dim], act[:, (at + 1) * dim : (at + 2) * dim]], axis=0
    )


def convolve(rows, conv):
    total = None
    for tap in range(CONV):
        start = 8 - (CONV - 1) + tap
        term = conv[tap : tap + 1] * rows[start : start + STRETCH]
        total = term if total is None else total + term
    return total


def rates(small, decay):
    beta = jnp.concatenate([sigmoid(small[:, 0:1]), sigmoid(small[:, 1:2])], axis=0)
    gamma = -jnp.exp(decay[0:1]) * softplus(small + decay[1:2])
    row, col = iotas(STRETCH, STRETCH)
    tri = low(jnp.where(row >= col, 1.0, 0.0))
    high = low(gamma)
    rest = gamma - high.astype(jnp.float32)
    middle = low(rest)
    last = low(rest - middle.astype(jnp.float32))
    running = (
        dot(tri, high, ((1,), (0,))) + dot(tri, middle, ((1,), (0,))) + dot(tri, last, ((1,), (0,)))
    )
    return beta, running


def decays(running):
    column = running[:, 2:3]
    across = jnp.transpose(running)[2:3, :]
    row, col = iotas(STRETCH, STRETCH)
    gap = jnp.broadcast_to(column, (STRETCH, STRETCH)) - across
    upto = jnp.where(row >= col, jnp.exp(jnp.where(row >= col, gap, 0.0)), 0.0)
    before = jnp.where(row > col, upto, 0.0)
    strict = jnp.concatenate(
        [
            jnp.concatenate([before, before], axis=1),
            jnp.concatenate([upto, before], axis=1),
        ],
        axis=0,
    )
    return strict, jnp.concatenate([upto, upto], axis=1)


def level_masks():
    row, col = iotas(WIDE, WIDE)
    row, col = order(row), order(col)
    masks, size = [], 1
    while size < WIDE:
        inside = (lax.div(row, 2 * size) == lax.div(col, 2 * size)) & (
            lax.div(row, size) != lax.div(col, size)
        )
        masks.append(jnp.where(inside, 1.0, 0.0))
        size *= 2
    return [masks[0]] + [low(mask) for mask in masks[1:]]


def inverses(systems, masks):
    row, col = iotas(WIDE, WIDE)
    eye = jnp.where(row == col, 1.0, 0.0)
    solved = [eye - masks[0] * system for system in systems]
    split = [halves(system) for system in systems]
    for mask in masks[1:]:
        parts = [halves(a) for a in solved]
        steps = [
            fold(
                dot(
                    jnp.concatenate([high * mask, rest * mask], axis=1),
                    right_nn(part),
                    ((1,), (0,)),
                )
            )
            for (high, rest), part in zip(split, parts)
        ]
        solved = [
            a - fold(dot(left_nn(part), right_nn(halves(step)), ((1,), (0,))))
            for a, part, step in zip(solved, parts, steps)
        ]
    return solved


def unit_rows(stacked):
    return lax.rsqrt(jnp.sum(stacked * stacked, axis=1, keepdims=True) + EPS)


def twice(column):
    return jnp.concatenate([column, column], axis=0)


def forward_kernel(linked, groups, *refs):
    proj, conv, decay, gain, *refs = refs
    halo = None
    if linked:
        halo, start, *refs = refs
    if groups:
        *parts, refs = refs[0], refs[1], refs[2], refs[3:]
    out, fresh, inv, weights, trans, states, *refs = refs
    if linked:
        final, product, *refs = refs
    if groups:
        mixed, *wholes, refs = refs[0], refs[1], refs[2], refs[3], refs[4:]
    local, offset, mixer, *sems = refs
    seqs, length, _ = proj.shape
    dim = gain.shape[1]
    blocks = length // STRETCH
    span = length // HEADS
    together = span // STRETCH
    turns = blocks // together
    plan = {}
    if groups:
        sends, recvs, c_send, c_recv, x_send, x_recv, own = sems
        spot = Spot(groups)
        spot.barrier()
        first_part = team_gather(
            spot, parts[0], lambda m: wholes[0].at[m, spot.group],
            sends.at[0], recvs.at[0], own.at[0],
        )
        gathers = [
            team_gather(
                spot, parts[k], lambda m, k=k: wholes[k].at[m], sends.at[k], recvs.at[k], own.at[k]
            )
            for k in (1, 2)
        ]
        copies = rep_gather(
            spot, wholes[0].at[:, spot.group], lambda g: wholes[0].at[:, g], c_send, c_recv, None
        )
        next(first_part)
        for gather in gathers:
            next(gather)
        plan = {
            2: [first_part], 3: gathers, 4: [first_part], 5: gathers, 6: [first_part],
            7: gathers,
        }
    masks = level_masks()
    row, col = iotas(dim, dim)
    diagonal = row == col

    def spots(step):
        return [(seq, step * together + k) for k in range(together) for seq in range(seqs)]

    def first(step, _):
        units = spots(step)
        kept = []
        for seq, block in units:
            base = pl.multiple_of(block * STRETCH, STRETCH)
            rows = window(proj, halo, seq, base, pl.ds(0, 5 * dim))
            pre = convolve(rows, conv)
            act = pre * sigmoid(pre)
            raw = stack(act, 1, dim)
            key = raw * unit_rows(raw)
            beta, running = rates(proj[seq, pl.ds(base, STRETCH), pl.ds(6 * dim, dim)], decay)
            kept.append((act[:, :dim], key, stack(act, 3, dim), beta, running))
        systems = []
        for (seq, block), (query, key, value, beta, running) in zip(units, kept):
            at = seq * blocks + block
            strict, upto = decays(running)
            key_halves = halves(key)
            both = fold(
                dot(
                    jnp.concatenate([left_nn(key_halves), left_nn(halves(query))], axis=0),
                    right_nt(key_halves),
                    ((1,), (1,)),
                )
            )
            systems.append(beta * both[:WIDE] * strict)
            local[at] = both[WIDE:] * upto
            offset[at] = query * jnp.exp(running[:, 2:3])
        for (seq, block), (query, key, value, beta, running), solved in zip(
            units, kept, inverses(systems, masks)
        ):
            at = seq * blocks + block
            inv[at] = solved
            grown = twice(jnp.exp(running[:, 2:3]))
            end = running[STRETCH - 1 :, 2:3]
            solved_left = left_nn(halves(solved))
            weight = fold(dot(solved_left, right_nn(halves(beta * key * grown)), ((1,), (0,))))
            value = fold(dot(solved_left, right_nn(halves(beta * value)), ((1,), (0,))))
            weights[at] = weight
            fresh[at] = value
            to_end = jnp.concatenate(halves(key * twice(jnp.exp(end - running[:, 2:3]))), axis=0)
            trans[at] = jnp.where(diagonal, jnp.exp(end), 0.0) - fold(
                dot(to_end, right_nn(halves(weight)), ((0,), (0,)))
            )
            states[at] = fold(dot(to_end, right_nn(halves(value)), ((0,), (0,))))
        return 0

    reached = 0
    for turn in sorted(plan):
        lax.fori_loop(reached, turn, first, 0)
        reached = turn
        for step in plan[turn]:
            next(step)
    lax.fori_loop(reached, turns, first, 0)
    if groups:
        finish(first_part)
        next(copies)

    def chain(block, carried):
        new = []
        for seq in range(seqs):
            at = seq * blocks + block
            state = carried[seq]
            added = states[at]
            states[at] = state
            new.append(mul(trans[at], state) + added)
            if linked:
                product[seq] = mul(trans[at], product[seq])
        return tuple(new)

    if linked:
        for seq in range(seqs):
            product[seq] = jnp.where(diagonal, 1.0, 0.0)
        begin = tuple(start[seq] for seq in range(seqs))
    else:
        begin = (jnp.zeros((dim, dim), jnp.float32),) * seqs
    ended = lax.fori_loop(0, blocks, chain, begin)
    if linked:
        for seq in range(seqs):
            final[seq] = ended[seq]
    if groups:
        next(copies)

    def block_of(ref, mate):
        return ref.at[:, pl.ds(pl.multiple_of(mate * span, span), span)]

    def columns_of(ref, mate):
        return ref.at[:, :, pl.ds(pl.multiple_of(mate * dim, dim), dim)]

    def to_mate(mate, slot):
        return remote(
            block_of(mixer, mate), columns_of(mixed, spot.mate),
            x_send.at[slot], x_recv.at[slot], spot.to_mate(mate),
        )

    def to_self():
        return pltpu.make_async_copy(
            block_of(mixer, spot.mate), columns_of(mixed, spot.mate), own.at[3]
        )

    def last(step, _):
        units = spots(step)
        reads = [
            mul(
                jnp.concatenate([weights[seq * blocks + block], offset[seq * blocks + block]], axis=0),
                states[seq * blocks + block],
            )
            for seq, block in units
        ]
        for (seq, block), read in zip(units, reads):
            at = seq * blocks + block
            base = pl.multiple_of(block * STRETCH, STRETCH)
            new = fresh[at] - read[:WIDE]
            fresh[at] = new
            result = read[WIDE:] + mul(local[at], new)
            out[seq, pl.ds(base, STRETCH)] = result
            gate = proj[seq, pl.ds(base, STRETCH), pl.ds(5 * dim, dim)]
            scale = lax.rsqrt(jnp.mean(result * result, axis=1, keepdims=True) + EPS)
            mixer[seq, pl.ds(base, STRETCH)] = low(
                result * scale * gain[...] * (gate * sigmoid(gate))
            )
        if groups:
            slot = lax.rem(step - spot.mate + HEADS, HEADS)

            @pl.when(slot == 0)
            def _():
                to_self().start()

            @pl.when(slot != 0)
            def _():
                to_mate(step, slot).start()

        return 0

    lax.fori_loop(0, turns, last, 0)
    if groups:
        finish(copies, *gathers)
        for k in range(1, HEADS):
            to_mate(spot.mate_off(k), k).wait_recv()
        for k in range(1, HEADS):
            to_mate(spot.mate_off(k), k).wait_send()
        to_self().wait()


def mixer_forward(proj, conv, decay, gain, parts=(), groups=0, link=()):
    seqs, length, _ = proj.shape
    dim = gain.shape[1]
    units = seqs * (length // STRETCH)
    square = jax.ShapeDtypeStruct((units, WIDE, dim), jnp.float32)
    state = jax.ShapeDtypeStruct((seqs, dim, dim), jnp.float32)
    shapes = (jax.ShapeDtypeStruct((seqs, length, dim), jnp.float32),) + (square,) * 5
    if link:
        shapes += (state, state)
    specs = [IN_VMEM] * len(shapes)
    scratch = [
        pltpu.VMEM((units, STRETCH, WIDE), jnp.float32),
        pltpu.VMEM((units, STRETCH, dim), jnp.float32),
        pltpu.VMEM((seqs, length, dim), jnp.bfloat16),
    ]
    if groups:
        low_ = jnp.bfloat16
        shapes += (
            jax.ShapeDtypeStruct((seqs, length // HEADS, HEADS * dim), low_),
            jax.ShapeDtypeStruct((HEADS, groups) + parts[0].shape, low_),
            jax.ShapeDtypeStruct((HEADS,) + parts[1].shape, low_),
            jax.ShapeDtypeStruct((HEADS,) + parts[2].shape, low_),
        )
        specs += [ANY] * 4
        scratch += [dma(3, TEAM_SEMS), dma(3, TEAM_SEMS), dma(groups), dma(groups)]
        scratch += [dma(HEADS), dma(HEADS), dma(4)]
    return pl.pallas_call(
        functools.partial(forward_kernel, bool(link), groups),
        out_shape=shapes,
        in_specs=[IN_VMEM] * (4 + len(link)) + [ANY] * len(parts),
        out_specs=specs,
        scratch_shapes=scratch,
        compiler_params=pltpu.CompilerParams(
            vmem_limit_bytes=56 * 2**20,
            collective_id=2 if groups else None,
            has_side_effects=bool(groups),
        ),
        cost_estimate=pl.CostEstimate(
            flops=units * 60 * WIDE * WIDE * WIDE,
            bytes_accessed=units * WIDE * WIDE * 30,
            transcendentals=units * WIDE * WIDE * 8,
        ),
        name="mixer_forward",
    )(proj, conv, decay, gain, *link, *parts)


def backward_kernel(linked, groups, *refs):
    proj, conv, decay, gain, out, fresh, inv, weights, trans, states, d_mixer, *refs = refs
    if linked:
        halo, end_state, *refs = refs
        d_proj, d_conv, d_small_sums, d_gain, d_start, d_first, *refs = refs
    else:
        halo = None
        d_proj, d_conv, d_small_sums, d_gain, *refs = refs
    d_out, chained, *refs = refs
    seqs, length, _ = proj.shape
    dim = gain.shape[1]
    blocks = length // STRETCH
    span = length // HEADS
    together = span // STRETCH
    if groups:
        d_tokens = d_mixer
        d_mixer, x_send, x_recv, own = refs
        spot = Spot(groups)
        spot.barrier(copies=False)

        def block_of(mate):
            return d_mixer.at[:, pl.ds(pl.multiple_of(mate * span, span), span)]

        def columns_of(mate):
            return d_tokens.at[:, :, pl.ds(pl.multiple_of(mate * dim, dim), dim)]

        def from_mate(mate, slot):
            return remote(
                columns_of(mate), block_of(mate), x_send.at[slot], x_recv.at[slot],
                spot.to_mate(mate),
            )

        def from_self():
            return pltpu.make_async_copy(columns_of(spot.mate), block_of(spot.mate), own.at[0])

        exchange = team_exchange(
            spot, columns_of, block_of, x_send, x_recv, own.at[0]
        )
        next(exchange)
    all_conv = pl.ds(0, 5 * dim)

    def spots(step):
        return [(seq, blocks - 1 - step * together - k) for k in range(together) for seq in range(seqs)]

    def first(step, gain_sum):
        units = spots(step)
        kept = []
        if groups:
            origin = HEADS - 1 - step
            slot = lax.rem(spot.mate - origin + HEADS, HEADS)

            @pl.when(slot == 0)
            def _():
                from_self().wait()

            @pl.when(slot != 0)
            def _():
                from_mate(origin, slot).wait_recv()

        for seq, block in units:
            at = seq * blocks + block
            base = pl.multiple_of(block * STRETCH, STRETCH)
            result = out[seq, pl.ds(base, STRETCH)]
            gate = proj[seq, pl.ds(base, STRETCH), pl.ds(5 * dim, dim)]
            given = d_mixer[seq, pl.ds(base, STRETCH)].astype(jnp.float32)
            scale = lax.rsqrt(jnp.mean(result * result, axis=1, keepdims=True) + EPS)
            normal = result * scale
            open_ = sigmoid(gate)
            silu = gate * open_
            gain_sum = gain_sum + jnp.sum(given * normal * silu, axis=0, keepdims=True)
            d_proj[seq, pl.ds(base, STRETCH), pl.ds(5 * dim, dim)] = low(
                given * normal * gain[...] * (open_ * (1.0 + gate * (1.0 - open_)))
            )
            inner = given * gain[...] * silu
            d_result = scale * (inner - normal * jnp.mean(inner * normal, axis=1, keepdims=True))
            d_out[at] = d_result
            pre = convolve(window(proj, halo, seq, base, pl.ds(0, 3 * dim)), conv[:, : 3 * dim])
            act = pre * sigmoid(pre)
            raw = stack(act, 1, dim)
            _, running = rates(proj[seq, pl.ds(base, STRETCH), pl.ds(6 * dim, dim)], decay)
            kept.append((act[:, :dim], raw * unit_rows(raw), running, d_result))
        scores = [
            mul_nt(query, key) * decays(running)[1] for query, key, running, _ in kept
        ]
        d_freshes = [mul_tn(score, unit[3]) for score, unit in zip(scores, kept)]
        for (seq, block), (query, _, running, d_result), d_fresh in zip(units, kept, d_freshes):
            at = seq * blocks + block
            chained[at] = mul_tn(
                jnp.concatenate([query * jnp.exp(running[:, 2:3]), -weights[at]], axis=0),
                jnp.concatenate([d_result, d_fresh], axis=0),
            )
        return gain_sum

    d_gain[...] = lax.fori_loop(0, blocks // together, first, jnp.zeros((1, dim), jnp.float32))

    def chain(step, carried):
        block = blocks - 1 - step
        new = []
        for seq in range(seqs):
            at = seq * blocks + block
            later = carried[seq]
            added = chained[at]
            chained[at] = later
            new.append(mul_tn(trans[at], later) + added)
        return tuple(new)

    if linked:
        begin = tuple(end_state[seq] for seq in range(seqs))
    else:
        begin = (jnp.zeros((dim, dim), jnp.float32),) * seqs
    ended = lax.fori_loop(0, blocks, chain, begin)
    if linked:
        for seq in range(seqs):
            d_start[seq] = ended[seq]

    def last(step, sums):
        conv_sum, small_sum, *rims = sums
        units = spots(step)
        ats = [seq * blocks + block for seq, block in units]
        bases = [pl.multiple_of(block * STRETCH, STRETCH) for _, block in units]
        acts, keys, rate_sets = [], [], []
        for (seq, _), base in zip(units, bases):
            pre = convolve(window(proj, halo, seq, base, all_conv), conv)
            gate = sigmoid(pre)
            act = pre * gate
            raw = stack(act, 1, dim)
            unit = unit_rows(raw)
            acts.append((act, gate * (1.0 + pre * (1.0 - gate)), unit))
            keys.append(raw * unit)
            rate_sets.append(rates(proj[seq, pl.ds(base, STRETCH), pl.ds(6 * dim, dim)], decay))
        nears = [
            mul_nt(jnp.concatenate([key, act[:, :dim]], axis=0), key)
            for (act, _, _), key in zip(acts, keys)
        ]
        masks = [decays(running) for _, running in rate_sets]
        d_freshes = [
            mul_tn(near[WIDE:] * upto, d_out[at])
            + mul(key * twice(jnp.exp(running[STRETCH - 1 :, 2:3] - running[:, 2:3])), chained[at])
            for near, (_, upto), at, key, (_, running) in zip(nears, masks, ats, keys, rate_sets)
        ]
        backs = [mul_tn(inv[at], d_fresh) for at, d_fresh in zip(ats, d_freshes)]
        reads = [
            stack(act, 3, dim) - mul(key * twice(jnp.exp(running[:, 2:3])), states[at])
            for (act, _, _), key, (_, running), at in zip(acts, keys, rate_sets, ats)
        ]
        to_state = [
            mul_nt(jnp.concatenate([beta * back, d_out[at]], axis=0), states[at])
            for (beta, _), back, at in zip(rate_sets, backs, ats)
        ]
        to_new = [
            mul_nt(jnp.concatenate([back, d_out[at]], axis=0), fresh[at])
            for back, at in zip(backs, ats)
        ]
        d_ends = [mul_nt(fresh[at], chained[at]) for at in ats]
        shaped = [-cross[:WIDE] * strict for cross, (strict, _) in zip(to_new, masks)]
        insides = [beta * a for (beta, _), a in zip(rate_sets, shaped)]
        d_nears = [cross[WIDE:] * upto for cross, (_, upto) in zip(to_new, masks)]
        towards = [
            mul(jnp.concatenate([inside, d_near], axis=0), key)
            for inside, d_near, key in zip(insides, d_nears, keys)
        ]
        away = [
            mul_tn(
                jnp.concatenate([inside, d_near], axis=0),
                jnp.concatenate([key, act[:, :dim]], axis=0),
            )
            for inside, d_near, key, (act, _, _) in zip(insides, d_nears, keys, acts)
        ]
        d_heres = []
        for k, ((seq, _), at, base) in enumerate(zip(units, ats, bases)):
            act, slope, unit = acts[k]
            query, key = act[:, :dim], keys[k]
            beta, running = rate_sets[k]
            small = proj[seq, pl.ds(base, STRETCH), pl.ds(6 * dim, dim)]
            g = running[:, 2:3]
            end = g[STRETCH - 1 :]
            grown, to_go = jnp.exp(g), jnp.exp(end - g)
            back = backs[k]
            d_scaled, d_query_scaled = -to_state[k][:WIDE], to_state[k][WIDE:]
            with_inside = shaped[k] * nears[k][:WIDE]
            d_beta = jnp.sum(back * reads[k] + with_inside, axis=1, keepdims=True)
            gaps = beta * with_inside
            score_gaps = d_nears[k] * nears[k][WIDE:]
            d_query = towards[k][WIDE:] + d_query_scaled * grown
            from_start, from_end = d_scaled * twice(grown), d_ends[k] * twice(to_go)
            d_key = towards[k][:WIDE] + away[k] + from_start + from_end
            ended = jnp.sum(from_end * key, axis=1, keepdims=True)
            row_terms = jnp.sum(gaps + from_start * key, axis=1, keepdims=True) - ended
            col_terms = jnp.sum(gaps, axis=0, keepdims=True) + jnp.sum(
                score_gaps, axis=0, keepdims=True
            )
            col_terms = jnp.transpose(jnp.broadcast_to(col_terms, (8, WIDE)))[:, 0:1]
            row_terms = row_terms - col_terms
            d_g = (
                row_terms[:STRETCH]
                + row_terms[STRETCH:]
                + jnp.sum(score_gaps + d_query_scaled * grown * query, axis=1, keepdims=True)
            )
            d_end = jnp.sum(ended, axis=0, keepdims=True) + jnp.exp(end) * jnp.sum(
                jnp.sum(states[at] * chained[at], axis=0, keepdims=True), axis=1, keepdims=True
            )
            row, col = iotas(STRETCH, STRETCH)
            across = jnp.transpose(jnp.broadcast_to(d_g, (STRETCH, WIDE)))[:STRETCH]
            d_gamma = jnp.sum(jnp.where(row <= col, across, 0.0), axis=1, keepdims=True) + d_end
            lane = iotas(STRETCH, dim)[1]
            shifted = small + decay[1:2]
            d_soft = -jnp.exp(decay[0:1]) * d_gamma
            d_logit = d_soft * sigmoid(shifted)
            d_rate = jnp.where(lane == 0, d_beta[:STRETCH], d_beta[STRETCH:])
            open_beta = sigmoid(small)
            d_small = jnp.where(
                lane < 2,
                d_rate * open_beta * (1.0 - open_beta),
                jnp.where(lane == 2, d_logit, 0.0),
            )
            d_proj[seq, pl.ds(base, STRETCH), pl.ds(6 * dim, dim)] = low(d_small)
            small_sum = small_sum + jnp.concatenate(
                [
                    jnp.sum(d_soft * softplus(shifted), axis=0, keepdims=True),
                    jnp.sum(d_logit, axis=0, keepdims=True),
                ],
                axis=0,
            )
            d_raw = unit * (d_key - key * jnp.sum(d_key * key, axis=1, keepdims=True))
            d_value = beta * back
            d_act = jnp.concatenate(
                [d_query, d_raw[:STRETCH], d_raw[STRETCH:], d_value[:STRETCH], d_value[STRETCH:]],
                axis=1,
            )
            d_heres.append(d_act * slope)
        for (seq, _), base, d_here in zip(units, bases, d_heres):
            rows = window(proj, halo, seq, base, all_conv)
            first_row = 8 - (CONV - 1)
            conv_sum = conv_sum + jnp.concatenate(
                [
                    jnp.sum(
                        d_here * rows[first_row + tap : first_row + tap + STRETCH],
                        axis=0,
                        keepdims=True,
                    )
                    for tap in range(CONV)
                ],
                axis=0,
            )
            ahead = jnp.concatenate([d_here, rims[seq]], axis=0)
            rims[seq] = d_here[:8]
            total = None
            for tap in range(CONV):
                start = CONV - 1 - tap
                term = conv[tap : tap + 1] * ahead[start : start + STRETCH]
                total = term if total is None else total + term
            d_proj[seq, pl.ds(base, STRETCH), all_conv] = low(total)
        return conv_sum, small_sum, *rims

    conv_sum, small_sum, *rims = lax.fori_loop(
        0,
        blocks // together,
        last,
        (jnp.zeros((CONV, 5 * dim), jnp.float32), jnp.zeros((2, dim), jnp.float32))
        + (jnp.zeros((8, 5 * dim), jnp.float32),) * seqs,
    )
    if linked:
        for seq in range(seqs):
            d_first[seq] = rims[seq]
    d_conv[...] = conv_sum
    d_small_sums[...] = small_sum
    if groups:
        for k in range(1, HEADS):
            from_mate(spot.mate_off(k), k).wait_send()


def mixer_backward(proj, conv, decay, gain, kept, d_mixer, groups=0, link=()):
    seqs, length, width = proj.shape
    dim = gain.shape[1]
    units = seqs * (length // STRETCH)
    shapes = (
        jax.ShapeDtypeStruct((seqs, length, width), jnp.bfloat16),
        jax.ShapeDtypeStruct((CONV, 5 * dim), jnp.float32),
        jax.ShapeDtypeStruct((2, dim), jnp.float32),
        jax.ShapeDtypeStruct((1, dim), jnp.float32),
    )
    if link:
        shapes += (
            jax.ShapeDtypeStruct((seqs, dim, dim), jnp.float32),
            jax.ShapeDtypeStruct((seqs, 8, 5 * dim), jnp.float32),
        )
    return pl.pallas_call(
        functools.partial(backward_kernel, bool(link), groups),
        out_shape=shapes,
        in_specs=[IN_VMEM] * (11 + len(link)),
        out_specs=[IN_VMEM] * len(shapes),
        scratch_shapes=[
            pltpu.VMEM((units, STRETCH, dim), jnp.float32),
            pltpu.VMEM((units, dim, dim), jnp.float32),
        ]
        + (
            [pltpu.VMEM((seqs, length, dim), jnp.bfloat16), dma(HEADS), dma(HEADS), dma(1)]
            if groups
            else []
        ),
        compiler_params=pltpu.CompilerParams(
            vmem_limit_bytes=60 * 2**20,
            collective_id=5 if groups else None,
            has_side_effects=bool(groups),
        ),
        cost_estimate=pl.CostEstimate(
            flops=units * 60 * WIDE * WIDE * WIDE,
            bytes_accessed=units * WIDE * WIDE * 30,
            transcendentals=units * WIDE * WIDE * 8,
        ),
        name="mixer_backward",
    )(proj, conv, decay, gain, *kept, d_mixer, *link)


def matmul(left, right):
    return jnp.dot(left, right, preferred_element_type=jnp.float32)


def times_transposed(left, right):
    return lax.dot_general(
        left, right, (((1,), (1,)), ((), ())), preferred_element_type=jnp.float32
    )


def transposed_times(left, right):
    return lax.dot_general(
        left, right, (((0,), (0,)), ((), ())), preferred_element_type=jnp.float32
    )


def batched(left, right):
    return jnp.einsum("sij,sjk->sik", left, right, precision=lax.Precision.HIGHEST)


def norm_scale(values):
    return lax.rsqrt(jnp.mean(values * values, axis=-1, keepdims=True) + EPS)


def norm_back(values, gain, given):
    scale = norm_scale(values)
    normal = values * scale
    inner = given * gain
    return scale * (inner - normal * jnp.mean(inner * normal, axis=-1, keepdims=True)), (
        given * normal
    )


def per_device(
    block_in,
    lengths,
    norm_gains,
    w_in,
    w_small,
    conv_weight,
    decay_log,
    decay_bias,
    out_norm_gain,
    w_out,
    gate_up_weight,
    w_down,
    out_cotangent,
):
    micro, seq_count, tokens, width = block_in.shape
    seqs = micro * seq_count
    count = lax.axis_size("ctx")
    groups = lax.axis_size("rep")
    place = lax.axis_index("ctx")
    group = lax.axis_index("rep")
    teams = count // HEADS
    head = lax.rem(place, HEADS)
    team = lax.div(place, HEADS)
    mates = peers = None
    if teams > 1:
        mates = [[t * HEADS + h for h in range(HEADS)] for t in range(teams)]
        peers = [[t * HEADS + h for t in range(teams)] for h in range(HEADS)]
    dim = width // HEADS
    length = HEADS * tokens
    rows = seqs * tokens
    kinds = 2 + 2 * STEPS
    rates_of = STEPS + 1
    f32, bf16 = jnp.float32, jnp.bfloat16

    def over_teams(array):
        if teams == 1:
            return array
        return lax.all_gather(array, "ctx", axis=0, tiled=True, axis_index_groups=peers)

    places = place * tokens + lax.broadcasted_iota(jnp.int32, (seqs, tokens), 1)
    valid = (places < lengths.reshape(seqs, 1)).astype(f32).reshape(rows, 1)
    grad_out = (out_cotangent.reshape(rows, width).astype(f32) * valid).astype(bf16)

    own = width // count
    small_block = jnp.concatenate(
        [norm_gains.reshape(-1), w_small.reshape(-1), conv_weight.reshape(-1)]
    )
    small_block = jnp.pad(small_block, (0, -small_block.size % 128)).reshape(-1, 128)
    piece = own // groups
    pieces = w_in.reshape(groups, piece, kinds, HEADS, dim).transpose(3, 0, 1, 2, 4)
    sequence, w_head, smalls, grad_all = prologue(
        block_in.reshape(seqs, tokens, width),
        pieces.reshape(HEADS, groups, piece, kinds * dim),
        small_block,
        grad_out,
        groups,
    )
    grad_all = grad_all.reshape(groups * rows, width)
    smalls = over_teams(smalls).reshape(count, -1)
    gains = smalls[:, : 2 * own].reshape(count, 2, own).transpose(1, 0, 2).reshape(2, width)
    gains = gains.astype(f32)
    small_all = smalls[:, 2 * own : (2 + HEADS * rates_of) * own].reshape(width, rates_of, HEADS)
    small_head = lax.dynamic_index_in_dim(small_all, head, 2, keepdims=False)
    taps_at = (2 + HEADS * rates_of) * own
    conv_all = smalls[:, taps_at : taps_at + conv_weight.size].reshape(count, CONV, -1)
    conv_all = conv_all.transpose(1, 0, 2).reshape(CONV, kinds - 1, HEADS, dim)
    conv_head = lax.dynamic_index_in_dim(conv_all, head, 2, keepdims=False)
    conv_head = conv_head.reshape(CONV, -1).astype(f32)
    w_head = jnp.concatenate(
        [
            over_teams(w_head).reshape(width, kinds * dim),
            small_head,
            jnp.zeros((width, dim - rates_of), bf16),
        ],
        axis=1,
    )
    hidden_own = w_down.shape[0] // groups
    hidden_units = count * hidden_own
    out_piece = lax.dynamic_index_in_dim(
        w_out.reshape(groups, piece, width), group, 0, keepdims=False
    )
    gate_up_part = lax.dynamic_index_in_dim(
        gate_up_weight.reshape(own, 2, count, groups, hidden_own), group, 3, keepdims=False
    ).reshape(own, -1)
    down_part = lax.dynamic_index_in_dim(
        w_down.reshape(groups, hidden_own, width), group, 0, keepdims=False
    )
    parts = (out_piece, gate_up_part, down_part)

    inputs_all = sequence.astype(f32)
    h_first = (inputs_all * norm_scale(inputs_all) * gains[0]).astype(bf16)
    proj = matmul(h_first.reshape(seqs * length, width), w_head).reshape(seqs, length, -1)
    decay = jnp.stack(
        [
            jnp.broadcast_to(lax.dynamic_index_in_dim(decay_log, head, 0), (dim,)),
            jnp.broadcast_to(lax.dynamic_index_in_dim(decay_bias, head, 0), (dim,)),
        ]
    )
    gain = out_norm_gain.reshape(1, dim)
    halo = None
    if teams > 1:
        onward = [(c, c + HEADS) for c in range(count - HEADS)]
        halo = lax.ppermute(proj[:, length - 8 :], "ctx", onward)
        start = jnp.zeros((seqs, dim, dim), f32)
        *_, offset, transfer = mixer_forward(
            proj, conv_head, decay, gain, link=(halo, start)
        )
        spans = lax.all_gather((transfer, offset), "ctx", axis_index_groups=peers)
        for turn in range(teams - 1):
            start = jnp.where(turn < team, batched(spans[0][turn], start) + spans[1][turn], start)
        link = (halo, start)
    else:
        link = ()
    *kept, mixer, w_out_full, gate_up_part, down_part = mixer_forward(
        proj, conv_head, decay, gain, parts, groups, link
    )
    kept = kept[:6]
    mixer = mixer.reshape(rows, width)
    w_out_full = over_teams(w_out_full).reshape(width, width)
    gate_up_part = over_teams(gate_up_part).reshape(width, 2 * hidden_units)
    down_part = over_teams(down_part).reshape(hidden_units, width)

    inputs = block_in.reshape(rows, width).astype(f32)
    resid = inputs + matmul(mixer, w_out_full)

    h_second = (resid * norm_scale(resid) * gains[1]).astype(bf16)
    h_all = gather_copies(h_second, groups, 3).reshape(groups * rows, width)
    gate_up = matmul(h_all, gate_up_part)
    gate, up = gate_up[:, :hidden_units], gate_up[:, hidden_units:]
    open_gate = jax.nn.sigmoid(gate)
    silu = gate * open_gate
    hidden = (silu * up).astype(bf16)
    down = lax.psum_scatter(
        matmul(hidden, down_part).astype(bf16), "rep", scatter_dimension=0, tiled=True
    )
    result = (valid * (resid + down.astype(f32))).astype(bf16)

    d_hidden = times_transposed(grad_all, down_part)
    d_gate_up = jnp.concatenate(
        [d_hidden * up * (open_gate * (1.0 + gate * (1.0 - open_gate))), d_hidden * silu], axis=1
    ).astype(bf16)
    d_second = reduce_copies(
        times_transposed(d_gate_up, gate_up_part).astype(bf16).reshape(groups, rows, width), 4
    )
    grad_down = transposed_times(hidden, grad_all)
    grad_gate_up = transposed_times(h_all, d_gate_up)
    d_norm, gain_terms_second = norm_back(resid, gains[1], d_second)
    d_resid = grad_out.astype(f32) + d_norm
    d_branch = d_resid.astype(bf16)
    grad_out_proj = transposed_times(mixer, d_branch)
    d_mixer = times_transposed(d_branch, w_out_full)

    d_mixer = d_mixer.astype(bf16)
    if teams > 1:
        def to_heads(array):
            split = array.reshape(rows, HEADS, dim).transpose(1, 0, 2)
            moved = lax.all_to_all(split, "ctx", 0, 0, tiled=True, axis_index_groups=mates)
            return moved.reshape(HEADS, seqs, tokens, dim).transpose(1, 0, 2, 3).reshape(
                seqs, length, dim
            )

        d_mixer = to_heads(d_mixer)
        later = jnp.zeros((seqs, dim, dim), f32)
        local = mixer_backward(proj, conv_head, decay, gain, kept, d_mixer, link=(halo, later))[4]
        locals_ = lax.all_gather(local, "ctx", axis_index_groups=peers)
        for turn in range(teams - 1, 0, -1):
            later = jnp.where(
                turn > team,
                batched(spans[0][turn].transpose(0, 2, 1), later) + locals_[turn],
                later,
            )
        d_proj, grad_conv, small_sums, grad_gain, _, rim = mixer_backward(
            proj, conv_head, decay, gain, kept, d_mixer, link=(halo, later)
        )
        rim = lax.ppermute(rim, "ctx", [(c, c - HEADS) for c in range(HEADS, count)])
        spill = jnp.zeros((seqs, CONV - 1, kinds * dim - dim), f32)
        for ahead in range(1, CONV):
            spill = spill.at[:, CONV - 1 - ahead :].add(
                conv_head[CONV - 1 - ahead] * rim[:, :ahead]
            )
        last = d_proj[:, length - CONV + 1 :, : (kinds - 1) * dim]
        d_proj = d_proj.at[:, length - CONV + 1 :, : (kinds - 1) * dim].set(
            (last.astype(f32) + spill).astype(bf16)
        )
    else:
        d_proj, grad_conv, small_sums, grad_gain = mixer_backward(
            proj, conv_head, decay, gain, kept, d_mixer.reshape(seqs, tokens, width), groups
        )
    d_proj = d_proj.reshape(seqs * length, -1)
    h_flat = h_first.reshape(seqs * length, width)
    grad_head = transposed_times(h_flat, d_proj[:, : kinds * dim]).astype(bf16)
    grad_small = transposed_times(d_proj[:, kinds * dim : kinds * dim + 8], h_flat)
    d_first = times_transposed(d_proj, w_head)
    normal_all = (inputs_all * norm_scale(inputs_all)).reshape(seqs * length, width)
    grad_gains = jnp.stack(
        [(d_first * normal_all).sum(axis=0), gain_terms_second.sum(axis=0)]
    )
    packed = jnp.concatenate(
        [
            grad_gains.reshape(-1, dim),
            grad_small[:rates_of].reshape(-1, dim),
            grad_conv.reshape(-1, dim),
            grad_gain,
            small_sums[:, STEPS : STEPS + 1] + jnp.zeros((1, dim), f32),
        ]
    )
    packed = jnp.pad(packed, ((0, -packed.shape[0] % 8), (0, 0)))
    if teams > 1:
        grad_head = lax.psum_scatter(
            grad_head, "ctx", scatter_dimension=0, tiled=True, axis_index_groups=peers
        )
        packed = lax.psum(packed, "ctx", axis_index_groups=peers)
    d_first, grad_in, packed = epilogue(
        d_first.astype(bf16).reshape(seqs, length, width),
        grad_head.reshape(HEADS, groups, piece, kinds * dim),
        packed,
    )
    d_inputs, _ = norm_back(inputs, gains[0], d_first.reshape(rows, width))
    in_grad = (d_resid + d_inputs).astype(bf16)
    grad_in = grad_in.reshape(groups, HEADS, piece, kinds, dim).transpose(0, 2, 3, 1, 4)
    grad_in = grad_in.reshape(own, -1)

    grad_gate_up = lax.psum_scatter(
        grad_gate_up.astype(bf16), "ctx", scatter_dimension=0, tiled=True
    )
    grad_gate_up = lax.all_gather(
        grad_gate_up.reshape(own, 2, count, hidden_own), "rep", axis=3
    ).reshape(own, -1)
    grad_down = lax.psum_scatter(grad_down.astype(bf16), "ctx", scatter_dimension=0, tiled=True)
    grad_down = lax.all_gather(grad_down, "rep", axis=0, tiled=True)
    grad_out_proj = lax.psum_scatter(
        grad_out_proj.astype(bf16), "ctx", scatter_dimension=0, tiled=True
    )
    grad_out_proj = lax.psum(grad_out_proj, "rep")

    def take(size):
        nonlocal packed
        part, packed = packed[:, :size], packed[:, size:]
        return part

    grad_gains = take(2 * HEADS).sum(axis=0).reshape(2, width)
    grad_small = take(rates_of * HEADS).reshape(HEADS, rates_of, width)
    grad_small = grad_small.transpose(2, 1, 0).reshape(width, rates_of * HEADS)
    grad_conv = take(CONV * (kinds - 1)).reshape(HEADS, CONV, kinds - 1, dim)
    grad_conv = grad_conv.transpose(1, 2, 0, 3).reshape(CONV, (kinds - 1) * width)
    grad_gain = take(1).sum(axis=0).reshape(dim)
    decays_sum = take(2)[:, :, 0].transpose(1, 0)

    def mine(array, axis, size):
        return lax.dynamic_slice_in_dim(array, place * size, size, axis)

    grad_gains = mine(grad_gains, 1, own)
    grad_small = mine(grad_small, 0, own)
    grad_conv = mine(grad_conv, 1, conv_weight.shape[1])
    return (
        result.reshape(block_in.shape),
        in_grad.reshape(block_in.shape),
        grad_gains,
        grad_in.astype(f32),
        grad_small,
        grad_conv,
        decays_sum[0],
        decays_sum[1],
        grad_gain,
        grad_out_proj.astype(f32),
        grad_gate_up.astype(f32),
        grad_down.astype(f32),
    )


def solution(mesh):
    placed = (
        P(None, "rep", "ctx", None),
        P(None, "rep"),
        P(None, "ctx"),
        P("ctx", None),
        P("ctx", None),
        P(None, "ctx"),
        P(),
        P(),
        P(),
        P("ctx", None),
        P("ctx", None),
        P("ctx", None),
        P(None, "rep", "ctx", None),
    )
    return jax.shard_map(
        per_device,
        mesh=mesh,
        in_specs=placed,
        out_specs=(
            P(None, "rep", "ctx", None),
            P(None, "rep", "ctx", None),
            P(None, "ctx"),
            P("ctx", None),
            P("ctx", None),
            P(None, "ctx"),
            P(),
            P(),
            P(),
            P("ctx", None),
            P("ctx", None),
            P("ctx", None),
        ),
        check_vma=False,
    )
```

```python
import functools
import jax
import jax.numpy as jnp
from jax import lax
from jax.experimental import pallas as pl
from jax.experimental.pallas import tpu as pltpu
from jax.sharding import PartitionSpec as P

STEPS = 2
CONV = 4
STRETCH = 64
HEADS = 8
EPS = 1e-06
WIDE = 2 * STRETCH


MESH = pl.DeviceIdType.MESH
ROWS = 2
COLS = HEADS // ROWS


class Spot:
    def __init__(self, groups):
        place = lax.axis_index("ctx")
        self.mate = lax.rem(place, HEADS)
        self.base = place - self.mate
        self.col = lax.div(self.mate, ROWS)
        self.row = lax.rem(self.mate, ROWS)
        self.groups = groups
        self.group = lax.axis_index("rep")
        self.side = lax.rem(self.group, 2)
        self.pair = lax.div(self.group, 2)
        self.twin = self.group + 1 - 2 * self.side

    def to_mate(self, mate):
        return {"ctx": self.base + mate}

    def to_group(self, group):
        return {"rep": group}

    def mate_off(self, k):
        return lax.rem(self.mate + k, HEADS)

    def group_off(self, k):
        return lax.rem(self.group + 2 * k, self.groups)

    def barrier(self, team=True, copies=True):
        sem = pltpu.get_barrier_semaphore()
        others = []
        if team:
            others += [self.to_mate(self.mate_off(k)) for k in range(1, HEADS)]
        if copies:
            others += [self.to_group(self.twin)]
            others += [self.to_group(self.group_off(k)) for k in range(1, self.groups // 2)]
        for other in others:
            pl.semaphore_signal(sem, inc=1, device_id=other, device_id_type=MESH)
        pl.semaphore_wait(sem, len(others))


def remote(src, dst, send, recv, where):
    return pltpu.make_async_remote_copy(
        src_ref=src,
        dst_ref=dst,
        send_sem=send,
        recv_sem=recv,
        device_id=where,
        device_id_type=MESH,
    )


TEAM_SEMS = 3 * COLS + 1


def team_gather(spot, src, out, send, recv, own):
    mate, col = spot.mate, spot.col
    up, down = spot.to_mate(mate + ROWS), spot.to_mate(mate - ROWS)
    across = spot.to_mate(mate + 1 - 2 * spot.row)
    other = mate + 1 - 2 * spot.row
    local = pltpu.make_async_copy(src, out(mate), own)

    def hop(block, origin, slot, where):
        return remote(block, out(origin), send.at[slot], recv.at[slot], where)

    rise, fall, cross_low, cross_high = 0, COLS - 1, 2 * COLS - 2, 3 * COLS - 3
    last = COLS - 1
    local.start()

    @pl.when(col < last)
    def _():
        hop(src, mate, rise, up).start()

    @pl.when(col > 0)
    def _():
        hop(src, mate, fall, down).start()

    hop(src, mate, cross_low, across).start()
    yield
    for k in range(1, COLS):
        below, above = mate - ROWS * k, mate + ROWS * k

        @pl.when(col >= k)
        def _():
            hop(out(below), below, rise + k - 1, up).wait_recv()
            if k < last:

                @pl.when(col < last)
                def _():
                    hop(out(below), below, rise + k, up).start()

            hop(out(below), below, cross_low + k, across).start()

        @pl.when(col + k <= last)
        def _():
            hop(out(above), above, fall + k - 1, down).wait_recv()
            if k < last:

                @pl.when(col > 0)
                def _():
                    hop(out(above), above, fall + k, down).start()

            hop(out(above), above, cross_high + k, across).start()

        yield
    hop(src, other, cross_low, across).wait_recv()
    for k in range(1, COLS):

        @pl.when(col >= k)
        def _():
            hop(src, other - ROWS * k, cross_low + k, across).wait_recv()

        @pl.when(col + k <= last)
        def _():
            hop(src, other + ROWS * k, cross_high + k, across).wait_recv()

    @pl.when(col < last)
    def _():
        hop(src, mate, rise, up).wait_send()

    @pl.when(col > 0)
    def _():
        hop(src, mate, fall, down).wait_send()

    hop(src, mate, cross_low, across).wait_send()
    for k in range(1, COLS):

        @pl.when(col >= k)
        def _():
            if k < last:

                @pl.when(col < last)
                def _():
                    hop(src, mate, rise + k, up).wait_send()

            hop(src, mate, cross_low + k, across).wait_send()

        @pl.when(col + k <= last)
        def _():
            if k < last:

                @pl.when(col > 0)
                def _():
                    hop(src, mate, fall + k, down).wait_send()

            hop(src, mate, cross_high + k, across).wait_send()

    local.wait()
    yield


def rep_gather(spot, src, out, send, recv, own):
    group, twin, half = spot.group, spot.twin, spot.groups // 2
    local = None
    if own is not None:
        local = pltpu.make_async_copy(src, out(group), own)
        local.start()

    def hop(block, origin, slot, where):
        return remote(block, out(origin), send.at[slot], recv.at[slot], spot.to_group(where))

    hop(src, group, 0, twin).start()
    for k in range(1, half):
        hop(src, group, k, spot.group_off(k)).start()
    yield
    for k in range(1, half):
        origin = spot.group_off(half - k)
        hop(out(origin), origin, k, twin).wait_recv()
        hop(out(origin), origin, half + k, twin).start()
    yield
    hop(src, twin, 0, twin).wait_recv()
    for k in range(1, half):
        origin = lax.rem(twin + 2 * (half - k), spot.groups)
        hop(src, origin, half + k, twin).wait_recv()
    hop(src, group, 0, twin).wait_send()
    for k in range(1, half):
        hop(src, group, k, twin).wait_send()
        hop(src, group, half + k, twin).wait_send()
    if local is not None:
        local.wait()
    yield


def team_exchange(spot, src, dst, send, recv, own):
    local = pltpu.make_async_copy(src(spot.mate), dst(spot.mate), own)
    local.start()

    def hop(k):
        to = spot.mate_off(k)
        return remote(src(to), dst(spot.mate), send.at[k], recv.at[k], spot.to_mate(to))

    for k in range(1, HEADS):
        hop(k).start()
    yield
    for k in range(1, HEADS):
        hop(k).wait_recv()
    for k in range(1, HEADS):
        hop(k).wait_send()
    local.wait()
    yield


def dma(*shape):
    return pltpu.SemaphoreType.DMA(shape)


ANY = pl.BlockSpec(memory_space=pl.ANY)
IN_VMEM = pl.BlockSpec(memory_space=pltpu.VMEM)


def finish(*steps):
    for step in steps:
        for _ in step:
            pass


def prologue_kernel(groups, tokens_in, pieces, smalls, given, sequence, w_head, smalls_all, given_all, *sems):
    (ex_send, ex_recv, sm_send, sm_recv, tok_send, tok_recv, rep_send, rep_recv, w_send, w_recv, own) = sems
    spot = Spot(groups)
    span = tokens_in.shape[1]
    spot.barrier()
    small = team_exchange(
        spot, lambda m: smalls, lambda m: smalls_all.at[m], sm_send, sm_recv, own.at[0]
    )
    exchange = team_exchange(
        spot,
        lambda m: pieces.at[m, spot.group],
        lambda m: w_head.at[m, spot.group],
        ex_send,
        ex_recv,
        own.at[1],
    )
    gathers = [
        team_gather(
            spot,
            tokens_in.at[seq],
            lambda m, seq=seq: sequence.at[seq, pl.ds(pl.multiple_of(m * span, span), span)],
            tok_send.at[seq],
            tok_recv.at[seq],
            own.at[4 + seq],
        )
        for seq in range(tokens_in.shape[0])
    ]
    copies = rep_gather(spot, given, lambda g: given_all.at[g], rep_send, rep_recv, own.at[2])
    next(exchange)
    next(small)
    for gather in gathers:
        next(gather)
    next(copies)
    finish(exchange)
    weights = rep_gather(
        spot, w_head.at[:, spot.group], lambda g: w_head.at[:, g], w_send, w_recv, None
    )
    next(weights)
    for _ in range(1, COLS):
        for gather in gathers:
            next(gather)
    next(weights)
    finish(weights, copies, small, *gathers)


def prologue(tokens_in, pieces, smalls, given, groups):
    seqs, span, width = tokens_in.shape
    return pl.pallas_call(
        functools.partial(prologue_kernel, groups),
        out_shape=(
            jax.ShapeDtypeStruct((seqs, HEADS * span, width), tokens_in.dtype),
            jax.ShapeDtypeStruct(pieces.shape, pieces.dtype),
            jax.ShapeDtypeStruct((HEADS,) + smalls.shape, smalls.dtype),
            jax.ShapeDtypeStruct((groups,) + given.shape, given.dtype),
        ),
        in_specs=[ANY] * 4,
        out_specs=[ANY] * 4,
        scratch_shapes=[
            dma(HEADS), dma(HEADS), dma(HEADS), dma(HEADS),
            dma(seqs, TEAM_SEMS), dma(seqs, TEAM_SEMS),
            dma(groups), dma(groups), dma(groups), dma(groups), dma(4 + seqs),
        ],
        compiler_params=pltpu.CompilerParams(collective_id=1, has_side_effects=True),
        name="prologue",
    )(tokens_in, pieces, smalls, given)


def copies_kernel(groups, block, out, send, recv, own):
    spot = Spot(groups)
    spot.barrier(team=False)
    finish(rep_gather(spot, block, lambda g: out.at[g], send, recv, own.at[0]))


def gather_copies(block, groups, number):
    return pl.pallas_call(
        functools.partial(copies_kernel, groups),
        out_shape=jax.ShapeDtypeStruct((groups,) + block.shape, block.dtype),
        in_specs=[ANY],
        out_specs=ANY,
        scratch_shapes=[dma(groups), dma(groups), dma(1)],
        compiler_params=pltpu.CompilerParams(collective_id=number, has_side_effects=True),
        name="gather_copies",
    )(block)


def rep_reduce(spot, part, sums, others, send, recv):
    half, side = spot.groups // 2, spot.side

    def to_twin(k):
        return remote(
            part(2 * k + 1 - side), sums.at[k], send.at[k], recv.at[k], spot.to_group(spot.twin)
        )

    def onward(k):
        slot = half + k
        return remote(
            sums.at[lax.rem(spot.pair + k, half)], others.at[k], send.at[slot], recv.at[slot], spot.to_group(spot.group_off(k))
        )

    for k in range(half):
        to_twin(k).start()
    yield
    for k in range(half):
        to_twin(k).wait_recv()

    def both(pair):
        return part(2 * pair + side)[...].astype(jnp.float32) + sums[pair].astype(jnp.float32)

    for k in range(1, half):
        pair = lax.rem(spot.pair + k, half)
        sums[pair] = both(pair).astype(sums.dtype)
        onward(k).start()
    yield
    total = both(spot.pair)
    for k in range(1, half):
        onward(k).wait_recv()
        total = total + others[k].astype(jnp.float32)
    for k in range(half):
        to_twin(k).wait_send()
    for k in range(1, half):
        onward(k).wait_send()
    yield total


def reduce_kernel(groups, parts, out, sums, others, send, recv):
    spot = Spot(groups)
    spot.barrier(team=False)
    *_, total = rep_reduce(spot, lambda g: parts.at[g], sums, others, send, recv)
    out[...] = total


def reduce_copies(parts, number):
    groups = parts.shape[0]
    block = (groups // 2,) + parts.shape[1:]
    return pl.pallas_call(
        functools.partial(reduce_kernel, groups),
        out_shape=jax.ShapeDtypeStruct(parts.shape[1:], jnp.float32),
        in_specs=[IN_VMEM],
        out_specs=IN_VMEM,
        scratch_shapes=[pltpu.VMEM(block, parts.dtype)] * 2 + [dma(groups), dma(groups)],
        compiler_params=pltpu.CompilerParams(
            collective_id=number, has_side_effects=True, vmem_limit_bytes=40 * 2**20
        ),
        name="reduce_copies",
    )(parts)


def team_reduce(spot, part, seqs, sums, passing, total, send, recv):
    mate, col, row = spot.mate, spot.col, spot.row
    up, down = spot.to_mate(mate + ROWS), spot.to_mate(mate - ROWS)
    across = spot.to_mate(mate + 1 - 2 * row)
    last = COLS - 1
    f32 = jnp.float32

    def cross(seq, d):
        return remote(
            part(ROWS * d + 1 - row, seq),
            sums.at[seq, d],
            send.at[0, seq, d],
            recv.at[0, seq, d],
            across,
        )

    def rise(seq, d):
        return remote(
            sums.at[seq, d], passing.at[seq, d + 1], send.at[1, seq, d], recv.at[1, seq, d], up
        )

    def fall(seq, d):
        return remote(
            sums.at[seq, d], passing.at[seq, d], send.at[2, seq, d], recv.at[2, seq, d], down
        )

    order_out = [d for pair in zip(range(last, -1, -1), range(COLS)) for d in pair][:COLS]
    for d in order_out:
        for seq in range(seqs):
            cross(seq, d).start()
    yield
    for d in order_out:
        for seq in range(seqs):
            cross(seq, d).wait_recv()

            def both(seq=seq, d=d):
                own = part(ROWS * d + row, seq)[...].astype(f32)
                return own + sums[seq, d].astype(f32)

            @pl.when(col == d)
            def _():
                total[seq] = both()

            if d > 0:

                @pl.when(col == 0)
                def _():
                    sums[seq, d] = both().astype(sums.dtype)

                @pl.when((col < d) & (col > 0))
                def _():
                    rise(seq, d).wait_recv()
                    sums[seq, d] = (both() + passing[seq, d + 1].astype(f32)).astype(sums.dtype)

                @pl.when(col < d)
                def _():
                    rise(seq, d).start()

            if d < last:

                @pl.when(col == last)
                def _():
                    sums[seq, d] = both().astype(sums.dtype)

                @pl.when((col > d) & (col < last))
                def _():
                    fall(seq, d).wait_recv()
                    sums[seq, d] = (both() + passing[seq, d].astype(f32)).astype(sums.dtype)

                @pl.when(col > d)
                def _():
                    fall(seq, d).start()

        yield
    for d in range(COLS):
        for seq in range(seqs):
            if d > 0:

                @pl.when(col == d)
                def _():
                    rise(seq, d).wait_recv()
                    total[seq] += passing[seq, d + 1].astype(f32)

            if d < last:

                @pl.when(col == d)
                def _():
                    fall(seq, d).wait_recv()
                    total[seq] += passing[seq, d].astype(f32)

    for d in range(COLS):
        for seq in range(seqs):
            cross(seq, d).wait_send()

            @pl.when(col < d)
            def _():
                rise(seq, d).wait_send()

            @pl.when(col > d)
            def _():
                fall(seq, d).wait_send()

    yield


def epilogue_kernel(groups, d_first, grads, smalls, gate_up, down, *refs):
    (d_own, grads_all, smalls_all, gate_up_all, down_all, sums, passing,
     pair_sums, others, quarter, copies, small_sum,
     t_send, t_recv, r_send, r_recv, e_send, e_recv, g_send, g_recv,
     s_send, s_recv, x_send, x_recv, f_send, f_recv, own) = refs
    spot = Spot(groups)
    seqs, length, _ = d_first.shape
    span = length // HEADS
    spot.barrier()
    tokens = team_reduce(
        spot,
        lambda m, seq: d_first.at[seq, pl.ds(pl.multiple_of(m * span, span), span)],
        seqs, sums, passing, d_own, t_send, t_recv,
    )
    weights = rep_reduce(
        spot, lambda g: grads.at[:, g], pair_sums, others, r_send, r_recv
    )
    small = rep_gather(spot, smalls, lambda g: copies.at[g], s_send, s_recv, own.at[0])
    ready = [
        rep_gather(spot, gate_up, lambda g: gate_up_all.at[g], f_send.at[0], f_recv.at[0], own.at[3]),
        rep_gather(spot, down, lambda g: down_all.at[g], f_send.at[1], f_recv.at[1], own.at[4]),
    ]
    next(weights)
    next(small)
    next(tokens)
    next(weights)
    next(small)
    for step in ready:
        next(step)
    next(tokens)
    quarter[...] = next(weights).astype(quarter.dtype)
    exchange = team_exchange(
        spot,
        lambda m: quarter.at[m],
        lambda m: grads_all.at[spot.group, m],
        e_send, e_recv, own.at[1],
    )
    next(exchange)
    finish(small)
    small_sum[...] = sum(copies[g] for g in range(groups))
    spread = team_exchange(
        spot, lambda m: small_sum, lambda m: smalls_all.at[m], x_send, x_recv, own.at[2]
    )
    next(spread)
    next(tokens)
    finish(exchange)
    gathered = rep_gather(
        spot, grads_all.at[spot.group], lambda g: grads_all.at[g], g_send, g_recv, None
    )
    next(gathered)
    for step in ready:
        next(step)
    next(tokens)
    next(gathered)
    finish(tokens, gathered, spread, *ready)


def epilogue(d_first, grads, smalls, gate_up, down):
    seqs, length, width = d_first.shape
    _, groups, piece, cols = grads.shape
    half = groups // 2
    low_, f32 = d_first.dtype, jnp.float32
    span = length // HEADS
    part = pltpu.VMEM((half, HEADS, piece, cols), low_)
    return pl.pallas_call(
        functools.partial(epilogue_kernel, groups),
        out_shape=(
            jax.ShapeDtypeStruct((seqs, span, width), f32),
            jax.ShapeDtypeStruct((groups, HEADS, piece, cols), low_),
            jax.ShapeDtypeStruct((HEADS,) + smalls.shape, f32),
            jax.ShapeDtypeStruct((groups,) + gate_up.shape, low_),
            jax.ShapeDtypeStruct((groups,) + down.shape, low_),
        ),
        in_specs=[IN_VMEM] * 5,
        out_specs=[IN_VMEM] * 5,
        scratch_shapes=[
            pltpu.VMEM((seqs, COLS, span, width), low_),
            pltpu.VMEM((seqs, COLS + 1, span, width), low_),
            part, part,
            pltpu.VMEM((HEADS, piece, cols), low_),
            pltpu.VMEM((groups,) + smalls.shape, f32),
            pltpu.VMEM(smalls.shape, f32),
            dma(3, seqs, COLS), dma(3, seqs, COLS),
            dma(groups), dma(groups), dma(HEADS), dma(HEADS), dma(groups), dma(groups),
            dma(groups), dma(groups), dma(HEADS), dma(HEADS), dma(2, groups), dma(2, groups), dma(5),
        ],
        compiler_params=pltpu.CompilerParams(
            collective_id=6, has_side_effects=True, vmem_limit_bytes=50 * 2**20
        ),
        name="epilogue",
    )(d_first, grads, smalls, gate_up, down)


def low(a):
    return a.astype(jnp.bfloat16)


def halves(a):
    high = low(a)
    return high, low(a - high.astype(jnp.float32))


def dot(a, b, dims):
    return lax.dot_general(a, b, (dims, ((), ())), preferred_element_type=jnp.float32)


def fold(out):
    half = out.shape[1] // 2
    return out[:, :half] + out[:, half:]


def left_nn(parts):
    return jnp.concatenate(parts, axis=1)


def right_nn(parts):
    row = jnp.concatenate(parts, axis=1)
    return jnp.concatenate([row, row], axis=0)


def right_nt(parts):
    high, rest = parts
    return jnp.concatenate(
        [jnp.concatenate([high, high], axis=1), jnp.concatenate([rest, rest], axis=1)], axis=0
    )


def mul(a, b):
    return fold(dot(left_nn(halves(a)), right_nn(halves(b)), ((1,), (0,))))


def mul_nt(a, b):
    return fold(dot(left_nn(halves(a)), right_nt(halves(b)), ((1,), (1,))))


def mul_tn(a, b):
    left = jnp.concatenate(halves(a), axis=0)
    return fold(dot(left, right_nn(halves(b)), ((0,), (0,))))


def low_nn(a, b):
    return dot(low(a), low(b), ((1,), (0,)))


def low_nt(a, b):
    return dot(low(a), low(b), ((1,), (1,)))


def low_tn(a, b):
    return dot(low(a), low(b), ((0,), (0,)))


def iotas(rows, cols):
    return (
        lax.broadcasted_iota(jnp.int32, (rows, cols), 0),
        lax.broadcasted_iota(jnp.int32, (rows, cols), 1),
    )


def order(index):
    return STEPS * lax.rem(index, STRETCH) + lax.div(index, STRETCH)


def sigmoid(a):
    return 1.0 / (1.0 + jnp.exp(-a))


def softplus(a):
    return jnp.maximum(a, 0.0) + jnp.log1p(jnp.exp(-jnp.abs(a)))


def window(ref, halo, seq, base, columns):
    before = ref[seq, pl.ds(pl.multiple_of(jnp.maximum(base - 8, 0), 8), 8), columns]
    ahead = 0.0 if halo is None else halo[seq, :, columns]
    return jnp.concatenate(
        [jnp.where(base == 0, ahead, before), ref[seq, pl.ds(base, STRETCH), columns]], axis=0
    )


def stack(act, at, dim):
    return jnp.concatenate(
        [act[:, at * dim : (at + 1) * dim], act[:, (at + 1) * dim : (at + 2) * dim]], axis=0
    )


def convolve(rows, conv):
    total = None
    for tap in range(CONV):
        start = 8 - (CONV - 1) + tap
        term = conv[tap : tap + 1] * rows[start : start + STRETCH]
        total = term if total is None else total + term
    return total


def rates(small, decay):
    beta = jnp.concatenate([sigmoid(small[:, 0:1]), sigmoid(small[:, 1:2])], axis=0)
    gamma = -jnp.exp(decay[0:1]) * softplus(small + decay[1:2])
    row, col = iotas(STRETCH, STRETCH)
    tri = low(jnp.where(row >= col, 1.0, 0.0))
    high = low(gamma)
    rest = gamma - high.astype(jnp.float32)
    middle = low(rest)
    last = low(rest - middle.astype(jnp.float32))
    running = (
        dot(tri, high, ((1,), (0,))) + dot(tri, middle, ((1,), (0,))) + dot(tri, last, ((1,), (0,)))
    )
    return beta, running


def decays(running):
    column = running[:, 2:3]
    across = jnp.transpose(running)[2:3, :]
    row, col = iotas(STRETCH, STRETCH)
    gap = jnp.broadcast_to(column, (STRETCH, STRETCH)) - across
    upto = jnp.where(row >= col, jnp.exp(jnp.where(row >= col, gap, 0.0)), 0.0)
    before = jnp.where(row > col, upto, 0.0)
    strict = jnp.concatenate(
        [
            jnp.concatenate([before, before], axis=1),
            jnp.concatenate([upto, before], axis=1),
        ],
        axis=0,
    )
    return strict, jnp.concatenate([upto, upto], axis=1)


def level_masks():
    row, col = iotas(WIDE, WIDE)
    row, col = order(row), order(col)
    masks, size = [], 1
    while size < WIDE:
        inside = (lax.div(row, 2 * size) == lax.div(col, 2 * size)) & (
            lax.div(row, size) != lax.div(col, size)
        )
        masks.append(jnp.where(inside, 1.0, 0.0))
        size *= 2
    return [masks[0]] + [low(mask) for mask in masks[1:]]


def inverses(systems, masks):
    row, col = iotas(WIDE, WIDE)
    eye = jnp.where(row == col, 1.0, 0.0)
    solved = [eye - masks[0] * system for system in systems]
    split = [halves(system) for system in systems]
    for mask in masks[1:]:
        parts = [halves(a) for a in solved]
        steps = [
            fold(
                dot(
                    jnp.concatenate([high * mask, rest * mask], axis=1),
                    right_nn(part),
                    ((1,), (0,)),
                )
            )
            for (high, rest), part in zip(split, parts)
        ]
        solved = [
            a - fold(dot(left_nn(part), right_nn(halves(step)), ((1,), (0,))))
            for a, part, step in zip(solved, parts, steps)
        ]
    return solved


def unit_rows(stacked):
    return lax.rsqrt(jnp.sum(stacked * stacked, axis=1, keepdims=True) + EPS)


def twice(column):
    return jnp.concatenate([column, column], axis=0)


def forward_kernel(linked, groups, *refs):
    proj, conv, decay, gain, *refs = refs
    halo = None
    if linked:
        halo, start, *refs = refs
    if groups:
        *parts, refs = refs[0], refs[1], refs[2], refs[3:]
    out, fresh, inv, weights, trans, states, *refs = refs
    if linked:
        final, product, *refs = refs
    if groups:
        mixed, *wholes, refs = refs[0], refs[1], refs[2], refs[3], refs[4:]
    local, offset, mixer, *sems = refs
    seqs, length, _ = proj.shape
    dim = gain.shape[1]
    blocks = length // STRETCH
    span = length // HEADS
    together = span // STRETCH
    turns = blocks // together
    plan = {}
    if groups:
        sends, recvs, c_send, c_recv, x_send, x_recv, own = sems
        spot = Spot(groups)
        spot.barrier()
        first_part = team_gather(
            spot, parts[0], lambda m: wholes[0].at[m, spot.group],
            sends.at[0], recvs.at[0], own.at[0],
        )
        gathers = [
            team_gather(
                spot, parts[k], lambda m, k=k: wholes[k].at[m], sends.at[k], recvs.at[k], own.at[k]
            )
            for k in (1, 2)
        ]
        copies = rep_gather(
            spot, wholes[0].at[:, spot.group], lambda g: wholes[0].at[:, g], c_send, c_recv, None
        )
        next(first_part)
        for gather in gathers:
            next(gather)
        plan = {
            2: [first_part], 3: gathers, 4: [first_part], 5: gathers, 6: [first_part],
            7: gathers,
        }
    masks = level_masks()
    row, col = iotas(dim, dim)
    diagonal = row == col

    def spots(step):
        return [(seq, step * together + k) for k in range(together) for seq in range(seqs)]

    def first(step, _):
        units = spots(step)
        kept = []
        for seq, block in units:
            base = pl.multiple_of(block * STRETCH, STRETCH)
            rows = window(proj, halo, seq, base, pl.ds(0, 5 * dim))
            pre = convolve(rows, conv)
            act = pre * sigmoid(pre)
            raw = stack(act, 1, dim)
            key = raw * unit_rows(raw)
            beta, running = rates(proj[seq, pl.ds(base, STRETCH), pl.ds(6 * dim, dim)], decay)
            kept.append((act[:, :dim], key, stack(act, 3, dim), beta, running))
        systems = []
        for (seq, block), (query, key, value, beta, running) in zip(units, kept):
            at = seq * blocks + block
            strict, upto = decays(running)
            key_halves = halves(key)
            both = fold(
                dot(
                    jnp.concatenate([left_nn(key_halves), left_nn(halves(query))], axis=0),
                    right_nt(key_halves),
                    ((1,), (1,)),
                )
            )
            systems.append(beta * both[:WIDE] * strict)
            local[at] = both[WIDE:] * upto
            offset[at] = query * jnp.exp(running[:, 2:3])
        for (seq, block), (query, key, value, beta, running), solved in zip(
            units, kept, inverses(systems, masks)
        ):
            at = seq * blocks + block
            inv[at] = solved
            grown = twice(jnp.exp(running[:, 2:3]))
            end = running[STRETCH - 1 :, 2:3]
            solved_left = left_nn(halves(solved))
            weight = fold(dot(solved_left, right_nn(halves(beta * key * grown)), ((1,), (0,))))
            value = fold(dot(solved_left, right_nn(halves(beta * value)), ((1,), (0,))))
            weights[at] = weight
            fresh[at] = value
            to_end = jnp.concatenate(halves(key * twice(jnp.exp(end - running[:, 2:3]))), axis=0)
            trans[at] = jnp.where(diagonal, jnp.exp(end), 0.0) - fold(
                dot(to_end, right_nn(halves(weight)), ((0,), (0,)))
            )
            states[at] = fold(dot(to_end, right_nn(halves(value)), ((0,), (0,))))
        return 0

    reached = 0
    for turn in sorted(plan):
        lax.fori_loop(reached, turn, first, 0)
        reached = turn
        for step in plan[turn]:
            next(step)
    lax.fori_loop(reached, turns, first, 0)
    if groups:
        finish(first_part)
        next(copies)

    def chain(block, carried):
        new = []
        for seq in range(seqs):
            at = seq * blocks + block
            state = carried[seq]
            added = states[at]
            states[at] = state
            new.append(mul(trans[at], state) + added)
            if linked:
                product[seq] = mul(trans[at], product[seq])
        return tuple(new)

    if linked:
        for seq in range(seqs):
            product[seq] = jnp.where(diagonal, 1.0, 0.0)
        begin = tuple(start[seq] for seq in range(seqs))
    else:
        begin = (jnp.zeros((dim, dim), jnp.float32),) * seqs
    ended = lax.fori_loop(0, blocks, chain, begin)
    if linked:
        for seq in range(seqs):
            final[seq] = ended[seq]
    if groups:
        next(copies)

    def block_of(ref, mate):
        return ref.at[:, pl.ds(pl.multiple_of(mate * span, span), span)]

    def columns_of(ref, mate):
        return ref.at[:, :, pl.ds(pl.multiple_of(mate * dim, dim), dim)]

    def to_mate(mate, slot):
        return remote(
            block_of(mixer, mate), columns_of(mixed, spot.mate),
            x_send.at[slot], x_recv.at[slot], spot.to_mate(mate),
        )

    def to_self():
        return pltpu.make_async_copy(
            block_of(mixer, spot.mate), columns_of(mixed, spot.mate), own.at[3]
        )

    def last(step, _):
        units = spots(step)
        reads = [
            mul(
                jnp.concatenate([weights[seq * blocks + block], offset[seq * blocks + block]], axis=0),
                states[seq * blocks + block],
            )
            for seq, block in units
        ]
        for (seq, block), read in zip(units, reads):
            at = seq * blocks + block
            base = pl.multiple_of(block * STRETCH, STRETCH)
            new = fresh[at] - read[:WIDE]
            fresh[at] = new
            result = read[WIDE:] + mul(local[at], new)
            out[seq, pl.ds(base, STRETCH)] = result
            gate = proj[seq, pl.ds(base, STRETCH), pl.ds(5 * dim, dim)]
            scale = lax.rsqrt(jnp.mean(result * result, axis=1, keepdims=True) + EPS)
            mixer[seq, pl.ds(base, STRETCH)] = low(
                result * scale * gain[...] * (gate * sigmoid(gate))
            )
        if groups:
            slot = lax.rem(step - spot.mate + HEADS, HEADS)

            @pl.when(slot == 0)
            def _():
                to_self().start()

            @pl.when(slot != 0)
            def _():
                to_mate(step, slot).start()

        return 0

    lax.fori_loop(0, turns, last, 0)
    if groups:
        finish(copies, *gathers)
        for k in range(1, HEADS):
            to_mate(spot.mate_off(k), k).wait_recv()
        for k in range(1, HEADS):
            to_mate(spot.mate_off(k), k).wait_send()
        to_self().wait()


def mixer_forward(proj, conv, decay, gain, parts=(), groups=0, link=()):
    seqs, length, _ = proj.shape
    dim = gain.shape[1]
    units = seqs * (length // STRETCH)
    square = jax.ShapeDtypeStruct((units, WIDE, dim), jnp.float32)
    state = jax.ShapeDtypeStruct((seqs, dim, dim), jnp.float32)
    shapes = (jax.ShapeDtypeStruct((seqs, length, dim), jnp.float32),) + (square,) * 5
    if link:
        shapes += (state, state)
    specs = [IN_VMEM] * len(shapes)
    scratch = [
        pltpu.VMEM((units, STRETCH, WIDE), jnp.float32),
        pltpu.VMEM((units, STRETCH, dim), jnp.float32),
        pltpu.VMEM((seqs, length, dim), jnp.bfloat16),
    ]
    if groups:
        low_ = jnp.bfloat16
        shapes += (
            jax.ShapeDtypeStruct((seqs, length // HEADS, HEADS * dim), low_),
            jax.ShapeDtypeStruct((HEADS, groups) + parts[0].shape, low_),
            jax.ShapeDtypeStruct((HEADS,) + parts[1].shape, low_),
            jax.ShapeDtypeStruct((HEADS,) + parts[2].shape, low_),
        )
        specs += [ANY] * 4
        scratch += [dma(3, TEAM_SEMS), dma(3, TEAM_SEMS), dma(groups), dma(groups)]
        scratch += [dma(HEADS), dma(HEADS), dma(4)]
    return pl.pallas_call(
        functools.partial(forward_kernel, bool(link), groups),
        out_shape=shapes,
        in_specs=[IN_VMEM] * (4 + len(link)) + [ANY] * len(parts),
        out_specs=specs,
        scratch_shapes=scratch,
        compiler_params=pltpu.CompilerParams(
            vmem_limit_bytes=56 * 2**20,
            collective_id=2 if groups else None,
            has_side_effects=bool(groups),
        ),
        cost_estimate=pl.CostEstimate(
            flops=units * 60 * WIDE * WIDE * WIDE,
            bytes_accessed=units * WIDE * WIDE * 30,
            transcendentals=units * WIDE * WIDE * 8,
        ),
        name="mixer_forward",
    )(proj, conv, decay, gain, *link, *parts)


def backward_kernel(linked, groups, *refs):
    proj, conv, decay, gain, out, fresh, inv, weights, trans, states, d_mixer, *refs = refs
    halo = None
    if linked:
        halo, end_state, *refs = refs
    if groups:
        parts, refs = refs[:4], refs[4:]
    d_proj, d_conv, d_small_sums, d_gain, *refs = refs
    if linked:
        d_start, d_first, *refs = refs
    if groups:
        results, refs = refs[:4], refs[4:]
    d_out, chained, *refs = refs
    seqs, length, _ = proj.shape
    dim = gain.shape[1]
    blocks = length // STRETCH
    span = length // HEADS
    together = span // STRETCH
    plan = {}
    if groups:
        d_tokens = d_mixer
        (d_mixer, x_send, x_recv, own,
         g_sums, g_passing, g_total, g_send, g_recv,
         w_sums, w_passing, w_total, w_send, w_recv,
         o_sums, o_others, o_send, o_recv, o_quarter, o_from, o_own, oe_send, oe_recv,
         oc_send, oc_recv, p_sums, p_others, p_send, p_recv) = refs
        gate_up_grad, down_grad, out_grad, down_parts = parts
        gate_up_own, down_own, out_all, down_sum = results
        spot = Spot(groups)
        spot.barrier()

        def block_of(mate):
            return d_mixer.at[:, pl.ds(pl.multiple_of(mate * span, span), span)]

        def columns_of(mate):
            return d_tokens.at[:, :, pl.ds(pl.multiple_of(mate * dim, dim), dim)]

        def from_mate(mate, slot):
            return remote(
                columns_of(mate), block_of(mate), x_send.at[slot], x_recv.at[slot],
                spot.to_mate(mate),
            )

        def from_self():
            return pltpu.make_async_copy(columns_of(spot.mate), block_of(spot.mate), own.at[0])

        exchange = team_exchange(
            spot, columns_of, block_of, x_send, x_recv, own.at[0]
        )
        next(exchange)
        reduces = [
            team_reduce(
                spot, lambda mate, seq: gate_up_grad.at[mate], 1,
                g_sums, g_passing, g_total, g_send, g_recv,
            ),
            team_reduce(
                spot, lambda mate, seq: down_grad.at[mate], 1,
                w_sums, w_passing, w_total, w_send, w_recv,
            ),
        ]
        out_reduce = rep_reduce(
            spot, lambda g: out_grad.at[:, g], o_sums, o_others, o_send, o_recv
        )
        out_exchange = team_exchange(
            spot, lambda mate: o_quarter.at[mate], lambda mate: o_from.at[mate],
            oe_send, oe_recv, own.at[1],
        )
        out_copies = rep_gather(
            spot, o_own, lambda g: out_all.at[g], oc_send, oc_recv, own.at[2]
        )
        down_reduce = rep_reduce(
            spot, lambda g: down_parts.at[g], p_sums, p_others, p_send, p_recv
        )

        def each(*steps):
            for step in steps:
                next(step)

        def deal_out():
            o_quarter[...] = next(out_reduce).astype(o_quarter.dtype)
            next(out_exchange)
            down_sum[...] = next(down_reduce)

        def own_out():
            finish(out_exchange)
            summed = o_from[0].astype(jnp.float32)
            for mate in range(1, HEADS):
                summed = summed + o_from[mate].astype(jnp.float32)
            o_own[...] = summed.astype(o_own.dtype)
            next(out_copies)

        plan = {
            (0, 1): lambda: each(*reduces, out_reduce, down_reduce),
            (0, 4): lambda: each(out_reduce, down_reduce),
            (1, 0): deal_out,
            (1, 1): lambda: each(*reduces),
            (1, 3): lambda: each(*reduces),
            (1, 4): own_out,
            (1, 5): lambda: each(*reduces, out_copies),
            (1, 7): lambda: each(*reduces),
        }

    def staged(phase, body, carried):
        reached, turns = 0, blocks // together
        for at, step in sorted(plan.items()):
            if at[0] == phase:
                carried = lax.fori_loop(reached, at[1], body, carried)
                reached = at[1]
                step()
        return lax.fori_loop(reached, turns, body, carried)
    all_conv = pl.ds(0, 5 * dim)

    def spots(step):
        return [(seq, blocks - 1 - step * together - k) for k in range(together) for seq in range(seqs)]

    def first(step, gain_sum):
        units = spots(step)
        kept = []
        if groups:
            origin = HEADS - 1 - step
            slot = lax.rem(spot.mate - origin + HEADS, HEADS)

            @pl.when(slot == 0)
            def _():
                from_self().wait()

            @pl.when(slot != 0)
            def _():
                from_mate(origin, slot).wait_recv()

        for seq, block in units:
            at = seq * blocks + block
            base = pl.multiple_of(block * STRETCH, STRETCH)
            result = out[seq, pl.ds(base, STRETCH)]
            gate = proj[seq, pl.ds(base, STRETCH), pl.ds(5 * dim, dim)]
            given = d_mixer[seq, pl.ds(base, STRETCH)].astype(jnp.float32)
            scale = lax.rsqrt(jnp.mean(result * result, axis=1, keepdims=True) + EPS)
            normal = result * scale
            open_ = sigmoid(gate)
            silu = gate * open_
            gain_sum = gain_sum + jnp.sum(given * normal * silu, axis=0, keepdims=True)
            d_proj[seq, pl.ds(base, STRETCH), pl.ds(5 * dim, dim)] = low(
                given * normal * gain[...] * (open_ * (1.0 + gate * (1.0 - open_)))
            )
            inner = given * gain[...] * silu
            d_result = scale * (inner - normal * jnp.mean(inner * normal, axis=1, keepdims=True))
            d_out[at] = d_result
            pre = convolve(window(proj, halo, seq, base, pl.ds(0, 3 * dim)), conv[:, : 3 * dim])
            act = pre * sigmoid(pre)
            raw = stack(act, 1, dim)
            _, running = rates(proj[seq, pl.ds(base, STRETCH), pl.ds(6 * dim, dim)], decay)
            kept.append((act[:, :dim], raw * unit_rows(raw), running, d_result))
        scores = [
            mul_nt(query, key) * decays(running)[1] for query, key, running, _ in kept
        ]
        d_freshes = [mul_tn(score, unit[3]) for score, unit in zip(scores, kept)]
        for (seq, block), (query, _, running, d_result), d_fresh in zip(units, kept, d_freshes):
            at = seq * blocks + block
            chained[at] = mul_tn(
                jnp.concatenate([query * jnp.exp(running[:, 2:3]), -weights[at]], axis=0),
                jnp.concatenate([d_result, d_fresh], axis=0),
            )
        return gain_sum

    d_gain[...] = staged(0, first, jnp.zeros((1, dim), jnp.float32))

    def chain(step, carried):
        block = blocks - 1 - step
        new = []
        for seq in range(seqs):
            at = seq * blocks + block
            later = carried[seq]
            added = chained[at]
            chained[at] = later
            new.append(mul_tn(trans[at], later) + added)
        return tuple(new)

    if linked:
        begin = tuple(end_state[seq] for seq in range(seqs))
    else:
        begin = (jnp.zeros((dim, dim), jnp.float32),) * seqs
    ended = lax.fori_loop(0, blocks, chain, begin)
    if linked:
        for seq in range(seqs):
            d_start[seq] = ended[seq]

    def last(step, sums):
        conv_sum, small_sum, *rims = sums
        units = spots(step)
        ats = [seq * blocks + block for seq, block in units]
        bases = [pl.multiple_of(block * STRETCH, STRETCH) for _, block in units]
        acts, keys, rate_sets = [], [], []
        for (seq, _), base in zip(units, bases):
            pre = convolve(window(proj, halo, seq, base, all_conv), conv)
            gate = sigmoid(pre)
            act = pre * gate
            raw = stack(act, 1, dim)
            unit = unit_rows(raw)
            acts.append((act, gate * (1.0 + pre * (1.0 - gate)), unit))
            keys.append(raw * unit)
            rate_sets.append(rates(proj[seq, pl.ds(base, STRETCH), pl.ds(6 * dim, dim)], decay))
        nears = [
            mul_nt(jnp.concatenate([key, act[:, :dim]], axis=0), key)
            for (act, _, _), key in zip(acts, keys)
        ]
        masks = [decays(running) for _, running in rate_sets]
        d_freshes = [
            mul_tn(near[WIDE:] * upto, d_out[at])
            + mul(key * twice(jnp.exp(running[STRETCH - 1 :, 2:3] - running[:, 2:3])), chained[at])
            for near, (_, upto), at, key, (_, running) in zip(nears, masks, ats, keys, rate_sets)
        ]
        backs = [mul_tn(inv[at], d_fresh) for at, d_fresh in zip(ats, d_freshes)]
        reads = [
            stack(act, 3, dim) - mul(key * twice(jnp.exp(running[:, 2:3])), states[at])
            for (act, _, _), key, (_, running), at in zip(acts, keys, rate_sets, ats)
        ]
        to_state = [
            mul_nt(jnp.concatenate([beta * back, d_out[at]], axis=0), states[at])
            for (beta, _), back, at in zip(rate_sets, backs, ats)
        ]
        to_new = [
            mul_nt(jnp.concatenate([back, d_out[at]], axis=0), fresh[at])
            for back, at in zip(backs, ats)
        ]
        d_ends = [mul_nt(fresh[at], chained[at]) for at in ats]
        shaped = [-cross[:WIDE] * strict for cross, (strict, _) in zip(to_new, masks)]
        insides = [beta * a for (beta, _), a in zip(rate_sets, shaped)]
        d_nears = [cross[WIDE:] * upto for cross, (_, upto) in zip(to_new, masks)]
        towards = [
            mul(jnp.concatenate([inside, d_near], axis=0), key)
            for inside, d_near, key in zip(insides, d_nears, keys)
        ]
        away = [
            mul_tn(
                jnp.concatenate([inside, d_near], axis=0),
                jnp.concatenate([key, act[:, :dim]], axis=0),
            )
            for inside, d_near, key, (act, _, _) in zip(insides, d_nears, keys, acts)
        ]
        d_heres = []
        for k, ((seq, _), at, base) in enumerate(zip(units, ats, bases)):
            act, slope, unit = acts[k]
            query, key = act[:, :dim], keys[k]
            beta, running = rate_sets[k]
            small = proj[seq, pl.ds(base, STRETCH), pl.ds(6 * dim, dim)]
            g = running[:, 2:3]
            end = g[STRETCH - 1 :]
            grown, to_go = jnp.exp(g), jnp.exp(end - g)
            back = backs[k]
            d_scaled, d_query_scaled = -to_state[k][:WIDE], to_state[k][WIDE:]
            with_inside = shaped[k] * nears[k][:WIDE]
            d_beta = jnp.sum(back * reads[k] + with_inside, axis=1, keepdims=True)
            gaps = beta * with_inside
            score_gaps = d_nears[k] * nears[k][WIDE:]
            d_query = towards[k][WIDE:] + d_query_scaled * grown
            from_start, from_end = d_scaled * twice(grown), d_ends[k] * twice(to_go)
            d_key = towards[k][:WIDE] + away[k] + from_start + from_end
            ended = jnp.sum(from_end * key, axis=1, keepdims=True)
            row_terms = jnp.sum(gaps + from_start * key, axis=1, keepdims=True) - ended
            col_terms = jnp.sum(gaps, axis=0, keepdims=True) + jnp.sum(
                score_gaps, axis=0, keepdims=True
            )
            col_terms = jnp.transpose(jnp.broadcast_to(col_terms, (8, WIDE)))[:, 0:1]
            row_terms = row_terms - col_terms
            d_g = (
                row_terms[:STRETCH]
                + row_terms[STRETCH:]
                + jnp.sum(score_gaps + d_query_scaled * grown * query, axis=1, keepdims=True)
            )
            d_end = jnp.sum(ended, axis=0, keepdims=True) + jnp.exp(end) * jnp.sum(
                jnp.sum(states[at] * chained[at], axis=0, keepdims=True), axis=1, keepdims=True
            )
            row, col = iotas(STRETCH, STRETCH)
            across = jnp.transpose(jnp.broadcast_to(d_g, (STRETCH, WIDE)))[:STRETCH]
            d_gamma = jnp.sum(jnp.where(row <= col, across, 0.0), axis=1, keepdims=True) + d_end
            lane = iotas(STRETCH, dim)[1]
            shifted = small + decay[1:2]
            d_soft = -jnp.exp(decay[0:1]) * d_gamma
            d_logit = d_soft * sigmoid(shifted)
            d_rate = jnp.where(lane == 0, d_beta[:STRETCH], d_beta[STRETCH:])
            open_beta = sigmoid(small)
            d_small = jnp.where(
                lane < 2,
                d_rate * open_beta * (1.0 - open_beta),
                jnp.where(lane == 2, d_logit, 0.0),
            )
            d_proj[seq, pl.ds(base, STRETCH), pl.ds(6 * dim, dim)] = low(d_small)
            small_sum = small_sum + jnp.concatenate(
                [
                    jnp.sum(d_soft * softplus(shifted), axis=0, keepdims=True),
                    jnp.sum(d_logit, axis=0, keepdims=True),
                ],
                axis=0,
            )
            d_raw = unit * (d_key - key * jnp.sum(d_key * key, axis=1, keepdims=True))
            d_value = beta * back
            d_act = jnp.concatenate(
                [d_query, d_raw[:STRETCH], d_raw[STRETCH:], d_value[:STRETCH], d_value[STRETCH:]],
                axis=1,
            )
            d_heres.append(d_act * slope)
        for (seq, _), base, d_here in zip(units, bases, d_heres):
            rows = window(proj, halo, seq, base, all_conv)
            first_row = 8 - (CONV - 1)
            conv_sum = conv_sum + jnp.concatenate(
                [
                    jnp.sum(
                        d_here * rows[first_row + tap : first_row + tap + STRETCH],
                        axis=0,
                        keepdims=True,
                    )
                    for tap in range(CONV)
                ],
                axis=0,
            )
            ahead = jnp.concatenate([d_here, rims[seq]], axis=0)
            rims[seq] = d_here[:8]
            total = None
            for tap in range(CONV):
                start = CONV - 1 - tap
                term = conv[tap : tap + 1] * ahead[start : start + STRETCH]
                total = term if total is None else total + term
            d_proj[seq, pl.ds(base, STRETCH), all_conv] = low(total)
        return conv_sum, small_sum, *rims

    conv_sum, small_sum, *rims = staged(
        1,
        last,
        (jnp.zeros((CONV, 5 * dim), jnp.float32), jnp.zeros((2, dim), jnp.float32))
        + (jnp.zeros((8, 5 * dim), jnp.float32),) * seqs,
    )
    if linked:
        for seq in range(seqs):
            d_first[seq] = rims[seq]
    d_conv[...] = conv_sum
    d_small_sums[...] = small_sum
    if groups:
        finish(*reduces, out_copies)
        gate_up_own[...] = low(g_total[0])
        down_own[...] = low(w_total[0])
        for k in range(1, HEADS):
            from_mate(spot.mate_off(k), k).wait_send()


def team_scratch(seqs, span, width):
    sums = pltpu.VMEM((seqs, COLS, span, width), jnp.bfloat16)
    passing = pltpu.VMEM((seqs, COLS + 1, span, width), jnp.bfloat16)
    total = pltpu.VMEM((seqs, span, width), jnp.float32)
    return [sums, passing, total, dma(3, seqs, COLS), dma(3, seqs, COLS)]


def mixer_backward(proj, conv, decay, gain, kept, d_mixer, parts=(), groups=0, link=()):
    seqs, length, width = proj.shape
    dim = gain.shape[1]
    units = seqs * (length // STRETCH)
    shapes = (
        jax.ShapeDtypeStruct((seqs, length, width), jnp.bfloat16),
        jax.ShapeDtypeStruct((CONV, 5 * dim), jnp.float32),
        jax.ShapeDtypeStruct((2, dim), jnp.float32),
        jax.ShapeDtypeStruct((1, dim), jnp.float32),
    )
    if link:
        shapes += (
            jax.ShapeDtypeStruct((seqs, dim, dim), jnp.float32),
            jax.ShapeDtypeStruct((seqs, 8, 5 * dim), jnp.float32),
        )
    scratch = [
        pltpu.VMEM((units, STRETCH, dim), jnp.float32),
        pltpu.VMEM((units, dim, dim), jnp.float32),
    ]
    if groups:
        gate_up_grad, down_grad, out_grad, down_parts = parts
        low_, half = jnp.bfloat16, groups // 2
        out_block = pltpu.VMEM((half, HEADS) + out_grad.shape[2:], low_)
        down_block = pltpu.VMEM((half,) + down_parts.shape[1:], low_)
        out_team = pltpu.VMEM((HEADS,) + out_grad.shape[2:], low_)
        shapes += (
            jax.ShapeDtypeStruct(gate_up_grad.shape[1:], low_),
            jax.ShapeDtypeStruct(down_grad.shape[1:], low_),
            jax.ShapeDtypeStruct(out_grad.shape[1:], low_),
            jax.ShapeDtypeStruct(down_parts.shape[1:], jnp.float32),
        )
        scratch += [pltpu.VMEM((seqs, length, dim), low_), dma(HEADS), dma(HEADS), dma(3)]
        scratch += team_scratch(1, *gate_up_grad.shape[1:]) + team_scratch(1, *down_grad.shape[1:])
        scratch += [out_block] * 2 + [dma(groups), dma(groups), out_team, out_team]
        scratch += [pltpu.VMEM(out_grad.shape[2:], low_), dma(HEADS), dma(HEADS)]
        scratch += [dma(groups), dma(groups)]
        scratch += [down_block] * 2 + [dma(groups), dma(groups)]
    return pl.pallas_call(
        functools.partial(backward_kernel, bool(link), groups),
        out_shape=shapes,
        in_specs=[IN_VMEM] * (11 + len(link) + len(parts)),
        out_specs=[IN_VMEM] * len(shapes),
        scratch_shapes=scratch,
        compiler_params=pltpu.CompilerParams(
            vmem_limit_bytes=60 * 2**20,
            collective_id=5 if groups else None,
            has_side_effects=bool(groups),
        ),
        cost_estimate=pl.CostEstimate(
            flops=units * 60 * WIDE * WIDE * WIDE,
            bytes_accessed=units * WIDE * WIDE * 30,
            transcendentals=units * WIDE * WIDE * 8,
        ),
        name="mixer_backward",
    )(proj, conv, decay, gain, *kept, d_mixer, *link, *parts)


def matmul(left, right):
    return jnp.dot(left, right, preferred_element_type=jnp.float32)


def times_transposed(left, right):
    return lax.dot_general(
        left, right, (((1,), (1,)), ((), ())), preferred_element_type=jnp.float32
    )


def transposed_times(left, right):
    return lax.dot_general(
        left, right, (((0,), (0,)), ((), ())), preferred_element_type=jnp.float32
    )


def batched(left, right):
    return jnp.einsum("sij,sjk->sik", left, right, precision=lax.Precision.HIGHEST)


def norm_scale(values):
    return lax.rsqrt(jnp.mean(values * values, axis=-1, keepdims=True) + EPS)


def norm_back(values, gain, given):
    scale = norm_scale(values)
    normal = values * scale
    inner = given * gain
    return scale * (inner - normal * jnp.mean(inner * normal, axis=-1, keepdims=True)), (
        given * normal
    )


def per_device(
    block_in,
    lengths,
    norm_gains,
    w_in,
    w_small,
    conv_weight,
    decay_log,
    decay_bias,
    out_norm_gain,
    w_out,
    gate_up_weight,
    w_down,
    out_cotangent,
):
    micro, seq_count, tokens, width = block_in.shape
    seqs = micro * seq_count
    count = lax.axis_size("ctx")
    groups = lax.axis_size("rep")
    place = lax.axis_index("ctx")
    group = lax.axis_index("rep")
    teams = count // HEADS
    head = lax.rem(place, HEADS)
    team = lax.div(place, HEADS)
    mates = peers = None
    if teams > 1:
        mates = [[t * HEADS + h for h in range(HEADS)] for t in range(teams)]
        peers = [[t * HEADS + h for t in range(teams)] for h in range(HEADS)]
    dim = width // HEADS
    length = HEADS * tokens
    rows = seqs * tokens
    kinds = 2 + 2 * STEPS
    rates_of = STEPS + 1
    f32, bf16 = jnp.float32, jnp.bfloat16

    def over_teams(array):
        if teams == 1:
            return array
        return lax.all_gather(array, "ctx", axis=0, tiled=True, axis_index_groups=peers)

    places = place * tokens + lax.broadcasted_iota(jnp.int32, (seqs, tokens), 1)
    valid = (places < lengths.reshape(seqs, 1)).astype(f32).reshape(rows, 1)
    grad_out = (out_cotangent.reshape(rows, width).astype(f32) * valid).astype(bf16)

    own = width // count
    small_block = jnp.concatenate(
        [norm_gains.reshape(-1), w_small.reshape(-1), conv_weight.reshape(-1)]
    )
    small_block = jnp.pad(small_block, (0, -small_block.size % 128)).reshape(-1, 128)
    piece = own // groups
    pieces = w_in.reshape(groups, piece, kinds, HEADS, dim).transpose(3, 0, 1, 2, 4)
    sequence, w_head, smalls, grad_all = prologue(
        block_in.reshape(seqs, tokens, width),
        pieces.reshape(HEADS, groups, piece, kinds * dim),
        small_block,
        grad_out,
        groups,
    )
    grad_all = grad_all.reshape(groups * rows, width)
    smalls = over_teams(smalls).reshape(count, -1)
    gains = smalls[:, : 2 * own].reshape(count, 2, own).transpose(1, 0, 2).reshape(2, width)
    gains = gains.astype(f32)
    small_all = smalls[:, 2 * own : (2 + HEADS * rates_of) * own].reshape(width, rates_of, HEADS)
    small_head = lax.dynamic_index_in_dim(small_all, head, 2, keepdims=False)
    taps_at = (2 + HEADS * rates_of) * own
    conv_all = smalls[:, taps_at : taps_at + conv_weight.size].reshape(count, CONV, -1)
    conv_all = conv_all.transpose(1, 0, 2).reshape(CONV, kinds - 1, HEADS, dim)
    conv_head = lax.dynamic_index_in_dim(conv_all, head, 2, keepdims=False)
    conv_head = conv_head.reshape(CONV, -1).astype(f32)
    w_head = jnp.concatenate(
        [
            over_teams(w_head).reshape(width, kinds * dim),
            small_head,
            jnp.zeros((width, dim - rates_of), bf16),
        ],
        axis=1,
    )
    hidden_own = w_down.shape[0] // groups
    hidden_units = count * hidden_own
    out_piece = lax.dynamic_index_in_dim(
        w_out.reshape(groups, piece, width), group, 0, keepdims=False
    )
    gate_up_part = lax.dynamic_index_in_dim(
        gate_up_weight.reshape(own, 2, count, groups, hidden_own), group, 3, keepdims=False
    ).reshape(own, -1)
    down_part = lax.dynamic_index_in_dim(
        w_down.reshape(groups, hidden_own, width), group, 0, keepdims=False
    )
    parts = (out_piece, gate_up_part, down_part)

    inputs_all = sequence.astype(f32)
    h_first = (inputs_all * norm_scale(inputs_all) * gains[0]).astype(bf16)
    proj = matmul(h_first.reshape(seqs * length, width), w_head).reshape(seqs, length, -1)
    decay = jnp.stack(
        [
            jnp.broadcast_to(lax.dynamic_index_in_dim(decay_log, head, 0), (dim,)),
            jnp.broadcast_to(lax.dynamic_index_in_dim(decay_bias, head, 0), (dim,)),
        ]
    )
    gain = out_norm_gain.reshape(1, dim)
    halo = None
    if teams > 1:
        onward = [(c, c + HEADS) for c in range(count - HEADS)]
        halo = lax.ppermute(proj[:, length - 8 :], "ctx", onward)
        start = jnp.zeros((seqs, dim, dim), f32)
        *_, offset, transfer = mixer_forward(
            proj, conv_head, decay, gain, link=(halo, start)
        )
        spans = lax.all_gather((transfer, offset), "ctx", axis_index_groups=peers)
        for turn in range(teams - 1):
            start = jnp.where(turn < team, batched(spans[0][turn], start) + spans[1][turn], start)
        link = (halo, start)
    else:
        link = ()
    *kept, mixer, w_out_full, gate_up_part, down_part = mixer_forward(
        proj, conv_head, decay, gain, parts, groups, link
    )
    kept = kept[:6]
    mixer = mixer.reshape(rows, width)
    w_out_full = over_teams(w_out_full).reshape(width, width)
    gate_up_part = over_teams(gate_up_part).reshape(width, 2 * hidden_units)
    down_part = over_teams(down_part).reshape(hidden_units, width)

    inputs = block_in.reshape(rows, width).astype(f32)
    resid = inputs + matmul(mixer, w_out_full)

    h_second = (resid * norm_scale(resid) * gains[1]).astype(bf16)
    h_all = gather_copies(h_second, groups, 3).reshape(groups * rows, width)
    gate_up = matmul(h_all, gate_up_part)
    gate, up = gate_up[:, :hidden_units], gate_up[:, hidden_units:]
    open_gate = jax.nn.sigmoid(gate)
    silu = gate * open_gate
    hidden = (silu * up).astype(bf16)
    down_parts = matmul(hidden, down_part).astype(bf16).reshape(groups, rows, width)
    d_hidden = times_transposed(grad_all, down_part)
    d_gate_up = jnp.concatenate(
        [d_hidden * up * (open_gate * (1.0 + gate * (1.0 - open_gate))), d_hidden * silu], axis=1
    ).astype(bf16)
    d_second = reduce_copies(
        times_transposed(d_gate_up, gate_up_part).astype(bf16).reshape(groups, rows, width), 4
    )
    grad_down = transposed_times(hidden, grad_all)
    grad_gate_up = transposed_times(h_all, d_gate_up)
    d_norm, gain_terms_second = norm_back(resid, gains[1], d_second)
    d_resid = grad_out.astype(f32) + d_norm
    d_branch = d_resid.astype(bf16)
    grad_out_proj = transposed_times(mixer, d_branch)
    d_mixer = times_transposed(d_branch, w_out_full)

    d_mixer = d_mixer.astype(bf16)

    def team_share(grad):
        grad = grad.astype(bf16)
        if teams == 1:
            return grad
        return lax.psum_scatter(
            grad, "ctx", scatter_dimension=0, tiled=True, axis_index_groups=peers
        )

    grad_parts = (
        team_share(grad_gate_up).reshape(HEADS, own, -1),
        team_share(grad_down).reshape(HEADS, hidden_own, width),
        team_share(grad_out_proj).reshape(HEADS, groups, piece, width),
        down_parts,
    )
    link = ()
    if teams > 1:
        def to_heads(array):
            split = array.reshape(rows, HEADS, dim).transpose(1, 0, 2)
            moved = lax.all_to_all(split, "ctx", 0, 0, tiled=True, axis_index_groups=mates)
            return moved.reshape(HEADS, seqs, tokens, dim).transpose(1, 0, 2, 3).reshape(
                seqs, length, dim
            )

        heads_own = to_heads(d_mixer)
        later = jnp.zeros((seqs, dim, dim), f32)
        local = mixer_backward(proj, conv_head, decay, gain, kept, heads_own, link=(halo, later))[4]
        locals_ = lax.all_gather(local, "ctx", axis_index_groups=peers)
        for turn in range(teams - 1, 0, -1):
            later = jnp.where(
                turn > team,
                batched(spans[0][turn].transpose(0, 2, 1), later) + locals_[turn],
                later,
            )
        link = (halo, later)
    d_proj, grad_conv, small_sums, grad_gain, *rims, grad_gate_up, grad_down, grad_out_proj, down = (
        mixer_backward(
            proj,
            conv_head,
            decay,
            gain,
            kept,
            d_mixer.reshape(seqs, tokens, width),
            grad_parts,
            groups,
            link,
        )
    )
    if teams > 1:
        rim = rims[1]
        rim = lax.ppermute(rim, "ctx", [(c, c - HEADS) for c in range(HEADS, count)])
        spill = jnp.zeros((seqs, CONV - 1, kinds * dim - dim), f32)
        for ahead in range(1, CONV):
            spill = spill.at[:, CONV - 1 - ahead :].add(
                conv_head[CONV - 1 - ahead] * rim[:, :ahead]
            )
        last = d_proj[:, length - CONV + 1 :, : (kinds - 1) * dim]
        d_proj = d_proj.at[:, length - CONV + 1 :, : (kinds - 1) * dim].set(
            (last.astype(f32) + spill).astype(bf16)
        )
    result = (valid * (resid + down)).astype(bf16)
    d_proj = d_proj.reshape(seqs * length, -1)
    h_flat = h_first.reshape(seqs * length, width)
    grad_head = transposed_times(h_flat, d_proj[:, : kinds * dim]).astype(bf16)
    grad_small = transposed_times(d_proj[:, kinds * dim : kinds * dim + 8], h_flat)
    d_first = times_transposed(d_proj, w_head)
    normal_all = (inputs_all * norm_scale(inputs_all)).reshape(seqs * length, width)
    grad_gains = jnp.stack(
        [(d_first * normal_all).sum(axis=0), gain_terms_second.sum(axis=0)]
    )
    packed = jnp.concatenate(
        [
            grad_gains.reshape(-1, dim),
            grad_small[:rates_of].reshape(-1, dim),
            grad_conv.reshape(-1, dim),
            grad_gain,
            small_sums[:, STEPS : STEPS + 1] + jnp.zeros((1, dim), f32),
        ]
    )
    packed = jnp.pad(packed, ((0, -packed.shape[0] % 8), (0, 0)))
    grad_head = team_share(grad_head)
    if teams > 1:
        packed = lax.psum(packed, "ctx", axis_index_groups=peers)
    d_first, grad_in, packed, grad_gate_up, grad_down = epilogue(
        d_first.astype(bf16).reshape(seqs, length, width),
        grad_head.reshape(HEADS, groups, piece, kinds * dim),
        packed,
        grad_gate_up,
        grad_down,
    )
    d_inputs, _ = norm_back(inputs, gains[0], d_first.reshape(rows, width))
    in_grad = (d_resid + d_inputs).astype(bf16)
    grad_in = grad_in.reshape(groups, HEADS, piece, kinds, dim).transpose(0, 2, 3, 1, 4)
    grad_in = grad_in.reshape(own, -1)

    grad_gate_up = grad_gate_up.reshape(groups, own, 2, count, hidden_own)
    grad_gate_up = grad_gate_up.transpose(1, 2, 3, 0, 4).reshape(own, -1)
    grad_down = grad_down.reshape(groups * hidden_own, width)
    grad_out_proj = grad_out_proj.reshape(own, width)

    def take(size):
        nonlocal packed
        part, packed = packed[:, :size], packed[:, size:]
        return part

    grad_gains = take(2 * HEADS).sum(axis=0).reshape(2, width)
    grad_small = take(rates_of * HEADS).reshape(HEADS, rates_of, width)
    grad_small = grad_small.transpose(2, 1, 0).reshape(width, rates_of * HEADS)
    grad_conv = take(CONV * (kinds - 1)).reshape(HEADS, CONV, kinds - 1, dim)
    grad_conv = grad_conv.transpose(1, 2, 0, 3).reshape(CONV, (kinds - 1) * width)
    grad_gain = take(1).sum(axis=0).reshape(dim)
    decays_sum = take(2)[:, :, 0].transpose(1, 0)

    def mine(array, axis, size):
        return lax.dynamic_slice_in_dim(array, place * size, size, axis)

    grad_gains = mine(grad_gains, 1, own)
    grad_small = mine(grad_small, 0, own)
    grad_conv = mine(grad_conv, 1, conv_weight.shape[1])
    return (
        result.reshape(block_in.shape),
        in_grad.reshape(block_in.shape),
        grad_gains,
        grad_in.astype(f32),
        grad_small,
        grad_conv,
        decays_sum[0],
        decays_sum[1],
        grad_gain,
        grad_out_proj.astype(f32),
        grad_gate_up.astype(f32),
        grad_down.astype(f32),
    )


def solution(mesh):
    placed = (
        P(None, "rep", "ctx", None),
        P(None, "rep"),
        P(None, "ctx"),
        P("ctx", None),
        P("ctx", None),
        P(None, "ctx"),
        P(),
        P(),
        P(),
        P("ctx", None),
        P("ctx", None),
        P("ctx", None),
        P(None, "rep", "ctx", None),
    )
    return jax.shard_map(
        per_device,
        mesh=mesh,
        in_specs=placed,
        out_specs=(
            P(None, "rep", "ctx", None),
            P(None, "rep", "ctx", None),
            P(None, "ctx"),
            P("ctx", None),
            P("ctx", None),
            P(None, "ctx"),
            P(),
            P(),
            P(),
            P("ctx", None),
            P("ctx", None),
            P("ctx", None),
        ),
        check_vma=False,
    )
```

```python
import functools
import jax
import jax.numpy as jnp
from jax import lax
from jax.experimental import pallas as pl
from jax.experimental.pallas import tpu as pltpu
from jax.sharding import PartitionSpec as P

STEPS = 2
CONV = 4
STRETCH = 64
HEADS = 8
EPS = 1e-06
WIDE = 2 * STRETCH


MESH = pl.DeviceIdType.MESH
ROWS = 2
COLS = HEADS // ROWS


class Spot:
    def __init__(self, groups):
        place = lax.axis_index("ctx")
        self.mate = lax.rem(place, HEADS)
        self.base = place - self.mate
        self.col = lax.div(self.mate, ROWS)
        self.row = lax.rem(self.mate, ROWS)
        self.groups = groups
        self.group = lax.axis_index("rep")
        self.side = lax.rem(self.group, 2)
        self.pair = lax.div(self.group, 2)
        self.twin = self.group + 1 - 2 * self.side

    def to_mate(self, mate):
        return {"ctx": self.base + mate}

    def to_group(self, group):
        return {"rep": group}

    def mate_off(self, k):
        return lax.rem(self.mate + k, HEADS)

    def group_off(self, k):
        return lax.rem(self.group + 2 * k, self.groups)

    def barrier(self, team=True, copies=True):
        sem = pltpu.get_barrier_semaphore()
        others = []
        if team:
            others += [self.to_mate(self.mate_off(k)) for k in range(1, HEADS)]
        if copies:
            others += [self.to_group(self.twin)]
            others += [self.to_group(self.group_off(k)) for k in range(1, self.groups // 2)]
        for other in others:
            pl.semaphore_signal(sem, inc=1, device_id=other, device_id_type=MESH)
        pl.semaphore_wait(sem, len(others))


def remote(src, dst, send, recv, where):
    return pltpu.make_async_remote_copy(
        src_ref=src,
        dst_ref=dst,
        send_sem=send,
        recv_sem=recv,
        device_id=where,
        device_id_type=MESH,
    )


TEAM_SEMS = 3 * COLS + 1


def team_gather(spot, src, out, send, recv, own):
    mate, col = spot.mate, spot.col
    up, down = spot.to_mate(mate + ROWS), spot.to_mate(mate - ROWS)
    across = spot.to_mate(mate + 1 - 2 * spot.row)
    other = mate + 1 - 2 * spot.row
    local = pltpu.make_async_copy(src, out(mate), own)

    def hop(block, origin, slot, where):
        return remote(block, out(origin), send.at[slot], recv.at[slot], where)

    rise, fall, cross_low, cross_high = 0, COLS - 1, 2 * COLS - 2, 3 * COLS - 3
    last = COLS - 1
    local.start()

    @pl.when(col < last)
    def _():
        hop(src, mate, rise, up).start()

    @pl.when(col > 0)
    def _():
        hop(src, mate, fall, down).start()

    hop(src, mate, cross_low, across).start()
    yield
    for k in range(1, COLS):
        below, above = mate - ROWS * k, mate + ROWS * k

        @pl.when(col >= k)
        def _():
            hop(out(below), below, rise + k - 1, up).wait_recv()
            if k < last:

                @pl.when(col < last)
                def _():
                    hop(out(below), below, rise + k, up).start()

            hop(out(below), below, cross_low + k, across).start()

        @pl.when(col + k <= last)
        def _():
            hop(out(above), above, fall + k - 1, down).wait_recv()
            if k < last:

                @pl.when(col > 0)
                def _():
                    hop(out(above), above, fall + k, down).start()

            hop(out(above), above, cross_high + k, across).start()

        yield
    hop(src, other, cross_low, across).wait_recv()
    for k in range(1, COLS):

        @pl.when(col >= k)
        def _():
            hop(src, other - ROWS * k, cross_low + k, across).wait_recv()

        @pl.when(col + k <= last)
        def _():
            hop(src, other + ROWS * k, cross_high + k, across).wait_recv()

    @pl.when(col < last)
    def _():
        hop(src, mate, rise, up).wait_send()

    @pl.when(col > 0)
    def _():
        hop(src, mate, fall, down).wait_send()

    hop(src, mate, cross_low, across).wait_send()
    for k in range(1, COLS):

        @pl.when(col >= k)
        def _():
            if k < last:

                @pl.when(col < last)
                def _():
                    hop(src, mate, rise + k, up).wait_send()

            hop(src, mate, cross_low + k, across).wait_send()

        @pl.when(col + k <= last)
        def _():
            if k < last:

                @pl.when(col > 0)
                def _():
                    hop(src, mate, fall + k, down).wait_send()

            hop(src, mate, cross_high + k, across).wait_send()

    local.wait()
    yield


def rep_gather(spot, src, out, send, recv, own):
    group, twin, half = spot.group, spot.twin, spot.groups // 2
    local = None
    if own is not None:
        local = pltpu.make_async_copy(src, out(group), own)
        local.start()

    def hop(block, origin, slot, where):
        return remote(block, out(origin), send.at[slot], recv.at[slot], spot.to_group(where))

    hop(src, group, 0, twin).start()
    for k in range(1, half):
        hop(src, group, k, spot.group_off(k)).start()
    yield
    for k in range(1, half):
        origin = spot.group_off(half - k)
        hop(out(origin), origin, k, twin).wait_recv()
        hop(out(origin), origin, half + k, twin).start()
    yield
    hop(src, twin, 0, twin).wait_recv()
    for k in range(1, half):
        origin = lax.rem(twin + 2 * (half - k), spot.groups)
        hop(src, origin, half + k, twin).wait_recv()
    hop(src, group, 0, twin).wait_send()
    for k in range(1, half):
        hop(src, group, k, twin).wait_send()
        hop(src, group, half + k, twin).wait_send()
    if local is not None:
        local.wait()
    yield


def team_exchange(spot, src, dst, send, recv, own):
    local = pltpu.make_async_copy(src(spot.mate), dst(spot.mate), own)
    local.start()

    def hop(k):
        to = spot.mate_off(k)
        return remote(src(to), dst(spot.mate), send.at[k], recv.at[k], spot.to_mate(to))

    for k in range(1, HEADS):
        hop(k).start()
    yield
    for k in range(1, HEADS):
        hop(k).wait_recv()
    for k in range(1, HEADS):
        hop(k).wait_send()
    local.wait()
    yield


def dma(*shape):
    return pltpu.SemaphoreType.DMA(shape)


ANY = pl.BlockSpec(memory_space=pl.ANY)
IN_VMEM = pl.BlockSpec(memory_space=pltpu.VMEM)


def finish(*steps):
    for step in steps:
        for _ in step:
            pass


def rep_reduce(spot, part, sums, others, send, recv):
    half, side = spot.groups // 2, spot.side

    def to_twin(k):
        return remote(
            part(2 * k + 1 - side), sums.at[k], send.at[k], recv.at[k], spot.to_group(spot.twin)
        )

    def onward(k):
        slot = half + k
        return remote(
            sums.at[lax.rem(spot.pair + k, half)], others.at[k], send.at[slot], recv.at[slot], spot.to_group(spot.group_off(k))
        )

    for k in range(half):
        to_twin(k).start()
    yield
    for k in range(half):
        to_twin(k).wait_recv()

    def both(pair):
        return part(2 * pair + side)[...].astype(jnp.float32) + sums[pair].astype(jnp.float32)

    for k in range(1, half):
        pair = lax.rem(spot.pair + k, half)
        sums[pair] = both(pair).astype(sums.dtype)
        onward(k).start()
    yield
    total = both(spot.pair)
    for k in range(1, half):
        onward(k).wait_recv()
        total = total + others[k].astype(jnp.float32)
    for k in range(half):
        to_twin(k).wait_send()
    for k in range(1, half):
        onward(k).wait_send()
    yield total


class Lane:
    def __init__(self, part, sums, passing, total, send, recv):
        self.part, self.sums, self.passing = part, sums, passing
        self.total, self.send, self.recv = total, send, recv


def team_reduce(spot, lanes, window):
    mate, col, row = spot.mate, spot.col, spot.row
    up, down = spot.to_mate(mate + ROWS), spot.to_mate(mate - ROWS)
    across = spot.to_mate(mate + 1 - 2 * row)
    last = COLS - 1
    f32 = jnp.float32

    def hop(lane, d, way):
        src = lane.part(ROWS * d + 1 - row) if way == 0 else lane.sums.at[d]
        dst = (lane.sums.at[d], lane.passing.at[d + 1], lane.passing.at[d])[way]
        return remote(
            src, dst, lane.send.at[way, d], lane.recv.at[way, d], (across, up, down)[way]
        )

    def both(lane, d):
        return lane.part(ROWS * d + row)[...].astype(f32) + lane.sums[d].astype(f32)

    def crossed(lane, d):
        hop(lane, d, 0).wait_recv()

        @pl.when(col == d)
        def _():
            lane.total[...] = both(lane, d)

        for end, way in ((0, 1), (last, 2)):
            if d != end:

                @pl.when(col == end)
                def _():
                    lane.sums[d] = both(lane, d).astype(lane.sums.dtype)
                    hop(lane, d, way).start()

    def passed(lane, d, c, way):
        @pl.when(col == c)
        def _():
            hop(lane, d, way).wait_recv()
            got = lane.passing[d + 2 - way].astype(f32)
            if c == d:
                lane.total[...] += got
            else:
                lane.sums[d] = (both(lane, d) + got).astype(lane.sums.dtype)
                hop(lane, d, way).start()

    order_out = [d for pair in zip(range(last, -1, -1), range(COLS)) for d in pair][:COLS]
    rounds = {}
    for i, d in enumerate(order_out):
        for k, lane in enumerate(lanes):
            time = i * len(lanes) + k
            rounds.setdefault(time, []).append(functools.partial(crossed, lane, d))
            for c in range(1, d + 1):
                step = functools.partial(passed, lane, d, c, 1)
                rounds.setdefault(time + c, []).append(step)
            for c in range(d, last):
                step = functools.partial(passed, lane, d, c, 2)
                rounds.setdefault(time + last - c, []).append(step)
    ahead = [(lane, d) for d in order_out for lane in lanes]
    for lane, d in ahead[:window]:
        hop(lane, d, 0).start()
    yield
    for time in sorted(rounds):
        for k, step in enumerate(rounds[time]):
            step()
            if k == 0 and time + window < len(ahead):
                lane, d = ahead[time + window]
                hop(lane, d, 0).start()
        yield
    for d in range(COLS):
        for lane in lanes:
            hop(lane, d, 0).wait_send()

            @pl.when(col < d)
            def _():
                hop(lane, d, 1).wait_send()

            @pl.when(col > d)
            def _():
                hop(lane, d, 2).wait_send()

    yield


def advance(step, count):
    for _ in range(count):
        next(step, None)


def lane_scratch(count, rows, width):
    return [
        pltpu.VMEM((count, COLS, rows, width), jnp.bfloat16),
        pltpu.VMEM((count, COLS + 1, rows, width), jnp.bfloat16),
        dma(count, 3, COLS),
        dma(count, 3, COLS),
    ]


class Job:
    def __init__(self, make, ins=(), outs=(), scratch=(), spaces=None):
        self.make, self.ins, self.outs, self.scratch = make, list(ins), list(outs), list(scratch)
        self.in_space, self.out_space = spaces or (ANY, ANY)


def fused_call(body, ins, outs, scratch, jobs, groups, number, name, vmem, cost=None, copies=True):
    def kernel(*refs):
        refs = list(refs)

        def take(count):
            part = refs[:count]
            del refs[:count]
            return part

        own_in = take(len(ins))
        jobs_in = [take(len(job.ins)) for job in jobs]
        own_out = take(len(outs))
        jobs_out = [take(len(job.outs)) for job in jobs]
        own_scratch = take(len(scratch))
        jobs_scratch = [take(len(job.scratch)) for job in jobs]
        spot = None
        if number:
            spot = Spot(groups)
            spot.barrier(copies=copies)
        steps = [
            job.make(spot, a, b, c)
            for job, a, b, c in zip(jobs, jobs_in, jobs_out, jobs_scratch)
        ]
        body(spot, own_in, own_out, own_scratch, steps)
        finish(*steps)

    results = pl.pallas_call(
        kernel,
        out_shape=[s for s, _ in outs] + [s for job in jobs for s in job.outs],
        in_specs=[spec for _, spec in ins] + [job.in_space for job in jobs for _ in job.ins],
        out_specs=[spec for _, spec in outs] + [job.out_space for job in jobs for _ in job.outs],
        scratch_shapes=list(scratch) + [s for job in jobs for s in job.scratch],
        compiler_params=pltpu.CompilerParams(
            collective_id=number, has_side_effects=bool(number), vmem_limit_bytes=vmem * 2**20
        ),
        cost_estimate=cost,
        name=name,
    )(*[a for a, _ in ins], *[a for job in jobs for a in job.ins])
    results = list(results)
    own, rest = results[: len(outs)], results[len(outs) :]
    given = []
    for job in jobs:
        given.append(rest[: len(job.outs)])
        rest = rest[len(job.outs) :]
    return own, given


def staged(turns, body, carried, marks):
    reached = 0
    for at in sorted(marks):
        if at > reached:
            carried = lax.fori_loop(reached, at, body, carried)
            reached = at
        marks[at]()
    if reached < turns:
        carried = lax.fori_loop(reached, turns, body, carried)
    return carried


def marks_of(plan, phase, steps):
    def mark(moves):
        def go():
            for job, count in moves:
                advance(steps[job], count)

        return go

    return {turn: mark(moves) for (at, turn), moves in plan.items() if at == phase}


def shape(dims, kind):
    return jax.ShapeDtypeStruct(tuple(dims), kind)


def team_gather_job(block, groups=None, twofold=False):
    low_ = block.dtype
    if not twofold:

        def make(spot, ins, outs, scratch):
            return team_gather(spot, ins[0], lambda m: outs[0].at[m], *scratch[:2], scratch[2].at[0])

        return Job(
            make, [block], [shape((HEADS,) + block.shape, low_)],
            [dma(TEAM_SEMS), dma(TEAM_SEMS), dma(1)],
        )

    def make(spot, ins, outs, scratch):
        whole = outs[0]
        yield from team_gather(
            spot, ins[0], lambda m: whole.at[m, spot.group], *scratch[:2], scratch[4].at[0]
        )
        yield from rep_gather(
            spot, whole.at[:, spot.group], lambda g: whole.at[:, g], *scratch[2:4], None
        )

    return Job(
        make, [block], [shape((HEADS, groups) + block.shape, low_)],
        [dma(TEAM_SEMS), dma(TEAM_SEMS), dma(groups), dma(groups), dma(1)],
    )


def sequences_job(block):
    seqs = block.shape[0]

    def make(spot, ins, outs, scratch):
        gathers = [
            team_gather(
                spot, ins[0].at[seq], lambda m, seq=seq: outs[0].at[seq, m],
                scratch[0].at[seq], scratch[1].at[seq], scratch[2].at[seq],
            )
            for seq in range(seqs)
        ]
        for _ in zip(*gathers):
            yield

    return Job(
        make, [block], [shape((seqs, HEADS) + block.shape[1:], block.dtype)],
        [dma(seqs, TEAM_SEMS), dma(seqs, TEAM_SEMS), dma(seqs)],
    )


def rep_gather_job(block, groups, space=ANY):
    def make(spot, ins, outs, scratch):
        return rep_gather(spot, ins[0], lambda g: outs[0].at[g], *scratch[:2], scratch[2].at[0])

    return Job(
        make, [block], [shape((groups,) + block.shape, block.dtype)],
        [dma(groups), dma(groups), dma(1)], (space, space),
    )


def rep_reduce_job(parts, groups):
    block = pltpu.VMEM((groups // 2,) + parts.shape[1:], parts.dtype)

    def make(spot, ins, outs, scratch):
        for total in rep_reduce(spot, lambda g: ins[0].at[g], *scratch):
            if total is not None:
                outs[0][...] = total
            yield

    return Job(
        make, [parts], [shape(parts.shape[1:], jnp.float32)],
        [block, block, dma(groups), dma(groups)], (IN_VMEM, IN_VMEM),
    )


def tokens_job(parts, halves):
    seqs, _, rows, width = parts.shape
    rows_of = rows // halves

    def make(spot, ins, outs, scratch):
        sums, passing, send, recv = scratch
        lanes = []
        for seq in range(seqs):
            for half in range(halves):
                k, own = seq * halves + half, pl.ds(half * rows_of, rows_of)
                lanes.append(
                    Lane(
                        lambda mate, seq=seq, own=own: ins[0].at[seq, mate, own],
                        sums.at[k], passing.at[k], outs[0].at[seq, own], send.at[k], recv.at[k],
                    )
                )
        return team_reduce(spot, lanes, 2 * halves)

    return Job(
        make, [parts], [shape((seqs, rows, width), jnp.float32)],
        lane_scratch(seqs * halves, rows_of, width), (IN_VMEM, IN_VMEM),
    )


def team_reduce_job(parts, pieces, window, kind):
    _, rows, width = parts.shape
    rows_of = rows // pieces

    def make(spot, ins, outs, scratch):
        sums, passing, send, recv, *total = scratch
        total = total[0] if total else outs[0]
        lanes = []
        for k in range(pieces):
            own = pl.ds(k * rows_of, rows_of)
            lanes.append(
                Lane(
                    lambda mate, own=own: ins[0].at[mate, own],
                    sums.at[k], passing.at[k], total.at[own], send.at[k], recv.at[k],
                )
            )
        yield from team_reduce(spot, lanes, window)
        if kind != jnp.float32:
            outs[0][...] = total[...].astype(kind)
        yield

    scratch = lane_scratch(pieces, rows_of, width)
    if kind != jnp.float32:
        scratch.append(pltpu.VMEM((rows, width), jnp.float32))
    return Job(make, [parts], [shape((rows, width), kind)], scratch, (IN_VMEM, IN_VMEM))


def both_reduce_job(parts, groups):
    heads, _, rows, width = parts.shape
    low_ = parts.dtype
    block = pltpu.VMEM((groups // 2, heads, rows, width), low_)
    team = pltpu.VMEM((heads, rows, width), low_)

    def make(spot, ins, outs, scratch):
        sums, others, quarter, arrived, r_send, r_recv, e_send, e_recv, own = scratch
        for total in rep_reduce(
            spot, lambda g: ins[0].at[:, g], sums, others, r_send, r_recv
        ):
            if total is None:
                yield
        quarter[...] = total.astype(low_)
        exchange = team_exchange(
            spot, lambda m: quarter.at[m], lambda m: arrived.at[m], e_send, e_recv, own.at[0]
        )
        next(exchange)
        yield
        finish(exchange)
        outs[0][...] = sum(arrived[m].astype(jnp.float32) for m in range(heads)).astype(low_)
        yield

    return Job(
        make, [parts], [shape((rows, width), low_)],
        [block, block, team, team]
        + [dma(groups), dma(groups), dma(HEADS), dma(HEADS), dma(1)],
        (IN_VMEM, IN_VMEM),
    )


def deal_job(parts, groups):
    heads, _, piece, cols = parts.shape
    low_, f32 = parts.dtype, jnp.float32
    kinds = 2 + 2 * STEPS
    dim = cols // kinds
    block = pltpu.VMEM((groups // 2, heads, piece, cols), low_)

    def make(spot, ins, outs, scratch):
        sums, others, quarter, dealt, r_send, r_recv, e_send, e_recv, g_send, g_recv, own = scratch
        for total in rep_reduce(
            spot, lambda g: ins[0].at[:, g], sums, others, r_send, r_recv
        ):
            if total is None:
                yield
        quarter[...] = total.astype(low_)
        exchange = team_exchange(
            spot, lambda m: quarter.at[m], lambda m: dealt.at[spot.group, m],
            e_send, e_recv, own.at[0],
        )
        next(exchange)
        yield
        finish(exchange)
        yield from rep_gather(
            spot, dealt.at[spot.group], lambda g: dealt.at[g], g_send, g_recv, None
        )
        for g in range(groups):
            for h in range(heads):
                rows = dealt[g, h].astype(f32)
                for k in range(kinds):
                    at = (k * heads + h) * dim
                    outs[0][g, :, at : at + dim] = rows[:, k * dim : (k + 1) * dim]
        yield

    return Job(
        make, [parts], [shape((groups, piece, heads * cols), f32)],
        [block, block, pltpu.VMEM((heads, piece, cols), low_)]
        + [pltpu.VMEM((groups, heads, piece, cols), low_)]
        + [dma(groups), dma(groups), dma(HEADS), dma(HEADS), dma(groups), dma(groups), dma(1)],
        (IN_VMEM, IN_VMEM),
    )


def small_job(smalls, groups):
    def make(spot, ins, outs, scratch):
        copies, total, s_send, s_recv, x_send, x_recv, own = scratch
        yield from rep_gather(spot, ins[0], lambda g: copies.at[g], s_send, s_recv, own.at[0])
        total[...] = sum(copies[g] for g in range(groups))
        yield from team_exchange(
            spot, lambda m: total, lambda m: outs[0].at[m], x_send, x_recv, own.at[1]
        )

    return Job(
        make, [smalls], [shape((HEADS,) + smalls.shape, jnp.float32)],
        [pltpu.VMEM((groups,) + smalls.shape, jnp.float32), pltpu.VMEM(smalls.shape, jnp.float32)]
        + [dma(groups), dma(groups), dma(HEADS), dma(HEADS), dma(2)],
        (IN_VMEM, IN_VMEM),
    )


def head_job(pieces, groups):
    def make(spot, ins, outs, scratch):
        e_send, e_recv, w_send, w_recv, own = scratch
        yield from team_exchange(
            spot, lambda m: ins[0].at[m, spot.group], lambda m: outs[0].at[m, spot.group],
            e_send, e_recv, own.at[0],
        )
        yield from rep_gather(
            spot, outs[0].at[:, spot.group], lambda g: outs[0].at[:, g], w_send, w_recv, None
        )

    return Job(
        make, [pieces], [shape(pieces.shape, pieces.dtype)],
        [dma(HEADS), dma(HEADS), dma(groups), dma(groups), dma(1)],
    )


def spread_job(block):
    def make(spot, ins, outs, scratch):
        return team_exchange(
            spot, lambda m: ins[0], lambda m: outs[0].at[m], *scratch[:2], scratch[2].at[0]
        )

    return Job(
        make, [block], [shape((HEADS,) + block.shape, block.dtype)], [dma(HEADS), dma(HEADS), dma(1)]
    )


def carry(jobs, plan, groups, number, name, vmem=40):
    def body(spot, ins, outs, scratch, steps):
        for job in plan:
            advance(steps[job], 1)

    return fused_call(body, [], [], [], jobs, groups, number, name, vmem)[1]


def low(a):
    return a.astype(jnp.bfloat16)


def halves(a):
    high = low(a)
    return high, low(a - high.astype(jnp.float32))


def dot(a, b, dims):
    return lax.dot_general(a, b, (dims, ((), ())), preferred_element_type=jnp.float32)


def fold(out):
    half = out.shape[1] // 2
    return out[:, :half] + out[:, half:]


def left_nn(parts):
    return jnp.concatenate(parts, axis=1)


def right_nn(parts):
    row = jnp.concatenate(parts, axis=1)
    return jnp.concatenate([row, row], axis=0)


def right_nt(parts):
    high, rest = parts
    return jnp.concatenate(
        [jnp.concatenate([high, high], axis=1), jnp.concatenate([rest, rest], axis=1)], axis=0
    )


def mul(a, b):
    return fold(dot(left_nn(halves(a)), right_nn(halves(b)), ((1,), (0,))))


def mul_nt(a, b):
    return fold(dot(left_nn(halves(a)), right_nt(halves(b)), ((1,), (1,))))


def mul_tn(a, b):
    left = jnp.concatenate(halves(a), axis=0)
    return fold(dot(left, right_nn(halves(b)), ((0,), (0,))))


def iotas(rows, cols):
    return (
        lax.broadcasted_iota(jnp.int32, (rows, cols), 0),
        lax.broadcasted_iota(jnp.int32, (rows, cols), 1),
    )


def order(index):
    return STEPS * lax.rem(index, STRETCH) + lax.div(index, STRETCH)


def sigmoid(a):
    return 1.0 / (1.0 + jnp.exp(-a))


def softplus(a):
    return jnp.maximum(a, 0.0) + jnp.log1p(jnp.exp(-jnp.abs(a)))


def window(ref, halo, length, base, columns):
    before = ref[pl.ds(pl.multiple_of(jnp.maximum(base - 8, 0), 8), 8), columns]
    ahead = 0.0
    if halo is not None:
        ahead = halo[pl.ds(pl.multiple_of(lax.div(base, length) * 8, 8), 8), columns]
    first = lax.rem(base, length) == 0
    return jnp.concatenate(
        [jnp.where(first, ahead, before), ref[pl.ds(base, STRETCH), columns]], axis=0
    )


def stack(act, at, dim):
    return jnp.concatenate(
        [act[:, at * dim : (at + 1) * dim], act[:, (at + 1) * dim : (at + 2) * dim]], axis=0
    )


def convolve(rows, conv):
    total = None
    for tap in range(CONV):
        start = 8 - (CONV - 1) + tap
        term = conv[tap : tap + 1] * rows[start : start + STRETCH]
        total = term if total is None else total + term
    return total


def rates(small, decay):
    beta = jnp.concatenate([sigmoid(small[:, 0:1]), sigmoid(small[:, 1:2])], axis=0)
    gamma = -jnp.exp(decay[0:1]) * softplus(small + decay[1:2])
    row, col = iotas(STRETCH, STRETCH)
    tri = low(jnp.where(row >= col, 1.0, 0.0))
    high = low(gamma)
    rest = gamma - high.astype(jnp.float32)
    middle = low(rest)
    last = low(rest - middle.astype(jnp.float32))
    running = (
        dot(tri, high, ((1,), (0,))) + dot(tri, middle, ((1,), (0,))) + dot(tri, last, ((1,), (0,)))
    )
    return beta, running


def decays(running):
    column = running[:, 2:3]
    across = jnp.transpose(running)[2:3, :]
    row, col = iotas(STRETCH, STRETCH)
    gap = jnp.broadcast_to(column, (STRETCH, STRETCH)) - across
    upto = jnp.where(row >= col, jnp.exp(jnp.where(row >= col, gap, 0.0)), 0.0)
    before = jnp.where(row > col, upto, 0.0)
    strict = jnp.concatenate(
        [
            jnp.concatenate([before, before], axis=1),
            jnp.concatenate([upto, before], axis=1),
        ],
        axis=0,
    )
    return strict, jnp.concatenate([upto, upto], axis=1)


def level_masks():
    row, col = iotas(WIDE, WIDE)
    row, col = order(row), order(col)
    masks, size = [], 1
    while size < WIDE:
        inside = (lax.div(row, 2 * size) == lax.div(col, 2 * size)) & (
            lax.div(row, size) != lax.div(col, size)
        )
        masks.append(jnp.where(inside, 1.0, 0.0))
        size *= 2
    return [masks[0]] + [low(mask) for mask in masks[1:]]


def inverses(systems, masks):
    row, col = iotas(WIDE, WIDE)
    eye = jnp.where(row == col, 1.0, 0.0)
    solved = [eye - masks[0] * system for system in systems]
    split = [halves(system) for system in systems]
    for mask in masks[1:]:
        parts = [halves(a) for a in solved]
        steps = [
            fold(
                dot(
                    jnp.concatenate([high * mask, rest * mask], axis=1),
                    right_nn(part),
                    ((1,), (0,)),
                )
            )
            for (high, rest), part in zip(split, parts)
        ]
        solved = [
            a - fold(dot(left_nn(part), right_nn(halves(step)), ((1,), (0,))))
            for a, part, step in zip(solved, parts, steps)
        ]
    return solved


def unit_rows(stacked):
    return lax.rsqrt(jnp.sum(stacked * stacked, axis=1, keepdims=True) + EPS)


def twice(column):
    return jnp.concatenate([column, column], axis=0)


TOGETHER = 4


def forward_body(linked, seqs, spot, ins, outs, scratch, steps, plan):
    tokens, norm_gain, head, conv, decay, gain, *link = ins
    proj, normed, out, fresh, inv, weights, trans, states, *more = outs
    local, offset, mixer, *sems = scratch
    halo = None
    if linked:
        halo, start = link
        final, product, *more = more
    length = proj.shape[0] // seqs
    dim = gain.shape[1]
    blocks = length // STRETCH
    each = TOGETHER // seqs
    turns = blocks // each
    masks = level_masks()
    row, col = iotas(dim, dim)
    diagonal = row == col

    def project(step, _):
        at = pl.ds(pl.multiple_of(step * TOGETHER * STRETCH, STRETCH), TOGETHER * STRETCH)
        rows = tokens[at].astype(jnp.float32)
        scale = lax.rsqrt(jnp.mean(rows * rows, axis=1, keepdims=True) + EPS)
        rows = low(rows * scale * norm_gain[...])
        normed[at] = rows
        proj[at] = dot(rows, head[...], ((1,), (0,)))
        return 0

    staged(seqs * blocks // TOGETHER, project, 0, marks_of(plan, 0, steps))

    def spots(step):
        return [seq * blocks + step * each + k for k in range(each) for seq in range(seqs)]

    def first(step, _):
        units = spots(step)
        kept = []
        for block in units:
            base = pl.multiple_of(block * STRETCH, STRETCH)
            rows = window(proj, halo, length, base, pl.ds(0, 5 * dim))
            pre = convolve(rows, conv)
            act = pre * sigmoid(pre)
            raw = stack(act, 1, dim)
            key = raw * unit_rows(raw)
            beta, running = rates(proj[pl.ds(base, STRETCH), pl.ds(6 * dim, dim)], decay)
            kept.append((act[:, :dim], key, stack(act, 3, dim), beta, running))
        systems = []
        for block, (query, key, value, beta, running) in zip(units, kept):
            at = block
            strict, upto = decays(running)
            key_halves = halves(key)
            both = fold(
                dot(
                    jnp.concatenate([left_nn(key_halves), left_nn(halves(query))], axis=0),
                    right_nt(key_halves),
                    ((1,), (1,)),
                )
            )
            systems.append(beta * both[:WIDE] * strict)
            local[at] = both[WIDE:] * upto
            offset[at] = query * jnp.exp(running[:, 2:3])
        for block, (query, key, value, beta, running), solved in zip(
            units, kept, inverses(systems, masks)
        ):
            at = block
            inv[at] = solved
            grown = twice(jnp.exp(running[:, 2:3]))
            end = running[STRETCH - 1 :, 2:3]
            solved_left = left_nn(halves(solved))
            weight = fold(dot(solved_left, right_nn(halves(beta * key * grown)), ((1,), (0,))))
            value = fold(dot(solved_left, right_nn(halves(beta * value)), ((1,), (0,))))
            weights[at] = weight
            fresh[at] = value
            to_end = jnp.concatenate(halves(key * twice(jnp.exp(end - running[:, 2:3]))), axis=0)
            trans[at] = jnp.where(diagonal, jnp.exp(end), 0.0) - fold(
                dot(to_end, right_nn(halves(weight)), ((0,), (0,)))
            )
            states[at] = fold(dot(to_end, right_nn(halves(value)), ((0,), (0,))))
        return 0

    staged(turns, first, 0, marks_of(plan, 1, steps))

    def chain(step, carried):
        new = []
        for seq, state in enumerate(carried):
            block = seq * blocks + step
            added = states[block]
            states[block] = state
            if linked:
                product[seq] = mul(trans[block], product[seq])
            new.append(mul(trans[block], state) + added)
        return tuple(new)

    begin = (jnp.zeros((dim, dim), jnp.float32),) * seqs
    if linked:
        for seq in range(seqs):
            product[seq] = jnp.where(diagonal, 1.0, 0.0)
        begin = tuple(start[seq] for seq in range(seqs))
    ended = lax.fori_loop(0, blocks, chain, begin)
    if linked:
        for seq in range(seqs):
            final[seq] = ended[seq]
    if spot is not None:
        (mixed,), (x_send, x_recv, own) = more, sems
        span = length // HEADS

        def block_of(seq, mate):
            return mixer.at[pl.ds(pl.multiple_of(seq * length + mate * span, span), span)]

        def columns_of(seq, mate):
            return mixed.at[seq, :, pl.ds(pl.multiple_of(mate * dim, dim), dim)]

        def to_mate(seq, mate, slot):
            return remote(
                block_of(seq, mate), columns_of(seq, spot.mate), x_send.at[seq, slot],
                x_recv.at[seq, slot], spot.to_mate(mate),
            )

        def to_self(seq):
            return pltpu.make_async_copy(
                block_of(seq, spot.mate), columns_of(seq, spot.mate), own.at[seq]
            )

    def last(step, _):
        units = spots(step)
        reads = [
            mul(
                jnp.concatenate([weights[block], offset[block]], axis=0),
                states[block],
            )
            for block in units
        ]
        for block, read in zip(units, reads):
            at = block
            base = pl.multiple_of(block * STRETCH, STRETCH)
            new = fresh[at] - read[:WIDE]
            fresh[at] = new
            result = read[WIDE:] + mul(local[at], new)
            out[pl.ds(base, STRETCH)] = result
            gate = proj[pl.ds(base, STRETCH), pl.ds(5 * dim, dim)]
            scale = lax.rsqrt(jnp.mean(result * result, axis=1, keepdims=True) + EPS)
            mixer[pl.ds(base, STRETCH)] = low(
                result * scale * gain[...] * (gate * sigmoid(gate))
            )
        if spot is not None:
            mates = each * STRETCH // span
            for k in range(mates):
                to = step * mates + k
                slot = lax.rem(to - spot.mate + HEADS, HEADS)

                @pl.when(slot == 0)
                def _():
                    for seq in range(seqs):
                        to_self(seq).start()

                @pl.when(slot != 0)
                def _():
                    for seq in range(seqs):
                        to_mate(seq, to, slot).start()

        return 0

    staged(turns, last, 0, marks_of(plan, 2, steps))
    if spot is not None:
        for seq in range(seqs):
            for k in range(1, HEADS):
                to_mate(seq, spot.mate_off(k), k).wait_recv()
            for k in range(1, HEADS):
                to_mate(seq, spot.mate_off(k), k).wait_send()
            to_self(seq).wait()


def mixer_cost(units):
    return pl.CostEstimate(
        flops=units * 60 * WIDE * WIDE * WIDE,
        bytes_accessed=units * WIDE * WIDE * 30,
        transcendentals=units * WIDE * WIDE * 8,
    )


def mixer_forward(
    tokens, norm_gain, head, conv, decay, gain, groups=0, number=None, link=(), jobs=(), plan=None
):
    seqs, length, width = tokens.shape
    tokens = tokens.reshape(seqs * length, width)
    dim = gain.shape[1]
    units = seqs * length // STRETCH
    f32, low_ = jnp.float32, jnp.bfloat16
    outs = [
        (shape((seqs * length, head.shape[1]), f32), IN_VMEM),
        (shape((seqs * length, width), low_), IN_VMEM),
        (shape((seqs * length, dim), f32), IN_VMEM),
    ]
    outs += [(shape((units, WIDE, dim), f32), IN_VMEM)] * 5
    if link:
        outs += [(shape((seqs, dim, dim), f32), IN_VMEM)] * 2
    scratch = [
        pltpu.VMEM((units, STRETCH, WIDE), f32),
        pltpu.VMEM((units, STRETCH, dim), f32),
        pltpu.VMEM((seqs * length, dim), low_),
    ]
    if number:
        outs += [(shape((seqs, length // HEADS, HEADS * dim), low_), ANY)]
        scratch += [dma(seqs, HEADS), dma(seqs, HEADS), dma(seqs)]

    def body(spot, ins, outs, scratch, steps):
        forward_body(bool(link), seqs, spot, ins, outs, scratch, steps, plan or {})

    return fused_call(
        body, [(a, IN_VMEM) for a in (tokens, norm_gain, head, conv, decay, gain, *link)], outs, scratch, jobs,
        groups, number, "mixer_forward", 56, mixer_cost(units),
    )


def backward_body(linked, seqs, spot, ins, outs, scratch, steps, plan):
    proj, conv, decay, gain, out, fresh, inv, weights, trans, states, d_mixer, tokens, head, *link = ins
    d_proj, d_conv, d_small_sums, d_gain, d_normed, d_norm_gain, *more = outs
    d_out, chained, *arrived = scratch
    halo = None
    if linked:
        halo, end_state = link
        d_start, d_first = more
    length = proj.shape[0] // seqs
    dim = gain.shape[1]
    blocks = length // STRETCH
    each = TOGETHER // seqs
    turns = blocks // each
    span = length // HEADS
    all_conv = pl.ds(0, 5 * dim)
    if spot is not None:
        d_tokens = d_mixer
        d_mixer, x_send, x_recv, own = arrived

        def block_of(seq, mate):
            return d_mixer.at[pl.ds(pl.multiple_of(seq * length + mate * span, span), span)]

        def columns_of(seq, mate):
            return d_tokens.at[seq, :, pl.ds(pl.multiple_of(mate * dim, dim), dim)]

        def from_mate(seq, mate, slot):
            return remote(
                columns_of(seq, mate), block_of(seq, mate), x_send.at[seq, slot],
                x_recv.at[seq, slot], spot.to_mate(mate),
            )

        def from_self(seq):
            return pltpu.make_async_copy(
                columns_of(seq, spot.mate), block_of(seq, spot.mate), own.at[seq]
            )

        for seq in range(seqs):
            next(
                team_exchange(
                    spot, functools.partial(columns_of, seq), functools.partial(block_of, seq),
                    x_send.at[seq], x_recv.at[seq], own.at[seq],
                )
            )

    def spots(step):
        return [
            seq * blocks + blocks - 1 - step * each - k for k in range(each) for seq in range(seqs)
        ]

    def first(step, gain_sum):
        units = spots(step)
        kept = []
        if spot is not None:
            mates = each * STRETCH // span
            for k in range(mates):
                origin = HEADS - 1 - step * mates - k
                slot = lax.rem(spot.mate - origin + HEADS, HEADS)

                @pl.when(slot == 0)
                def _():
                    for seq in range(seqs):
                        from_self(seq).wait()

                @pl.when(slot != 0)
                def _():
                    for seq in range(seqs):
                        from_mate(seq, origin, slot).wait_recv()

        for block in units:
            at = block
            base = pl.multiple_of(block * STRETCH, STRETCH)
            result = out[pl.ds(base, STRETCH)]
            gate = proj[pl.ds(base, STRETCH), pl.ds(5 * dim, dim)]
            given = d_mixer[pl.ds(base, STRETCH)].astype(jnp.float32)
            scale = lax.rsqrt(jnp.mean(result * result, axis=1, keepdims=True) + EPS)
            normal = result * scale
            open_ = sigmoid(gate)
            silu = gate * open_
            gain_sum = gain_sum + jnp.sum(given * normal * silu, axis=0, keepdims=True)
            d_proj[pl.ds(base, STRETCH), pl.ds(5 * dim, dim)] = low(
                given * normal * gain[...] * (open_ * (1.0 + gate * (1.0 - open_)))
            )
            inner = given * gain[...] * silu
            d_result = scale * (inner - normal * jnp.mean(inner * normal, axis=1, keepdims=True))
            d_out[at] = d_result
            pre = convolve(window(proj, halo, length, base, pl.ds(0, 3 * dim)), conv[:, : 3 * dim])
            act = pre * sigmoid(pre)
            raw = stack(act, 1, dim)
            _, running = rates(proj[pl.ds(base, STRETCH), pl.ds(6 * dim, dim)], decay)
            kept.append((act[:, :dim], raw * unit_rows(raw), running, d_result))
        scores = [
            mul_nt(query, key) * decays(running)[1] for query, key, running, _ in kept
        ]
        d_freshes = [mul_tn(score, unit[3]) for score, unit in zip(scores, kept)]
        for block, (query, _, running, d_result), d_fresh in zip(units, kept, d_freshes):
            at = block
            chained[at] = mul_tn(
                jnp.concatenate([query * jnp.exp(running[:, 2:3]), -weights[at]], axis=0),
                jnp.concatenate([d_result, d_fresh], axis=0),
            )
        return gain_sum

    d_gain[...] = staged(
        turns, first, jnp.zeros((1, dim), jnp.float32), marks_of(plan, 0, steps)
    )

    def chain(step, carried):
        new = []
        for seq, later in enumerate(carried):
            block = seq * blocks + blocks - 1 - step
            added = chained[block]
            chained[block] = later
            new.append(mul_tn(trans[block], later) + added)
        return tuple(new)

    begin = (jnp.zeros((dim, dim), jnp.float32),) * seqs
    if linked:
        begin = tuple(end_state[seq] for seq in range(seqs))
    ended = lax.fori_loop(0, blocks, chain, begin)
    if linked:
        for seq in range(seqs):
            d_start[seq] = ended[seq]

    def last(step, sums):
        conv_sum, small_sum, *rims = sums
        units = spots(step)
        ats = units
        bases = [pl.multiple_of(block * STRETCH, STRETCH) for block in units]
        acts, keys, rate_sets = [], [], []
        for base in bases:
            pre = convolve(window(proj, halo, length, base, all_conv), conv)
            gate = sigmoid(pre)
            act = pre * gate
            raw = stack(act, 1, dim)
            unit = unit_rows(raw)
            acts.append((act, gate * (1.0 + pre * (1.0 - gate)), unit))
            keys.append(raw * unit)
            rate_sets.append(rates(proj[pl.ds(base, STRETCH), pl.ds(6 * dim, dim)], decay))
        nears = [
            mul_nt(jnp.concatenate([key, act[:, :dim]], axis=0), key)
            for (act, _, _), key in zip(acts, keys)
        ]
        masks = [decays(running) for _, running in rate_sets]
        d_freshes = [
            mul_tn(near[WIDE:] * upto, d_out[at])
            + mul(key * twice(jnp.exp(running[STRETCH - 1 :, 2:3] - running[:, 2:3])), chained[at])
            for near, (_, upto), at, key, (_, running) in zip(nears, masks, ats, keys, rate_sets)
        ]
        backs = [mul_tn(inv[at], d_fresh) for at, d_fresh in zip(ats, d_freshes)]
        reads = [
            stack(act, 3, dim) - mul(key * twice(jnp.exp(running[:, 2:3])), states[at])
            for (act, _, _), key, (_, running), at in zip(acts, keys, rate_sets, ats)
        ]
        to_state = [
            mul_nt(jnp.concatenate([beta * back, d_out[at]], axis=0), states[at])
            for (beta, _), back, at in zip(rate_sets, backs, ats)
        ]
        to_new = [
            mul_nt(jnp.concatenate([back, d_out[at]], axis=0), fresh[at])
            for back, at in zip(backs, ats)
        ]
        d_ends = [mul_nt(fresh[at], chained[at]) for at in ats]
        shaped = [-cross[:WIDE] * strict for cross, (strict, _) in zip(to_new, masks)]
        insides = [beta * a for (beta, _), a in zip(rate_sets, shaped)]
        d_nears = [cross[WIDE:] * upto for cross, (_, upto) in zip(to_new, masks)]
        towards = [
            mul(jnp.concatenate([inside, d_near], axis=0), key)
            for inside, d_near, key in zip(insides, d_nears, keys)
        ]
        away = [
            mul_tn(
                jnp.concatenate([inside, d_near], axis=0),
                jnp.concatenate([key, act[:, :dim]], axis=0),
            )
            for inside, d_near, key, (act, _, _) in zip(insides, d_nears, keys, acts)
        ]
        d_heres = []
        for k, (at, base) in enumerate(zip(ats, bases)):
            act, slope, unit = acts[k]
            query, key = act[:, :dim], keys[k]
            beta, running = rate_sets[k]
            small = proj[pl.ds(base, STRETCH), pl.ds(6 * dim, dim)]
            g = running[:, 2:3]
            end = g[STRETCH - 1 :]
            grown, to_go = jnp.exp(g), jnp.exp(end - g)
            back = backs[k]
            d_scaled, d_query_scaled = -to_state[k][:WIDE], to_state[k][WIDE:]
            with_inside = shaped[k] * nears[k][:WIDE]
            d_beta = jnp.sum(back * reads[k] + with_inside, axis=1, keepdims=True)
            gaps = beta * with_inside
            score_gaps = d_nears[k] * nears[k][WIDE:]
            d_query = towards[k][WIDE:] + d_query_scaled * grown
            from_start, from_end = d_scaled * twice(grown), d_ends[k] * twice(to_go)
            d_key = towards[k][:WIDE] + away[k] + from_start + from_end
            ended = jnp.sum(from_end * key, axis=1, keepdims=True)
            row_terms = jnp.sum(gaps + from_start * key, axis=1, keepdims=True) - ended
            col_terms = jnp.sum(gaps, axis=0, keepdims=True) + jnp.sum(
                score_gaps, axis=0, keepdims=True
            )
            col_terms = jnp.transpose(jnp.broadcast_to(col_terms, (8, WIDE)))[:, 0:1]
            row_terms = row_terms - col_terms
            d_g = (
                row_terms[:STRETCH]
                + row_terms[STRETCH:]
                + jnp.sum(score_gaps + d_query_scaled * grown * query, axis=1, keepdims=True)
            )
            d_end = jnp.sum(ended, axis=0, keepdims=True) + jnp.exp(end) * jnp.sum(
                jnp.sum(states[at] * chained[at], axis=0, keepdims=True), axis=1, keepdims=True
            )
            row, col = iotas(STRETCH, STRETCH)
            across = jnp.transpose(jnp.broadcast_to(d_g, (STRETCH, WIDE)))[:STRETCH]
            d_gamma = jnp.sum(jnp.where(row <= col, across, 0.0), axis=1, keepdims=True) + d_end
            lane = iotas(STRETCH, dim)[1]
            shifted = small + decay[1:2]
            d_soft = -jnp.exp(decay[0:1]) * d_gamma
            d_logit = d_soft * sigmoid(shifted)
            d_rate = jnp.where(lane == 0, d_beta[:STRETCH], d_beta[STRETCH:])
            open_beta = sigmoid(small)
            d_small = jnp.where(
                lane < 2,
                d_rate * open_beta * (1.0 - open_beta),
                jnp.where(lane == 2, d_logit, 0.0),
            )
            d_proj[pl.ds(base, STRETCH), pl.ds(6 * dim, dim)] = low(d_small)
            small_sum = small_sum + jnp.concatenate(
                [
                    jnp.sum(d_soft * softplus(shifted), axis=0, keepdims=True),
                    jnp.sum(d_logit, axis=0, keepdims=True),
                ],
                axis=0,
            )
            d_raw = unit * (d_key - key * jnp.sum(d_key * key, axis=1, keepdims=True))
            d_value = beta * back
            d_act = jnp.concatenate(
                [d_query, d_raw[:STRETCH], d_raw[STRETCH:], d_value[:STRETCH], d_value[STRETCH:]],
                axis=1,
            )
            d_heres.append(d_act * slope)
        for k, (base, d_here) in enumerate(zip(bases, d_heres)):
            rows = window(proj, halo, length, base, all_conv)
            first_row = 8 - (CONV - 1)
            conv_sum = conv_sum + jnp.concatenate(
                [
                    jnp.sum(
                        d_here * rows[first_row + tap : first_row + tap + STRETCH],
                        axis=0,
                        keepdims=True,
                    )
                    for tap in range(CONV)
                ],
                axis=0,
            )
            ahead = jnp.concatenate([d_here, rims[k % seqs]], axis=0)
            rims[k % seqs] = d_here[:8]
            total = None
            for tap in range(CONV):
                start = CONV - 1 - tap
                term = conv[tap : tap + 1] * ahead[start : start + STRETCH]
                total = term if total is None else total + term
            d_proj[pl.ds(base, STRETCH), all_conv] = low(total)
        return conv_sum, small_sum, *rims

    conv_sum, small_sum, *rims = staged(
        turns,
        last,
        (
            jnp.zeros((CONV, 5 * dim), jnp.float32),
            jnp.zeros((2, dim), jnp.float32),
        )
        + (jnp.zeros((8, 5 * dim), jnp.float32),) * seqs,
        marks_of(plan, 1, steps),
    )
    def unproject(step, total):
        at = pl.ds(pl.multiple_of(step * TOGETHER * STRETCH, STRETCH), TOGETHER * STRETCH)
        given = dot(d_proj[at], head[...], ((1,), (1,)))
        d_normed[at] = low(given)
        rows = tokens[at].astype(jnp.float32)
        scale = lax.rsqrt(jnp.mean(rows * rows, axis=1, keepdims=True) + EPS)
        return total + jnp.sum(given * (rows * scale), axis=0, keepdims=True)

    d_norm_gain[...] = staged(
        seqs * blocks // TOGETHER,
        unproject,
        jnp.zeros((1, tokens.shape[1]), jnp.float32),
        marks_of(plan, 2, steps),
    )
    if linked:
        for seq in range(seqs):
            d_first[seq] = rims[seq]
    d_conv[...] = conv_sum
    d_small_sums[...] = small_sum
    if spot is not None:
        for seq in range(seqs):
            for k in range(1, HEADS):
                from_mate(seq, spot.mate_off(k), k).wait_send()


def mixer_backward(
    proj, conv, decay, gain, kept, d_mixer, tokens, head, groups=0, number=None, link=(), jobs=(), plan=None
):
    seqs, length, _ = tokens.shape
    width = proj.shape[1]
    tokens = tokens.reshape(seqs * length, -1)
    dim = gain.shape[1]
    units = seqs * length // STRETCH
    f32, low_ = jnp.float32, jnp.bfloat16
    outs = [
        shape((seqs * length, width), low_),
        shape((CONV, 5 * dim), f32),
        shape((2, dim), f32),
        shape((1, dim), f32),
        shape(tokens.shape, low_),
        shape((1, tokens.shape[1]), f32),
    ]
    if link:
        outs += [shape((seqs, dim, dim), f32), shape((seqs, 8, 5 * dim), f32)]
    scratch = [pltpu.VMEM((units, STRETCH, dim), f32), pltpu.VMEM((units, dim, dim), f32)]
    if number:
        scratch += [pltpu.VMEM((seqs * length, dim), low_)]
        scratch += [dma(seqs, HEADS), dma(seqs, HEADS), dma(seqs)]

    def body(spot, ins, outs, scratch, steps):
        backward_body(bool(link), seqs, spot, ins, outs, scratch, steps, plan or {})

    return fused_call(
        body,
        [(a, IN_VMEM) for a in (proj, conv, decay, gain, *kept, d_mixer, tokens, head, *link)],
        [(a, IN_VMEM) for a in outs], scratch, jobs, groups, number, "mixer_backward", 60,
        mixer_cost(units),
    )


PROLOGUE_PLAN = (1, 0, 3, 1, 2, 3, 2, 0, 2, 0, 2, 0, 3, 0, 2)
EPILOGUE_PLAN = (2, 2, 2, 4, 2, 1, 1, 4, 5, 6, 2, 2, 2, 1, 3, 2, 0, 5, 2, 0, 0, 6, 2, 1, 2, 0, 5, 2, 2, 0, 6, 3, 2, 2, 0, 2, 2, 2, 4, 1, 0, 2, 3, 2)
FORWARD_PLAN = {
    (0, 0): ((0, 1), (1, 1)),
    (0, 6): ((1, 1), (0, 1), (2, 1)),
    (1, 3): ((0, 1), (1, 1)),
    (1, 4): ((1, 1),),
    (1, 5): ((0, 1),),
    (1, 6): ((0, 1), (2, 1), (0, 1)),
    (1, 7): ((2, 1),),
    (1, 8): ((2, 1),),
    (2, 0): ((0, 1),),
    (2, 4): ((2, 1),),
}
BACKWARD_PLAN = {
    (0, 0): ((1, 1), (0, 1)),
    (0, 2): ((0, 1),),
    (0, 6): ((0, 1),),
    (0, 8): ((1, 1), (0, 1)),
    (1, 0): ((0, 1),),
    (1, 1): ((0, 1),),
    (1, 2): ((0, 1),),
    (1, 4): ((0, 1),),
    (1, 5): ((1, 1),),
    (1, 6): ((0, 1),),
    (2, 2): ((0, 1),),
    (2, 6): ((0, 1), (0, 1), (1, 1)),
    (2, 7): ((0, 1),),
}
REDUCE_PLAN = (1, 0, 1, 0, 1, 1, 1, 0, 1, 1, 1, 1)
def matmul(left, right):
    return jnp.dot(left, right, preferred_element_type=jnp.float32)


def times_transposed(left, right):
    return lax.dot_general(
        left, right, (((1,), (1,)), ((), ())), preferred_element_type=jnp.float32
    )


def transposed_times(left, right):
    return lax.dot_general(
        left, right, (((0,), (0,)), ((), ())), preferred_element_type=jnp.float32
    )


def exact(left, right):
    return jnp.einsum("sij,sjk->sik", left, right, precision=lax.Precision.HIGHEST)


def norm_scale(values):
    return lax.rsqrt(jnp.mean(values * values, axis=-1, keepdims=True) + EPS)


def norm_back(values, gain, given):
    scale = norm_scale(values)
    normal = values * scale
    inner = given * gain
    return scale * (inner - normal * jnp.mean(inner * normal, axis=-1, keepdims=True)), (
        given * normal
    )


def per_device(
    block_in,
    lengths,
    norm_gains,
    w_in,
    w_small,
    conv_weight,
    decay_log,
    decay_bias,
    out_norm_gain,
    w_out,
    gate_up_weight,
    w_down,
    out_cotangent,
):
    micro, seq_count, tokens, width = block_in.shape
    seqs = micro * seq_count
    count = lax.axis_size("ctx")
    groups = lax.axis_size("rep")
    place = lax.axis_index("ctx")
    group = lax.axis_index("rep")
    teams = count // HEADS
    head = lax.rem(place, HEADS)
    team = lax.div(place, HEADS)
    mates = peers = None
    if teams > 1:
        mates = [[t * HEADS + h for h in range(HEADS)] for t in range(teams)]
        peers = [[t * HEADS + h for t in range(teams)] for h in range(HEADS)]
    dim = width // HEADS
    length = HEADS * tokens
    rows = seqs * tokens
    kinds = 2 + 2 * STEPS
    rates_of = STEPS + 1
    f32, bf16 = jnp.float32, jnp.bfloat16

    def over_teams(array):
        if teams == 1:
            return array
        return lax.all_gather(array, "ctx", axis=0, tiled=True, axis_index_groups=peers)

    places = place * tokens + lax.broadcasted_iota(jnp.int32, (seqs, tokens), 1)
    valid = (places < lengths.reshape(seqs, 1)).astype(f32).reshape(rows, 1)
    grad_out = (out_cotangent.reshape(rows, width).astype(f32) * valid).astype(bf16)

    own = width // count
    piece = own // groups
    small_block = jnp.concatenate(
        [norm_gains.reshape(-1), conv_weight.reshape(-1)]
    )
    small_block = jnp.pad(small_block, (0, -small_block.size % 128)).reshape(-1, 128)
    pieces = w_in.reshape(groups, piece, kinds, HEADS, dim).transpose(3, 0, 1, 2, 4)
    small_pieces = lax.optimization_barrier(
        jnp.stack([w_small[:, h::HEADS] for h in range(HEADS)]).reshape(HEADS, groups, piece, rates_of)
    )
    pieces = jnp.concatenate(
        [
            pieces.reshape(HEADS, groups, piece, kinds * dim),
            jnp.pad(small_pieces, ((0, 0), (0, 0), (0, 0), (0, dim - rates_of))),
        ],
        axis=3,
    )
    (w_head,), (smalls,), (sequences,), (grad_all,) = carry(
        [
            head_job(pieces, groups),
            spread_job(small_block),
            sequences_job(block_in.reshape(seqs, tokens, width)),
            rep_gather_job(grad_out, groups),
        ],
        PROLOGUE_PLAN,
        groups,
        1,
        "prologue",
    )
    sequences = sequences.reshape(seqs, length, width)
    grad_all = grad_all.reshape(groups * rows, width)
    smalls = over_teams(smalls).reshape(count, -1)
    gains = smalls[:, : 2 * own].reshape(count, 2, own).transpose(1, 0, 2).reshape(2, width)
    gains = gains.astype(f32)
    taps_at = 2 * own
    conv_all = smalls[:, taps_at : taps_at + conv_weight.size].reshape(count, CONV, -1)
    conv_all = conv_all.transpose(1, 0, 2).reshape(CONV, kinds - 1, HEADS, dim)
    conv_head = lax.dynamic_index_in_dim(conv_all, head, 2, keepdims=False)
    conv_head = conv_head.reshape(CONV, -1).astype(f32)
    w_head = over_teams(w_head).reshape(width, -1)
    hidden_own = w_down.shape[0] // groups
    hidden_units = count * hidden_own
    out_piece = lax.dynamic_index_in_dim(
        w_out.reshape(groups, piece, width), group, 0, keepdims=False
    )
    gate_up_part = lax.dynamic_index_in_dim(
        gate_up_weight.reshape(own, 2, count, groups, hidden_own), group, 3, keepdims=False
    ).reshape(own, -1)
    down_part = lax.dynamic_index_in_dim(
        w_down.reshape(groups, hidden_own, width), group, 0, keepdims=False
    )

    decay = jnp.stack(
        [
            jnp.broadcast_to(lax.dynamic_index_in_dim(decay_log, head, 0), (dim,)),
            jnp.broadcast_to(lax.dynamic_index_in_dim(decay_bias, head, 0), (dim,)),
        ]
    )
    gain = out_norm_gain.reshape(1, dim)
    head_args = (sequences, gains[:1], w_head, conv_head, decay, gain)
    link = ()
    if teams > 1:
        onward = [(c, c + HEADS) for c in range(count - HEADS)]
        tail = sequences[:, length - 8 :].reshape(seqs * 8, width).astype(f32)
        tail = (tail * norm_scale(tail) * gains[0]).astype(bf16)
        halo = lax.ppermute(matmul(tail, w_head), "ctx", onward)
        start = jnp.zeros((seqs, dim, dim), f32)
        (*_, offset, transfer), _ = mixer_forward(*head_args, link=(halo, start))
        spans = lax.all_gather((transfer, offset), "ctx", axis_index_groups=peers)
        for turn in range(teams - 1):
            start = jnp.where(turn < team, exact(spans[0][turn], start) + spans[1][turn], start)
        link = (halo, start)
    (proj, h_flat, *kept), given = mixer_forward(
        *head_args, groups, 2, link,
        [
            team_gather_job(out_piece, groups, twofold=True),
            team_gather_job(gate_up_part),
            team_gather_job(down_part),
        ],
        FORWARD_PLAN,
    )
    (w_out_full,), (gate_up_part,), (down_part,) = given
    mixer = kept[-1].reshape(rows, width)
    kept = kept[:6]
    w_out_full = over_teams(w_out_full).reshape(width, width)
    gate_up_part = over_teams(gate_up_part).reshape(width, 2 * hidden_units)
    inputs = block_in.reshape(rows, width).astype(f32)
    resid = inputs + matmul(mixer, w_out_full)

    def team_share(grad):
        grad = grad.astype(bf16)
        if teams == 1:
            return grad
        return lax.psum_scatter(
            grad, "ctx", scatter_dimension=0, tiled=True, axis_index_groups=peers
        )

    h_second = (resid * norm_scale(resid) * gains[1]).astype(bf16)
    ((h_all,),) = carry([rep_gather_job(h_second, groups)], (), groups, 3, "gather_copies")
    h_all = h_all.reshape(groups * rows, width)
    down_part = over_teams(down_part).reshape(hidden_units, width)
    gate_up = matmul(h_all, gate_up_part)
    gate, up = gate_up[:, :hidden_units], gate_up[:, hidden_units:]
    open_gate = jax.nn.sigmoid(gate)
    silu = gate * open_gate
    hidden = (silu * up).astype(bf16)
    d_hidden = times_transposed(grad_all, down_part)
    d_gate_up = jnp.concatenate(
        [d_hidden * up * (open_gate * (1.0 + gate * (1.0 - open_gate))), d_hidden * silu], axis=1
    ).astype(bf16)
    d_second = times_transposed(d_gate_up, gate_up_part).astype(bf16)
    grad_down = team_share(transposed_times(hidden, grad_all)).reshape(HEADS, hidden_own, width)
    (d_second,), (grad_down,) = carry(
        [
            rep_reduce_job(d_second.reshape(groups, rows, width), groups),
            team_reduce_job(grad_down, 1, 2, bf16),
        ],
        REDUCE_PLAN,
        groups,
        4,
        "reduce_copies",
    )
    down_parts = matmul(hidden, down_part).astype(bf16).reshape(groups, rows, width)
    grad_gate_up = transposed_times(h_all, d_gate_up)
    d_norm, gain_terms_second = norm_back(resid, gains[1], d_second)
    d_resid = grad_out.astype(f32) + d_norm
    d_branch = d_resid.astype(bf16)
    grad_out_proj = transposed_times(mixer, d_branch)
    d_mixer = times_transposed(d_branch, w_out_full).astype(bf16).reshape(seqs, tokens, width)

    grad_gate_up = team_share(grad_gate_up).reshape(HEADS, own, -1)
    grad_out_proj = team_share(grad_out_proj).reshape(HEADS, groups, piece, width)

    link = ()
    if teams > 1:
        later = jnp.zeros((seqs, dim, dim), f32)
        heads_own = lax.all_to_all(
            d_mixer.reshape(rows, HEADS, dim).transpose(1, 0, 2),
            "ctx", 0, 0, tiled=True, axis_index_groups=mates,
        )
        heads_own = heads_own.reshape(HEADS, seqs, tokens, dim).transpose(1, 0, 2, 3)
        local = mixer_backward(
            proj, conv_head, decay, gain, kept, heads_own.reshape(seqs * length, dim), sequences,
            w_head, link=(halo, later),
        )[0][6]
        locals_ = lax.all_gather(local, "ctx", axis_index_groups=peers)
        for turn in range(teams - 1, 0, -1):
            later = jnp.where(
                turn > team,
                exact(spans[0][turn].transpose(0, 2, 1), later) + locals_[turn],
                later,
            )
        link = (halo, later)
    (d_proj, grad_conv, small_sums, grad_gain, d_first, gain_sum, *rims), given = mixer_backward(
        proj, conv_head, decay, gain, kept, d_mixer, sequences, w_head, groups, 5, link,
        [
            team_reduce_job(grad_gate_up, 2, 3, bf16),
            both_reduce_job(grad_out_proj, groups),
        ],
        BACKWARD_PLAN,
    )
    (grad_gate_up,), (grad_out_proj,) = given
    if teams > 1:
        rim = lax.ppermute(rims[1], "ctx", [(c, c - HEADS) for c in range(HEADS, count)])
        spill = jnp.zeros((seqs, CONV - 1, kinds * dim - dim), f32)
        for ahead in range(1, CONV):
            spill = spill.at[:, CONV - 1 - ahead :].add(
                conv_head[CONV - 1 - ahead] * rim[:, :ahead]
            )
        d_proj = d_proj.reshape(seqs, length, -1)
        end = d_proj[:, length - CONV + 1 :, : (kinds - 1) * dim]
        d_proj = d_proj.at[:, length - CONV + 1 :, : (kinds - 1) * dim].set(
            (end.astype(f32) + spill).astype(bf16)
        )
        d_proj = d_proj.reshape(seqs * length, -1)
        d_first = times_transposed(d_proj, w_head)
        normal = sequences.reshape(seqs * length, width).astype(f32)
        gain_sum = (d_first * (normal * norm_scale(normal))).sum(axis=0)
        d_first = d_first.astype(bf16)

    grad_head = transposed_times(h_flat, d_proj[:, : kinds * dim])
    grad_small = transposed_times(d_proj[:, kinds * dim : kinds * dim + 8], h_flat)
    packed = jnp.concatenate(
        [
            jnp.stack([gain_sum.reshape(width), gain_terms_second.sum(axis=0)]).reshape(-1, dim),
            grad_small[:rates_of].reshape(-1, dim),
            grad_conv.reshape(-1, dim),
            grad_gain,
            small_sums[:, STEPS : STEPS + 1] + jnp.zeros((1, dim), f32),
        ]
    )
    packed = jnp.pad(packed, ((0, -packed.shape[0] % 8), (0, 0)))
    grad_head = team_share(grad_head)
    if teams > 1:
        packed = lax.psum(packed, "ctx", axis_index_groups=peers)
    (grad_in,), (packed,), (d_first,), (grad_gate_up,), (grad_down,), (grad_out_proj,), (down,) = carry(
        [
            deal_job(grad_head.reshape(HEADS, groups, piece, kinds * dim), groups),
            small_job(packed, groups),
            tokens_job(d_first.reshape(seqs, HEADS, tokens, width), 2),
            rep_gather_job(grad_gate_up, groups, IN_VMEM),
            rep_gather_job(grad_down, groups, IN_VMEM),
            rep_gather_job(grad_out_proj, groups, IN_VMEM),
            rep_reduce_job(down_parts, groups),
        ],
        EPILOGUE_PLAN,
        groups,
        6,
        "epilogue",
    )
    d_inputs, _ = norm_back(inputs, gains[0], d_first.reshape(rows, width))
    in_grad = (d_resid + d_inputs).astype(bf16)
    result = (valid * (resid + down)).astype(bf16)
    grad_in = grad_in.reshape(own, -1)
    grad_gate_up = grad_gate_up.reshape(groups, own, 2, count, hidden_own)
    grad_gate_up = grad_gate_up.transpose(1, 2, 3, 0, 4).reshape(own, -1)
    grad_down = grad_down.reshape(groups * hidden_own, width)
    grad_out_proj = grad_out_proj.reshape(own, width)

    def take(size):
        nonlocal packed
        part, packed = packed[:, :size], packed[:, size:]
        return part

    grad_gains = take(2 * HEADS).sum(axis=0).reshape(2, width)
    grad_small = take(rates_of * HEADS).reshape(HEADS, rates_of, width)
    grad_small = grad_small.transpose(2, 1, 0).reshape(width, rates_of * HEADS)
    grad_conv = take(CONV * (kinds - 1)).reshape(HEADS, CONV, kinds - 1, dim)
    grad_conv = grad_conv.transpose(1, 2, 0, 3).reshape(CONV, (kinds - 1) * width)
    grad_gain = take(1).sum(axis=0).reshape(dim)
    decays_sum = take(2)[:, :, 0].transpose(1, 0)

    def mine(array, axis, size):
        return lax.dynamic_slice_in_dim(array, place * size, size, axis)

    grad_gains = mine(grad_gains, 1, own)
    grad_small = mine(grad_small, 0, own)
    grad_conv = mine(grad_conv, 1, conv_weight.shape[1])
    return (
        result.reshape(block_in.shape),
        in_grad.reshape(block_in.shape),
        grad_gains,
        grad_in.astype(f32),
        grad_small,
        grad_conv,
        decays_sum[0],
        decays_sum[1],
        grad_gain,
        grad_out_proj.astype(f32),
        grad_gate_up.astype(f32),
        grad_down.astype(f32),
    )


def solution(mesh):
    placed = (
        P(None, "rep", "ctx", None),
        P(None, "rep"),
        P(None, "ctx"),
        P("ctx", None),
        P("ctx", None),
        P(None, "ctx"),
        P(),
        P(),
        P(),
        P("ctx", None),
        P("ctx", None),
        P("ctx", None),
        P(None, "rep", "ctx", None),
    )
    return jax.shard_map(
        per_device,
        mesh=mesh,
        in_specs=placed,
        out_specs=(
            P(None, "rep", "ctx", None),
            P(None, "rep", "ctx", None),
            P(None, "ctx"),
            P("ctx", None),
            P("ctx", None),
            P(None, "ctx"),
            P(),
            P(),
            P(),
            P("ctx", None),
            P("ctx", None),
            P("ctx", None),
        ),
        check_vma=False,
    )
```

```python
import functools
import jax
import jax.numpy as jnp
from jax import lax
from jax.experimental import pallas as pl
from jax.experimental.pallas import tpu as pltpu
from jax.sharding import PartitionSpec as P

STEPS = 2
CONV = 4
STRETCH = 64
HEADS = 8
EPS = 1e-06
WIDE = 2 * STRETCH


MESH = pl.DeviceIdType.MESH
ROWS = 2
COLS = HEADS // ROWS


class Spot:
    def __init__(self, groups):
        place = lax.axis_index("ctx")
        self.mate = lax.rem(place, HEADS)
        self.base = place - self.mate
        self.col = lax.div(self.mate, ROWS)
        self.row = lax.rem(self.mate, ROWS)
        self.groups = groups
        self.group = lax.axis_index("rep")
        self.side = lax.rem(self.group, 2)
        self.pair = lax.div(self.group, 2)
        self.twin = self.group + 1 - 2 * self.side

    def to_mate(self, mate):
        return {"ctx": self.base + mate}

    def to_group(self, group):
        return {"rep": group}

    def mate_off(self, k):
        return lax.rem(self.mate + k, HEADS)

    def group_off(self, k):
        return lax.rem(self.group + 2 * k, self.groups)

    def barrier(self, team=True, copies=True):
        sem = pltpu.get_barrier_semaphore()
        others = []
        if team:
            others += [self.to_mate(self.mate_off(k)) for k in range(1, HEADS)]
        if copies:
            others += [self.to_group(self.twin)]
            others += [self.to_group(self.group_off(k)) for k in range(1, self.groups // 2)]
        for other in others:
            pl.semaphore_signal(sem, inc=1, device_id=other, device_id_type=MESH)
        pl.semaphore_wait(sem, len(others))


def remote(src, dst, send, recv, where):
    return pltpu.make_async_remote_copy(
        src_ref=src,
        dst_ref=dst,
        send_sem=send,
        recv_sem=recv,
        device_id=where,
        device_id_type=MESH,
    )


TEAM_SEMS = 3 * COLS + 1


def team_gather(spot, src, out, send, recv, own):
    mate, col = spot.mate, spot.col
    up, down = spot.to_mate(mate + ROWS), spot.to_mate(mate - ROWS)
    across = spot.to_mate(mate + 1 - 2 * spot.row)
    other = mate + 1 - 2 * spot.row
    local = pltpu.make_async_copy(src, out(mate), own)

    def hop(block, origin, slot, where):
        return remote(block, out(origin), send.at[slot], recv.at[slot], where)

    rise, fall, cross_low, cross_high = 0, COLS - 1, 2 * COLS - 2, 3 * COLS - 3
    last = COLS - 1
    local.start()

    @pl.when(col < last)
    def _():
        hop(src, mate, rise, up).start()

    @pl.when(col > 0)
    def _():
        hop(src, mate, fall, down).start()

    hop(src, mate, cross_low, across).start()
    yield
    for k in range(1, COLS):
        below, above = mate - ROWS * k, mate + ROWS * k

        @pl.when(col >= k)
        def _():
            hop(out(below), below, rise + k - 1, up).wait_recv()
            if k < last:

                @pl.when(col < last)
                def _():
                    hop(out(below), below, rise + k, up).start()

            hop(out(below), below, cross_low + k, across).start()

        @pl.when(col + k <= last)
        def _():
            hop(out(above), above, fall + k - 1, down).wait_recv()
            if k < last:

                @pl.when(col > 0)
                def _():
                    hop(out(above), above, fall + k, down).start()

            hop(out(above), above, cross_high + k, across).start()

        yield
    hop(src, other, cross_low, across).wait_recv()
    for k in range(1, COLS):

        @pl.when(col >= k)
        def _():
            hop(src, other - ROWS * k, cross_low + k, across).wait_recv()

        @pl.when(col + k <= last)
        def _():
            hop(src, other + ROWS * k, cross_high + k, across).wait_recv()

    @pl.when(col < last)
    def _():
        hop(src, mate, rise, up).wait_send()

    @pl.when(col > 0)
    def _():
        hop(src, mate, fall, down).wait_send()

    hop(src, mate, cross_low, across).wait_send()
    for k in range(1, COLS):

        @pl.when(col >= k)
        def _():
            if k < last:

                @pl.when(col < last)
                def _():
                    hop(src, mate, rise + k, up).wait_send()

            hop(src, mate, cross_low + k, across).wait_send()

        @pl.when(col + k <= last)
        def _():
            if k < last:

                @pl.when(col > 0)
                def _():
                    hop(src, mate, fall + k, down).wait_send()

            hop(src, mate, cross_high + k, across).wait_send()

    local.wait()
    yield


def rep_gather(spot, src, out, send, recv, own):
    group, twin, half = spot.group, spot.twin, spot.groups // 2
    local = None
    if own is not None:
        local = pltpu.make_async_copy(src, out(group), own)
        local.start()

    def hop(block, origin, slot, where):
        return remote(block, out(origin), send.at[slot], recv.at[slot], spot.to_group(where))

    hop(src, group, 0, twin).start()
    for k in range(1, half):
        hop(src, group, k, spot.group_off(k)).start()
    yield
    for k in range(1, half):
        origin = spot.group_off(half - k)
        hop(out(origin), origin, k, twin).wait_recv()
        hop(out(origin), origin, half + k, twin).start()
    yield
    hop(src, twin, 0, twin).wait_recv()
    for k in range(1, half):
        origin = lax.rem(twin + 2 * (half - k), spot.groups)
        hop(src, origin, half + k, twin).wait_recv()
    hop(src, group, 0, twin).wait_send()
    for k in range(1, half):
        hop(src, group, k, twin).wait_send()
        hop(src, group, half + k, twin).wait_send()
    if local is not None:
        local.wait()
    yield


def team_exchange(spot, src, dst, send, recv, own):
    local = pltpu.make_async_copy(src(spot.mate), dst(spot.mate), own)
    local.start()

    def hop(k):
        to = spot.mate_off(k)
        return remote(src(to), dst(spot.mate), send.at[k], recv.at[k], spot.to_mate(to))

    for k in range(1, HEADS):
        hop(k).start()
    yield
    for k in range(1, HEADS):
        hop(k).wait_recv()
    for k in range(1, HEADS):
        hop(k).wait_send()
    local.wait()
    yield


def dma(*shape):
    return pltpu.SemaphoreType.DMA(shape)


ANY = pl.BlockSpec(memory_space=pl.ANY)
IN_VMEM = pl.BlockSpec(memory_space=pltpu.VMEM)


def finish(*steps):
    for step in steps:
        for _ in step:
            pass


def rep_reduce(spot, part, sums, others, send, recv):
    half, side = spot.groups // 2, spot.side

    def to_twin(k):
        return remote(
            part(2 * k + 1 - side), sums.at[k], send.at[k], recv.at[k], spot.to_group(spot.twin)
        )

    def onward(k):
        slot = half + k
        return remote(
            sums.at[lax.rem(spot.pair + k, half)], others.at[k], send.at[slot], recv.at[slot], spot.to_group(spot.group_off(k))
        )

    for k in range(half):
        to_twin(k).start()
    yield
    for k in range(half):
        to_twin(k).wait_recv()

    def both(pair):
        return part(2 * pair + side)[...].astype(jnp.float32) + sums[pair].astype(jnp.float32)

    for k in range(1, half):
        pair = lax.rem(spot.pair + k, half)
        sums[pair] = both(pair).astype(sums.dtype)
        onward(k).start()
    yield
    total = both(spot.pair)
    for k in range(1, half):
        onward(k).wait_recv()
        total = total + others[k].astype(jnp.float32)
    for k in range(half):
        to_twin(k).wait_send()
    for k in range(1, half):
        onward(k).wait_send()
    yield total


class Lane:
    def __init__(self, part, sums, passing, total, send, recv):
        self.part, self.sums, self.passing = part, sums, passing
        self.total, self.send, self.recv = total, send, recv


def team_reduce(spot, lanes, window):
    mate, col, row = spot.mate, spot.col, spot.row
    up, down = spot.to_mate(mate + ROWS), spot.to_mate(mate - ROWS)
    across = spot.to_mate(mate + 1 - 2 * row)
    last = COLS - 1
    f32 = jnp.float32

    def hop(lane, d, way):
        src = lane.part(ROWS * d + 1 - row) if way == 0 else lane.sums.at[d]
        dst = (lane.sums.at[d], lane.passing.at[d + 1], lane.passing.at[d])[way]
        return remote(
            src, dst, lane.send.at[way, d], lane.recv.at[way, d], (across, up, down)[way]
        )

    def both(lane, d):
        return lane.part(ROWS * d + row)[...].astype(f32) + lane.sums[d].astype(f32)

    def crossed(lane, d):
        hop(lane, d, 0).wait_recv()

        @pl.when(col == d)
        def _():
            lane.total[...] = both(lane, d)

        for end, way in ((0, 1), (last, 2)):
            if d != end:

                @pl.when(col == end)
                def _():
                    lane.sums[d] = both(lane, d).astype(lane.sums.dtype)
                    hop(lane, d, way).start()

    def passed(lane, d, c, way):
        @pl.when(col == c)
        def _():
            hop(lane, d, way).wait_recv()
            got = lane.passing[d + 2 - way].astype(f32)
            if c == d:
                lane.total[...] += got
            else:
                lane.sums[d] = (both(lane, d) + got).astype(lane.sums.dtype)
                hop(lane, d, way).start()

    order_out = [d for pair in zip(range(last, -1, -1), range(COLS)) for d in pair][:COLS]
    rounds = {}
    for i, d in enumerate(order_out):
        for k, lane in enumerate(lanes):
            time = i * len(lanes) + k
            rounds.setdefault(time, []).append(functools.partial(crossed, lane, d))
            for c in range(1, d + 1):
                step = functools.partial(passed, lane, d, c, 1)
                rounds.setdefault(time + c, []).append(step)
            for c in range(d, last):
                step = functools.partial(passed, lane, d, c, 2)
                rounds.setdefault(time + last - c, []).append(step)
    ahead = [(lane, d) for d in order_out for lane in lanes]
    for lane, d in ahead[:window]:
        hop(lane, d, 0).start()
    yield
    for time in sorted(rounds):
        for k, step in enumerate(rounds[time]):
            step()
            if k == 0 and time + window < len(ahead):
                lane, d = ahead[time + window]
                hop(lane, d, 0).start()
        yield
    for d in range(COLS):
        for lane in lanes:
            hop(lane, d, 0).wait_send()

            @pl.when(col < d)
            def _():
                hop(lane, d, 1).wait_send()

            @pl.when(col > d)
            def _():
                hop(lane, d, 2).wait_send()

    yield


def advance(step, count):
    for _ in range(count):
        next(step, None)


def lane_scratch(count, rows, width):
    return [
        pltpu.VMEM((count, COLS, rows, width), jnp.bfloat16),
        pltpu.VMEM((count, COLS + 1, rows, width), jnp.bfloat16),
        dma(count, 3, COLS),
        dma(count, 3, COLS),
    ]


class Job:
    def __init__(self, make, ins=(), outs=(), scratch=(), spaces=None):
        self.make, self.ins, self.outs, self.scratch = make, list(ins), list(outs), list(scratch)
        self.in_space, self.out_space = spaces or (ANY, ANY)


def fused_call(body, ins, outs, scratch, jobs, groups, number, name, vmem, cost=None, copies=True):
    def kernel(*refs):
        refs = list(refs)

        def take(count):
            part = refs[:count]
            del refs[:count]
            return part

        own_in = take(len(ins))
        jobs_in = [take(len(job.ins)) for job in jobs]
        own_out = take(len(outs))
        jobs_out = [take(len(job.outs)) for job in jobs]
        own_scratch = take(len(scratch))
        jobs_scratch = [take(len(job.scratch)) for job in jobs]
        spot = None
        if number:
            spot = Spot(groups)
            spot.barrier(copies=copies)
        steps = [
            job.make(spot, a, b, c)
            for job, a, b, c in zip(jobs, jobs_in, jobs_out, jobs_scratch)
        ]
        body(spot, own_in, own_out, own_scratch, steps)
        finish(*steps)

    results = pl.pallas_call(
        kernel,
        out_shape=[s for s, _ in outs] + [s for job in jobs for s in job.outs],
        in_specs=[spec for _, spec in ins] + [job.in_space for job in jobs for _ in job.ins],
        out_specs=[spec for _, spec in outs] + [job.out_space for job in jobs for _ in job.outs],
        scratch_shapes=list(scratch) + [s for job in jobs for s in job.scratch],
        compiler_params=pltpu.CompilerParams(
            collective_id=number, has_side_effects=bool(number), vmem_limit_bytes=vmem * 2**20
        ),
        cost_estimate=cost,
        name=name,
    )(*[a for a, _ in ins], *[a for job in jobs for a in job.ins])
    results = list(results)
    own, rest = results[: len(outs)], results[len(outs) :]
    given = []
    for job in jobs:
        given.append(rest[: len(job.outs)])
        rest = rest[len(job.outs) :]
    return own, given


def staged(turns, body, carried, marks):
    reached = 0
    for at in sorted(marks):
        if at > reached:
            carried = lax.fori_loop(reached, at, body, carried)
            reached = at
        marks[at]()
    if reached < turns:
        carried = lax.fori_loop(reached, turns, body, carried)
    return carried


def marks_of(plan, phase, steps):
    def mark(moves):
        def go():
            for job, count in moves:
                advance(steps[job], count)

        return go

    return {turn: mark(moves) for (at, turn), moves in plan.items() if at == phase}


def shape(dims, kind):
    return jax.ShapeDtypeStruct(tuple(dims), kind)


def team_gather_job(block, groups=None, twofold=False):
    low_ = block.dtype
    if not twofold:

        def make(spot, ins, outs, scratch):
            return team_gather(spot, ins[0], lambda m: outs[0].at[m], *scratch[:2], scratch[2].at[0])

        return Job(
            make, [block], [shape((HEADS,) + block.shape, low_)],
            [dma(TEAM_SEMS), dma(TEAM_SEMS), dma(1)],
        )

    def make(spot, ins, outs, scratch):
        whole = outs[0]
        yield from team_gather(
            spot, ins[0], lambda m: whole.at[m, spot.group], *scratch[:2], scratch[4].at[0]
        )
        yield from rep_gather(
            spot, whole.at[:, spot.group], lambda g: whole.at[:, g], *scratch[2:4], None
        )

    return Job(
        make, [block], [shape((HEADS, groups) + block.shape, low_)],
        [dma(TEAM_SEMS), dma(TEAM_SEMS), dma(groups), dma(groups), dma(1)],
    )


def sequences_job(block):
    seqs = block.shape[0]

    def make(spot, ins, outs, scratch):
        gathers = [
            team_gather(
                spot, ins[0].at[seq], lambda m, seq=seq: outs[0].at[seq, m],
                scratch[0].at[seq], scratch[1].at[seq], scratch[2].at[seq],
            )
            for seq in range(seqs)
        ]
        for _ in zip(*gathers):
            yield

    return Job(
        make, [block], [shape((seqs, HEADS) + block.shape[1:], block.dtype)],
        [dma(seqs, TEAM_SEMS), dma(seqs, TEAM_SEMS), dma(seqs)],
    )


def rep_gather_job(block, groups, space=ANY):
    def make(spot, ins, outs, scratch):
        return rep_gather(spot, ins[0], lambda g: outs[0].at[g], *scratch[:2], scratch[2].at[0])

    return Job(
        make, [block], [shape((groups,) + block.shape, block.dtype)],
        [dma(groups), dma(groups), dma(1)], (space, space),
    )


def rep_reduce_job(parts, groups):
    block = pltpu.VMEM((groups // 2,) + parts.shape[1:], parts.dtype)

    def make(spot, ins, outs, scratch):
        for total in rep_reduce(spot, lambda g: ins[0].at[g], *scratch):
            if total is not None:
                outs[0][...] = total
            yield

    return Job(
        make, [parts], [shape(parts.shape[1:], jnp.float32)],
        [block, block, dma(groups), dma(groups)], (IN_VMEM, IN_VMEM),
    )


def tokens_job(parts, halves):
    seqs, _, rows, width = parts.shape
    rows_of = rows // halves

    def make(spot, ins, outs, scratch):
        sums, passing, send, recv = scratch
        lanes = []
        for seq in range(seqs):
            for half in range(halves):
                k, own = seq * halves + half, pl.ds(half * rows_of, rows_of)
                lanes.append(
                    Lane(
                        lambda mate, seq=seq, own=own: ins[0].at[seq, mate, own],
                        sums.at[k], passing.at[k], outs[0].at[seq, own], send.at[k], recv.at[k],
                    )
                )
        return team_reduce(spot, lanes, 2 * halves)

    return Job(
        make, [parts], [shape((seqs, rows, width), jnp.float32)],
        lane_scratch(seqs * halves, rows_of, width), (IN_VMEM, IN_VMEM),
    )


def team_reduce_job(parts, pieces, window, kind):
    _, rows, width = parts.shape
    rows_of = rows // pieces

    def make(spot, ins, outs, scratch):
        sums, passing, send, recv, *total = scratch
        total = total[0] if total else outs[0]
        lanes = []
        for k in range(pieces):
            own = pl.ds(k * rows_of, rows_of)
            lanes.append(
                Lane(
                    lambda mate, own=own: ins[0].at[mate, own],
                    sums.at[k], passing.at[k], total.at[own], send.at[k], recv.at[k],
                )
            )
        yield from team_reduce(spot, lanes, window)
        if kind != jnp.float32:
            outs[0][...] = total[...].astype(kind)
        yield

    scratch = lane_scratch(pieces, rows_of, width)
    if kind != jnp.float32:
        scratch.append(pltpu.VMEM((rows, width), jnp.float32))
    return Job(make, [parts], [shape((rows, width), kind)], scratch, (IN_VMEM, IN_VMEM))


def both_reduce_job(parts, groups):
    heads, _, rows, width = parts.shape
    low_ = parts.dtype
    block = pltpu.VMEM((groups // 2, heads, rows, width), low_)
    team = pltpu.VMEM((heads, rows, width), low_)

    def make(spot, ins, outs, scratch):
        sums, others, quarter, arrived, r_send, r_recv, e_send, e_recv, own = scratch
        for total in rep_reduce(
            spot, lambda g: ins[0].at[:, g], sums, others, r_send, r_recv
        ):
            if total is None:
                yield
        quarter[...] = total.astype(low_)
        exchange = team_exchange(
            spot, lambda m: quarter.at[m], lambda m: arrived.at[m], e_send, e_recv, own.at[0]
        )
        next(exchange)
        yield
        finish(exchange)
        outs[0][...] = sum(arrived[m].astype(jnp.float32) for m in range(heads)).astype(low_)
        yield

    return Job(
        make, [parts], [shape((rows, width), low_)],
        [block, block, team, team]
        + [dma(groups), dma(groups), dma(HEADS), dma(HEADS), dma(1)],
        (IN_VMEM, IN_VMEM),
    )


def tile_product(left, right, tile, width):
    return low(dot(left[:, tile * 128 : (tile + 1) * 128], right[:, :width], ((0,), (0,))))


def product_job(left, right):
    rows, width = left.shape[1], right.shape[1]

    def make(spot, ins, outs, scratch):
        for tile in range(rows // 128):
            outs[0][tile * 128 : (tile + 1) * 128] = tile_product(ins[0], ins[1], tile, width)
            yield

    return Job(
        make, [left, right], [shape((rows, width), jnp.bfloat16)], (), (IN_VMEM, IN_VMEM)
    )


def deal_job(ins, dims, groups):
    heads, _, piece, cols = dims
    low_ = jnp.bfloat16
    kinds = 2 + 2 * STEPS
    dim = cols // kinds
    block = pltpu.VMEM((groups // 2, heads, piece, cols), low_)
    made = len(ins) == 2

    def make(spot, ins, outs, scratch):
        sums, others, quarter, dealt, r_send, r_recv, e_send, e_recv, g_send, g_recv, own = scratch[:11]
        parts = ins[0]
        if made:
            parts = scratch[11]
            for mate in range(heads):
                tile = tile_product(ins[0], ins[1], mate, cols)
                for g in range(groups):
                    parts[mate, g] = tile[g * piece : (g + 1) * piece]
                if mate % 2:
                    yield
        for total in rep_reduce(
            spot, lambda g: parts.at[:, g], sums, others, r_send, r_recv
        ):
            if total is None:
                yield
        quarter[...] = total.astype(low_)
        exchange = team_exchange(
            spot, lambda m: quarter.at[m], lambda m: dealt.at[spot.group, m],
            e_send, e_recv, own.at[0],
        )
        next(exchange)
        yield
        finish(exchange)
        yield from rep_gather(
            spot, dealt.at[spot.group], lambda g: dealt.at[g], g_send, g_recv, None
        )
        for g in range(groups):
            for h in range(heads):
                rows = dealt[g, h]
                for k in range(kinds):
                    at = (k * heads + h) * dim
                    outs[0][g, :, at : at + dim] = rows[:, k * dim : (k + 1) * dim]
        yield

    return Job(
        make, ins, [shape((groups, piece, heads * cols), low_)],
        [block, block, pltpu.VMEM((heads, piece, cols), low_)]
        + [pltpu.VMEM((groups, heads, piece, cols), low_)]
        + [dma(groups), dma(groups), dma(HEADS), dma(HEADS), dma(groups), dma(groups), dma(1)]
        + ([pltpu.VMEM(dims, low_)] if made else []),
        (IN_VMEM, IN_VMEM),
    )


def small_job(smalls, groups):
    def make(spot, ins, outs, scratch):
        copies, total, s_send, s_recv, x_send, x_recv, own = scratch
        yield from rep_gather(spot, ins[0], lambda g: copies.at[g], s_send, s_recv, own.at[0])
        total[...] = sum(copies[g] for g in range(groups))
        yield from team_exchange(
            spot, lambda m: total, lambda m: outs[0].at[m], x_send, x_recv, own.at[1]
        )

    return Job(
        make, [smalls], [shape((HEADS,) + smalls.shape, jnp.float32)],
        [pltpu.VMEM((groups,) + smalls.shape, jnp.float32), pltpu.VMEM(smalls.shape, jnp.float32)]
        + [dma(groups), dma(groups), dma(HEADS), dma(HEADS), dma(2)],
        (IN_VMEM, IN_VMEM),
    )


def head_job(w_in, w_small, groups):
    own, width = w_in.shape
    kinds, piece = 2 + 2 * STEPS, own // groups
    dim = width // (kinds * HEADS)
    rates_of = w_small.shape[1] // HEADS
    dims = (HEADS, groups, piece, (kinds + 1) * dim)

    def make(spot, ins, outs, scratch):
        pieces, e_send, e_recv, w_send, w_recv, local = scratch
        row, col = iotas(w_small.shape[1], dim)
        for h in range(HEADS):
            chosen = low(jnp.where((row == col * HEADS + h) & (col < rates_of), 1.0, 0.0))
            blocks = [ins[0][:, (k * HEADS + h) * dim : (k * HEADS + h + 1) * dim] for k in range(kinds)]
            blocks.append(low(dot(ins[1][...], chosen, ((1,), (0,)))))
            for k, block in enumerate(blocks):
                block = block.astype(jnp.float32)
                for g in range(groups):
                    pieces[h, g, :, k * dim : (k + 1) * dim] = low(
                        block[g * piece : (g + 1) * piece]
                    )
        yield from team_exchange(
            spot, lambda m: pieces.at[m, spot.group], lambda m: outs[0].at[m, spot.group],
            e_send, e_recv, local.at[0],
        )
        yield from rep_gather(
            spot, outs[0].at[:, spot.group], lambda g: outs[0].at[:, g], w_send, w_recv, None
        )

    return Job(
        make, [w_in, w_small], [shape(dims, w_in.dtype)],
        [pltpu.VMEM(dims, w_in.dtype)]
        + [dma(HEADS), dma(HEADS), dma(groups), dma(groups), dma(1)],
        (IN_VMEM, ANY),
    )


def spread_job(block):
    def make(spot, ins, outs, scratch):
        return team_exchange(
            spot, lambda m: ins[0], lambda m: outs[0].at[m], *scratch[:2], scratch[2].at[0]
        )

    return Job(
        make, [block], [shape((HEADS,) + block.shape, block.dtype)], [dma(HEADS), dma(HEADS), dma(1)]
    )


def carry(jobs, plan, groups, number, name, vmem=40):
    def body(spot, ins, outs, scratch, steps):
        for job in plan:
            advance(steps[job], 1)

    return fused_call(body, [], [], [], jobs, groups, number, name, vmem)[1]


def low(a):
    return a.astype(jnp.bfloat16)


def halves(a):
    high = low(a)
    return high, low(a - high.astype(jnp.float32))


def dot(a, b, dims):
    return lax.dot_general(a, b, (dims, ((), ())), preferred_element_type=jnp.float32)


def fold(out):
    half = out.shape[1] // 2
    return out[:, :half] + out[:, half:]


def left_nn(parts):
    return jnp.concatenate(parts, axis=1)


def right_nn(parts):
    row = jnp.concatenate(parts, axis=1)
    return jnp.concatenate([row, row], axis=0)


def right_nt(parts):
    high, rest = parts
    return jnp.concatenate(
        [jnp.concatenate([high, high], axis=1), jnp.concatenate([rest, rest], axis=1)], axis=0
    )


def mul(a, b):
    return fold(dot(left_nn(halves(a)), right_nn(halves(b)), ((1,), (0,))))


def mul_nt(a, b):
    return fold(dot(left_nn(halves(a)), right_nt(halves(b)), ((1,), (1,))))


def mul_tn(a, b):
    left = jnp.concatenate(halves(a), axis=0)
    return fold(dot(left, right_nn(halves(b)), ((0,), (0,))))


def iotas(rows, cols):
    return (
        lax.broadcasted_iota(jnp.int32, (rows, cols), 0),
        lax.broadcasted_iota(jnp.int32, (rows, cols), 1),
    )


def order(index):
    return STEPS * lax.rem(index, STRETCH) + lax.div(index, STRETCH)


def sigmoid(a):
    return 1.0 / (1.0 + jnp.exp(-a))


def softplus(a):
    return jnp.maximum(a, 0.0) + jnp.log1p(jnp.exp(-jnp.abs(a)))


def window(ref, halo, length, base, columns):
    before = ref[pl.ds(pl.multiple_of(jnp.maximum(base - 8, 0), 8), 8), columns]
    ahead = 0.0
    if halo is not None:
        ahead = halo[pl.ds(pl.multiple_of(lax.div(base, length) * 8, 8), 8), columns]
    first = lax.rem(base, length) == 0
    return jnp.concatenate(
        [jnp.where(first, ahead, before), ref[pl.ds(base, STRETCH), columns]], axis=0
    )


def stack(act, at, dim):
    return jnp.concatenate(
        [act[:, at * dim : (at + 1) * dim], act[:, (at + 1) * dim : (at + 2) * dim]], axis=0
    )


def convolve(rows, conv):
    total = None
    for tap in range(CONV):
        start = 8 - (CONV - 1) + tap
        term = conv[tap : tap + 1] * rows[start : start + STRETCH]
        total = term if total is None else total + term
    return total


def rates(small, decay):
    beta = jnp.concatenate([sigmoid(small[:, 0:1]), sigmoid(small[:, 1:2])], axis=0)
    gamma = -jnp.exp(decay[0:1]) * softplus(small + decay[1:2])
    row, col = iotas(STRETCH, STRETCH)
    tri = low(jnp.where(row >= col, 1.0, 0.0))
    high = low(gamma)
    rest = gamma - high.astype(jnp.float32)
    middle = low(rest)
    last = low(rest - middle.astype(jnp.float32))
    running = (
        dot(tri, high, ((1,), (0,))) + dot(tri, middle, ((1,), (0,))) + dot(tri, last, ((1,), (0,)))
    )
    return beta, running


def decays(running):
    column = running[:, 2:3]
    across = jnp.transpose(running)[2:3, :]
    row, col = iotas(STRETCH, STRETCH)
    gap = jnp.broadcast_to(column, (STRETCH, STRETCH)) - across
    upto = jnp.where(row >= col, jnp.exp(jnp.where(row >= col, gap, 0.0)), 0.0)
    before = jnp.where(row > col, upto, 0.0)
    strict = jnp.concatenate(
        [
            jnp.concatenate([before, before], axis=1),
            jnp.concatenate([upto, before], axis=1),
        ],
        axis=0,
    )
    return strict, jnp.concatenate([upto, upto], axis=1)


def level_masks():
    row, col = iotas(WIDE, WIDE)
    row, col = order(row), order(col)
    masks, size = [], 1
    while size < WIDE:
        inside = (lax.div(row, 2 * size) == lax.div(col, 2 * size)) & (
            lax.div(row, size) != lax.div(col, size)
        )
        masks.append(jnp.where(inside, 1.0, 0.0))
        size *= 2
    return [masks[0]] + [low(mask) for mask in masks[1:]]


def inverses(systems, masks):
    row, col = iotas(WIDE, WIDE)
    eye = jnp.where(row == col, 1.0, 0.0)
    solved = [eye - masks[0] * system for system in systems]
    split = [halves(system) for system in systems]
    for mask in masks[1:]:
        parts = [halves(a) for a in solved]
        steps = [
            fold(
                dot(
                    jnp.concatenate([high * mask, rest * mask], axis=1),
                    right_nn(part),
                    ((1,), (0,)),
                )
            )
            for (high, rest), part in zip(split, parts)
        ]
        solved = [
            a - fold(dot(left_nn(part), right_nn(halves(step)), ((1,), (0,))))
            for a, part, step in zip(solved, parts, steps)
        ]
    return solved


def unit_rows(stacked):
    return lax.rsqrt(jnp.sum(stacked * stacked, axis=1, keepdims=True) + EPS)


def twice(column):
    return jnp.concatenate([column, column], axis=0)


TOGETHER = 4


def forward_body(linked, seqs, spot, ins, outs, scratch, steps, plan):
    tokens, norm_gain, head, conv, decay, gain, *link = ins
    proj, normed, out, fresh, inv, weights, trans, states, *more = outs
    local, offset, mixer, *sems = scratch
    halo = None
    if linked:
        halo, start = link
        final, product, *more = more
    length = proj.shape[0] // seqs
    dim = gain.shape[1]
    blocks = length // STRETCH
    each = TOGETHER // seqs
    turns = blocks // each
    masks = level_masks()
    row, col = iotas(dim, dim)
    diagonal = row == col

    def project(step, _):
        at = pl.ds(pl.multiple_of(step * TOGETHER * STRETCH, STRETCH), TOGETHER * STRETCH)
        rows = tokens[at].astype(jnp.float32)
        scale = lax.rsqrt(jnp.mean(rows * rows, axis=1, keepdims=True) + EPS)
        rows = low(rows * scale * norm_gain[...])
        normed[at] = rows
        proj[at] = dot(rows, head[...], ((1,), (0,)))
        return 0

    staged(seqs * blocks // TOGETHER, project, 0, marks_of(plan, 0, steps))

    def spots(step):
        return [seq * blocks + step * each + k for k in range(each) for seq in range(seqs)]

    def first(step, _):
        units = spots(step)
        kept = []
        for block in units:
            base = pl.multiple_of(block * STRETCH, STRETCH)
            rows = window(proj, halo, length, base, pl.ds(0, 5 * dim))
            pre = convolve(rows, conv)
            act = pre * sigmoid(pre)
            raw = stack(act, 1, dim)
            key = raw * unit_rows(raw)
            beta, running = rates(proj[pl.ds(base, STRETCH), pl.ds(6 * dim, dim)], decay)
            kept.append((act[:, :dim], key, stack(act, 3, dim), beta, running))
        systems = []
        for block, (query, key, value, beta, running) in zip(units, kept):
            at = block
            strict, upto = decays(running)
            key_halves = halves(key)
            both = fold(
                dot(
                    jnp.concatenate([left_nn(key_halves), left_nn(halves(query))], axis=0),
                    right_nt(key_halves),
                    ((1,), (1,)),
                )
            )
            systems.append(beta * both[:WIDE] * strict)
            local[at] = both[WIDE:] * upto
            offset[at] = query * jnp.exp(running[:, 2:3])
        for block, (query, key, value, beta, running), solved in zip(
            units, kept, inverses(systems, masks)
        ):
            at = block
            inv[at] = solved
            grown = twice(jnp.exp(running[:, 2:3]))
            end = running[STRETCH - 1 :, 2:3]
            solved_left = left_nn(halves(solved))
            weight = fold(dot(solved_left, right_nn(halves(beta * key * grown)), ((1,), (0,))))
            value = fold(dot(solved_left, right_nn(halves(beta * value)), ((1,), (0,))))
            weights[at] = weight
            fresh[at] = value
            to_end = jnp.concatenate(halves(key * twice(jnp.exp(end - running[:, 2:3]))), axis=0)
            trans[at] = jnp.where(diagonal, jnp.exp(end), 0.0) - fold(
                dot(to_end, right_nn(halves(weight)), ((0,), (0,)))
            )
            states[at] = fold(dot(to_end, right_nn(halves(value)), ((0,), (0,))))
        return 0

    staged(turns, first, 0, marks_of(plan, 1, steps))

    def chain(step, carried):
        new = []
        for seq, state in enumerate(carried):
            block = seq * blocks + step
            added = states[block]
            states[block] = state
            if linked:
                product[seq] = mul(trans[block], product[seq])
            new.append(mul(trans[block], state) + added)
        return tuple(new)

    begin = (jnp.zeros((dim, dim), jnp.float32),) * seqs
    if linked:
        for seq in range(seqs):
            product[seq] = jnp.where(diagonal, 1.0, 0.0)
        begin = tuple(start[seq] for seq in range(seqs))
    ended = lax.fori_loop(0, blocks, chain, begin)
    if linked:
        for seq in range(seqs):
            final[seq] = ended[seq]
    if spot is not None:
        (mixed,), (x_send, x_recv, own) = more, sems
        span = length // HEADS

        def block_of(seq, mate):
            return mixer.at[pl.ds(pl.multiple_of(seq * length + mate * span, span), span)]

        def columns_of(seq, mate):
            return mixed.at[seq, :, pl.ds(pl.multiple_of(mate * dim, dim), dim)]

        def to_mate(seq, mate, slot):
            return remote(
                block_of(seq, mate), columns_of(seq, spot.mate), x_send.at[seq, slot],
                x_recv.at[seq, slot], spot.to_mate(mate),
            )

        def to_self(seq):
            return pltpu.make_async_copy(
                block_of(seq, spot.mate), columns_of(seq, spot.mate), own.at[seq]
            )

    def last(step, _):
        units = spots(step)
        reads = [
            mul(
                jnp.concatenate([weights[block], offset[block]], axis=0),
                states[block],
            )
            for block in units
        ]
        for block, read in zip(units, reads):
            at = block
            base = pl.multiple_of(block * STRETCH, STRETCH)
            new = fresh[at] - read[:WIDE]
            fresh[at] = new
            result = read[WIDE:] + mul(local[at], new)
            out[pl.ds(base, STRETCH)] = result
            gate = proj[pl.ds(base, STRETCH), pl.ds(5 * dim, dim)]
            scale = lax.rsqrt(jnp.mean(result * result, axis=1, keepdims=True) + EPS)
            mixer[pl.ds(base, STRETCH)] = low(
                result * scale * gain[...] * (gate * sigmoid(gate))
            )
        if spot is not None:
            mates = each * STRETCH // span
            for k in range(mates):
                to = step * mates + k
                slot = lax.rem(to - spot.mate + HEADS, HEADS)

                @pl.when(slot == 0)
                def _():
                    for seq in range(seqs):
                        to_self(seq).start()

                @pl.when(slot != 0)
                def _():
                    for seq in range(seqs):
                        to_mate(seq, to, slot).start()

        return 0

    staged(turns, last, 0, marks_of(plan, 2, steps))
    if spot is not None:
        for seq in range(seqs):
            for k in range(1, HEADS):
                to_mate(seq, spot.mate_off(k), k).wait_recv()
            for k in range(1, HEADS):
                to_mate(seq, spot.mate_off(k), k).wait_send()
            to_self(seq).wait()


def mixer_cost(units):
    return pl.CostEstimate(
        flops=units * 60 * WIDE * WIDE * WIDE,
        bytes_accessed=units * WIDE * WIDE * 30,
        transcendentals=units * WIDE * WIDE * 8,
    )


def mixer_forward(
    tokens, norm_gain, head, conv, decay, gain, groups=0, number=None, link=(), jobs=(), plan=None
):
    seqs, length, width = tokens.shape
    tokens = tokens.reshape(seqs * length, width)
    dim = gain.shape[1]
    units = seqs * length // STRETCH
    f32, low_ = jnp.float32, jnp.bfloat16
    outs = [
        (shape((seqs * length, head.shape[1]), f32), IN_VMEM),
        (shape((seqs * length, width), low_), IN_VMEM),
        (shape((seqs * length, dim), f32), IN_VMEM),
    ]
    outs += [(shape((units, WIDE, dim), f32), IN_VMEM)] * 5
    if link:
        outs += [(shape((seqs, dim, dim), f32), IN_VMEM)] * 2
    scratch = [
        pltpu.VMEM((units, STRETCH, WIDE), f32),
        pltpu.VMEM((units, STRETCH, dim), f32),
        pltpu.VMEM((seqs * length, dim), low_),
    ]
    if number:
        outs += [(shape((seqs, length // HEADS, HEADS * dim), low_), ANY)]
        scratch += [dma(seqs, HEADS), dma(seqs, HEADS), dma(seqs)]

    def body(spot, ins, outs, scratch, steps):
        forward_body(bool(link), seqs, spot, ins, outs, scratch, steps, plan or {})

    return fused_call(
        body, [(a, IN_VMEM) for a in (tokens, norm_gain, head, conv, decay, gain, *link)], outs, scratch, jobs,
        groups, number, "mixer_forward", 56, mixer_cost(units),
    )


def backward_body(linked, seqs, spot, ins, outs, scratch, steps, plan):
    proj, conv, decay, gain, out, fresh, inv, weights, trans, states, d_mixer, tokens, head, *link = ins
    d_proj, d_conv, d_small_sums, d_gain, d_normed, d_norm_gain, *more = outs
    d_out, chained, *arrived = scratch
    halo = None
    if linked:
        halo, end_state = link
        d_start, d_first = more
    length = proj.shape[0] // seqs
    dim = gain.shape[1]
    blocks = length // STRETCH
    each = TOGETHER // seqs
    turns = blocks // each
    span = length // HEADS
    all_conv = pl.ds(0, 5 * dim)
    if spot is not None:
        d_tokens = d_mixer
        d_mixer, x_send, x_recv, own = arrived

        def block_of(seq, mate):
            return d_mixer.at[pl.ds(pl.multiple_of(seq * length + mate * span, span), span)]

        def columns_of(seq, mate):
            return d_tokens.at[seq, :, pl.ds(pl.multiple_of(mate * dim, dim), dim)]

        def from_mate(seq, mate, slot):
            return remote(
                columns_of(seq, mate), block_of(seq, mate), x_send.at[seq, slot],
                x_recv.at[seq, slot], spot.to_mate(mate),
            )

        def from_self(seq):
            return pltpu.make_async_copy(
                columns_of(seq, spot.mate), block_of(seq, spot.mate), own.at[seq]
            )

        for seq in range(seqs):
            next(
                team_exchange(
                    spot, functools.partial(columns_of, seq), functools.partial(block_of, seq),
                    x_send.at[seq], x_recv.at[seq], own.at[seq],
                )
            )

    def spots(step):
        return [
            seq * blocks + blocks - 1 - step * each - k for k in range(each) for seq in range(seqs)
        ]

    def first(step, gain_sum):
        units = spots(step)
        kept = []
        if spot is not None:
            mates = each * STRETCH // span
            for k in range(mates):
                origin = HEADS - 1 - step * mates - k
                slot = lax.rem(spot.mate - origin + HEADS, HEADS)

                @pl.when(slot == 0)
                def _():
                    for seq in range(seqs):
                        from_self(seq).wait()

                @pl.when(slot != 0)
                def _():
                    for seq in range(seqs):
                        from_mate(seq, origin, slot).wait_recv()

        for block in units:
            at = block
            base = pl.multiple_of(block * STRETCH, STRETCH)
            result = out[pl.ds(base, STRETCH)]
            gate = proj[pl.ds(base, STRETCH), pl.ds(5 * dim, dim)]
            given = d_mixer[pl.ds(base, STRETCH)].astype(jnp.float32)
            scale = lax.rsqrt(jnp.mean(result * result, axis=1, keepdims=True) + EPS)
            normal = result * scale
            open_ = sigmoid(gate)
            silu = gate * open_
            gain_sum = gain_sum + jnp.sum(given * normal * silu, axis=0, keepdims=True)
            d_proj[pl.ds(base, STRETCH), pl.ds(5 * dim, dim)] = low(
                given * normal * gain[...] * (open_ * (1.0 + gate * (1.0 - open_)))
            )
            inner = given * gain[...] * silu
            d_result = scale * (inner - normal * jnp.mean(inner * normal, axis=1, keepdims=True))
            d_out[at] = d_result
            pre = convolve(window(proj, halo, length, base, pl.ds(0, 3 * dim)), conv[:, : 3 * dim])
            act = pre * sigmoid(pre)
            raw = stack(act, 1, dim)
            _, running = rates(proj[pl.ds(base, STRETCH), pl.ds(6 * dim, dim)], decay)
            kept.append((act[:, :dim], raw * unit_rows(raw), running, d_result))
        scores = [
            mul_nt(query, key) * decays(running)[1] for query, key, running, _ in kept
        ]
        d_freshes = [mul_tn(score, unit[3]) for score, unit in zip(scores, kept)]
        for block, (query, _, running, d_result), d_fresh in zip(units, kept, d_freshes):
            at = block
            chained[at] = mul_tn(
                jnp.concatenate([query * jnp.exp(running[:, 2:3]), -weights[at]], axis=0),
                jnp.concatenate([d_result, d_fresh], axis=0),
            )
        return gain_sum

    d_gain[...] = staged(
        turns, first, jnp.zeros((1, dim), jnp.float32), marks_of(plan, 0, steps)
    )

    def chain(step, carried):
        new = []
        for seq, later in enumerate(carried):
            block = seq * blocks + blocks - 1 - step
            added = chained[block]
            chained[block] = later
            new.append(mul_tn(trans[block], later) + added)
        return tuple(new)

    begin = (jnp.zeros((dim, dim), jnp.float32),) * seqs
    if linked:
        begin = tuple(end_state[seq] for seq in range(seqs))
    ended = lax.fori_loop(0, blocks, chain, begin)
    if linked:
        for seq in range(seqs):
            d_start[seq] = ended[seq]

    def last(step, sums):
        conv_sum, small_sum, *rims = sums
        units = spots(step)
        ats = units
        bases = [pl.multiple_of(block * STRETCH, STRETCH) for block in units]
        acts, keys, rate_sets = [], [], []
        for base in bases:
            pre = convolve(window(proj, halo, length, base, all_conv), conv)
            gate = sigmoid(pre)
            act = pre * gate
            raw = stack(act, 1, dim)
            unit = unit_rows(raw)
            acts.append((act, gate * (1.0 + pre * (1.0 - gate)), unit))
            keys.append(raw * unit)
            rate_sets.append(rates(proj[pl.ds(base, STRETCH), pl.ds(6 * dim, dim)], decay))
        nears = [
            mul_nt(jnp.concatenate([key, act[:, :dim]], axis=0), key)
            for (act, _, _), key in zip(acts, keys)
        ]
        masks = [decays(running) for _, running in rate_sets]
        d_freshes = [
            mul_tn(near[WIDE:] * upto, d_out[at])
            + mul(key * twice(jnp.exp(running[STRETCH - 1 :, 2:3] - running[:, 2:3])), chained[at])
            for near, (_, upto), at, key, (_, running) in zip(nears, masks, ats, keys, rate_sets)
        ]
        backs = [mul_tn(inv[at], d_fresh) for at, d_fresh in zip(ats, d_freshes)]
        reads = [
            stack(act, 3, dim) - mul(key * twice(jnp.exp(running[:, 2:3])), states[at])
            for (act, _, _), key, (_, running), at in zip(acts, keys, rate_sets, ats)
        ]
        to_state = [
            mul_nt(jnp.concatenate([beta * back, d_out[at]], axis=0), states[at])
            for (beta, _), back, at in zip(rate_sets, backs, ats)
        ]
        to_new = [
            mul_nt(jnp.concatenate([back, d_out[at]], axis=0), fresh[at])
            for back, at in zip(backs, ats)
        ]
        d_ends = [mul_nt(fresh[at], chained[at]) for at in ats]
        shaped = [-cross[:WIDE] * strict for cross, (strict, _) in zip(to_new, masks)]
        insides = [beta * a for (beta, _), a in zip(rate_sets, shaped)]
        d_nears = [cross[WIDE:] * upto for cross, (_, upto) in zip(to_new, masks)]
        towards = [
            mul(jnp.concatenate([inside, d_near], axis=0), key)
            for inside, d_near, key in zip(insides, d_nears, keys)
        ]
        away = [
            mul_tn(
                jnp.concatenate([inside, d_near], axis=0),
                jnp.concatenate([key, act[:, :dim]], axis=0),
            )
            for inside, d_near, key, (act, _, _) in zip(insides, d_nears, keys, acts)
        ]
        d_heres = []
        for k, (at, base) in enumerate(zip(ats, bases)):
            act, slope, unit = acts[k]
            query, key = act[:, :dim], keys[k]
            beta, running = rate_sets[k]
            small = proj[pl.ds(base, STRETCH), pl.ds(6 * dim, dim)]
            g = running[:, 2:3]
            end = g[STRETCH - 1 :]
            grown, to_go = jnp.exp(g), jnp.exp(end - g)
            back = backs[k]
            d_scaled, d_query_scaled = -to_state[k][:WIDE], to_state[k][WIDE:]
            with_inside = shaped[k] * nears[k][:WIDE]
            d_beta = jnp.sum(back * reads[k] + with_inside, axis=1, keepdims=True)
            gaps = beta * with_inside
            score_gaps = d_nears[k] * nears[k][WIDE:]
            d_query = towards[k][WIDE:] + d_query_scaled * grown
            from_start, from_end = d_scaled * twice(grown), d_ends[k] * twice(to_go)
            d_key = towards[k][:WIDE] + away[k] + from_start + from_end
            ended = jnp.sum(from_end * key, axis=1, keepdims=True)
            row_terms = jnp.sum(gaps + from_start * key, axis=1, keepdims=True) - ended
            col_terms = jnp.sum(gaps, axis=0, keepdims=True) + jnp.sum(
                score_gaps, axis=0, keepdims=True
            )
            col_terms = jnp.transpose(jnp.broadcast_to(col_terms, (8, WIDE)))[:, 0:1]
            row_terms = row_terms - col_terms
            d_g = (
                row_terms[:STRETCH]
                + row_terms[STRETCH:]
                + jnp.sum(score_gaps + d_query_scaled * grown * query, axis=1, keepdims=True)
            )
            d_end = jnp.sum(ended, axis=0, keepdims=True) + jnp.exp(end) * jnp.sum(
                jnp.sum(states[at] * chained[at], axis=0, keepdims=True), axis=1, keepdims=True
            )
            row, col = iotas(STRETCH, STRETCH)
            across = jnp.transpose(jnp.broadcast_to(d_g, (STRETCH, WIDE)))[:STRETCH]
            d_gamma = jnp.sum(jnp.where(row <= col, across, 0.0), axis=1, keepdims=True) + d_end
            lane = iotas(STRETCH, dim)[1]
            shifted = small + decay[1:2]
            d_soft = -jnp.exp(decay[0:1]) * d_gamma
            d_logit = d_soft * sigmoid(shifted)
            d_rate = jnp.where(lane == 0, d_beta[:STRETCH], d_beta[STRETCH:])
            open_beta = sigmoid(small)
            d_small = jnp.where(
                lane < 2,
                d_rate * open_beta * (1.0 - open_beta),
                jnp.where(lane == 2, d_logit, 0.0),
            )
            d_proj[pl.ds(base, STRETCH), pl.ds(6 * dim, dim)] = low(d_small)
            small_sum = small_sum + jnp.concatenate(
                [
                    jnp.sum(d_soft * softplus(shifted), axis=0, keepdims=True),
                    jnp.sum(d_logit, axis=0, keepdims=True),
                ],
                axis=0,
            )
            d_raw = unit * (d_key - key * jnp.sum(d_key * key, axis=1, keepdims=True))
            d_value = beta * back
            d_act = jnp.concatenate(
                [d_query, d_raw[:STRETCH], d_raw[STRETCH:], d_value[:STRETCH], d_value[STRETCH:]],
                axis=1,
            )
            d_heres.append(d_act * slope)
        for k, (base, d_here) in enumerate(zip(bases, d_heres)):
            rows = window(proj, halo, length, base, all_conv)
            first_row = 8 - (CONV - 1)
            conv_sum = conv_sum + jnp.concatenate(
                [
                    jnp.sum(
                        d_here * rows[first_row + tap : first_row + tap + STRETCH],
                        axis=0,
                        keepdims=True,
                    )
                    for tap in range(CONV)
                ],
                axis=0,
            )
            ahead = jnp.concatenate([d_here, rims[k % seqs]], axis=0)
            rims[k % seqs] = d_here[:8]
            total = None
            for tap in range(CONV):
                start = CONV - 1 - tap
                term = conv[tap : tap + 1] * ahead[start : start + STRETCH]
                total = term if total is None else total + term
            d_proj[pl.ds(base, STRETCH), all_conv] = low(total)
        return conv_sum, small_sum, *rims

    conv_sum, small_sum, *rims = staged(
        turns,
        last,
        (
            jnp.zeros((CONV, 5 * dim), jnp.float32),
            jnp.zeros((2, dim), jnp.float32),
        )
        + (jnp.zeros((8, 5 * dim), jnp.float32),) * seqs,
        marks_of(plan, 1, steps),
    )
    def unproject(step, total):
        at = pl.ds(pl.multiple_of(step * TOGETHER * STRETCH, STRETCH), TOGETHER * STRETCH)
        given = dot(d_proj[at], head[...], ((1,), (1,)))
        d_normed[at] = low(given)
        rows = tokens[at].astype(jnp.float32)
        scale = lax.rsqrt(jnp.mean(rows * rows, axis=1, keepdims=True) + EPS)
        return total + jnp.sum(given * (rows * scale), axis=0, keepdims=True)

    d_norm_gain[...] = staged(
        seqs * blocks // TOGETHER,
        unproject,
        jnp.zeros((1, tokens.shape[1]), jnp.float32),
        marks_of(plan, 2, steps),
    )
    if linked:
        for seq in range(seqs):
            d_first[seq] = rims[seq]
    d_conv[...] = conv_sum
    d_small_sums[...] = small_sum
    if spot is not None:
        for seq in range(seqs):
            for k in range(1, HEADS):
                from_mate(seq, spot.mate_off(k), k).wait_send()


def mixer_backward(
    proj, conv, decay, gain, kept, d_mixer, tokens, head, groups=0, number=None, link=(), jobs=(), plan=None
):
    seqs, length, _ = tokens.shape
    width = proj.shape[1]
    tokens = tokens.reshape(seqs * length, -1)
    dim = gain.shape[1]
    units = seqs * length // STRETCH
    f32, low_ = jnp.float32, jnp.bfloat16
    outs = [
        shape((seqs * length, width), low_),
        shape((CONV, 5 * dim), f32),
        shape((2, dim), f32),
        shape((1, dim), f32),
        shape(tokens.shape, low_),
        shape((1, tokens.shape[1]), f32),
    ]
    if link:
        outs += [shape((seqs, dim, dim), f32), shape((seqs, 8, 5 * dim), f32)]
    scratch = [pltpu.VMEM((units, STRETCH, dim), f32), pltpu.VMEM((units, dim, dim), f32)]
    if number:
        scratch += [pltpu.VMEM((seqs * length, dim), low_)]
        scratch += [dma(seqs, HEADS), dma(seqs, HEADS), dma(seqs)]

    def body(spot, ins, outs, scratch, steps):
        backward_body(bool(link), seqs, spot, ins, outs, scratch, steps, plan or {})

    return fused_call(
        body,
        [(a, IN_VMEM) for a in (proj, conv, decay, gain, *kept, d_mixer, tokens, head, *link)],
        [(a, IN_VMEM) for a in outs], scratch, jobs, groups, number, "mixer_backward", 60,
        mixer_cost(units),
    )


PROLOGUE_PLAN = (1, 0, 3, 1, 2, 3, 2, 0, 2, 0, 2, 0, 3, 0, 2)
EPILOGUE_PLAN = (
    2, 0, 2, 2, 0, 4, 2, 2, 4, 6, 5, 2, 5, 2, 2, 1, 3, 0, 2, 1, 4, 2, 6, 2, 0, 2, 0, 1, 3, 2, 2, 2, 0, 2,
    0, 2, 5, 0, 2, 1, 0, 6, 2, 2, 0, 3, 0, 1,
)
FORWARD_PLAN = {
    (0, 0): ((0, 1), (1, 1)),
    (0, 6): ((1, 1), (0, 1), (2, 1)),
    (1, 3): ((0, 1), (1, 1)),
    (1, 4): ((1, 1),),
    (1, 5): ((0, 1),),
    (1, 6): ((0, 1), (2, 1), (0, 1)),
    (1, 7): ((2, 1),),
    (1, 8): ((2, 1),),
    (2, 0): ((0, 1),),
    (2, 4): ((2, 1),),
}
BACKWARD_PLAN = {
    (0, 0): ((1, 1), (0, 1)),
    (0, 2): ((0, 1),),
    (0, 6): ((0, 1),),
    (0, 8): ((1, 1), (0, 1)),
    (1, 0): ((0, 1),),
    (1, 1): ((0, 1),),
    (1, 2): ((0, 1),),
    (1, 4): ((0, 1),),
    (1, 5): ((1, 1),),
    (1, 6): ((0, 1),),
    (2, 2): ((0, 1),),
    (2, 6): ((0, 1), (0, 1), (1, 1)),
    (2, 7): ((0, 1),),
}
REDUCE_PLAN = (
    1, 2, 0, 2, 2, 2, 1, 2, 2, 0, 1, 2, 1, 1, 2, 1, 1, 1, 1, 0,
)
def matmul(left, right):
    return jnp.dot(left, right, preferred_element_type=jnp.float32)


def times_transposed(left, right):
    return lax.dot_general(
        left, right, (((1,), (1,)), ((), ())), preferred_element_type=jnp.float32
    )


def transposed_times(left, right):
    return lax.dot_general(
        left, right, (((0,), (0,)), ((), ())), preferred_element_type=jnp.float32
    )


def exact(left, right):
    return jnp.einsum("sij,sjk->sik", left, right, precision=lax.Precision.HIGHEST)


def norm_scale(values):
    return lax.rsqrt(jnp.mean(values * values, axis=-1, keepdims=True) + EPS)


def norm_back(values, gain, given):
    scale = norm_scale(values)
    normal = values * scale
    inner = given * gain
    return scale * (inner - normal * jnp.mean(inner * normal, axis=-1, keepdims=True)), (
        given * normal
    )


def per_device(
    block_in,
    lengths,
    norm_gains,
    w_in,
    w_small,
    conv_weight,
    decay_log,
    decay_bias,
    out_norm_gain,
    w_out,
    gate_up_weight,
    w_down,
    out_cotangent,
):
    micro, seq_count, tokens, width = block_in.shape
    seqs = micro * seq_count
    count = lax.axis_size("ctx")
    groups = lax.axis_size("rep")
    place = lax.axis_index("ctx")
    group = lax.axis_index("rep")
    teams = count // HEADS
    head = lax.rem(place, HEADS)
    team = lax.div(place, HEADS)
    mates = peers = None
    if teams > 1:
        mates = [[t * HEADS + h for h in range(HEADS)] for t in range(teams)]
        peers = [[t * HEADS + h for t in range(teams)] for h in range(HEADS)]
    dim = width // HEADS
    length = HEADS * tokens
    rows = seqs * tokens
    kinds = 2 + 2 * STEPS
    rates_of = STEPS + 1
    f32, bf16 = jnp.float32, jnp.bfloat16

    def over_teams(array):
        if teams == 1:
            return array
        return lax.all_gather(array, "ctx", axis=0, tiled=True, axis_index_groups=peers)

    places = place * tokens + lax.broadcasted_iota(jnp.int32, (seqs, tokens), 1)
    valid = (places < lengths.reshape(seqs, 1)).astype(f32).reshape(rows, 1)
    grad_out = (out_cotangent.reshape(rows, width).astype(f32) * valid).astype(bf16)

    own = width // count
    piece = own // groups
    small_block = jnp.concatenate(
        [norm_gains.reshape(-1), conv_weight.reshape(-1)]
    )
    small_block = jnp.pad(small_block, (0, -small_block.size % 128)).reshape(-1, 128)
    (w_head,), (smalls,), (sequences,), (grad_all,) = carry(
        [
            head_job(w_in, w_small, groups),
            spread_job(small_block),
            sequences_job(block_in.reshape(seqs, tokens, width)),
            rep_gather_job(grad_out, groups),
        ],
        PROLOGUE_PLAN,
        groups,
        1,
        "prologue",
    )
    sequences = sequences.reshape(seqs, length, width)
    grad_all = grad_all.reshape(groups * rows, width)
    smalls = over_teams(smalls).reshape(count, -1)
    gains = smalls[:, : 2 * own].reshape(count, 2, own).transpose(1, 0, 2).reshape(2, width)
    gains = gains.astype(f32)
    taps_at = 2 * own
    conv_all = smalls[:, taps_at : taps_at + conv_weight.size].reshape(count, CONV, -1)
    conv_all = conv_all.transpose(1, 0, 2).reshape(CONV, kinds - 1, HEADS, dim)
    conv_head = lax.dynamic_index_in_dim(conv_all, head, 2, keepdims=False)
    conv_head = conv_head.reshape(CONV, -1).astype(f32)
    w_head = over_teams(w_head).reshape(width, -1)
    hidden_own = w_down.shape[0] // groups
    hidden_units = count * hidden_own
    out_piece = lax.dynamic_index_in_dim(
        w_out.reshape(groups, piece, width), group, 0, keepdims=False
    )
    gate_up_part = lax.dynamic_index_in_dim(
        gate_up_weight.reshape(own, 2, count, groups, hidden_own), group, 3, keepdims=False
    ).reshape(own, -1)
    down_part = lax.dynamic_index_in_dim(
        w_down.reshape(groups, hidden_own, width), group, 0, keepdims=False
    )

    mine_only = lax.broadcasted_iota(jnp.int32, (2, HEADS), 1) == head
    decay = jnp.where(mine_only, jnp.stack([decay_log, decay_bias]), 0.0).sum(axis=1, keepdims=True)
    decay = jnp.broadcast_to(decay, (2, dim))
    gain = out_norm_gain.reshape(1, dim)
    head_args = (sequences, gains[:1], w_head, conv_head, decay, gain)
    link = ()
    if teams > 1:
        onward = [(c, c + HEADS) for c in range(count - HEADS)]
        tail = sequences[:, length - 8 :].reshape(seqs * 8, width).astype(f32)
        tail = (tail * norm_scale(tail) * gains[0]).astype(bf16)
        halo = lax.ppermute(matmul(tail, w_head), "ctx", onward)
        start = jnp.zeros((seqs, dim, dim), f32)
        (*_, offset, transfer), _ = mixer_forward(*head_args, link=(halo, start))
        spans = lax.all_gather((transfer, offset), "ctx", axis_index_groups=peers)
        for turn in range(teams - 1):
            start = jnp.where(turn < team, exact(spans[0][turn], start) + spans[1][turn], start)
        link = (halo, start)
    (proj, h_flat, *kept), given = mixer_forward(
        *head_args, groups, 2, link,
        [
            team_gather_job(out_piece, groups, twofold=True),
            team_gather_job(gate_up_part),
            team_gather_job(down_part),
        ],
        FORWARD_PLAN,
    )
    (w_out_full,), (gate_up_part,), (down_part,) = given
    mixer = kept[-1].reshape(rows, width)
    kept = kept[:6]
    w_out_full = over_teams(w_out_full).reshape(width, width)
    gate_up_part = over_teams(gate_up_part).reshape(width, 2 * hidden_units)
    inputs = block_in.reshape(rows, width).astype(f32)
    resid = inputs + matmul(mixer, w_out_full)

    def team_share(grad):
        grad = grad.astype(bf16)
        if teams == 1:
            return grad
        return lax.psum_scatter(
            grad, "ctx", scatter_dimension=0, tiled=True, axis_index_groups=peers
        )

    h_second = (resid * norm_scale(resid) * gains[1]).astype(bf16)
    ((h_all,),) = carry([rep_gather_job(h_second, groups)], (), groups, 3, "gather_copies")
    h_all = h_all.reshape(groups * rows, width)
    down_part = over_teams(down_part).reshape(hidden_units, width)
    gate_up = matmul(h_all, gate_up_part)
    gate, up = gate_up[:, :hidden_units], gate_up[:, hidden_units:]
    open_gate = jax.nn.sigmoid(gate)
    silu = gate * open_gate
    hidden = (silu * up).astype(bf16)
    d_hidden = times_transposed(grad_all, down_part)
    d_gate_up = jnp.concatenate(
        [d_hidden * up * (open_gate * (1.0 + gate * (1.0 - open_gate))), d_hidden * silu], axis=1
    ).astype(bf16)
    d_second = times_transposed(d_gate_up, gate_up_part).astype(bf16)
    grad_down = team_share(transposed_times(hidden, grad_all)).reshape(HEADS, hidden_own, width)
    (d_second,), (grad_down,), (grad_gate_up,) = carry(
        [
            rep_reduce_job(d_second.reshape(groups, rows, width), groups),
            team_reduce_job(grad_down, 1, 2, bf16),
            product_job(h_all, d_gate_up),
        ],
        REDUCE_PLAN,
        groups,
        4,
        "reduce_copies",
    )
    down_parts = matmul(hidden, down_part).astype(bf16).reshape(groups, rows, width)
    d_norm, gain_terms_second = norm_back(resid, gains[1], d_second)
    d_resid = grad_out.astype(f32) + d_norm
    d_branch = d_resid.astype(bf16)
    grad_out_proj = transposed_times(mixer, d_branch)
    d_mixer = times_transposed(d_branch, w_out_full).astype(bf16).reshape(seqs, tokens, width)

    grad_gate_up = team_share(grad_gate_up).reshape(HEADS, own, -1)
    grad_out_proj = team_share(grad_out_proj).reshape(HEADS, groups, piece, width)

    link = ()
    if teams > 1:
        later = jnp.zeros((seqs, dim, dim), f32)
        heads_own = lax.all_to_all(
            d_mixer.reshape(rows, HEADS, dim).transpose(1, 0, 2),
            "ctx", 0, 0, tiled=True, axis_index_groups=mates,
        )
        heads_own = heads_own.reshape(HEADS, seqs, tokens, dim).transpose(1, 0, 2, 3)
        local = mixer_backward(
            proj, conv_head, decay, gain, kept, heads_own.reshape(seqs * length, dim), sequences,
            w_head, link=(halo, later),
        )[0][6]
        locals_ = lax.all_gather(local, "ctx", axis_index_groups=peers)
        for turn in range(teams - 1, 0, -1):
            later = jnp.where(
                turn > team,
                exact(spans[0][turn].transpose(0, 2, 1), later) + locals_[turn],
                later,
            )
        link = (halo, later)
    (d_proj, grad_conv, small_sums, grad_gain, d_first, gain_sum, *rims), given = mixer_backward(
        proj, conv_head, decay, gain, kept, d_mixer, sequences, w_head, groups, 5, link,
        [
            team_reduce_job(grad_gate_up, 2, 3, bf16),
            both_reduce_job(grad_out_proj, groups),
        ],
        BACKWARD_PLAN,
    )
    (grad_gate_up,), (grad_out_proj,) = given
    if teams > 1:
        rim = lax.ppermute(rims[1], "ctx", [(c, c - HEADS) for c in range(HEADS, count)])
        spill = jnp.zeros((seqs, CONV - 1, kinds * dim - dim), f32)
        for ahead in range(1, CONV):
            spill = spill.at[:, CONV - 1 - ahead :].add(
                conv_head[CONV - 1 - ahead] * rim[:, :ahead]
            )
        d_proj = d_proj.reshape(seqs, length, -1)
        end = d_proj[:, length - CONV + 1 :, : (kinds - 1) * dim]
        d_proj = d_proj.at[:, length - CONV + 1 :, : (kinds - 1) * dim].set(
            (end.astype(f32) + spill).astype(bf16)
        )
        d_proj = d_proj.reshape(seqs * length, -1)
        d_first = times_transposed(d_proj, w_head)
        normal = sequences.reshape(seqs * length, width).astype(f32)
        gain_sum = (d_first * (normal * norm_scale(normal))).sum(axis=0)
        d_first = d_first.astype(bf16)

    grad_small = transposed_times(d_proj[:, kinds * dim : kinds * dim + 8], h_flat)
    packed = jnp.concatenate(
        [
            jnp.stack([gain_sum.reshape(width), gain_terms_second.sum(axis=0)]).reshape(-1, dim),
            grad_small[:rates_of].reshape(-1, dim),
            grad_conv.reshape(-1, dim),
            grad_gain,
            small_sums[:, STEPS : STEPS + 1] + jnp.zeros((1, dim), f32),
        ]
    )
    packed = jnp.pad(packed, ((0, -packed.shape[0] % 8), (0, 0)))
    factors = [h_flat, d_proj]
    if teams > 1:
        grad_head = team_share(transposed_times(h_flat, d_proj[:, : kinds * dim]))
        factors = [grad_head.reshape(HEADS, groups, piece, kinds * dim)]
    if teams > 1:
        packed = lax.psum(packed, "ctx", axis_index_groups=peers)
    (grad_in,), (packed,), (d_first,), (grad_gate_up,), (grad_down,), (grad_out_proj,), (down,) = carry(
        [
            deal_job(factors, (HEADS, groups, piece, kinds * dim), groups),
            small_job(packed, groups),
            tokens_job(d_first.reshape(seqs, HEADS, tokens, width), 2),
            rep_gather_job(grad_gate_up, groups, IN_VMEM),
            rep_gather_job(grad_down, groups, IN_VMEM),
            rep_gather_job(grad_out_proj, groups, IN_VMEM),
            rep_reduce_job(down_parts, groups),
        ],
        EPILOGUE_PLAN,
        groups,
        6,
        "epilogue",
    )
    d_inputs, _ = norm_back(inputs, gains[0], d_first.reshape(rows, width))
    in_grad = (d_resid + d_inputs).astype(bf16)
    result = (valid * (resid + down)).astype(bf16)
    grad_in = grad_in.reshape(own, -1)
    grad_gate_up = grad_gate_up.reshape(groups, own, 2, count, hidden_own)
    grad_gate_up = lax.optimization_barrier(
        grad_gate_up.transpose(1, 2, 3, 0, 4).reshape(own, -1)
    )
    grad_down = grad_down.reshape(groups * hidden_own, width)
    grad_out_proj = grad_out_proj.reshape(own, width)

    def take(size):
        nonlocal packed
        part, packed = packed[:, :size], packed[:, size:]
        return part

    grad_gains = take(2 * HEADS).sum(axis=0).reshape(2, width)
    grad_small = take(rates_of * HEADS).reshape(HEADS, rates_of, width)
    grad_small = grad_small.transpose(2, 1, 0).reshape(width, rates_of * HEADS)
    grad_conv = take(CONV * (kinds - 1)).reshape(HEADS, CONV, kinds - 1, dim)
    grad_conv = grad_conv.transpose(1, 2, 0, 3).reshape(CONV, (kinds - 1) * width)
    grad_gain = take(1).sum(axis=0).reshape(dim)
    decays_sum = take(2)[:, :, 0].transpose(1, 0)

    def mine(array, axis, size):
        return lax.dynamic_slice_in_dim(array, place * size, size, axis)

    grad_gains = mine(grad_gains, 1, own)
    grad_small = mine(grad_small, 0, own)
    grad_conv = mine(grad_conv, 1, conv_weight.shape[1])
    return (
        result.reshape(block_in.shape),
        in_grad.reshape(block_in.shape),
        grad_gains,
        grad_in.astype(f32),
        grad_small,
        grad_conv,
        decays_sum[0],
        decays_sum[1],
        grad_gain,
        grad_out_proj.astype(f32),
        grad_gate_up.astype(f32),
        grad_down.astype(f32),
    )


def solution(mesh):
    placed = (
        P(None, "rep", "ctx", None),
        P(None, "rep"),
        P(None, "ctx"),
        P("ctx", None),
        P("ctx", None),
        P(None, "ctx"),
        P(),
        P(),
        P(),
        P("ctx", None),
        P("ctx", None),
        P("ctx", None),
        P(None, "rep", "ctx", None),
    )
    return jax.shard_map(
        per_device,
        mesh=mesh,
        in_specs=placed,
        out_specs=(
            P(None, "rep", "ctx", None),
            P(None, "rep", "ctx", None),
            P(None, "ctx"),
            P("ctx", None),
            P("ctx", None),
            P(None, "ctx"),
            P(),
            P(),
            P(),
            P("ctx", None),
            P("ctx", None),
            P("ctx", None),
        ),
        check_vma=False,
    )
```

```python
import functools
import jax
import jax.numpy as jnp
from jax import lax
from jax.experimental import pallas as pl
from jax.experimental.pallas import tpu as pltpu
from jax.sharding import PartitionSpec as P

STEPS = 2
CONV = 4
STRETCH = 64
HEADS = 8
EPS = 1e-06
WIDE = 2 * STRETCH


MESH = pl.DeviceIdType.MESH
ROWS = 2
COLS = HEADS // ROWS


class Spot:
    def __init__(self, groups):
        place = lax.axis_index("ctx")
        self.mate = lax.rem(place, HEADS)
        self.base = place - self.mate
        self.col = lax.div(self.mate, ROWS)
        self.row = lax.rem(self.mate, ROWS)
        self.groups = groups
        self.group = lax.axis_index("rep")
        self.side = lax.rem(self.group, 2)
        self.pair = lax.div(self.group, 2)
        self.twin = self.group + 1 - 2 * self.side

    def to_mate(self, mate):
        return {"ctx": self.base + mate}

    def to_group(self, group):
        return {"rep": group}

    def mate_off(self, k):
        return lax.rem(self.mate + k, HEADS)

    def group_off(self, k):
        return lax.rem(self.group + 2 * k, self.groups)

    def barrier(self, team=True, copies=True):
        sem = pltpu.get_barrier_semaphore()
        others = []
        if team:
            others += [self.to_mate(self.mate_off(k)) for k in range(1, HEADS)]
        if copies:
            others += [self.to_group(self.twin)]
            others += [self.to_group(self.group_off(k)) for k in range(1, self.groups // 2)]
        for other in others:
            pl.semaphore_signal(sem, inc=1, device_id=other, device_id_type=MESH)
        pl.semaphore_wait(sem, len(others))


def remote(src, dst, send, recv, where):
    return pltpu.make_async_remote_copy(
        src_ref=src,
        dst_ref=dst,
        send_sem=send,
        recv_sem=recv,
        device_id=where,
        device_id_type=MESH,
    )


TEAM_SEMS = 3 * COLS + 1


def team_gather(spot, src, out, send, recv, own):
    mate, col = spot.mate, spot.col
    up, down = spot.to_mate(mate + ROWS), spot.to_mate(mate - ROWS)
    across = spot.to_mate(mate + 1 - 2 * spot.row)
    other = mate + 1 - 2 * spot.row
    local = pltpu.make_async_copy(src, out(mate), own)

    def hop(block, origin, slot, where):
        return remote(block, out(origin), send.at[slot], recv.at[slot], where)

    rise, fall, cross_low, cross_high = 0, COLS - 1, 2 * COLS - 2, 3 * COLS - 3
    last = COLS - 1
    local.start()

    @pl.when(col < last)
    def _():
        hop(src, mate, rise, up).start()

    @pl.when(col > 0)
    def _():
        hop(src, mate, fall, down).start()

    hop(src, mate, cross_low, across).start()
    yield
    for k in range(1, COLS):
        below, above = mate - ROWS * k, mate + ROWS * k

        @pl.when(col >= k)
        def _():
            hop(out(below), below, rise + k - 1, up).wait_recv()
            if k < last:

                @pl.when(col < last)
                def _():
                    hop(out(below), below, rise + k, up).start()

            hop(out(below), below, cross_low + k, across).start()

        @pl.when(col + k <= last)
        def _():
            hop(out(above), above, fall + k - 1, down).wait_recv()
            if k < last:

                @pl.when(col > 0)
                def _():
                    hop(out(above), above, fall + k, down).start()

            hop(out(above), above, cross_high + k, across).start()

        yield
    hop(src, other, cross_low, across).wait_recv()
    for k in range(1, COLS):

        @pl.when(col >= k)
        def _():
            hop(src, other - ROWS * k, cross_low + k, across).wait_recv()

        @pl.when(col + k <= last)
        def _():
            hop(src, other + ROWS * k, cross_high + k, across).wait_recv()

    @pl.when(col < last)
    def _():
        hop(src, mate, rise, up).wait_send()

    @pl.when(col > 0)
    def _():
        hop(src, mate, fall, down).wait_send()

    hop(src, mate, cross_low, across).wait_send()
    for k in range(1, COLS):

        @pl.when(col >= k)
        def _():
            if k < last:

                @pl.when(col < last)
                def _():
                    hop(src, mate, rise + k, up).wait_send()

            hop(src, mate, cross_low + k, across).wait_send()

        @pl.when(col + k <= last)
        def _():
            if k < last:

                @pl.when(col > 0)
                def _():
                    hop(src, mate, fall + k, down).wait_send()

            hop(src, mate, cross_high + k, across).wait_send()

    local.wait()
    yield


def rep_gather(spot, src, out, send, recv, own):
    group, twin, half = spot.group, spot.twin, spot.groups // 2
    local = None
    if own is not None:
        local = pltpu.make_async_copy(src, out(group), own)
        local.start()

    def hop(block, origin, slot, where):
        return remote(block, out(origin), send.at[slot], recv.at[slot], spot.to_group(where))

    hop(src, group, 0, twin).start()
    for k in range(1, half):
        hop(src, group, k, spot.group_off(k)).start()
    yield
    for k in range(1, half):
        origin = spot.group_off(half - k)
        hop(out(origin), origin, k, twin).wait_recv()
        hop(out(origin), origin, half + k, twin).start()
    yield
    hop(src, twin, 0, twin).wait_recv()
    for k in range(1, half):
        origin = lax.rem(twin + 2 * (half - k), spot.groups)
        hop(src, origin, half + k, twin).wait_recv()
    hop(src, group, 0, twin).wait_send()
    for k in range(1, half):
        hop(src, group, k, twin).wait_send()
        hop(src, group, half + k, twin).wait_send()
    if local is not None:
        local.wait()
    yield


def team_exchange(spot, src, dst, send, recv, own):
    local = pltpu.make_async_copy(src(spot.mate), dst(spot.mate), own)
    local.start()

    def hop(k):
        to = spot.mate_off(k)
        return remote(src(to), dst(spot.mate), send.at[k], recv.at[k], spot.to_mate(to))

    for k in range(1, HEADS):
        hop(k).start()
    yield
    for k in range(1, HEADS):
        hop(k).wait_recv()
    for k in range(1, HEADS):
        hop(k).wait_send()
    local.wait()
    yield


def dma(*shape):
    return pltpu.SemaphoreType.DMA(shape)


ANY = pl.BlockSpec(memory_space=pl.ANY)
IN_VMEM = pl.BlockSpec(memory_space=pltpu.VMEM)


def finish(*steps):
    for step in steps:
        for _ in step:
            pass


def rep_reduce(spot, part, sums, others, send, recv):
    half, side = spot.groups // 2, spot.side

    def to_twin(k):
        return remote(
            part(2 * k + 1 - side), sums.at[k], send.at[k], recv.at[k], spot.to_group(spot.twin)
        )

    def onward(k):
        slot = half + k
        return remote(
            sums.at[lax.rem(spot.pair + k, half)], others.at[k], send.at[slot], recv.at[slot], spot.to_group(spot.group_off(k))
        )

    for k in range(half):
        to_twin(k).start()
    yield
    for k in range(half):
        to_twin(k).wait_recv()

    def both(pair):
        return part(2 * pair + side)[...].astype(jnp.float32) + sums[pair].astype(jnp.float32)

    for k in range(1, half):
        pair = lax.rem(spot.pair + k, half)
        sums[pair] = both(pair).astype(sums.dtype)
        onward(k).start()
    yield
    total = both(spot.pair)
    for k in range(1, half):
        onward(k).wait_recv()
        total = total + others[k].astype(jnp.float32)
    for k in range(half):
        to_twin(k).wait_send()
    for k in range(1, half):
        onward(k).wait_send()
    yield total


class Lane:
    def __init__(self, part, sums, passing, total, send, recv):
        self.part, self.sums, self.passing = part, sums, passing
        self.total, self.send, self.recv = total, send, recv


def team_reduce(spot, lanes, window):
    mate, col, row = spot.mate, spot.col, spot.row
    up, down = spot.to_mate(mate + ROWS), spot.to_mate(mate - ROWS)
    across = spot.to_mate(mate + 1 - 2 * row)
    last = COLS - 1
    f32 = jnp.float32

    def hop(lane, d, way):
        src = lane.part(ROWS * d + 1 - row) if way == 0 else lane.sums.at[d]
        dst = (lane.sums.at[d], lane.passing.at[d + 1], lane.passing.at[d])[way]
        return remote(
            src, dst, lane.send.at[way, d], lane.recv.at[way, d], (across, up, down)[way]
        )

    def both(lane, d):
        return lane.part(ROWS * d + row)[...].astype(f32) + lane.sums[d].astype(f32)

    def crossed(lane, d):
        hop(lane, d, 0).wait_recv()

        @pl.when(col == d)
        def _():
            lane.total[...] = both(lane, d)

        for end, way in ((0, 1), (last, 2)):
            if d != end:

                @pl.when(col == end)
                def _():
                    lane.sums[d] = both(lane, d).astype(lane.sums.dtype)
                    hop(lane, d, way).start()

    def passed(lane, d, c, way):
        @pl.when(col == c)
        def _():
            hop(lane, d, way).wait_recv()
            got = lane.passing[d + 2 - way].astype(f32)
            if c == d:
                lane.total[...] += got
            else:
                lane.sums[d] = (both(lane, d) + got).astype(lane.sums.dtype)
                hop(lane, d, way).start()

    order_out = [d for pair in zip(range(last, -1, -1), range(COLS)) for d in pair][:COLS]
    rounds = {}
    for i, d in enumerate(order_out):
        for k, lane in enumerate(lanes):
            time = i * len(lanes) + k
            rounds.setdefault(time, []).append(functools.partial(crossed, lane, d))
            for c in range(1, d + 1):
                step = functools.partial(passed, lane, d, c, 1)
                rounds.setdefault(time + c, []).append(step)
            for c in range(d, last):
                step = functools.partial(passed, lane, d, c, 2)
                rounds.setdefault(time + last - c, []).append(step)
    ahead = [(lane, d) for d in order_out for lane in lanes]
    for lane, d in ahead[:window]:
        hop(lane, d, 0).start()
    yield
    for time in sorted(rounds):
        for k, step in enumerate(rounds[time]):
            step()
            if k == 0 and time + window < len(ahead):
                lane, d = ahead[time + window]
                hop(lane, d, 0).start()
        yield
    for d in range(COLS):
        for lane in lanes:
            hop(lane, d, 0).wait_send()

            @pl.when(col < d)
            def _():
                hop(lane, d, 1).wait_send()

            @pl.when(col > d)
            def _():
                hop(lane, d, 2).wait_send()

    yield


def advance(step, count):
    for _ in range(count):
        next(step, None)


def lane_scratch(count, rows, width):
    return [
        pltpu.VMEM((count, COLS, rows, width), jnp.bfloat16),
        pltpu.VMEM((count, COLS + 1, rows, width), jnp.bfloat16),
        dma(count, 3, COLS),
        dma(count, 3, COLS),
    ]


class Job:
    def __init__(self, make, ins=(), outs=(), scratch=(), spaces=None):
        self.make, self.ins, self.outs, self.scratch = make, list(ins), list(outs), list(scratch)
        self.in_space, self.out_space = spaces or (ANY, ANY)


def fused_call(body, ins, outs, scratch, jobs, groups, number, name, vmem, cost=None, copies=True):
    def kernel(*refs):
        refs = list(refs)

        def take(count):
            part = refs[:count]
            del refs[:count]
            return part

        own_in = take(len(ins))
        jobs_in = [take(len(job.ins)) for job in jobs]
        own_out = take(len(outs))
        jobs_out = [take(len(job.outs)) for job in jobs]
        own_scratch = take(len(scratch))
        jobs_scratch = [take(len(job.scratch)) for job in jobs]
        spot = None
        if number:
            spot = Spot(groups)
            spot.barrier(copies=copies)
        steps = [
            job.make(spot, a, b, c)
            for job, a, b, c in zip(jobs, jobs_in, jobs_out, jobs_scratch)
        ]
        body(spot, own_in, own_out, own_scratch, steps)
        finish(*steps)

    results = pl.pallas_call(
        kernel,
        out_shape=[s for s, _ in outs] + [s for job in jobs for s in job.outs],
        in_specs=[spec for _, spec in ins] + [job.in_space for job in jobs for _ in job.ins],
        out_specs=[spec for _, spec in outs] + [job.out_space for job in jobs for _ in job.outs],
        scratch_shapes=list(scratch) + [s for job in jobs for s in job.scratch],
        compiler_params=pltpu.CompilerParams(
            collective_id=number, has_side_effects=bool(number), vmem_limit_bytes=vmem * 2**20
        ),
        cost_estimate=cost,
        name=name,
    )(*[a for a, _ in ins], *[a for job in jobs for a in job.ins])
    results = list(results)
    own, rest = results[: len(outs)], results[len(outs) :]
    given = []
    for job in jobs:
        given.append(rest[: len(job.outs)])
        rest = rest[len(job.outs) :]
    return own, given


def staged(turns, body, carried, marks):
    reached = 0
    for at in sorted(marks):
        if at > reached:
            carried = lax.fori_loop(reached, at, body, carried)
            reached = at
        marks[at]()
    if reached < turns:
        carried = lax.fori_loop(reached, turns, body, carried)
    return carried


def marks_of(plan, phase, steps):
    def mark(moves):
        def go():
            for job, count in moves:
                advance(steps[job], count)

        return go

    return {turn: mark(moves) for (at, turn), moves in plan.items() if at == phase}


def shape(dims, kind):
    return jax.ShapeDtypeStruct(tuple(dims), kind)


def team_gather_job(block, groups=None, twofold=False):
    low_ = block.dtype
    if not twofold:

        def make(spot, ins, outs, scratch):
            return team_gather(spot, ins[0], lambda m: outs[0].at[m], *scratch[:2], scratch[2].at[0])

        return Job(
            make, [block], [shape((HEADS,) + block.shape, low_)],
            [dma(TEAM_SEMS), dma(TEAM_SEMS), dma(1)],
        )

    def make(spot, ins, outs, scratch):
        whole = outs[0]
        yield from team_gather(
            spot, ins[0], lambda m: whole.at[m, spot.group], *scratch[:2], scratch[4].at[0]
        )
        yield from rep_gather(
            spot, whole.at[:, spot.group], lambda g: whole.at[:, g], *scratch[2:4], None
        )

    return Job(
        make, [block], [shape((HEADS, groups) + block.shape, low_)],
        [dma(TEAM_SEMS), dma(TEAM_SEMS), dma(groups), dma(groups), dma(1)],
    )


def sequences_job(block):
    seqs = block.shape[0]

    def make(spot, ins, outs, scratch):
        gathers = [
            team_gather(
                spot, ins[0].at[seq], lambda m, seq=seq: outs[0].at[seq, m],
                scratch[0].at[seq], scratch[1].at[seq], scratch[2].at[seq],
            )
            for seq in range(seqs)
        ]
        for _ in zip(*gathers):
            yield

    return Job(
        make, [block], [shape((seqs, HEADS) + block.shape[1:], block.dtype)],
        [dma(seqs, TEAM_SEMS), dma(seqs, TEAM_SEMS), dma(seqs)],
    )


def rep_gather_job(block, groups, space=ANY):
    def make(spot, ins, outs, scratch):
        return rep_gather(spot, ins[0], lambda g: outs[0].at[g], *scratch[:2], scratch[2].at[0])

    return Job(
        make, [block], [shape((groups,) + block.shape, block.dtype)],
        [dma(groups), dma(groups), dma(1)], (space, space),
    )


def rep_reduce_job(parts, groups):
    block = pltpu.VMEM((groups // 2,) + parts.shape[1:], parts.dtype)

    def make(spot, ins, outs, scratch):
        for total in rep_reduce(spot, lambda g: ins[0].at[g], *scratch):
            if total is not None:
                outs[0][...] = total
            yield

    return Job(
        make, [parts], [shape(parts.shape[1:], jnp.float32)],
        [block, block, dma(groups), dma(groups)], (IN_VMEM, IN_VMEM),
    )


def tokens_job(parts, halves):
    seqs, _, rows, width = parts.shape
    rows_of = rows // halves

    def make(spot, ins, outs, scratch):
        sums, passing, send, recv = scratch
        lanes = []
        for seq in range(seqs):
            for half in range(halves):
                k, own = seq * halves + half, pl.ds(half * rows_of, rows_of)
                lanes.append(
                    Lane(
                        lambda mate, seq=seq, own=own: ins[0].at[seq, mate, own],
                        sums.at[k], passing.at[k], outs[0].at[seq, own], send.at[k], recv.at[k],
                    )
                )
        return team_reduce(spot, lanes, 2 * halves)

    return Job(
        make, [parts], [shape((seqs, rows, width), jnp.float32)],
        lane_scratch(seqs * halves, rows_of, width), (IN_VMEM, IN_VMEM),
    )


def team_reduce_job(parts, pieces, window, kind):
    _, rows, width = parts.shape
    rows_of = rows // pieces

    def make(spot, ins, outs, scratch):
        sums, passing, send, recv, *total = scratch
        total = total[0] if total else outs[0]
        lanes = []
        for k in range(pieces):
            own = pl.ds(k * rows_of, rows_of)
            lanes.append(
                Lane(
                    lambda mate, own=own: ins[0].at[mate, own],
                    sums.at[k], passing.at[k], total.at[own], send.at[k], recv.at[k],
                )
            )
        yield from team_reduce(spot, lanes, window)
        if kind != jnp.float32:
            outs[0][...] = total[...].astype(kind)
        yield

    scratch = lane_scratch(pieces, rows_of, width)
    if kind != jnp.float32:
        scratch.append(pltpu.VMEM((rows, width), jnp.float32))
    return Job(make, [parts], [shape((rows, width), kind)], scratch, (IN_VMEM, IN_VMEM))


def both_reduce_job(parts, groups):
    heads, _, rows, width = parts.shape
    low_ = parts.dtype
    block = pltpu.VMEM((groups // 2, heads, rows, width), low_)
    team = pltpu.VMEM((heads, rows, width), low_)

    def make(spot, ins, outs, scratch):
        sums, others, quarter, arrived, r_send, r_recv, e_send, e_recv, own = scratch
        for total in rep_reduce(
            spot, lambda g: ins[0].at[:, g], sums, others, r_send, r_recv
        ):
            if total is None:
                yield
        quarter[...] = total.astype(low_)
        exchange = team_exchange(
            spot, lambda m: quarter.at[m], lambda m: arrived.at[m], e_send, e_recv, own.at[0]
        )
        next(exchange)
        yield
        finish(exchange)
        outs[0][...] = sum(arrived[m].astype(jnp.float32) for m in range(heads)).astype(low_)
        yield

    return Job(
        make, [parts], [shape((rows, width), low_)],
        [block, block, team, team]
        + [dma(groups), dma(groups), dma(HEADS), dma(HEADS), dma(1)],
        (IN_VMEM, IN_VMEM),
    )


def tile_product(left, right, tile, width):
    return low(dot(left[:, tile * 128 : (tile + 1) * 128], right[:, :width], ((0,), (0,))))


def product_job(left, right):
    rows, width = left.shape[1], right.shape[1]

    def make(spot, ins, outs, scratch):
        for tile in range(rows // 128):
            outs[0][tile * 128 : (tile + 1) * 128] = tile_product(ins[0], ins[1], tile, width)
            yield

    return Job(
        make, [left, right], [shape((rows, width), jnp.bfloat16)], (), (IN_VMEM, IN_VMEM)
    )


def deal_job(ins, dims, groups):
    heads, _, piece, cols = dims
    low_ = jnp.bfloat16
    kinds = 2 + 2 * STEPS
    dim = cols // kinds
    block = pltpu.VMEM((groups // 2, heads, piece, cols), low_)
    made = len(ins) == 2

    def make(spot, ins, outs, scratch):
        sums, others, quarter, dealt, r_send, r_recv, e_send, e_recv, g_send, g_recv, own = scratch[:11]
        parts = ins[0]
        if made:
            parts = scratch[11]
            for mate in range(heads):
                tile = tile_product(ins[0], ins[1], mate, cols)
                for g in range(groups):
                    parts[mate, g] = tile[g * piece : (g + 1) * piece]
                if mate % 2:
                    yield
        for total in rep_reduce(
            spot, lambda g: parts.at[:, g], sums, others, r_send, r_recv
        ):
            if total is None:
                yield
        quarter[...] = total.astype(low_)
        exchange = team_exchange(
            spot, lambda m: quarter.at[m], lambda m: dealt.at[spot.group, m],
            e_send, e_recv, own.at[0],
        )
        next(exchange)
        yield
        finish(exchange)
        yield from rep_gather(
            spot, dealt.at[spot.group], lambda g: dealt.at[g], g_send, g_recv, None
        )
        for g in range(groups):
            for h in range(heads):
                rows = dealt[g, h]
                for k in range(kinds):
                    at = (k * heads + h) * dim
                    outs[0][g, :, at : at + dim] = rows[:, k * dim : (k + 1) * dim]
        yield

    return Job(
        make, ins, [shape((groups, piece, heads * cols), low_)],
        [block, block, pltpu.VMEM((heads, piece, cols), low_)]
        + [pltpu.VMEM((groups, heads, piece, cols), low_)]
        + [dma(groups), dma(groups), dma(HEADS), dma(HEADS), dma(groups), dma(groups), dma(1)]
        + ([pltpu.VMEM(dims, low_)] if made else []),
        (IN_VMEM, IN_VMEM),
    )


def small_job(smalls, groups):
    def make(spot, ins, outs, scratch):
        copies, total, s_send, s_recv, x_send, x_recv, own = scratch
        yield from rep_gather(spot, ins[0], lambda g: copies.at[g], s_send, s_recv, own.at[0])
        total[...] = sum(copies[g] for g in range(groups))
        yield from team_exchange(
            spot, lambda m: total, lambda m: outs[0].at[m], x_send, x_recv, own.at[1]
        )

    return Job(
        make, [smalls], [shape((HEADS,) + smalls.shape, jnp.float32)],
        [pltpu.VMEM((groups,) + smalls.shape, jnp.float32), pltpu.VMEM(smalls.shape, jnp.float32)]
        + [dma(groups), dma(groups), dma(HEADS), dma(HEADS), dma(2)],
        (IN_VMEM, IN_VMEM),
    )


def head_job(w_in, w_small, groups):
    own, width = w_in.shape
    kinds, piece = 2 + 2 * STEPS, own // groups
    dim = width // (kinds * HEADS)
    rates_of = w_small.shape[1] // HEADS
    dims = (HEADS, groups, piece, (kinds + 1) * dim)

    def make(spot, ins, outs, scratch):
        pieces, e_send, e_recv, w_send, w_recv, local = scratch
        row, col = iotas(w_small.shape[1], dim)
        for h in range(HEADS):
            chosen = low(jnp.where((row == col * HEADS + h) & (col < rates_of), 1.0, 0.0))
            blocks = [ins[0][:, (k * HEADS + h) * dim : (k * HEADS + h + 1) * dim] for k in range(kinds)]
            blocks.append(low(dot(ins[1][...], chosen, ((1,), (0,)))))
            for k, block in enumerate(blocks):
                block = block.astype(jnp.float32)
                for g in range(groups):
                    pieces[h, g, :, k * dim : (k + 1) * dim] = low(
                        block[g * piece : (g + 1) * piece]
                    )
        yield from team_exchange(
            spot, lambda m: pieces.at[m, spot.group], lambda m: outs[0].at[m, spot.group],
            e_send, e_recv, local.at[0],
        )
        yield from rep_gather(
            spot, outs[0].at[:, spot.group], lambda g: outs[0].at[:, g], w_send, w_recv, None
        )

    return Job(
        make, [w_in, w_small], [shape(dims, w_in.dtype)],
        [pltpu.VMEM(dims, w_in.dtype)]
        + [dma(HEADS), dma(HEADS), dma(groups), dma(groups), dma(1)],
        (IN_VMEM, ANY),
    )


def spread_job(block):
    def make(spot, ins, outs, scratch):
        return team_exchange(
            spot, lambda m: ins[0], lambda m: outs[0].at[m], *scratch[:2], scratch[2].at[0]
        )

    return Job(
        make, [block], [shape((HEADS,) + block.shape, block.dtype)], [dma(HEADS), dma(HEADS), dma(1)]
    )


def weave(parts, piece):
    groups, rows, width = parts.shape

    def kernel(parts_ref, out):
        for k in range(width // piece):
            blocks = [
                parts_ref[g, :, k * piece : (k + 1) * piece].astype(jnp.float32)
                for g in range(groups)
            ]
            at = k * groups * piece
            out[:, at : at + groups * piece] = jnp.concatenate(blocks, axis=1)

    return pl.pallas_call(
        kernel,
        out_shape=shape((rows, groups * width), jnp.float32),
        in_specs=[IN_VMEM],
        out_specs=IN_VMEM,
        name="weave",
    )(parts)


def carry(jobs, plan, groups, number, name, vmem=40):
    def body(spot, ins, outs, scratch, steps):
        for job in plan:
            advance(steps[job], 1)

    return fused_call(body, [], [], [], jobs, groups, number, name, vmem)[1]


def low(a):
    return a.astype(jnp.bfloat16)


def halves(a):
    high = low(a)
    return high, low(a - high.astype(jnp.float32))


def dot(a, b, dims):
    return lax.dot_general(a, b, (dims, ((), ())), preferred_element_type=jnp.float32)


def fold(out):
    half = out.shape[1] // 2
    return out[:, :half] + out[:, half:]


def left_nn(parts):
    return jnp.concatenate(parts, axis=1)


def right_nn(parts):
    row = jnp.concatenate(parts, axis=1)
    return jnp.concatenate([row, row], axis=0)


def right_nt(parts):
    high, rest = parts
    return jnp.concatenate(
        [jnp.concatenate([high, high], axis=1), jnp.concatenate([rest, rest], axis=1)], axis=0
    )


def mul(a, b):
    return fold(dot(left_nn(halves(a)), right_nn(halves(b)), ((1,), (0,))))


def mul_nt(a, b):
    return fold(dot(left_nn(halves(a)), right_nt(halves(b)), ((1,), (1,))))


def mul_tn(a, b):
    left = jnp.concatenate(halves(a), axis=0)
    return fold(dot(left, right_nn(halves(b)), ((0,), (0,))))


def iotas(rows, cols):
    return (
        lax.broadcasted_iota(jnp.int32, (rows, cols), 0),
        lax.broadcasted_iota(jnp.int32, (rows, cols), 1),
    )


def order(index):
    return STEPS * lax.rem(index, STRETCH) + lax.div(index, STRETCH)


def sigmoid(a):
    return 1.0 / (1.0 + jnp.exp(-a))


def softplus(a):
    return jnp.maximum(a, 0.0) + jnp.log1p(jnp.exp(-jnp.abs(a)))


def window(ref, halo, length, base, columns):
    before = ref[pl.ds(pl.multiple_of(jnp.maximum(base - 8, 0), 8), 8), columns]
    ahead = 0.0
    if halo is not None:
        ahead = halo[pl.ds(pl.multiple_of(lax.div(base, length) * 8, 8), 8), columns]
    first = lax.rem(base, length) == 0
    return jnp.concatenate(
        [jnp.where(first, ahead, before), ref[pl.ds(base, STRETCH), columns]], axis=0
    )


def stack(act, at, dim):
    return jnp.concatenate(
        [act[:, at * dim : (at + 1) * dim], act[:, (at + 1) * dim : (at + 2) * dim]], axis=0
    )


def convolve(rows, conv):
    total = None
    for tap in range(CONV):
        start = 8 - (CONV - 1) + tap
        term = conv[tap : tap + 1] * rows[start : start + STRETCH]
        total = term if total is None else total + term
    return total


def rates(small, decay):
    beta = jnp.concatenate([sigmoid(small[:, 0:1]), sigmoid(small[:, 1:2])], axis=0)
    gamma = -jnp.exp(decay[0:1]) * softplus(small + decay[1:2])
    row, col = iotas(STRETCH, STRETCH)
    tri = low(jnp.where(row >= col, 1.0, 0.0))
    high = low(gamma)
    rest = gamma - high.astype(jnp.float32)
    middle = low(rest)
    last = low(rest - middle.astype(jnp.float32))
    running = (
        dot(tri, high, ((1,), (0,))) + dot(tri, middle, ((1,), (0,))) + dot(tri, last, ((1,), (0,)))
    )
    return beta, running


def decays(running):
    column = running[:, 2:3]
    across = jnp.transpose(running)[2:3, :]
    row, col = iotas(STRETCH, STRETCH)
    gap = jnp.broadcast_to(column, (STRETCH, STRETCH)) - across
    upto = jnp.where(row >= col, jnp.exp(jnp.where(row >= col, gap, 0.0)), 0.0)
    before = jnp.where(row > col, upto, 0.0)
    strict = jnp.concatenate(
        [
            jnp.concatenate([before, before], axis=1),
            jnp.concatenate([upto, before], axis=1),
        ],
        axis=0,
    )
    return strict, jnp.concatenate([upto, upto], axis=1)


def level_masks():
    row, col = iotas(WIDE, WIDE)
    row, col = order(row), order(col)
    masks, size = [], 1
    while size < WIDE:
        inside = (lax.div(row, 2 * size) == lax.div(col, 2 * size)) & (
            lax.div(row, size) != lax.div(col, size)
        )
        masks.append(jnp.where(inside, 1.0, 0.0))
        size *= 2
    return [masks[0]] + [low(mask) for mask in masks[1:]]


def inverses(systems, masks):
    row, col = iotas(WIDE, WIDE)
    eye = jnp.where(row == col, 1.0, 0.0)
    solved = [eye - masks[0] * system for system in systems]
    split = [halves(system) for system in systems]
    for mask in masks[1:]:
        parts = [halves(a) for a in solved]
        steps = [
            fold(
                dot(
                    jnp.concatenate([high * mask, rest * mask], axis=1),
                    right_nn(part),
                    ((1,), (0,)),
                )
            )
            for (high, rest), part in zip(split, parts)
        ]
        solved = [
            a - fold(dot(left_nn(part), right_nn(halves(step)), ((1,), (0,))))
            for a, part, step in zip(solved, parts, steps)
        ]
    return solved


def unit_rows(stacked):
    return lax.rsqrt(jnp.sum(stacked * stacked, axis=1, keepdims=True) + EPS)


def twice(column):
    return jnp.concatenate([column, column], axis=0)


TOGETHER = 4


def forward_body(linked, seqs, spot, ins, outs, scratch, steps, plan):
    tokens, norm_gain, head, conv, decay, gain, *link = ins
    proj, normed, out, fresh, inv, weights, trans, states, *more = outs
    local, offset, mixer, *sems = scratch
    halo = None
    if linked:
        halo, start = link
        final, product, *more = more
    length = proj.shape[0] // seqs
    dim = gain.shape[1]
    blocks = length // STRETCH
    each = TOGETHER // seqs
    turns = blocks // each
    masks = level_masks()
    row, col = iotas(dim, dim)
    diagonal = row == col

    def project(step, _):
        at = pl.ds(pl.multiple_of(step * TOGETHER * STRETCH, STRETCH), TOGETHER * STRETCH)
        rows = tokens[at].astype(jnp.float32)
        scale = lax.rsqrt(jnp.mean(rows * rows, axis=1, keepdims=True) + EPS)
        rows = low(rows * scale * norm_gain[...])
        normed[at] = rows
        proj[at] = dot(rows, head[...], ((1,), (0,)))
        return 0

    staged(seqs * blocks // TOGETHER, project, 0, marks_of(plan, 0, steps))

    def spots(step):
        return [seq * blocks + step * each + k for k in range(each) for seq in range(seqs)]

    def first(step, _):
        units = spots(step)
        kept = []
        for block in units:
            base = pl.multiple_of(block * STRETCH, STRETCH)
            rows = window(proj, halo, length, base, pl.ds(0, 5 * dim))
            pre = convolve(rows, conv)
            act = pre * sigmoid(pre)
            raw = stack(act, 1, dim)
            key = raw * unit_rows(raw)
            beta, running = rates(proj[pl.ds(base, STRETCH), pl.ds(6 * dim, dim)], decay)
            kept.append((act[:, :dim], key, stack(act, 3, dim), beta, running))
        systems = []
        for block, (query, key, value, beta, running) in zip(units, kept):
            at = block
            strict, upto = decays(running)
            key_halves = halves(key)
            both = fold(
                dot(
                    jnp.concatenate([left_nn(key_halves), left_nn(halves(query))], axis=0),
                    right_nt(key_halves),
                    ((1,), (1,)),
                )
            )
            systems.append(beta * both[:WIDE] * strict)
            local[at] = both[WIDE:] * upto
            offset[at] = query * jnp.exp(running[:, 2:3])
        for block, (query, key, value, beta, running), solved in zip(
            units, kept, inverses(systems, masks)
        ):
            at = block
            inv[at] = solved
            grown = twice(jnp.exp(running[:, 2:3]))
            end = running[STRETCH - 1 :, 2:3]
            solved_left = left_nn(halves(solved))
            weight = fold(dot(solved_left, right_nn(halves(beta * key * grown)), ((1,), (0,))))
            value = fold(dot(solved_left, right_nn(halves(beta * value)), ((1,), (0,))))
            weights[at] = weight
            fresh[at] = value
            to_end = jnp.concatenate(halves(key * twice(jnp.exp(end - running[:, 2:3]))), axis=0)
            trans[at] = jnp.where(diagonal, jnp.exp(end), 0.0) - fold(
                dot(to_end, right_nn(halves(weight)), ((0,), (0,)))
            )
            states[at] = fold(dot(to_end, right_nn(halves(value)), ((0,), (0,))))
        return 0

    staged(turns, first, 0, marks_of(plan, 1, steps))

    def chain(step, carried):
        new = []
        for seq, state in enumerate(carried):
            block = seq * blocks + step
            added = states[block]
            states[block] = state
            if linked:
                product[seq] = mul(trans[block], product[seq])
            new.append(mul(trans[block], state) + added)
        return tuple(new)

    begin = (jnp.zeros((dim, dim), jnp.float32),) * seqs
    if linked:
        for seq in range(seqs):
            product[seq] = jnp.where(diagonal, 1.0, 0.0)
        begin = tuple(start[seq] for seq in range(seqs))
    ended = lax.fori_loop(0, blocks, chain, begin)
    if linked:
        for seq in range(seqs):
            final[seq] = ended[seq]
    if spot is not None:
        (mixed,), (x_send, x_recv, own) = more, sems
        span = length // HEADS

        def block_of(seq, mate):
            return mixer.at[pl.ds(pl.multiple_of(seq * length + mate * span, span), span)]

        def columns_of(seq, mate):
            return mixed.at[seq, :, pl.ds(pl.multiple_of(mate * dim, dim), dim)]

        def to_mate(seq, mate, slot):
            return remote(
                block_of(seq, mate), columns_of(seq, spot.mate), x_send.at[seq, slot],
                x_recv.at[seq, slot], spot.to_mate(mate),
            )

        def to_self(seq):
            return pltpu.make_async_copy(
                block_of(seq, spot.mate), columns_of(seq, spot.mate), own.at[seq]
            )

    def last(step, _):
        units = spots(step)
        reads = [
            mul(
                jnp.concatenate([weights[block], offset[block]], axis=0),
                states[block],
            )
            for block in units
        ]
        for block, read in zip(units, reads):
            at = block
            base = pl.multiple_of(block * STRETCH, STRETCH)
            new = fresh[at] - read[:WIDE]
            fresh[at] = new
            result = read[WIDE:] + mul(local[at], new)
            out[pl.ds(base, STRETCH)] = result
            gate = proj[pl.ds(base, STRETCH), pl.ds(5 * dim, dim)]
            scale = lax.rsqrt(jnp.mean(result * result, axis=1, keepdims=True) + EPS)
            mixer[pl.ds(base, STRETCH)] = low(
                result * scale * gain[...] * (gate * sigmoid(gate))
            )
        if spot is not None:
            mates = each * STRETCH // span
            for k in range(mates):
                to = step * mates + k
                slot = lax.rem(to - spot.mate + HEADS, HEADS)

                @pl.when(slot == 0)
                def _():
                    for seq in range(seqs):
                        to_self(seq).start()

                @pl.when(slot != 0)
                def _():
                    for seq in range(seqs):
                        to_mate(seq, to, slot).start()

        return 0

    staged(turns, last, 0, marks_of(plan, 2, steps))
    if spot is not None:
        for seq in range(seqs):
            for k in range(1, HEADS):
                to_mate(seq, spot.mate_off(k), k).wait_recv()
            for k in range(1, HEADS):
                to_mate(seq, spot.mate_off(k), k).wait_send()
            to_self(seq).wait()


def mixer_cost(units):
    return pl.CostEstimate(
        flops=units * 60 * WIDE * WIDE * WIDE,
        bytes_accessed=units * WIDE * WIDE * 30,
        transcendentals=units * WIDE * WIDE * 8,
    )


def mixer_forward(
    tokens, norm_gain, head, conv, decay, gain, groups=0, number=None, link=(), jobs=(), plan=None
):
    seqs, length, width = tokens.shape
    tokens = tokens.reshape(seqs * length, width)
    dim = gain.shape[1]
    units = seqs * length // STRETCH
    f32, low_ = jnp.float32, jnp.bfloat16
    outs = [
        (shape((seqs * length, head.shape[1]), f32), IN_VMEM),
        (shape((seqs * length, width), low_), IN_VMEM),
        (shape((seqs * length, dim), f32), IN_VMEM),
    ]
    outs += [(shape((units, WIDE, dim), f32), IN_VMEM)] * 5
    if link:
        outs += [(shape((seqs, dim, dim), f32), IN_VMEM)] * 2
    scratch = [
        pltpu.VMEM((units, STRETCH, WIDE), f32),
        pltpu.VMEM((units, STRETCH, dim), f32),
        pltpu.VMEM((seqs * length, dim), low_),
    ]
    if number:
        outs += [(shape((seqs, length // HEADS, HEADS * dim), low_), ANY)]
        scratch += [dma(seqs, HEADS), dma(seqs, HEADS), dma(seqs)]

    def body(spot, ins, outs, scratch, steps):
        forward_body(bool(link), seqs, spot, ins, outs, scratch, steps, plan or {})

    return fused_call(
        body, [(a, IN_VMEM) for a in (tokens, norm_gain, head, conv, decay, gain, *link)], outs, scratch, jobs,
        groups, number, "mixer_forward", 56, mixer_cost(units),
    )


def backward_body(linked, seqs, spot, ins, outs, scratch, steps, plan):
    proj, conv, decay, gain, out, fresh, inv, weights, trans, states, d_mixer, tokens, head, *link = ins
    d_proj, d_conv, d_small_sums, d_gain, d_normed, d_norm_gain, *more = outs
    d_out, chained, *arrived = scratch
    halo = None
    if linked:
        halo, end_state = link
        d_start, d_first = more
    length = proj.shape[0] // seqs
    dim = gain.shape[1]
    blocks = length // STRETCH
    each = TOGETHER // seqs
    turns = blocks // each
    span = length // HEADS
    all_conv = pl.ds(0, 5 * dim)
    if spot is not None:
        d_tokens = d_mixer
        d_mixer, x_send, x_recv, own = arrived

        def block_of(seq, mate):
            return d_mixer.at[pl.ds(pl.multiple_of(seq * length + mate * span, span), span)]

        def columns_of(seq, mate):
            return d_tokens.at[seq, :, pl.ds(pl.multiple_of(mate * dim, dim), dim)]

        def from_mate(seq, mate, slot):
            return remote(
                columns_of(seq, mate), block_of(seq, mate), x_send.at[seq, slot],
                x_recv.at[seq, slot], spot.to_mate(mate),
            )

        def from_self(seq):
            return pltpu.make_async_copy(
                columns_of(seq, spot.mate), block_of(seq, spot.mate), own.at[seq]
            )

        for seq in range(seqs):
            next(
                team_exchange(
                    spot, functools.partial(columns_of, seq), functools.partial(block_of, seq),
                    x_send.at[seq], x_recv.at[seq], own.at[seq],
                )
            )

    def spots(step):
        return [
            seq * blocks + blocks - 1 - step * each - k for k in range(each) for seq in range(seqs)
        ]

    def first(step, gain_sum):
        units = spots(step)
        kept = []
        if spot is not None:
            mates = each * STRETCH // span
            for k in range(mates):
                origin = HEADS - 1 - step * mates - k
                slot = lax.rem(spot.mate - origin + HEADS, HEADS)

                @pl.when(slot == 0)
                def _():
                    for seq in range(seqs):
                        from_self(seq).wait()

                @pl.when(slot != 0)
                def _():
                    for seq in range(seqs):
                        from_mate(seq, origin, slot).wait_recv()

        for block in units:
            at = block
            base = pl.multiple_of(block * STRETCH, STRETCH)
            result = out[pl.ds(base, STRETCH)]
            gate = proj[pl.ds(base, STRETCH), pl.ds(5 * dim, dim)]
            given = d_mixer[pl.ds(base, STRETCH)].astype(jnp.float32)
            scale = lax.rsqrt(jnp.mean(result * result, axis=1, keepdims=True) + EPS)
            normal = result * scale
            open_ = sigmoid(gate)
            silu = gate * open_
            gain_sum = gain_sum + jnp.sum(given * normal * silu, axis=0, keepdims=True)
            d_proj[pl.ds(base, STRETCH), pl.ds(5 * dim, dim)] = low(
                given * normal * gain[...] * (open_ * (1.0 + gate * (1.0 - open_)))
            )
            inner = given * gain[...] * silu
            d_result = scale * (inner - normal * jnp.mean(inner * normal, axis=1, keepdims=True))
            d_out[at] = d_result
            pre = convolve(window(proj, halo, length, base, pl.ds(0, 3 * dim)), conv[:, : 3 * dim])
            act = pre * sigmoid(pre)
            raw = stack(act, 1, dim)
            _, running = rates(proj[pl.ds(base, STRETCH), pl.ds(6 * dim, dim)], decay)
            kept.append((act[:, :dim], raw * unit_rows(raw), running, d_result))
        scores = [
            mul_nt(query, key) * decays(running)[1] for query, key, running, _ in kept
        ]
        d_freshes = [mul_tn(score, unit[3]) for score, unit in zip(scores, kept)]
        for block, (query, _, running, d_result), d_fresh in zip(units, kept, d_freshes):
            at = block
            chained[at] = mul_tn(
                jnp.concatenate([query * jnp.exp(running[:, 2:3]), -weights[at]], axis=0),
                jnp.concatenate([d_result, d_fresh], axis=0),
            )
        return gain_sum

    d_gain[...] = staged(
        turns, first, jnp.zeros((1, dim), jnp.float32), marks_of(plan, 0, steps)
    )

    def chain(step, carried):
        new = []
        for seq, later in enumerate(carried):
            block = seq * blocks + blocks - 1 - step
            added = chained[block]
            chained[block] = later
            new.append(mul_tn(trans[block], later) + added)
        return tuple(new)

    begin = (jnp.zeros((dim, dim), jnp.float32),) * seqs
    if linked:
        begin = tuple(end_state[seq] for seq in range(seqs))
    ended = lax.fori_loop(0, blocks, chain, begin)
    if linked:
        for seq in range(seqs):
            d_start[seq] = ended[seq]

    def last(step, sums):
        conv_sum, small_sum, *rims = sums
        units = spots(step)
        ats = units
        bases = [pl.multiple_of(block * STRETCH, STRETCH) for block in units]
        acts, keys, rate_sets = [], [], []
        for base in bases:
            pre = convolve(window(proj, halo, length, base, all_conv), conv)
            gate = sigmoid(pre)
            act = pre * gate
            raw = stack(act, 1, dim)
            unit = unit_rows(raw)
            acts.append((act, gate * (1.0 + pre * (1.0 - gate)), unit))
            keys.append(raw * unit)
            rate_sets.append(rates(proj[pl.ds(base, STRETCH), pl.ds(6 * dim, dim)], decay))
        nears = [
            mul_nt(jnp.concatenate([key, act[:, :dim]], axis=0), key)
            for (act, _, _), key in zip(acts, keys)
        ]
        masks = [decays(running) for _, running in rate_sets]
        d_freshes = [
            mul_tn(near[WIDE:] * upto, d_out[at])
            + mul(key * twice(jnp.exp(running[STRETCH - 1 :, 2:3] - running[:, 2:3])), chained[at])
            for near, (_, upto), at, key, (_, running) in zip(nears, masks, ats, keys, rate_sets)
        ]
        backs = [mul_tn(inv[at], d_fresh) for at, d_fresh in zip(ats, d_freshes)]
        reads = [
            stack(act, 3, dim) - mul(key * twice(jnp.exp(running[:, 2:3])), states[at])
            for (act, _, _), key, (_, running), at in zip(acts, keys, rate_sets, ats)
        ]
        to_state = [
            mul_nt(jnp.concatenate([beta * back, d_out[at]], axis=0), states[at])
            for (beta, _), back, at in zip(rate_sets, backs, ats)
        ]
        to_new = [
            mul_nt(jnp.concatenate([back, d_out[at]], axis=0), fresh[at])
            for back, at in zip(backs, ats)
        ]
        d_ends = [mul_nt(fresh[at], chained[at]) for at in ats]
        shaped = [-cross[:WIDE] * strict for cross, (strict, _) in zip(to_new, masks)]
        insides = [beta * a for (beta, _), a in zip(rate_sets, shaped)]
        d_nears = [cross[WIDE:] * upto for cross, (_, upto) in zip(to_new, masks)]
        towards = [
            mul(jnp.concatenate([inside, d_near], axis=0), key)
            for inside, d_near, key in zip(insides, d_nears, keys)
        ]
        away = [
            mul_tn(
                jnp.concatenate([inside, d_near], axis=0),
                jnp.concatenate([key, act[:, :dim]], axis=0),
            )
            for inside, d_near, key, (act, _, _) in zip(insides, d_nears, keys, acts)
        ]
        d_heres = []
        for k, (at, base) in enumerate(zip(ats, bases)):
            act, slope, unit = acts[k]
            query, key = act[:, :dim], keys[k]
            beta, running = rate_sets[k]
            small = proj[pl.ds(base, STRETCH), pl.ds(6 * dim, dim)]
            g = running[:, 2:3]
            end = g[STRETCH - 1 :]
            grown, to_go = jnp.exp(g), jnp.exp(end - g)
            back = backs[k]
            d_scaled, d_query_scaled = -to_state[k][:WIDE], to_state[k][WIDE:]
            with_inside = shaped[k] * nears[k][:WIDE]
            d_beta = jnp.sum(back * reads[k] + with_inside, axis=1, keepdims=True)
            gaps = beta * with_inside
            score_gaps = d_nears[k] * nears[k][WIDE:]
            d_query = towards[k][WIDE:] + d_query_scaled * grown
            from_start, from_end = d_scaled * twice(grown), d_ends[k] * twice(to_go)
            d_key = towards[k][:WIDE] + away[k] + from_start + from_end
            ended = jnp.sum(from_end * key, axis=1, keepdims=True)
            row_terms = jnp.sum(gaps + from_start * key, axis=1, keepdims=True) - ended
            col_terms = jnp.sum(gaps, axis=0, keepdims=True) + jnp.sum(
                score_gaps, axis=0, keepdims=True
            )
            col_terms = jnp.transpose(jnp.broadcast_to(col_terms, (8, WIDE)))[:, 0:1]
            row_terms = row_terms - col_terms
            d_g = (
                row_terms[:STRETCH]
                + row_terms[STRETCH:]
                + jnp.sum(score_gaps + d_query_scaled * grown * query, axis=1, keepdims=True)
            )
            d_end = jnp.sum(ended, axis=0, keepdims=True) + jnp.exp(end) * jnp.sum(
                jnp.sum(states[at] * chained[at], axis=0, keepdims=True), axis=1, keepdims=True
            )
            row, col = iotas(STRETCH, STRETCH)
            across = jnp.transpose(jnp.broadcast_to(d_g, (STRETCH, WIDE)))[:STRETCH]
            d_gamma = jnp.sum(jnp.where(row <= col, across, 0.0), axis=1, keepdims=True) + d_end
            lane = iotas(STRETCH, dim)[1]
            shifted = small + decay[1:2]
            d_soft = -jnp.exp(decay[0:1]) * d_gamma
            d_logit = d_soft * sigmoid(shifted)
            d_rate = jnp.where(lane == 0, d_beta[:STRETCH], d_beta[STRETCH:])
            open_beta = sigmoid(small)
            d_small = jnp.where(
                lane < 2,
                d_rate * open_beta * (1.0 - open_beta),
                jnp.where(lane == 2, d_logit, 0.0),
            )
            d_proj[pl.ds(base, STRETCH), pl.ds(6 * dim, dim)] = low(d_small)
            small_sum = small_sum + jnp.concatenate(
                [
                    jnp.sum(d_soft * softplus(shifted), axis=0, keepdims=True),
                    jnp.sum(d_logit, axis=0, keepdims=True),
                ],
                axis=0,
            )
            d_raw = unit * (d_key - key * jnp.sum(d_key * key, axis=1, keepdims=True))
            d_value = beta * back
            d_act = jnp.concatenate(
                [d_query, d_raw[:STRETCH], d_raw[STRETCH:], d_value[:STRETCH], d_value[STRETCH:]],
                axis=1,
            )
            d_heres.append(d_act * slope)
        for k, (base, d_here) in enumerate(zip(bases, d_heres)):
            rows = window(proj, halo, length, base, all_conv)
            first_row = 8 - (CONV - 1)
            conv_sum = conv_sum + jnp.concatenate(
                [
                    jnp.sum(
                        d_here * rows[first_row + tap : first_row + tap + STRETCH],
                        axis=0,
                        keepdims=True,
                    )
                    for tap in range(CONV)
                ],
                axis=0,
            )
            ahead = jnp.concatenate([d_here, rims[k % seqs]], axis=0)
            rims[k % seqs] = d_here[:8]
            total = None
            for tap in range(CONV):
                start = CONV - 1 - tap
                term = conv[tap : tap + 1] * ahead[start : start + STRETCH]
                total = term if total is None else total + term
            d_proj[pl.ds(base, STRETCH), all_conv] = low(total)
        return conv_sum, small_sum, *rims

    conv_sum, small_sum, *rims = staged(
        turns,
        last,
        (
            jnp.zeros((CONV, 5 * dim), jnp.float32),
            jnp.zeros((2, dim), jnp.float32),
        )
        + (jnp.zeros((8, 5 * dim), jnp.float32),) * seqs,
        marks_of(plan, 1, steps),
    )
    def unproject(step, total):
        at = pl.ds(pl.multiple_of(step * TOGETHER * STRETCH, STRETCH), TOGETHER * STRETCH)
        given = dot(d_proj[at], head[...], ((1,), (1,)))
        d_normed[at] = low(given)
        rows = tokens[at].astype(jnp.float32)
        scale = lax.rsqrt(jnp.mean(rows * rows, axis=1, keepdims=True) + EPS)
        return total + jnp.sum(given * (rows * scale), axis=0, keepdims=True)

    d_norm_gain[...] = staged(
        seqs * blocks // TOGETHER,
        unproject,
        jnp.zeros((1, tokens.shape[1]), jnp.float32),
        marks_of(plan, 2, steps),
    )
    if linked:
        for seq in range(seqs):
            d_first[seq] = rims[seq]
    d_conv[...] = conv_sum
    d_small_sums[...] = small_sum
    if spot is not None:
        for seq in range(seqs):
            for k in range(1, HEADS):
                from_mate(seq, spot.mate_off(k), k).wait_send()


def mixer_backward(
    proj, conv, decay, gain, kept, d_mixer, tokens, head, groups=0, number=None, link=(), jobs=(), plan=None
):
    seqs, length, _ = tokens.shape
    width = proj.shape[1]
    tokens = tokens.reshape(seqs * length, -1)
    dim = gain.shape[1]
    units = seqs * length // STRETCH
    f32, low_ = jnp.float32, jnp.bfloat16
    outs = [
        shape((seqs * length, width), low_),
        shape((CONV, 5 * dim), f32),
        shape((2, dim), f32),
        shape((1, dim), f32),
        shape(tokens.shape, low_),
        shape((1, tokens.shape[1]), f32),
    ]
    if link:
        outs += [shape((seqs, dim, dim), f32), shape((seqs, 8, 5 * dim), f32)]
    scratch = [pltpu.VMEM((units, STRETCH, dim), f32), pltpu.VMEM((units, dim, dim), f32)]
    if number:
        scratch += [pltpu.VMEM((seqs * length, dim), low_)]
        scratch += [dma(seqs, HEADS), dma(seqs, HEADS), dma(seqs)]

    def body(spot, ins, outs, scratch, steps):
        backward_body(bool(link), seqs, spot, ins, outs, scratch, steps, plan or {})

    return fused_call(
        body,
        [(a, IN_VMEM) for a in (proj, conv, decay, gain, *kept, d_mixer, tokens, head, *link)],
        [(a, IN_VMEM) for a in outs], scratch, jobs, groups, number, "mixer_backward", 60,
        mixer_cost(units),
    )


PROLOGUE_PLAN = (1, 0, 3, 1, 2, 3, 2, 0, 2, 0, 2, 0, 3, 0, 2)
EPILOGUE_PLAN = (
    2, 0, 2, 2, 0, 4, 2, 2, 4, 6, 5, 2, 5, 2, 2, 1, 3, 0, 2, 1, 4, 2, 6, 2, 0, 2, 0, 1, 3, 2, 2, 2, 0, 2,
    0, 2, 5, 0, 2, 1, 0, 6, 2, 2, 0, 3, 0, 1,
)
FORWARD_PLAN = {
    (0, 0): ((0, 1), (1, 1)),
    (0, 6): ((1, 1), (0, 1), (2, 1)),
    (1, 3): ((0, 1), (1, 1)),
    (1, 4): ((1, 1),),
    (1, 5): ((0, 1),),
    (1, 6): ((0, 1), (2, 1), (0, 1)),
    (1, 7): ((2, 1),),
    (1, 8): ((2, 1),),
    (2, 0): ((0, 1),),
    (2, 4): ((2, 1),),
}
BACKWARD_PLAN = {
    (0, 0): ((1, 1), (0, 1)),
    (0, 2): ((0, 1),),
    (0, 6): ((0, 1),),
    (0, 8): ((1, 1), (0, 1)),
    (1, 0): ((0, 1),),
    (1, 1): ((0, 1),),
    (1, 2): ((0, 1),),
    (1, 4): ((0, 1),),
    (1, 5): ((1, 1),),
    (1, 6): ((0, 1),),
    (2, 2): ((0, 1),),
    (2, 6): ((0, 1), (0, 1), (1, 1)),
    (2, 7): ((0, 1),),
}
REDUCE_PLAN = (
    1, 2, 0, 2, 2, 2, 1, 2, 2, 0, 1, 2, 1, 1, 2, 1, 1, 1, 1, 0,
)
def matmul(left, right):
    return jnp.dot(left, right, preferred_element_type=jnp.float32)


def times_transposed(left, right):
    return lax.dot_general(
        left, right, (((1,), (1,)), ((), ())), preferred_element_type=jnp.float32
    )


def transposed_times(left, right):
    return lax.dot_general(
        left, right, (((0,), (0,)), ((), ())), preferred_element_type=jnp.float32
    )


def exact(left, right):
    return jnp.einsum("sij,sjk->sik", left, right, precision=lax.Precision.HIGHEST)


def norm_scale(values):
    return lax.rsqrt(jnp.mean(values * values, axis=-1, keepdims=True) + EPS)


def norm_back(values, gain, given):
    scale = norm_scale(values)
    normal = values * scale
    inner = given * gain
    return scale * (inner - normal * jnp.mean(inner * normal, axis=-1, keepdims=True)), (
        given * normal
    )


def per_device(
    block_in,
    lengths,
    norm_gains,
    w_in,
    w_small,
    conv_weight,
    decay_log,
    decay_bias,
    out_norm_gain,
    w_out,
    gate_up_weight,
    w_down,
    out_cotangent,
):
    micro, seq_count, tokens, width = block_in.shape
    seqs = micro * seq_count
    count = lax.axis_size("ctx")
    groups = lax.axis_size("rep")
    place = lax.axis_index("ctx")
    group = lax.axis_index("rep")
    teams = count // HEADS
    head = lax.rem(place, HEADS)
    team = lax.div(place, HEADS)
    mates = peers = None
    if teams > 1:
        mates = [[t * HEADS + h for h in range(HEADS)] for t in range(teams)]
        peers = [[t * HEADS + h for t in range(teams)] for h in range(HEADS)]
    dim = width // HEADS
    length = HEADS * tokens
    rows = seqs * tokens
    kinds = 2 + 2 * STEPS
    rates_of = STEPS + 1
    f32, bf16 = jnp.float32, jnp.bfloat16

    def over_teams(array):
        if teams == 1:
            return array
        return lax.all_gather(array, "ctx", axis=0, tiled=True, axis_index_groups=peers)

    places = place * tokens + lax.broadcasted_iota(jnp.int32, (seqs, tokens), 1)
    valid = (places < lengths.reshape(seqs, 1)).astype(f32).reshape(rows, 1)
    grad_out = (out_cotangent.reshape(rows, width).astype(f32) * valid).astype(bf16)

    own = width // count
    piece = own // groups
    small_block = jnp.concatenate(
        [norm_gains.reshape(-1), conv_weight.reshape(-1)]
    )
    small_block = jnp.pad(small_block, (0, -small_block.size % 128)).reshape(-1, 128)
    (w_head,), (smalls,), (sequences,), (grad_all,) = carry(
        [
            head_job(w_in, w_small, groups),
            spread_job(small_block),
            sequences_job(block_in.reshape(seqs, tokens, width)),
            rep_gather_job(grad_out, groups),
        ],
        PROLOGUE_PLAN,
        groups,
        1,
        "prologue",
    )
    sequences = sequences.reshape(seqs, length, width)
    grad_all = grad_all.reshape(groups * rows, width)
    smalls = over_teams(smalls).reshape(count, -1)
    gains = smalls[:, : 2 * own].reshape(count, 2, own).transpose(1, 0, 2).reshape(2, width)
    gains = gains.astype(f32)
    taps_at = 2 * own
    conv_all = smalls[:, taps_at : taps_at + conv_weight.size].reshape(count, CONV, -1)
    conv_all = conv_all.transpose(1, 0, 2).reshape(CONV, kinds - 1, HEADS, dim)
    conv_head = lax.dynamic_index_in_dim(conv_all, head, 2, keepdims=False)
    conv_head = conv_head.reshape(CONV, -1).astype(f32)
    w_head = over_teams(w_head).reshape(width, -1)
    hidden_own = w_down.shape[0] // groups
    hidden_units = count * hidden_own
    out_piece = lax.dynamic_index_in_dim(
        w_out.reshape(groups, piece, width), group, 0, keepdims=False
    )
    gate_up_part = lax.dynamic_index_in_dim(
        gate_up_weight.reshape(own, 2, count, groups, hidden_own), group, 3, keepdims=False
    ).reshape(own, -1)
    down_part = lax.dynamic_index_in_dim(
        w_down.reshape(groups, hidden_own, width), group, 0, keepdims=False
    )

    mine_only = lax.broadcasted_iota(jnp.int32, (2, HEADS), 1) == head
    decay = jnp.where(mine_only, jnp.stack([decay_log, decay_bias]), 0.0).sum(axis=1, keepdims=True)
    decay = jnp.broadcast_to(decay, (2, dim))
    gain = out_norm_gain.reshape(1, dim)
    head_args = (sequences, gains[:1], w_head, conv_head, decay, gain)
    link = ()
    if teams > 1:
        onward = [(c, c + HEADS) for c in range(count - HEADS)]
        tail = sequences[:, length - 8 :].reshape(seqs * 8, width).astype(f32)
        tail = (tail * norm_scale(tail) * gains[0]).astype(bf16)
        halo = lax.ppermute(matmul(tail, w_head), "ctx", onward)
        start = jnp.zeros((seqs, dim, dim), f32)
        (*_, offset, transfer), _ = mixer_forward(*head_args, link=(halo, start))
        spans = lax.all_gather((transfer, offset), "ctx", axis_index_groups=peers)
        for turn in range(teams - 1):
            start = jnp.where(turn < team, exact(spans[0][turn], start) + spans[1][turn], start)
        link = (halo, start)
    (proj, h_flat, *kept), given = mixer_forward(
        *head_args, groups, 2, link,
        [
            team_gather_job(out_piece, groups, twofold=True),
            team_gather_job(gate_up_part),
            team_gather_job(down_part),
        ],
        FORWARD_PLAN,
    )
    (w_out_full,), (gate_up_part,), (down_part,) = given
    mixer = kept[-1].reshape(rows, width)
    kept = kept[:6]
    w_out_full = over_teams(w_out_full).reshape(width, width)
    gate_up_part = over_teams(gate_up_part).reshape(width, 2 * hidden_units)
    inputs = block_in.reshape(rows, width).astype(f32)
    resid = inputs + matmul(mixer, w_out_full)

    def team_share(grad):
        grad = grad.astype(bf16)
        if teams == 1:
            return grad
        return lax.psum_scatter(
            grad, "ctx", scatter_dimension=0, tiled=True, axis_index_groups=peers
        )

    h_second = (resid * norm_scale(resid) * gains[1]).astype(bf16)
    ((h_all,),) = carry([rep_gather_job(h_second, groups)], (), groups, 3, "gather_copies")
    h_all = h_all.reshape(groups * rows, width)
    down_part = over_teams(down_part).reshape(hidden_units, width)
    gate_up = matmul(h_all, gate_up_part)
    gate, up = gate_up[:, :hidden_units], gate_up[:, hidden_units:]
    open_gate = jax.nn.sigmoid(gate)
    silu = gate * open_gate
    hidden = (silu * up).astype(bf16)
    d_hidden = times_transposed(grad_all, down_part)
    d_gate_up = jnp.concatenate(
        [d_hidden * up * (open_gate * (1.0 + gate * (1.0 - open_gate))), d_hidden * silu], axis=1
    ).astype(bf16)
    d_second = times_transposed(d_gate_up, gate_up_part).astype(bf16)
    grad_down = team_share(transposed_times(hidden, grad_all)).reshape(HEADS, hidden_own, width)
    (d_second,), (grad_down,), (grad_gate_up,) = carry(
        [
            rep_reduce_job(d_second.reshape(groups, rows, width), groups),
            team_reduce_job(grad_down, 1, 2, bf16),
            product_job(h_all, d_gate_up),
        ],
        REDUCE_PLAN,
        groups,
        4,
        "reduce_copies",
    )
    down_parts = matmul(hidden, down_part).astype(bf16).reshape(groups, rows, width)
    d_norm, gain_terms_second = norm_back(resid, gains[1], d_second)
    d_resid = grad_out.astype(f32) + d_norm
    d_branch = d_resid.astype(bf16)
    grad_out_proj = transposed_times(mixer, d_branch)
    d_mixer = times_transposed(d_branch, w_out_full).astype(bf16).reshape(seqs, tokens, width)

    grad_gate_up = team_share(grad_gate_up).reshape(HEADS, own, -1)
    grad_out_proj = team_share(grad_out_proj).reshape(HEADS, groups, piece, width)

    link = ()
    if teams > 1:
        later = jnp.zeros((seqs, dim, dim), f32)
        heads_own = lax.all_to_all(
            d_mixer.reshape(rows, HEADS, dim).transpose(1, 0, 2),
            "ctx", 0, 0, tiled=True, axis_index_groups=mates,
        )
        heads_own = heads_own.reshape(HEADS, seqs, tokens, dim).transpose(1, 0, 2, 3)
        local = mixer_backward(
            proj, conv_head, decay, gain, kept, heads_own.reshape(seqs * length, dim), sequences,
            w_head, link=(halo, later),
        )[0][6]
        locals_ = lax.all_gather(local, "ctx", axis_index_groups=peers)
        for turn in range(teams - 1, 0, -1):
            later = jnp.where(
                turn > team,
                exact(spans[0][turn].transpose(0, 2, 1), later) + locals_[turn],
                later,
            )
        link = (halo, later)
    (d_proj, grad_conv, small_sums, grad_gain, d_first, gain_sum, *rims), given = mixer_backward(
        proj, conv_head, decay, gain, kept, d_mixer, sequences, w_head, groups, 5, link,
        [
            team_reduce_job(grad_gate_up, 2, 3, bf16),
            both_reduce_job(grad_out_proj, groups),
        ],
        BACKWARD_PLAN,
    )
    (grad_gate_up,), (grad_out_proj,) = given
    if teams > 1:
        rim = lax.ppermute(rims[1], "ctx", [(c, c - HEADS) for c in range(HEADS, count)])
        spill = jnp.zeros((seqs, CONV - 1, kinds * dim - dim), f32)
        for ahead in range(1, CONV):
            spill = spill.at[:, CONV - 1 - ahead :].add(
                conv_head[CONV - 1 - ahead] * rim[:, :ahead]
            )
        d_proj = d_proj.reshape(seqs, length, -1)
        end = d_proj[:, length - CONV + 1 :, : (kinds - 1) * dim]
        d_proj = d_proj.at[:, length - CONV + 1 :, : (kinds - 1) * dim].set(
            (end.astype(f32) + spill).astype(bf16)
        )
        d_proj = d_proj.reshape(seqs * length, -1)
        d_first = times_transposed(d_proj, w_head)
        normal = sequences.reshape(seqs * length, width).astype(f32)
        gain_sum = (d_first * (normal * norm_scale(normal))).sum(axis=0)
        d_first = d_first.astype(bf16)

    grad_small = transposed_times(d_proj[:, kinds * dim : kinds * dim + 8], h_flat)
    packed = jnp.concatenate(
        [
            jnp.stack([gain_sum.reshape(width), gain_terms_second.sum(axis=0)]).reshape(-1, dim),
            grad_small[:rates_of].reshape(-1, dim),
            grad_conv.reshape(-1, dim),
            grad_gain,
            small_sums[:, STEPS : STEPS + 1] + jnp.zeros((1, dim), f32),
        ]
    )
    packed = jnp.pad(packed, ((0, -packed.shape[0] % 8), (0, 0)))
    factors = [h_flat, d_proj]
    if teams > 1:
        grad_head = team_share(transposed_times(h_flat, d_proj[:, : kinds * dim]))
        factors = [grad_head.reshape(HEADS, groups, piece, kinds * dim)]
    if teams > 1:
        packed = lax.psum(packed, "ctx", axis_index_groups=peers)
    (grad_in,), (packed,), (d_first,), (grad_gate_up,), (grad_down,), (grad_out_proj,), (down,) = carry(
        [
            deal_job(factors, (HEADS, groups, piece, kinds * dim), groups),
            small_job(packed, groups),
            tokens_job(d_first.reshape(seqs, HEADS, tokens, width), 2),
            rep_gather_job(grad_gate_up, groups, IN_VMEM),
            rep_gather_job(grad_down, groups, IN_VMEM),
            rep_gather_job(grad_out_proj, groups, IN_VMEM),
            rep_reduce_job(down_parts, groups),
        ],
        EPILOGUE_PLAN,
        groups,
        6,
        "epilogue",
    )
    d_inputs, _ = norm_back(inputs, gains[0], d_first.reshape(rows, width))
    in_grad = (d_resid + d_inputs).astype(bf16)
    result = (valid * (resid + down)).astype(bf16)
    grad_in = grad_in.reshape(own, -1)
    grad_gate_up = weave(grad_gate_up, hidden_own)
    grad_down = grad_down.reshape(groups * hidden_own, width)
    grad_out_proj = grad_out_proj.reshape(own, width)

    def take(size):
        nonlocal packed
        part, packed = packed[:, :size], packed[:, size:]
        return part

    grad_gains = take(2 * HEADS).sum(axis=0).reshape(2, width)
    grad_small = take(rates_of * HEADS).reshape(HEADS, rates_of, width)
    grad_small = grad_small.transpose(2, 1, 0).reshape(width, rates_of * HEADS)
    grad_conv = take(CONV * (kinds - 1)).reshape(HEADS, CONV, kinds - 1, dim)
    grad_conv = grad_conv.transpose(1, 2, 0, 3).reshape(CONV, (kinds - 1) * width)
    grad_gain = take(1).sum(axis=0).reshape(dim)
    decays_sum = take(2)[:, :, 0].transpose(1, 0)

    def mine(array, axis, size):
        return lax.dynamic_slice_in_dim(array, place * size, size, axis)

    grad_gains = mine(grad_gains, 1, own)
    grad_small = mine(grad_small, 0, own)
    grad_conv = mine(grad_conv, 1, conv_weight.shape[1])
    return (
        result.reshape(block_in.shape),
        in_grad.reshape(block_in.shape),
        grad_gains,
        grad_in.astype(f32),
        grad_small,
        grad_conv,
        decays_sum[0],
        decays_sum[1],
        grad_gain,
        grad_out_proj.astype(f32),
        grad_gate_up.astype(f32),
        grad_down.astype(f32),
    )


def solution(mesh):
    placed = (
        P(None, "rep", "ctx", None),
        P(None, "rep"),
        P(None, "ctx"),
        P("ctx", None),
        P("ctx", None),
        P(None, "ctx"),
        P(),
        P(),
        P(),
        P("ctx", None),
        P("ctx", None),
        P("ctx", None),
        P(None, "rep", "ctx", None),
    )
    return jax.shard_map(
        per_device,
        mesh=mesh,
        in_specs=placed,
        out_specs=(
            P(None, "rep", "ctx", None),
            P(None, "rep", "ctx", None),
            P(None, "ctx"),
            P("ctx", None),
            P("ctx", None),
            P(None, "ctx"),
            P(),
            P(),
            P(),
            P("ctx", None),
            P("ctx", None),
            P("ctx", None),
        ),
        check_vma=False,
    )
```

```python
import functools
import jax
import jax.numpy as jnp
from jax import lax
from jax.experimental import pallas as pl
from jax.experimental.pallas import tpu as pltpu
from jax.sharding import PartitionSpec as P

STEPS = 2
CONV = 4
STRETCH = 64
HEADS = 8
EPS = 1e-06
WIDE = 2 * STRETCH


MESH = pl.DeviceIdType.MESH
ROWS = 2
COLS = HEADS // ROWS


class Spot:
    def __init__(self, groups):
        place = lax.axis_index("ctx")
        self.mate = lax.rem(place, HEADS)
        self.base = place - self.mate
        self.col = lax.div(self.mate, ROWS)
        self.row = lax.rem(self.mate, ROWS)
        self.groups = groups
        self.group = lax.axis_index("rep")
        self.side = lax.rem(self.group, 2)
        self.pair = lax.div(self.group, 2)
        self.twin = self.group + 1 - 2 * self.side

    def to_mate(self, mate):
        return {"ctx": self.base + mate}

    def to_group(self, group):
        return {"rep": group}

    def mate_off(self, k):
        return lax.rem(self.mate + k, HEADS)

    def group_off(self, k):
        return lax.rem(self.group + 2 * k, self.groups)

    def barrier(self, team=True, copies=True):
        sem = pltpu.get_barrier_semaphore()
        others = []
        if team:
            others += [self.to_mate(self.mate_off(k)) for k in range(1, HEADS)]
        if copies:
            others += [self.to_group(self.twin)]
            others += [self.to_group(self.group_off(k)) for k in range(1, self.groups // 2)]
        for other in others:
            pl.semaphore_signal(sem, inc=1, device_id=other, device_id_type=MESH)
        pl.semaphore_wait(sem, len(others))


def remote(src, dst, send, recv, where):
    return pltpu.make_async_remote_copy(
        src_ref=src,
        dst_ref=dst,
        send_sem=send,
        recv_sem=recv,
        device_id=where,
        device_id_type=MESH,
    )


TEAM_SEMS = 3 * COLS + 1


def team_gather(spot, src, out, send, recv, own):
    mate, col = spot.mate, spot.col
    up, down = spot.to_mate(mate + ROWS), spot.to_mate(mate - ROWS)
    across = spot.to_mate(mate + 1 - 2 * spot.row)
    other = mate + 1 - 2 * spot.row
    local = pltpu.make_async_copy(src, out(mate), own)

    def hop(block, origin, slot, where):
        return remote(block, out(origin), send.at[slot], recv.at[slot], where)

    rise, fall, cross_low, cross_high = 0, COLS - 1, 2 * COLS - 2, 3 * COLS - 3
    last = COLS - 1
    local.start()

    @pl.when(col < last)
    def _():
        hop(src, mate, rise, up).start()

    @pl.when(col > 0)
    def _():
        hop(src, mate, fall, down).start()

    hop(src, mate, cross_low, across).start()
    yield
    for k in range(1, COLS):
        below, above = mate - ROWS * k, mate + ROWS * k

        @pl.when(col >= k)
        def _():
            hop(out(below), below, rise + k - 1, up).wait_recv()
            if k < last:

                @pl.when(col < last)
                def _():
                    hop(out(below), below, rise + k, up).start()

            hop(out(below), below, cross_low + k, across).start()

        @pl.when(col + k <= last)
        def _():
            hop(out(above), above, fall + k - 1, down).wait_recv()
            if k < last:

                @pl.when(col > 0)
                def _():
                    hop(out(above), above, fall + k, down).start()

            hop(out(above), above, cross_high + k, across).start()

        yield
    hop(src, other, cross_low, across).wait_recv()
    for k in range(1, COLS):

        @pl.when(col >= k)
        def _():
            hop(src, other - ROWS * k, cross_low + k, across).wait_recv()

        @pl.when(col + k <= last)
        def _():
            hop(src, other + ROWS * k, cross_high + k, across).wait_recv()

    @pl.when(col < last)
    def _():
        hop(src, mate, rise, up).wait_send()

    @pl.when(col > 0)
    def _():
        hop(src, mate, fall, down).wait_send()

    hop(src, mate, cross_low, across).wait_send()
    for k in range(1, COLS):

        @pl.when(col >= k)
        def _():
            if k < last:

                @pl.when(col < last)
                def _():
                    hop(src, mate, rise + k, up).wait_send()

            hop(src, mate, cross_low + k, across).wait_send()

        @pl.when(col + k <= last)
        def _():
            if k < last:

                @pl.when(col > 0)
                def _():
                    hop(src, mate, fall + k, down).wait_send()

            hop(src, mate, cross_high + k, across).wait_send()

    local.wait()
    yield


def rep_gather(spot, src, out, send, recv, own):
    group, twin, half = spot.group, spot.twin, spot.groups // 2
    local = None
    if own is not None:
        local = pltpu.make_async_copy(src, out(group), own)
        local.start()

    def hop(block, origin, slot, where):
        return remote(block, out(origin), send.at[slot], recv.at[slot], spot.to_group(where))

    hop(src, group, 0, twin).start()
    for k in range(1, half):
        hop(src, group, k, spot.group_off(k)).start()
    yield
    for k in range(1, half):
        origin = spot.group_off(half - k)
        hop(out(origin), origin, k, twin).wait_recv()
        hop(out(origin), origin, half + k, twin).start()
    yield
    hop(src, twin, 0, twin).wait_recv()
    for k in range(1, half):
        origin = lax.rem(twin + 2 * (half - k), spot.groups)
        hop(src, origin, half + k, twin).wait_recv()
    hop(src, group, 0, twin).wait_send()
    for k in range(1, half):
        hop(src, group, k, twin).wait_send()
        hop(src, group, half + k, twin).wait_send()
    if local is not None:
        local.wait()
    yield


def team_exchange(spot, src, dst, send, recv, own):
    local = pltpu.make_async_copy(src(spot.mate), dst(spot.mate), own)
    local.start()

    def hop(k):
        to = spot.mate_off(k)
        return remote(src(to), dst(spot.mate), send.at[k], recv.at[k], spot.to_mate(to))

    for k in range(1, HEADS):
        hop(k).start()
    yield
    for k in range(1, HEADS):
        hop(k).wait_recv()
    for k in range(1, HEADS):
        hop(k).wait_send()
    local.wait()
    yield


def dma(*shape):
    return pltpu.SemaphoreType.DMA(shape)


ANY = pl.BlockSpec(memory_space=pl.ANY)
IN_VMEM = pl.BlockSpec(memory_space=pltpu.VMEM)


def finish(*steps):
    for step in steps:
        for _ in step:
            pass


def rep_reduce(spot, part, sums, others, send, recv):
    half, side = spot.groups // 2, spot.side

    def to_twin(k):
        return remote(
            part(2 * k + 1 - side), sums.at[k], send.at[k], recv.at[k], spot.to_group(spot.twin)
        )

    def onward(k):
        slot = half + k
        return remote(
            sums.at[lax.rem(spot.pair + k, half)], others.at[k], send.at[slot], recv.at[slot], spot.to_group(spot.group_off(k))
        )

    for k in range(half):
        to_twin(k).start()
    yield
    for k in range(half):
        to_twin(k).wait_recv()

    def both(pair):
        return part(2 * pair + side)[...].astype(jnp.float32) + sums[pair].astype(jnp.float32)

    for k in range(1, half):
        pair = lax.rem(spot.pair + k, half)
        sums[pair] = both(pair).astype(sums.dtype)
        onward(k).start()
    yield
    total = both(spot.pair)
    for k in range(1, half):
        onward(k).wait_recv()
        total = total + others[k].astype(jnp.float32)
    for k in range(half):
        to_twin(k).wait_send()
    for k in range(1, half):
        onward(k).wait_send()
    yield total


class Lane:
    def __init__(self, part, sums, passing, total, send, recv):
        self.part, self.sums, self.passing = part, sums, passing
        self.total, self.send, self.recv = total, send, recv


def team_reduce(spot, lanes, window):
    mate, col, row = spot.mate, spot.col, spot.row
    up, down = spot.to_mate(mate + ROWS), spot.to_mate(mate - ROWS)
    across = spot.to_mate(mate + 1 - 2 * row)
    last = COLS - 1
    f32 = jnp.float32

    def hop(lane, d, way):
        src = lane.part(ROWS * d + 1 - row) if way == 0 else lane.sums.at[d]
        dst = (lane.sums.at[d], lane.passing.at[d + 1], lane.passing.at[d])[way]
        return remote(
            src, dst, lane.send.at[way, d], lane.recv.at[way, d], (across, up, down)[way]
        )

    def both(lane, d):
        return lane.part(ROWS * d + row)[...].astype(f32) + lane.sums[d].astype(f32)

    def crossed(lane, d):
        hop(lane, d, 0).wait_recv()

        @pl.when(col == d)
        def _():
            lane.total[...] = both(lane, d)

        for end, way in ((0, 1), (last, 2)):
            if d != end:

                @pl.when(col == end)
                def _():
                    lane.sums[d] = both(lane, d).astype(lane.sums.dtype)
                    hop(lane, d, way).start()

    def passed(lane, d, c, way):
        @pl.when(col == c)
        def _():
            hop(lane, d, way).wait_recv()
            got = lane.passing[d + 2 - way].astype(f32)
            if c == d:
                lane.total[...] += got
            else:
                lane.sums[d] = (both(lane, d) + got).astype(lane.sums.dtype)
                hop(lane, d, way).start()

    order_out = [d for pair in zip(range(last, -1, -1), range(COLS)) for d in pair][:COLS]
    rounds = {}
    for i, d in enumerate(order_out):
        for k, lane in enumerate(lanes):
            time = i * len(lanes) + k
            rounds.setdefault(time, []).append(functools.partial(crossed, lane, d))
            for c in range(1, d + 1):
                step = functools.partial(passed, lane, d, c, 1)
                rounds.setdefault(time + c, []).append(step)
            for c in range(d, last):
                step = functools.partial(passed, lane, d, c, 2)
                rounds.setdefault(time + last - c, []).append(step)
    ahead = [(lane, d) for d in order_out for lane in lanes]
    for lane, d in ahead[:window]:
        hop(lane, d, 0).start()
    yield
    for time in sorted(rounds):
        for k, step in enumerate(rounds[time]):
            step()
            if k == 0 and time + window < len(ahead):
                lane, d = ahead[time + window]
                hop(lane, d, 0).start()
        yield
    for d in range(COLS):
        for lane in lanes:
            hop(lane, d, 0).wait_send()

            @pl.when(col < d)
            def _():
                hop(lane, d, 1).wait_send()

            @pl.when(col > d)
            def _():
                hop(lane, d, 2).wait_send()

    yield


def advance(step, count):
    for _ in range(count):
        next(step, None)


def lane_scratch(count, rows, width):
    return [
        pltpu.VMEM((count, COLS, rows, width), jnp.bfloat16),
        pltpu.VMEM((count, COLS + 1, rows, width), jnp.bfloat16),
        dma(count, 3, COLS),
        dma(count, 3, COLS),
    ]


class Job:
    def __init__(self, make, ins=(), outs=(), scratch=(), spaces=None):
        self.make, self.ins, self.outs, self.scratch = make, list(ins), list(outs), list(scratch)
        self.in_space, self.out_space = spaces or (ANY, ANY)


def fused_call(body, ins, outs, scratch, jobs, groups, number, name, vmem, cost=None, copies=True):
    def kernel(*refs):
        refs = list(refs)

        def take(count):
            part = refs[:count]
            del refs[:count]
            return part

        own_in = take(len(ins))
        jobs_in = [take(len(job.ins)) for job in jobs]
        own_out = take(len(outs))
        jobs_out = [take(len(job.outs)) for job in jobs]
        own_scratch = take(len(scratch))
        jobs_scratch = [take(len(job.scratch)) for job in jobs]
        spot = None
        if number:
            spot = Spot(groups)
            spot.barrier(copies=copies)
        steps = [
            job.make(spot, a, b, c)
            for job, a, b, c in zip(jobs, jobs_in, jobs_out, jobs_scratch)
        ]
        body(spot, own_in, own_out, own_scratch, steps)
        finish(*steps)

    results = pl.pallas_call(
        kernel,
        out_shape=[s for s, _ in outs] + [s for job in jobs for s in job.outs],
        in_specs=[spec for _, spec in ins] + [job.in_space for job in jobs for _ in job.ins],
        out_specs=[spec for _, spec in outs] + [job.out_space for job in jobs for _ in job.outs],
        scratch_shapes=list(scratch) + [s for job in jobs for s in job.scratch],
        compiler_params=pltpu.CompilerParams(
            collective_id=number, has_side_effects=bool(number), vmem_limit_bytes=vmem * 2**20
        ),
        cost_estimate=cost,
        name=name,
    )(*[a for a, _ in ins], *[a for job in jobs for a in job.ins])
    results = list(results)
    own, rest = results[: len(outs)], results[len(outs) :]
    given = []
    for job in jobs:
        given.append(rest[: len(job.outs)])
        rest = rest[len(job.outs) :]
    return own, given


def staged(turns, body, carried, marks):
    reached = 0
    for at in sorted(marks):
        if at > reached:
            carried = lax.fori_loop(reached, at, body, carried)
            reached = at
        marks[at]()
    if reached < turns:
        carried = lax.fori_loop(reached, turns, body, carried)
    return carried


def marks_of(plan, phase, steps):
    def mark(moves):
        def go():
            for job, count in moves:
                advance(steps[job], count)

        return go

    return {turn: mark(moves) for (at, turn), moves in plan.items() if at == phase}


def shape(dims, kind):
    return jax.ShapeDtypeStruct(tuple(dims), kind)


def team_gather_job(block, groups=None, twofold=False):
    low_ = block.dtype
    if not twofold:

        def make(spot, ins, outs, scratch):
            return team_gather(spot, ins[0], lambda m: outs[0].at[m], *scratch[:2], scratch[2].at[0])

        return Job(
            make, [block], [shape((HEADS,) + block.shape, low_)],
            [dma(TEAM_SEMS), dma(TEAM_SEMS), dma(1)],
        )

    def make(spot, ins, outs, scratch):
        whole = outs[0]
        yield from team_gather(
            spot, ins[0], lambda m: whole.at[m, spot.group], *scratch[:2], scratch[4].at[0]
        )
        yield from rep_gather(
            spot, whole.at[:, spot.group], lambda g: whole.at[:, g], *scratch[2:4], None
        )

    return Job(
        make, [block], [shape((HEADS, groups) + block.shape, low_)],
        [dma(TEAM_SEMS), dma(TEAM_SEMS), dma(groups), dma(groups), dma(1)],
    )


def sequences_job(block):
    seqs = block.shape[0]

    def make(spot, ins, outs, scratch):
        gathers = [
            team_gather(
                spot, ins[0].at[seq], lambda m, seq=seq: outs[0].at[seq, m],
                scratch[0].at[seq], scratch[1].at[seq], scratch[2].at[seq],
            )
            for seq in range(seqs)
        ]
        for _ in zip(*gathers):
            yield

    return Job(
        make, [block], [shape((seqs, HEADS) + block.shape[1:], block.dtype)],
        [dma(seqs, TEAM_SEMS), dma(seqs, TEAM_SEMS), dma(seqs)],
    )


def rep_gather_job(block, groups, space=ANY):
    def make(spot, ins, outs, scratch):
        return rep_gather(spot, ins[0], lambda g: outs[0].at[g], *scratch[:2], scratch[2].at[0])

    return Job(
        make, [block], [shape((groups,) + block.shape, block.dtype)],
        [dma(groups), dma(groups), dma(1)], (space, space),
    )


def rep_reduce_job(parts, groups):
    block = pltpu.VMEM((groups // 2,) + parts.shape[1:], parts.dtype)

    def make(spot, ins, outs, scratch):
        for total in rep_reduce(spot, lambda g: ins[0].at[g], *scratch):
            if total is not None:
                outs[0][...] = total
            yield

    return Job(
        make, [parts], [shape(parts.shape[1:], jnp.float32)],
        [block, block, dma(groups), dma(groups)], (IN_VMEM, IN_VMEM),
    )


def tokens_job(parts, halves):
    seqs, _, rows, width = parts.shape
    rows_of = rows // halves

    def make(spot, ins, outs, scratch):
        sums, passing, send, recv = scratch
        lanes = []
        for seq in range(seqs):
            for half in range(halves):
                k, own = seq * halves + half, pl.ds(half * rows_of, rows_of)
                lanes.append(
                    Lane(
                        lambda mate, seq=seq, own=own: ins[0].at[seq, mate, own],
                        sums.at[k], passing.at[k], outs[0].at[seq, own], send.at[k], recv.at[k],
                    )
                )
        return team_reduce(spot, lanes, 2 * halves)

    return Job(
        make, [parts], [shape((seqs, rows, width), jnp.float32)],
        lane_scratch(seqs * halves, rows_of, width), (IN_VMEM, IN_VMEM),
    )


def team_reduce_job(parts, pieces, window, kind):
    _, rows, width = parts.shape
    rows_of = rows // pieces

    def make(spot, ins, outs, scratch):
        sums, passing, send, recv, *total = scratch
        total = total[0] if total else outs[0]
        lanes = []
        for k in range(pieces):
            own = pl.ds(k * rows_of, rows_of)
            lanes.append(
                Lane(
                    lambda mate, own=own: ins[0].at[mate, own],
                    sums.at[k], passing.at[k], total.at[own], send.at[k], recv.at[k],
                )
            )
        yield from team_reduce(spot, lanes, window)
        if kind != jnp.float32:
            outs[0][...] = total[...].astype(kind)
        yield

    scratch = lane_scratch(pieces, rows_of, width)
    if kind != jnp.float32:
        scratch.append(pltpu.VMEM((rows, width), jnp.float32))
    return Job(make, [parts], [shape((rows, width), kind)], scratch, (IN_VMEM, IN_VMEM))


def both_reduce_job(parts, groups):
    heads, _, rows, width = parts.shape
    low_ = parts.dtype
    block = pltpu.VMEM((groups // 2, heads, rows, width), low_)
    team = pltpu.VMEM((heads, rows, width), low_)

    def make(spot, ins, outs, scratch):
        sums, others, quarter, arrived, r_send, r_recv, e_send, e_recv, own = scratch
        for total in rep_reduce(
            spot, lambda g: ins[0].at[:, g], sums, others, r_send, r_recv
        ):
            if total is None:
                yield
        quarter[...] = total.astype(low_)
        exchange = team_exchange(
            spot, lambda m: quarter.at[m], lambda m: arrived.at[m], e_send, e_recv, own.at[0]
        )
        next(exchange)
        yield
        finish(exchange)
        outs[0][...] = sum(arrived[m].astype(jnp.float32) for m in range(heads)).astype(low_)
        yield

    return Job(
        make, [parts], [shape((rows, width), low_)],
        [block, block, team, team]
        + [dma(groups), dma(groups), dma(HEADS), dma(HEADS), dma(1)],
        (IN_VMEM, IN_VMEM),
    )


def tile_product(left, right, tile, width):
    return low(dot(left[:, tile * 128 : (tile + 1) * 128], right[:, :width], ((0,), (0,))))


def product_job(left, right):
    rows, width = left.shape[1], right.shape[1]

    def make(spot, ins, outs, scratch):
        for tile in range(rows // 128):
            outs[0][tile * 128 : (tile + 1) * 128] = tile_product(ins[0], ins[1], tile, width)
            yield

    return Job(
        make, [left, right], [shape((rows, width), jnp.bfloat16)], (), (IN_VMEM, IN_VMEM)
    )


def deal_job(ins, dims, groups):
    heads, _, piece, cols = dims
    low_ = jnp.bfloat16
    kinds = 2 + 2 * STEPS
    dim = cols // kinds
    block = pltpu.VMEM((groups // 2, heads, piece, cols), low_)
    made = len(ins) == 2

    def make(spot, ins, outs, scratch):
        sums, others, quarter, dealt, r_send, r_recv, e_send, e_recv, g_send, g_recv, own = scratch[:11]
        parts = ins[0]
        if made:
            parts = scratch[11]
            for mate in range(heads):
                tile = tile_product(ins[0], ins[1], mate, cols)
                for g in range(groups):
                    parts[mate, g] = tile[g * piece : (g + 1) * piece]
                if mate % 2:
                    yield
        for total in rep_reduce(
            spot, lambda g: parts.at[:, g], sums, others, r_send, r_recv
        ):
            if total is None:
                yield
        quarter[...] = total.astype(low_)
        exchange = team_exchange(
            spot, lambda m: quarter.at[m], lambda m: dealt.at[spot.group, m],
            e_send, e_recv, own.at[0],
        )
        next(exchange)
        yield
        finish(exchange)
        yield from rep_gather(
            spot, dealt.at[spot.group], lambda g: dealt.at[g], g_send, g_recv, None
        )
        for g in range(groups):
            for h in range(heads):
                rows = dealt[g, h]
                for k in range(kinds):
                    at = (k * heads + h) * dim
                    outs[0][g, :, at : at + dim] = rows[:, k * dim : (k + 1) * dim]
        yield

    return Job(
        make, ins, [shape((groups, piece, heads * cols), low_)],
        [block, block, pltpu.VMEM((heads, piece, cols), low_)]
        + [pltpu.VMEM((groups, heads, piece, cols), low_)]
        + [dma(groups), dma(groups), dma(HEADS), dma(HEADS), dma(groups), dma(groups), dma(1)]
        + ([pltpu.VMEM(dims, low_)] if made else []),
        (IN_VMEM, IN_VMEM),
    )


def small_job(smalls, groups):
    def make(spot, ins, outs, scratch):
        copies, total, s_send, s_recv, x_send, x_recv, own = scratch
        yield from rep_gather(spot, ins[0], lambda g: copies.at[g], s_send, s_recv, own.at[0])
        total[...] = sum(copies[g] for g in range(groups))
        yield from team_exchange(
            spot, lambda m: total, lambda m: outs[0].at[m], x_send, x_recv, own.at[1]
        )

    return Job(
        make, [smalls], [shape((HEADS,) + smalls.shape, jnp.float32)],
        [pltpu.VMEM((groups,) + smalls.shape, jnp.float32), pltpu.VMEM(smalls.shape, jnp.float32)]
        + [dma(groups), dma(groups), dma(HEADS), dma(HEADS), dma(2)],
        (IN_VMEM, IN_VMEM),
    )


def head_job(w_in, w_small, groups):
    own, width = w_in.shape
    kinds, piece = 2 + 2 * STEPS, own // groups
    dim = width // (kinds * HEADS)
    rates_of = w_small.shape[1] // HEADS
    dims = (HEADS, groups, piece, (kinds + 1) * dim)

    def make(spot, ins, outs, scratch):
        pieces, e_send, e_recv, w_send, w_recv, local = scratch
        row, col = iotas(w_small.shape[1], dim)
        for h in range(HEADS):
            chosen = low(jnp.where((row == col * HEADS + h) & (col < rates_of), 1.0, 0.0))
            blocks = [ins[0][:, (k * HEADS + h) * dim : (k * HEADS + h + 1) * dim] for k in range(kinds)]
            blocks.append(low(dot(ins[1][...], chosen, ((1,), (0,)))))
            for k, block in enumerate(blocks):
                block = block.astype(jnp.float32)
                for g in range(groups):
                    pieces[h, g, :, k * dim : (k + 1) * dim] = low(
                        block[g * piece : (g + 1) * piece]
                    )
        yield from team_exchange(
            spot, lambda m: pieces.at[m, spot.group], lambda m: outs[0].at[m, spot.group],
            e_send, e_recv, local.at[0],
        )
        yield from rep_gather(
            spot, outs[0].at[:, spot.group], lambda g: outs[0].at[:, g], w_send, w_recv, None
        )

    return Job(
        make, [w_in, w_small], [shape(dims, w_in.dtype)],
        [pltpu.VMEM(dims, w_in.dtype)]
        + [dma(HEADS), dma(HEADS), dma(groups), dma(groups), dma(1)],
        (IN_VMEM, ANY),
    )


def spread_job(block):
    def make(spot, ins, outs, scratch):
        return team_exchange(
            spot, lambda m: ins[0], lambda m: outs[0].at[m], *scratch[:2], scratch[2].at[0]
        )

    return Job(
        make, [block], [shape((HEADS,) + block.shape, block.dtype)], [dma(HEADS), dma(HEADS), dma(1)]
    )


def weave(parts, piece):
    groups, rows, width = parts.shape

    def kernel(parts_ref, out):
        for k in range(width // piece):
            blocks = [
                parts_ref[g, :, k * piece : (k + 1) * piece].astype(jnp.float32)
                for g in range(groups)
            ]
            at = k * groups * piece
            out[:, at : at + groups * piece] = jnp.concatenate(blocks, axis=1)

    return pl.pallas_call(
        kernel,
        out_shape=shape((rows, groups * width), jnp.float32),
        in_specs=[IN_VMEM],
        out_specs=IN_VMEM,
        name="weave",
    )(parts)


def carry(jobs, plan, groups, number, name, vmem=40):
    def body(spot, ins, outs, scratch, steps):
        for job in plan:
            advance(steps[job], 1)

    return fused_call(body, [], [], [], jobs, groups, number, name, vmem)[1]


def low(a):
    return a.astype(jnp.bfloat16)


def halves(a):
    high = low(a)
    return high, low(a - high.astype(jnp.float32))


def dot(a, b, dims):
    return lax.dot_general(a, b, (dims, ((), ())), preferred_element_type=jnp.float32)


def fold(out):
    half = out.shape[1] // 2
    return out[:, :half] + out[:, half:]


def left_nn(parts):
    return jnp.concatenate(parts, axis=1)


def right_nn(parts):
    row = jnp.concatenate(parts, axis=1)
    return jnp.concatenate([row, row], axis=0)


def right_nt(parts):
    high, rest = parts
    return jnp.concatenate(
        [jnp.concatenate([high, high], axis=1), jnp.concatenate([rest, rest], axis=1)], axis=0
    )


def mul(a, b):
    return fold(dot(left_nn(halves(a)), right_nn(halves(b)), ((1,), (0,))))


def mul_nt(a, b):
    return fold(dot(left_nn(halves(a)), right_nt(halves(b)), ((1,), (1,))))


def mul_tn(a, b):
    left = jnp.concatenate(halves(a), axis=0)
    return fold(dot(left, right_nn(halves(b)), ((0,), (0,))))


def iotas(rows, cols):
    return (
        lax.broadcasted_iota(jnp.int32, (rows, cols), 0),
        lax.broadcasted_iota(jnp.int32, (rows, cols), 1),
    )


def order(index):
    return STEPS * lax.rem(index, STRETCH) + lax.div(index, STRETCH)


def sigmoid(a):
    return 1.0 / (1.0 + jnp.exp(-a))


def softplus(a):
    return jnp.maximum(a, 0.0) + jnp.log1p(jnp.exp(-jnp.abs(a)))


def window(ref, halo, length, base, columns):
    before = ref[pl.ds(pl.multiple_of(jnp.maximum(base - 8, 0), 8), 8), columns]
    ahead = 0.0
    if halo is not None:
        ahead = halo[pl.ds(pl.multiple_of(lax.div(base, length) * 8, 8), 8), columns]
    first = lax.rem(base, length) == 0
    return jnp.concatenate(
        [jnp.where(first, ahead, before), ref[pl.ds(base, STRETCH), columns]], axis=0
    )


def stack(act, at, dim):
    return jnp.concatenate(
        [act[:, at * dim : (at + 1) * dim], act[:, (at + 1) * dim : (at + 2) * dim]], axis=0
    )


def convolve(rows, conv):
    total = None
    for tap in range(CONV):
        start = 8 - (CONV - 1) + tap
        term = conv[tap : tap + 1] * rows[start : start + STRETCH]
        total = term if total is None else total + term
    return total


def rates(small, decay):
    beta = jnp.concatenate([sigmoid(small[:, 0:1]), sigmoid(small[:, 1:2])], axis=0)
    gamma = -jnp.exp(decay[0:1]) * softplus(small + decay[1:2])
    row, col = iotas(STRETCH, STRETCH)
    tri = low(jnp.where(row >= col, 1.0, 0.0))
    high = low(gamma)
    rest = gamma - high.astype(jnp.float32)
    middle = low(rest)
    last = low(rest - middle.astype(jnp.float32))
    running = (
        dot(tri, high, ((1,), (0,))) + dot(tri, middle, ((1,), (0,))) + dot(tri, last, ((1,), (0,)))
    )
    return beta, running


def decays(running):
    column = running[:, 2:3]
    across = jnp.transpose(running)[2:3, :]
    row, col = iotas(STRETCH, STRETCH)
    gap = jnp.broadcast_to(column, (STRETCH, STRETCH)) - across
    upto = jnp.where(row >= col, jnp.exp(jnp.where(row >= col, gap, 0.0)), 0.0)
    before = jnp.where(row > col, upto, 0.0)
    strict = jnp.concatenate(
        [
            jnp.concatenate([before, before], axis=1),
            jnp.concatenate([upto, before], axis=1),
        ],
        axis=0,
    )
    return strict, jnp.concatenate([upto, upto], axis=1)


def level_masks():
    row, col = iotas(WIDE, WIDE)
    row, col = order(row), order(col)
    masks, size = [], 1
    while size < WIDE:
        inside = (lax.div(row, 2 * size) == lax.div(col, 2 * size)) & (
            lax.div(row, size) != lax.div(col, size)
        )
        masks.append(jnp.where(inside, 1.0, 0.0))
        size *= 2
    return [masks[0]] + [low(mask) for mask in masks[1:]]


def inverses(systems, masks):
    row, col = iotas(WIDE, WIDE)
    eye = jnp.where(row == col, 1.0, 0.0)
    solved = [eye - masks[0] * system for system in systems]
    split = [halves(system) for system in systems]
    for mask in masks[1:]:
        parts = [halves(a) for a in solved]
        steps = [
            fold(
                dot(
                    jnp.concatenate([high * mask, rest * mask], axis=1),
                    right_nn(part),
                    ((1,), (0,)),
                )
            )
            for (high, rest), part in zip(split, parts)
        ]
        solved = [
            a - fold(dot(left_nn(part), right_nn(halves(step)), ((1,), (0,))))
            for a, part, step in zip(solved, parts, steps)
        ]
    return solved


def unit_rows(stacked):
    return lax.rsqrt(jnp.sum(stacked * stacked, axis=1, keepdims=True) + EPS)


def twice(column):
    return jnp.concatenate([column, column], axis=0)


TOGETHER = 4


def forward_body(linked, seqs, spot, ins, outs, scratch, steps, plan):
    tokens, norm_gain, head, conv, decay, gain, *link = ins
    proj, normed, out, fresh, inv, weights, trans, states, *more = outs
    local, offset, mixer, *sems = scratch
    halo = None
    if linked:
        halo, start = link
        final, product, *more = more
    length = proj.shape[0] // seqs
    dim = gain.shape[1]
    blocks = length // STRETCH
    each = TOGETHER // seqs
    turns = blocks // each
    masks = level_masks()
    row, col = iotas(dim, dim)
    diagonal = row == col

    def project(step, _):
        at = pl.ds(pl.multiple_of(step * TOGETHER * STRETCH, STRETCH), TOGETHER * STRETCH)
        rows = tokens[at].astype(jnp.float32)
        scale = lax.rsqrt(jnp.mean(rows * rows, axis=1, keepdims=True) + EPS)
        rows = low(rows * scale * norm_gain[...])
        normed[at] = rows
        proj[at] = dot(rows, head[...], ((1,), (0,)))
        return 0

    staged(seqs * blocks // TOGETHER, project, 0, marks_of(plan, 0, steps))

    def spots(step):
        return [seq * blocks + step * each + k for k in range(each) for seq in range(seqs)]

    def first(step, _):
        units = spots(step)
        kept = []
        for block in units:
            base = pl.multiple_of(block * STRETCH, STRETCH)
            rows = window(proj, halo, length, base, pl.ds(0, 5 * dim))
            pre = convolve(rows, conv)
            act = pre * sigmoid(pre)
            raw = stack(act, 1, dim)
            key = raw * unit_rows(raw)
            beta, running = rates(proj[pl.ds(base, STRETCH), pl.ds(6 * dim, dim)], decay)
            kept.append((act[:, :dim], key, stack(act, 3, dim), beta, running))
        systems = []
        for block, (query, key, value, beta, running) in zip(units, kept):
            at = block
            strict, upto = decays(running)
            key_halves = halves(key)
            both = fold(
                dot(
                    jnp.concatenate([left_nn(key_halves), left_nn(halves(query))], axis=0),
                    right_nt(key_halves),
                    ((1,), (1,)),
                )
            )
            systems.append(beta * both[:WIDE] * strict)
            local[at] = both[WIDE:] * upto
            offset[at] = query * jnp.exp(running[:, 2:3])
        for block, (query, key, value, beta, running), solved in zip(
            units, kept, inverses(systems, masks)
        ):
            at = block
            inv[at] = solved
            grown = twice(jnp.exp(running[:, 2:3]))
            end = running[STRETCH - 1 :, 2:3]
            solved_left = left_nn(halves(solved))
            weight = fold(dot(solved_left, right_nn(halves(beta * key * grown)), ((1,), (0,))))
            value = fold(dot(solved_left, right_nn(halves(beta * value)), ((1,), (0,))))
            weights[at] = weight
            fresh[at] = value
            to_end = jnp.concatenate(halves(key * twice(jnp.exp(end - running[:, 2:3]))), axis=0)
            trans[at] = jnp.where(diagonal, jnp.exp(end), 0.0) - fold(
                dot(to_end, right_nn(halves(weight)), ((0,), (0,)))
            )
            states[at] = fold(dot(to_end, right_nn(halves(value)), ((0,), (0,))))
        return 0

    staged(turns, first, 0, marks_of(plan, 1, steps))

    def chain(step, carried):
        new = []
        for seq, state in enumerate(carried):
            block = seq * blocks + step
            added = states[block]
            states[block] = state
            if linked:
                product[seq] = mul(trans[block], product[seq])
            new.append(mul(trans[block], state) + added)
        return tuple(new)

    begin = (jnp.zeros((dim, dim), jnp.float32),) * seqs
    if linked:
        for seq in range(seqs):
            product[seq] = jnp.where(diagonal, 1.0, 0.0)
        begin = tuple(start[seq] for seq in range(seqs))
    ended = lax.fori_loop(0, blocks, chain, begin)
    if linked:
        for seq in range(seqs):
            final[seq] = ended[seq]
    if spot is not None:
        (mixed,), (x_send, x_recv, own) = more, sems
        span = length // HEADS

        def block_of(seq, mate):
            return mixer.at[pl.ds(pl.multiple_of(seq * length + mate * span, span), span)]

        def columns_of(seq, mate):
            return mixed.at[seq, :, pl.ds(pl.multiple_of(mate * dim, dim), dim)]

        def to_mate(seq, mate, slot):
            return remote(
                block_of(seq, mate), columns_of(seq, spot.mate), x_send.at[seq, slot],
                x_recv.at[seq, slot], spot.to_mate(mate),
            )

        def to_self(seq):
            return pltpu.make_async_copy(
                block_of(seq, spot.mate), columns_of(seq, spot.mate), own.at[seq]
            )

    def last(step, _):
        units = spots(step)
        reads = [
            mul(
                jnp.concatenate([weights[block], offset[block]], axis=0),
                states[block],
            )
            for block in units
        ]
        for block, read in zip(units, reads):
            at = block
            base = pl.multiple_of(block * STRETCH, STRETCH)
            new = fresh[at] - read[:WIDE]
            fresh[at] = new
            result = read[WIDE:] + mul(local[at], new)
            out[pl.ds(base, STRETCH)] = result
            gate = proj[pl.ds(base, STRETCH), pl.ds(5 * dim, dim)]
            scale = lax.rsqrt(jnp.mean(result * result, axis=1, keepdims=True) + EPS)
            mixer[pl.ds(base, STRETCH)] = low(
                result * scale * gain[...] * (gate * sigmoid(gate))
            )
        if spot is not None:
            mates = each * STRETCH // span
            for k in range(mates):
                to = step * mates + k
                slot = lax.rem(to - spot.mate + HEADS, HEADS)

                @pl.when(slot == 0)
                def _():
                    for seq in range(seqs):
                        to_self(seq).start()

                @pl.when(slot != 0)
                def _():
                    for seq in range(seqs):
                        to_mate(seq, to, slot).start()

        return 0

    staged(turns, last, 0, marks_of(plan, 2, steps))
    if spot is not None:
        for seq in range(seqs):
            for k in range(1, HEADS):
                to_mate(seq, spot.mate_off(k), k).wait_recv()
            for k in range(1, HEADS):
                to_mate(seq, spot.mate_off(k), k).wait_send()
            to_self(seq).wait()


def mixer_cost(units):
    return pl.CostEstimate(
        flops=units * 60 * WIDE * WIDE * WIDE,
        bytes_accessed=units * WIDE * WIDE * 30,
        transcendentals=units * WIDE * WIDE * 8,
    )


def mixer_forward(
    tokens, norm_gain, head, conv, decay, gain, groups=0, number=None, link=(), jobs=(), plan=None
):
    seqs, length, width = tokens.shape
    tokens = tokens.reshape(seqs * length, width)
    dim = gain.shape[1]
    units = seqs * length // STRETCH
    f32, low_ = jnp.float32, jnp.bfloat16
    outs = [
        (shape((seqs * length, head.shape[1]), f32), IN_VMEM),
        (shape((seqs * length, width), low_), IN_VMEM),
        (shape((seqs * length, dim), f32), IN_VMEM),
    ]
    outs += [(shape((units, WIDE, dim), f32), IN_VMEM)] * 5
    if link:
        outs += [(shape((seqs, dim, dim), f32), IN_VMEM)] * 2
    scratch = [
        pltpu.VMEM((units, STRETCH, WIDE), f32),
        pltpu.VMEM((units, STRETCH, dim), f32),
        pltpu.VMEM((seqs * length, dim), low_),
    ]
    if number:
        outs += [(shape((seqs, length // HEADS, HEADS * dim), low_), ANY)]
        scratch += [dma(seqs, HEADS), dma(seqs, HEADS), dma(seqs)]

    def body(spot, ins, outs, scratch, steps):
        forward_body(bool(link), seqs, spot, ins, outs, scratch, steps, plan or {})

    return fused_call(
        body, [(a, IN_VMEM) for a in (tokens, norm_gain, head, conv, decay, gain, *link)], outs, scratch, jobs,
        groups, number, "mixer_forward", 56, mixer_cost(units),
    )


def backward_body(linked, seqs, spot, ins, outs, scratch, steps, plan):
    proj, conv, decay, gain, out, fresh, inv, weights, trans, states, d_mixer, tokens, head, *link = ins
    d_proj, d_conv, d_small_sums, d_gain, d_normed, d_norm_gain, *more = outs
    d_out, chained, *arrived = scratch
    halo = None
    if linked:
        halo, end_state = link
        d_start, d_first = more
    length = proj.shape[0] // seqs
    dim = gain.shape[1]
    blocks = length // STRETCH
    each = TOGETHER // seqs
    turns = blocks // each
    span = length // HEADS
    all_conv = pl.ds(0, 5 * dim)
    if spot is not None:
        d_tokens = d_mixer
        d_mixer, x_send, x_recv, own = arrived

        def block_of(seq, mate):
            return d_mixer.at[pl.ds(pl.multiple_of(seq * length + mate * span, span), span)]

        def columns_of(seq, mate):
            return d_tokens.at[seq, :, pl.ds(pl.multiple_of(mate * dim, dim), dim)]

        def from_mate(seq, mate, slot):
            return remote(
                columns_of(seq, mate), block_of(seq, mate), x_send.at[seq, slot],
                x_recv.at[seq, slot], spot.to_mate(mate),
            )

        def from_self(seq):
            return pltpu.make_async_copy(
                columns_of(seq, spot.mate), block_of(seq, spot.mate), own.at[seq]
            )

        for seq in range(seqs):
            next(
                team_exchange(
                    spot, functools.partial(columns_of, seq), functools.partial(block_of, seq),
                    x_send.at[seq], x_recv.at[seq], own.at[seq],
                )
            )

    def spots(step):
        return [
            seq * blocks + blocks - 1 - step * each - k for k in range(each) for seq in range(seqs)
        ]

    def first(step, gain_sum):
        units = spots(step)
        kept = []
        if spot is not None:
            mates = each * STRETCH // span
            for k in range(mates):
                origin = HEADS - 1 - step * mates - k
                slot = lax.rem(spot.mate - origin + HEADS, HEADS)

                @pl.when(slot == 0)
                def _():
                    for seq in range(seqs):
                        from_self(seq).wait()

                @pl.when(slot != 0)
                def _():
                    for seq in range(seqs):
                        from_mate(seq, origin, slot).wait_recv()

        for block in units:
            at = block
            base = pl.multiple_of(block * STRETCH, STRETCH)
            result = out[pl.ds(base, STRETCH)]
            gate = proj[pl.ds(base, STRETCH), pl.ds(5 * dim, dim)]
            given = d_mixer[pl.ds(base, STRETCH)].astype(jnp.float32)
            scale = lax.rsqrt(jnp.mean(result * result, axis=1, keepdims=True) + EPS)
            normal = result * scale
            open_ = sigmoid(gate)
            silu = gate * open_
            gain_sum = gain_sum + jnp.sum(given * normal * silu, axis=0, keepdims=True)
            d_proj[pl.ds(base, STRETCH), pl.ds(5 * dim, dim)] = low(
                given * normal * gain[...] * (open_ * (1.0 + gate * (1.0 - open_)))
            )
            inner = given * gain[...] * silu
            d_result = scale * (inner - normal * jnp.mean(inner * normal, axis=1, keepdims=True))
            d_out[at] = d_result
            pre = convolve(window(proj, halo, length, base, pl.ds(0, 3 * dim)), conv[:, : 3 * dim])
            act = pre * sigmoid(pre)
            raw = stack(act, 1, dim)
            _, running = rates(proj[pl.ds(base, STRETCH), pl.ds(6 * dim, dim)], decay)
            kept.append((act[:, :dim], raw * unit_rows(raw), running, d_result))
        scores = [
            mul_nt(query, key) * decays(running)[1] for query, key, running, _ in kept
        ]
        d_freshes = [mul_tn(score, unit[3]) for score, unit in zip(scores, kept)]
        for block, (query, _, running, d_result), d_fresh in zip(units, kept, d_freshes):
            at = block
            chained[at] = mul_tn(
                jnp.concatenate([query * jnp.exp(running[:, 2:3]), -weights[at]], axis=0),
                jnp.concatenate([d_result, d_fresh], axis=0),
            )
        return gain_sum

    d_gain[...] = staged(
        turns, first, jnp.zeros((1, dim), jnp.float32), marks_of(plan, 0, steps)
    )

    def chain(step, carried):
        new = []
        for seq, later in enumerate(carried):
            block = seq * blocks + blocks - 1 - step
            added = chained[block]
            chained[block] = later
            new.append(mul_tn(trans[block], later) + added)
        return tuple(new)

    begin = (jnp.zeros((dim, dim), jnp.float32),) * seqs
    if linked:
        begin = tuple(end_state[seq] for seq in range(seqs))
    ended = lax.fori_loop(0, blocks, chain, begin)
    if linked:
        for seq in range(seqs):
            d_start[seq] = ended[seq]

    def last(step, sums):
        conv_sum, small_sum, *rims = sums
        units = spots(step)
        ats = units
        bases = [pl.multiple_of(block * STRETCH, STRETCH) for block in units]
        acts, keys, rate_sets = [], [], []
        for base in bases:
            pre = convolve(window(proj, halo, length, base, all_conv), conv)
            gate = sigmoid(pre)
            act = pre * gate
            raw = stack(act, 1, dim)
            unit = unit_rows(raw)
            acts.append((act, gate * (1.0 + pre * (1.0 - gate)), unit))
            keys.append(raw * unit)
            rate_sets.append(rates(proj[pl.ds(base, STRETCH), pl.ds(6 * dim, dim)], decay))
        nears = [
            mul_nt(jnp.concatenate([key, act[:, :dim]], axis=0), key)
            for (act, _, _), key in zip(acts, keys)
        ]
        masks = [decays(running) for _, running in rate_sets]
        d_freshes = [
            mul_tn(near[WIDE:] * upto, d_out[at])
            + mul(key * twice(jnp.exp(running[STRETCH - 1 :, 2:3] - running[:, 2:3])), chained[at])
            for near, (_, upto), at, key, (_, running) in zip(nears, masks, ats, keys, rate_sets)
        ]
        backs = [mul_tn(inv[at], d_fresh) for at, d_fresh in zip(ats, d_freshes)]
        reads = [
            stack(act, 3, dim) - mul(key * twice(jnp.exp(running[:, 2:3])), states[at])
            for (act, _, _), key, (_, running), at in zip(acts, keys, rate_sets, ats)
        ]
        to_state = [
            mul_nt(jnp.concatenate([beta * back, d_out[at]], axis=0), states[at])
            for (beta, _), back, at in zip(rate_sets, backs, ats)
        ]
        to_new = [
            mul_nt(jnp.concatenate([back, d_out[at]], axis=0), fresh[at])
            for back, at in zip(backs, ats)
        ]
        d_ends = [mul_nt(fresh[at], chained[at]) for at in ats]
        shaped = [-cross[:WIDE] * strict for cross, (strict, _) in zip(to_new, masks)]
        insides = [beta * a for (beta, _), a in zip(rate_sets, shaped)]
        d_nears = [cross[WIDE:] * upto for cross, (_, upto) in zip(to_new, masks)]
        towards = [
            mul(jnp.concatenate([inside, d_near], axis=0), key)
            for inside, d_near, key in zip(insides, d_nears, keys)
        ]
        away = [
            mul_tn(
                jnp.concatenate([inside, d_near], axis=0),
                jnp.concatenate([key, act[:, :dim]], axis=0),
            )
            for inside, d_near, key, (act, _, _) in zip(insides, d_nears, keys, acts)
        ]
        d_heres = []
        for k, (at, base) in enumerate(zip(ats, bases)):
            act, slope, unit = acts[k]
            query, key = act[:, :dim], keys[k]
            beta, running = rate_sets[k]
            small = proj[pl.ds(base, STRETCH), pl.ds(6 * dim, dim)]
            g = running[:, 2:3]
            end = g[STRETCH - 1 :]
            grown, to_go = jnp.exp(g), jnp.exp(end - g)
            back = backs[k]
            d_scaled, d_query_scaled = -to_state[k][:WIDE], to_state[k][WIDE:]
            with_inside = shaped[k] * nears[k][:WIDE]
            d_beta = jnp.sum(back * reads[k] + with_inside, axis=1, keepdims=True)
            gaps = beta * with_inside
            score_gaps = d_nears[k] * nears[k][WIDE:]
            d_query = towards[k][WIDE:] + d_query_scaled * grown
            from_start, from_end = d_scaled * twice(grown), d_ends[k] * twice(to_go)
            d_key = towards[k][:WIDE] + away[k] + from_start + from_end
            ended = jnp.sum(from_end * key, axis=1, keepdims=True)
            row_terms = jnp.sum(gaps + from_start * key, axis=1, keepdims=True) - ended
            col_terms = jnp.sum(gaps, axis=0, keepdims=True) + jnp.sum(
                score_gaps, axis=0, keepdims=True
            )
            col_terms = jnp.transpose(jnp.broadcast_to(col_terms, (8, WIDE)))[:, 0:1]
            row_terms = row_terms - col_terms
            d_g = (
                row_terms[:STRETCH]
                + row_terms[STRETCH:]
                + jnp.sum(score_gaps + d_query_scaled * grown * query, axis=1, keepdims=True)
            )
            d_end = jnp.sum(ended, axis=0, keepdims=True) + jnp.exp(end) * jnp.sum(
                jnp.sum(states[at] * chained[at], axis=0, keepdims=True), axis=1, keepdims=True
            )
            row, col = iotas(STRETCH, STRETCH)
            across = jnp.transpose(jnp.broadcast_to(d_g, (STRETCH, WIDE)))[:STRETCH]
            d_gamma = jnp.sum(jnp.where(row <= col, across, 0.0), axis=1, keepdims=True) + d_end
            lane = iotas(STRETCH, dim)[1]
            shifted = small + decay[1:2]
            d_soft = -jnp.exp(decay[0:1]) * d_gamma
            d_logit = d_soft * sigmoid(shifted)
            d_rate = jnp.where(lane == 0, d_beta[:STRETCH], d_beta[STRETCH:])
            open_beta = sigmoid(small)
            d_small = jnp.where(
                lane < 2,
                d_rate * open_beta * (1.0 - open_beta),
                jnp.where(lane == 2, d_logit, 0.0),
            )
            d_proj[pl.ds(base, STRETCH), pl.ds(6 * dim, dim)] = low(d_small)
            small_sum = small_sum + jnp.concatenate(
                [
                    jnp.sum(d_soft * softplus(shifted), axis=0, keepdims=True),
                    jnp.sum(d_logit, axis=0, keepdims=True),
                ],
                axis=0,
            )
            d_raw = unit * (d_key - key * jnp.sum(d_key * key, axis=1, keepdims=True))
            d_value = beta * back
            d_act = jnp.concatenate(
                [d_query, d_raw[:STRETCH], d_raw[STRETCH:], d_value[:STRETCH], d_value[STRETCH:]],
                axis=1,
            )
            d_heres.append(d_act * slope)
        for k, (base, d_here) in enumerate(zip(bases, d_heres)):
            rows = window(proj, halo, length, base, all_conv)
            first_row = 8 - (CONV - 1)
            conv_sum = conv_sum + jnp.concatenate(
                [
                    jnp.sum(
                        d_here * rows[first_row + tap : first_row + tap + STRETCH],
                        axis=0,
                        keepdims=True,
                    )
                    for tap in range(CONV)
                ],
                axis=0,
            )
            ahead = jnp.concatenate([d_here, rims[k % seqs]], axis=0)
            rims[k % seqs] = d_here[:8]
            total = None
            for tap in range(CONV):
                start = CONV - 1 - tap
                term = conv[tap : tap + 1] * ahead[start : start + STRETCH]
                total = term if total is None else total + term
            d_proj[pl.ds(base, STRETCH), all_conv] = low(total)
        return conv_sum, small_sum, *rims

    conv_sum, small_sum, *rims = staged(
        turns,
        last,
        (
            jnp.zeros((CONV, 5 * dim), jnp.float32),
            jnp.zeros((2, dim), jnp.float32),
        )
        + (jnp.zeros((8, 5 * dim), jnp.float32),) * seqs,
        marks_of(plan, 1, steps),
    )
    def unproject(step, total):
        at = pl.ds(pl.multiple_of(step * TOGETHER * STRETCH, STRETCH), TOGETHER * STRETCH)
        given = dot(d_proj[at], head[...], ((1,), (1,)))
        d_normed[at] = low(given)
        rows = tokens[at].astype(jnp.float32)
        scale = lax.rsqrt(jnp.mean(rows * rows, axis=1, keepdims=True) + EPS)
        return total + jnp.sum(given * (rows * scale), axis=0, keepdims=True)

    d_norm_gain[...] = staged(
        seqs * blocks // TOGETHER,
        unproject,
        jnp.zeros((1, tokens.shape[1]), jnp.float32),
        marks_of(plan, 2, steps),
    )
    if linked:
        for seq in range(seqs):
            d_first[seq] = rims[seq]
    d_conv[...] = conv_sum
    d_small_sums[...] = small_sum
    if spot is not None:
        for seq in range(seqs):
            for k in range(1, HEADS):
                from_mate(seq, spot.mate_off(k), k).wait_send()


def mixer_backward(
    proj, conv, decay, gain, kept, d_mixer, tokens, head, groups=0, number=None, link=(), jobs=(), plan=None
):
    seqs, length, _ = tokens.shape
    width = proj.shape[1]
    tokens = tokens.reshape(seqs * length, -1)
    dim = gain.shape[1]
    units = seqs * length // STRETCH
    f32, low_ = jnp.float32, jnp.bfloat16
    outs = [
        shape((seqs * length, width), low_),
        shape((CONV, 5 * dim), f32),
        shape((2, dim), f32),
        shape((1, dim), f32),
        shape(tokens.shape, low_),
        shape((1, tokens.shape[1]), f32),
    ]
    if link:
        outs += [shape((seqs, dim, dim), f32), shape((seqs, 8, 5 * dim), f32)]
    scratch = [pltpu.VMEM((units, STRETCH, dim), f32), pltpu.VMEM((units, dim, dim), f32)]
    if number:
        scratch += [pltpu.VMEM((seqs * length, dim), low_)]
        scratch += [dma(seqs, HEADS), dma(seqs, HEADS), dma(seqs)]

    def body(spot, ins, outs, scratch, steps):
        backward_body(bool(link), seqs, spot, ins, outs, scratch, steps, plan or {})

    return fused_call(
        body,
        [(a, IN_VMEM) for a in (proj, conv, decay, gain, *kept, d_mixer, tokens, head, *link)],
        [(a, IN_VMEM) for a in outs], scratch, jobs, groups, number, "mixer_backward", 60,
        mixer_cost(units),
    )


PROLOGUE_PLAN = (1, 0, 1, 3, 2, 0, 0, 2, 0, 2, 0, 3, 2, 3, 2)
EPILOGUE_PLAN = (
    2, 0, 2, 2, 0, 4, 2, 2, 4, 6, 5, 2, 5, 2, 2, 1, 3, 0, 2, 1, 4, 2, 6, 2, 0, 2, 0, 1, 3, 2, 2, 2, 0, 2,
    0, 2, 5, 0, 2, 1, 0, 6, 2, 2, 0, 3, 0, 1,
)
FORWARD_PLAN = {
    (0, 0): ((0, 1), (1, 1)),
    (0, 3): ((0, 1),),
    (0, 5): ((2, 1), (1, 1)),
    (1, 2): ((0, 1),),
    (1, 3): ((1, 1), (2, 1)),
    (1, 5): ((0, 1), (1, 1)),
    (1, 8): ((0, 1), (2, 1), (0, 1)),
    (2, 2): ((1, 1),),
    (2, 4): ((0, 1),),
    (2, 5): ((2, 1),),
    (2, 8): ((2, 1), (0, 1)),
}
BACKWARD_PLAN = {
    (0, 0): ((1, 1), (0, 1)),
    (0, 2): ((0, 1),),
    (0, 6): ((0, 1),),
    (0, 8): ((1, 1), (0, 1)),
    (1, 0): ((0, 1),),
    (1, 1): ((0, 1),),
    (1, 2): ((0, 1),),
    (1, 4): ((0, 1),),
    (1, 5): ((1, 1),),
    (1, 6): ((0, 1),),
    (2, 2): ((0, 1),),
    (2, 6): ((0, 1), (0, 1), (1, 1)),
    (2, 7): ((0, 1),),
}
REDUCE_PLAN = (
    1, 2, 0, 2, 2, 2, 1, 2, 2, 0, 1, 2, 1, 1, 2, 1, 1, 1, 1, 0,
)
def matmul(left, right):
    return jnp.dot(left, right, preferred_element_type=jnp.float32)


def times_transposed(left, right):
    return lax.dot_general(
        left, right, (((1,), (1,)), ((), ())), preferred_element_type=jnp.float32
    )


def transposed_times(left, right):
    return lax.dot_general(
        left, right, (((0,), (0,)), ((), ())), preferred_element_type=jnp.float32
    )


def exact(left, right):
    return jnp.einsum("sij,sjk->sik", left, right, precision=lax.Precision.HIGHEST)


def norm_scale(values):
    return lax.rsqrt(jnp.mean(values * values, axis=-1, keepdims=True) + EPS)


def norm_back(values, gain, given):
    scale = norm_scale(values)
    normal = values * scale
    inner = given * gain
    return scale * (inner - normal * jnp.mean(inner * normal, axis=-1, keepdims=True)), (
        given * normal
    )


def per_device(
    block_in,
    lengths,
    norm_gains,
    w_in,
    w_small,
    conv_weight,
    decay_log,
    decay_bias,
    out_norm_gain,
    w_out,
    gate_up_weight,
    w_down,
    out_cotangent,
):
    micro, seq_count, tokens, width = block_in.shape
    seqs = micro * seq_count
    count = lax.axis_size("ctx")
    groups = lax.axis_size("rep")
    place = lax.axis_index("ctx")
    group = lax.axis_index("rep")
    teams = count // HEADS
    head = lax.rem(place, HEADS)
    team = lax.div(place, HEADS)
    mates = peers = None
    if teams > 1:
        mates = [[t * HEADS + h for h in range(HEADS)] for t in range(teams)]
        peers = [[t * HEADS + h for t in range(teams)] for h in range(HEADS)]
    dim = width // HEADS
    length = HEADS * tokens
    rows = seqs * tokens
    kinds = 2 + 2 * STEPS
    rates_of = STEPS + 1
    f32, bf16 = jnp.float32, jnp.bfloat16

    def over_teams(array):
        if teams == 1:
            return array
        return lax.all_gather(array, "ctx", axis=0, tiled=True, axis_index_groups=peers)

    places = place * tokens + lax.broadcasted_iota(jnp.int32, (seqs, tokens), 1)
    valid = (places < lengths.reshape(seqs, 1)).astype(f32).reshape(rows, 1)
    grad_out = (out_cotangent.reshape(rows, width).astype(f32) * valid).astype(bf16)

    own = width // count
    piece = own // groups
    small_block = jnp.concatenate(
        [norm_gains.reshape(-1), conv_weight.reshape(-1)]
    )
    small_block = jnp.pad(small_block, (0, -small_block.size % 128)).reshape(-1, 128)
    (w_head,), (smalls,), (sequences,), (grad_all,) = carry(
        [
            head_job(w_in, w_small, groups),
            spread_job(small_block),
            sequences_job(block_in.reshape(seqs, tokens, width)),
            rep_gather_job(grad_out, groups),
        ],
        PROLOGUE_PLAN,
        groups,
        1,
        "prologue",
    )
    sequences = sequences.reshape(seqs, length, width)
    grad_all = grad_all.reshape(groups * rows, width)
    smalls = over_teams(smalls).reshape(count, -1)
    gains = smalls[:, : 2 * own].reshape(count, 2, own).transpose(1, 0, 2).reshape(2, width)
    gains = gains.astype(f32)
    taps_at = 2 * own
    conv_all = smalls[:, taps_at : taps_at + conv_weight.size].reshape(count, CONV, -1)
    conv_all = conv_all.transpose(1, 0, 2).reshape(CONV, kinds - 1, HEADS, dim)
    conv_head = lax.dynamic_index_in_dim(conv_all, head, 2, keepdims=False)
    conv_head = conv_head.reshape(CONV, -1).astype(f32)
    w_head = over_teams(w_head).reshape(width, -1)
    hidden_own = w_down.shape[0] // groups
    hidden_units = count * hidden_own
    out_piece = lax.dynamic_index_in_dim(
        w_out.reshape(groups, piece, width), group, 0, keepdims=False
    )
    gate_up_part = lax.dynamic_index_in_dim(
        gate_up_weight.reshape(own, 2, count, groups, hidden_own), group, 3, keepdims=False
    ).reshape(own, -1)
    down_part = lax.dynamic_index_in_dim(
        w_down.reshape(groups, hidden_own, width), group, 0, keepdims=False
    )

    mine_only = lax.broadcasted_iota(jnp.int32, (2, HEADS), 1) == head
    decay = jnp.where(mine_only, jnp.stack([decay_log, decay_bias]), 0.0).sum(axis=1, keepdims=True)
    decay = jnp.broadcast_to(decay, (2, dim))
    gain = out_norm_gain.reshape(1, dim)
    head_args = (sequences, gains[:1], w_head, conv_head, decay, gain)
    link = ()
    if teams > 1:
        onward = [(c, c + HEADS) for c in range(count - HEADS)]
        tail = sequences[:, length - 8 :].reshape(seqs * 8, width).astype(f32)
        tail = (tail * norm_scale(tail) * gains[0]).astype(bf16)
        halo = lax.ppermute(matmul(tail, w_head), "ctx", onward)
        start = jnp.zeros((seqs, dim, dim), f32)
        (*_, offset, transfer), _ = mixer_forward(*head_args, link=(halo, start))
        spans = lax.all_gather((transfer, offset), "ctx", axis_index_groups=peers)
        for turn in range(teams - 1):
            start = jnp.where(turn < team, exact(spans[0][turn], start) + spans[1][turn], start)
        link = (halo, start)
    (proj, h_flat, *kept), given = mixer_forward(
        *head_args, groups, 2, link,
        [
            team_gather_job(out_piece, groups, twofold=True),
            team_gather_job(gate_up_part),
            team_gather_job(down_part),
        ],
        FORWARD_PLAN,
    )
    (w_out_full,), (gate_up_part,), (down_part,) = given
    mixer = kept[-1].reshape(rows, width)
    kept = kept[:6]
    w_out_full = over_teams(w_out_full).reshape(width, width)
    gate_up_part = over_teams(gate_up_part).reshape(width, 2 * hidden_units)
    inputs = block_in.reshape(rows, width).astype(f32)
    resid = inputs + matmul(mixer, w_out_full)

    def team_share(grad):
        grad = grad.astype(bf16)
        if teams == 1:
            return grad
        return lax.psum_scatter(
            grad, "ctx", scatter_dimension=0, tiled=True, axis_index_groups=peers
        )

    h_second = (resid * norm_scale(resid) * gains[1]).astype(bf16)
    ((h_all,),) = carry([rep_gather_job(h_second, groups)], (), groups, 3, "gather_copies")
    h_all = h_all.reshape(groups * rows, width)
    down_part = over_teams(down_part).reshape(hidden_units, width)
    gate_up = matmul(h_all, gate_up_part)
    gate, up = gate_up[:, :hidden_units], gate_up[:, hidden_units:]
    open_gate = jax.nn.sigmoid(gate)
    silu = gate * open_gate
    hidden = (silu * up).astype(bf16)
    d_hidden = times_transposed(grad_all, down_part)
    d_gate_up = jnp.concatenate(
        [d_hidden * up * (open_gate * (1.0 + gate * (1.0 - open_gate))), d_hidden * silu], axis=1
    ).astype(bf16)
    d_second = times_transposed(d_gate_up, gate_up_part).astype(bf16)
    grad_down = team_share(transposed_times(hidden, grad_all)).reshape(HEADS, hidden_own, width)
    (d_second,), (grad_down,), (grad_gate_up,) = carry(
        [
            rep_reduce_job(d_second.reshape(groups, rows, width), groups),
            team_reduce_job(grad_down, 1, 2, bf16),
            product_job(h_all, d_gate_up),
        ],
        REDUCE_PLAN,
        groups,
        4,
        "reduce_copies",
    )
    down_parts = matmul(hidden, down_part).astype(bf16).reshape(groups, rows, width)
    d_norm, gain_terms_second = norm_back(resid, gains[1], d_second)
    d_resid = grad_out.astype(f32) + d_norm
    d_branch = d_resid.astype(bf16)
    grad_out_proj = transposed_times(mixer, d_branch)
    d_mixer = times_transposed(d_branch, w_out_full).astype(bf16).reshape(seqs, tokens, width)

    grad_gate_up = team_share(grad_gate_up).reshape(HEADS, own, -1)
    grad_out_proj = team_share(grad_out_proj).reshape(HEADS, groups, piece, width)

    link = ()
    if teams > 1:
        later = jnp.zeros((seqs, dim, dim), f32)
        heads_own = lax.all_to_all(
            d_mixer.reshape(rows, HEADS, dim).transpose(1, 0, 2),
            "ctx", 0, 0, tiled=True, axis_index_groups=mates,
        )
        heads_own = heads_own.reshape(HEADS, seqs, tokens, dim).transpose(1, 0, 2, 3)
        local = mixer_backward(
            proj, conv_head, decay, gain, kept, heads_own.reshape(seqs * length, dim), sequences,
            w_head, link=(halo, later),
        )[0][6]
        locals_ = lax.all_gather(local, "ctx", axis_index_groups=peers)
        for turn in range(teams - 1, 0, -1):
            later = jnp.where(
                turn > team,
                exact(spans[0][turn].transpose(0, 2, 1), later) + locals_[turn],
                later,
            )
        link = (halo, later)
    (d_proj, grad_conv, small_sums, grad_gain, d_first, gain_sum, *rims), given = mixer_backward(
        proj, conv_head, decay, gain, kept, d_mixer, sequences, w_head, groups, 5, link,
        [
            team_reduce_job(grad_gate_up, 2, 3, bf16),
            both_reduce_job(grad_out_proj, groups),
        ],
        BACKWARD_PLAN,
    )
    (grad_gate_up,), (grad_out_proj,) = given
    if teams > 1:
        rim = lax.ppermute(rims[1], "ctx", [(c, c - HEADS) for c in range(HEADS, count)])
        spill = jnp.zeros((seqs, CONV - 1, kinds * dim - dim), f32)
        for ahead in range(1, CONV):
            spill = spill.at[:, CONV - 1 - ahead :].add(
                conv_head[CONV - 1 - ahead] * rim[:, :ahead]
            )
        d_proj = d_proj.reshape(seqs, length, -1)
        end = d_proj[:, length - CONV + 1 :, : (kinds - 1) * dim]
        d_proj = d_proj.at[:, length - CONV + 1 :, : (kinds - 1) * dim].set(
            (end.astype(f32) + spill).astype(bf16)
        )
        d_proj = d_proj.reshape(seqs * length, -1)
        d_first = times_transposed(d_proj, w_head)
        normal = sequences.reshape(seqs * length, width).astype(f32)
        gain_sum = (d_first * (normal * norm_scale(normal))).sum(axis=0)
        d_first = d_first.astype(bf16)

    grad_small = transposed_times(d_proj[:, kinds * dim : kinds * dim + 8], h_flat)
    packed = jnp.concatenate(
        [
            jnp.stack([gain_sum.reshape(width), gain_terms_second.sum(axis=0)]).reshape(-1, dim),
            grad_small[:rates_of].reshape(-1, dim),
            grad_conv.reshape(-1, dim),
            grad_gain,
            small_sums[:, STEPS : STEPS + 1] + jnp.zeros((1, dim), f32),
        ]
    )
    packed = jnp.pad(packed, ((0, -packed.shape[0] % 8), (0, 0)))
    factors = [h_flat, d_proj]
    if teams > 1:
        grad_head = team_share(transposed_times(h_flat, d_proj[:, : kinds * dim]))
        factors = [grad_head.reshape(HEADS, groups, piece, kinds * dim)]
    if teams > 1:
        packed = lax.psum(packed, "ctx", axis_index_groups=peers)
    (grad_in,), (packed,), (d_first,), (grad_gate_up,), (grad_down,), (grad_out_proj,), (down,) = carry(
        [
            deal_job(factors, (HEADS, groups, piece, kinds * dim), groups),
            small_job(packed, groups),
            tokens_job(d_first.reshape(seqs, HEADS, tokens, width), 2),
            rep_gather_job(grad_gate_up, groups, IN_VMEM),
            rep_gather_job(grad_down, groups, IN_VMEM),
            rep_gather_job(grad_out_proj, groups, IN_VMEM),
            rep_reduce_job(down_parts, groups),
        ],
        EPILOGUE_PLAN,
        groups,
        6,
        "epilogue",
    )
    d_inputs, _ = norm_back(inputs, gains[0], d_first.reshape(rows, width))
    in_grad = (d_resid + d_inputs).astype(bf16)
    result = (valid * (resid + down)).astype(bf16)
    grad_in = grad_in.reshape(own, -1)
    grad_gate_up = weave(grad_gate_up, hidden_own)
    grad_down = grad_down.reshape(groups * hidden_own, width)
    grad_out_proj = grad_out_proj.reshape(own, width)

    def take(size):
        nonlocal packed
        part, packed = packed[:, :size], packed[:, size:]
        return part

    grad_gains = take(2 * HEADS).sum(axis=0).reshape(2, width)
    grad_small = take(rates_of * HEADS).reshape(HEADS, rates_of, width)
    grad_small = grad_small.transpose(2, 1, 0).reshape(width, rates_of * HEADS)
    grad_conv = take(CONV * (kinds - 1)).reshape(HEADS, CONV, kinds - 1, dim)
    grad_conv = grad_conv.transpose(1, 2, 0, 3).reshape(CONV, (kinds - 1) * width)
    grad_gain = take(1).sum(axis=0).reshape(dim)
    decays_sum = take(2)[:, :, 0].transpose(1, 0)

    def mine(array, axis, size):
        return lax.dynamic_slice_in_dim(array, place * size, size, axis)

    grad_gains = mine(grad_gains, 1, own)
    grad_small = mine(grad_small, 0, own)
    grad_conv = mine(grad_conv, 1, conv_weight.shape[1])
    return (
        result.reshape(block_in.shape),
        in_grad.reshape(block_in.shape),
        grad_gains,
        grad_in.astype(f32),
        grad_small,
        grad_conv,
        decays_sum[0],
        decays_sum[1],
        grad_gain,
        grad_out_proj.astype(f32),
        grad_gate_up.astype(f32),
        grad_down.astype(f32),
    )


def solution(mesh):
    placed = (
        P(None, "rep", "ctx", None),
        P(None, "rep"),
        P(None, "ctx"),
        P("ctx", None),
        P("ctx", None),
        P(None, "ctx"),
        P(),
        P(),
        P(),
        P("ctx", None),
        P("ctx", None),
        P("ctx", None),
        P(None, "rep", "ctx", None),
    )
    return jax.shard_map(
        per_device,
        mesh=mesh,
        in_specs=placed,
        out_specs=(
            P(None, "rep", "ctx", None),
            P(None, "rep", "ctx", None),
            P(None, "ctx"),
            P("ctx", None),
            P("ctx", None),
            P(None, "ctx"),
            P(),
            P(),
            P(),
            P("ctx", None),
            P("ctx", None),
            P("ctx", None),
        ),
        check_vma=False,
    )
```
